32 devices in a mesh: row: 2 (over x), col: 16 (over z, y, core).
Axes of the slice: x: 2, y: 2, z: 4, core: 2. Of those that a mesh axis runs over, the one named last changes fastest.
Arguments:
- tokens: bfloat16 [4096, 1024], P(('row', 'col')), may hold values from -6 to 6
- variate_ids: int32 [4096], P(('row', 'col')), may hold values from 0 to 3
- time_ids: int32 [4096], P(('row', 'col')), may hold values from 0 to 1023
- lengths: int32 [2, 6], P('row'), may hold values from 1 to 8, 16 in all within a row
- deal: int32 [2, 16, 16], P('row', 'col'), may hold values from 0 to 15, each once within a row
- w_qkv: bfloat16 [1024, 3072], P(('row', 'col')), may hold values from -0.1875 to 0.1875
- w_out: bfloat16 [1024, 1024], P(('row', 'col')), may hold values from -3 to 3
- w_gate_up: bfloat16 [1024, 8192], P(('row', 'col')), may hold values from -0.1875 to 0.1875
- w_down: bfloat16 [4096, 1024], P(('row', 'col')), may hold values from -0.09375 to 0.09375
- gain_attn: bfloat16 [1024], P(('row', 'col')), may hold values from 0.5 to 1.5
- gain_ffn: bfloat16 [1024], P(('row', 'col')), may hold values from 0.5 to 1.5
- var_bias: float32 [2, 16], replicated, may hold values from -3 to 3
- cotangent: bfloat16 [4096, 1024], P(('row', 'col')), may hold values from -6 to 6
Outputs:
- output: bfloat16 [4096, 1024], P(('row', 'col'))
- grad_tokens: bfloat16 [4096, 1024], P(('row', 'col'))
- grad_w_qkv: float32 [1024, 3072], P(('row', 'col'))
- grad_w_out: float32 [1024, 1024], P(('row', 'col'))
- grad_w_gate_up: float32 [1024, 8192], P(('row', 'col'))
- grad_w_down: float32 [4096, 1024], P(('row', 'col'))
- grad_gain_attn: float32 [1024], P(('row', 'col'))
- grad_gain_ffn: float32 [1024], P(('row', 'col'))
- grad_var_bias: float32 [2, 16], replicated
The draws below stay inside these ranges and needn't reach their ends.
All inputs are finite; a program needn't handle non-finite values.
Results may differ from the reference program's by a relative error of at most 0.018.
The reference program's roundings to bfloat16 on the way count: a program that leaves them out, or rounds other values in their place, can miss the bound.
Values may be sent and summed in bfloat16 or wider, within the bound.
A program may use at most 320 MiB of HBM per device.

```python
import math
from functools import partial
import jax
import jax.numpy as jnp
import numpy as np
from jax import lax

D = 1024
FF = 4096
HEAD_DIM = 64
HEADS = 16
TOK_DEV = 128
UNIT = 128
GROUP = 2048
UNITS_GRP = 16
LONG = 8
NSEQ = 6
TOKENS = 4096
N_ROW = 2
N_COL = 16


def plant(values, stream_key, low, high):
    longest = values.shape.index(max(values.shape))
    spots = []
    for shift in (0, 1):
        where = [jax.random.randint(jax.random.fold_in(stream_key, axis), (), 0, length) for axis, length in enumerate(values.shape)]
        where[longest] = (where[longest] + shift) % values.shape[longest]
        spots.append(tuple(where))
    return values.at[spots[0]].set(low).at[spots[1]].set(high)


def raised(array, own_key, source, target, parts, factor):
    def block_of(axis_at):
        return (jnp.arange(array.shape[axis_at]) // (array.shape[axis_at] // parts)).reshape((-1,) + (1,) * (array.ndim - 1 - axis_at))

    near = jax.random.permutation(own_key, parts)[block_of(target)]
    other_side = (block_of(target) + parts // 2) % parts
    return jnp.where((block_of(source) == near) | (block_of(source) == other_side), factor * array, array)


def shard_levels(stream_key, extent, pieces, least, top_value):
    loudness, own = 1.0, jax.random.fold_in(stream_key, 6)
    for axis_at, shards_of in pieces:
        draws = jnp.exp(jax.random.uniform(jax.random.fold_in(own, axis_at), (shards_of,), jnp.float32, least / len(pieces), top_value / len(pieces)))
        loudness = loudness * jnp.repeat(draws, extent[axis_at] // shards_of).reshape([-1 if axis == axis_at else 1 for axis in range(len(extent))])
    return loudness


def profile(amount, total, limit, lean):
    weights = [(1 << 20) // math.isqrt(grade ** lean) + 1 for grade in range(2, amount + 1)]
    spare, given = total - limit - (amount - 1), [1] * (amount - 1)
    while spare > 0:
        free = [i for i in range(amount - 1) if given[i] < limit]
        whole, budget = sum([weights[i] for i in free]), spare
        for i in free:
            addition = min(limit - given[i], max(1, budget * weights[i] // whole), spare)
            given[i] = given[i] + addition
            spare = spare - addition
    return np.array([limit] + given)


def uneven(key, amount, total, bound, lean):
    if amount == 2:
        one = jax.random.randint(key, (), max(1, total - bound), min(bound, total - 1) + 1)
        return jnp.stack([one, total - one])
    tallies = jnp.asarray(profile(amount, total, bound, lean), jnp.int32)
    pairs = (amount - 1) // 2
    source_of, receiver = tallies[1:1 + 2 * pairs:2], tallies[2:2 + 2 * pairs:2]
    slack = jnp.minimum(source_of - 1, bound - receiver)
    passed = jax.random.randint(jax.random.fold_in(key, 1), (pairs,), 0, 1 << 20) % (slack + 1)
    tallies = tallies.at[1:1 + 2 * pairs:2].set(source_of - passed).at[2:2 + 2 * pairs:2].set(receiver + passed)
    return tallies[jax.random.permutation(jax.random.fold_in(key, 2), amount)]


def bell_draw(rng, extent, spread, reach, cuts=(), held_as=jnp.bfloat16):
    array = jax.random.normal(rng, extent, jnp.float32) * spread
    if len(cuts) > 0:
        array = shard_levels(rng, extent, cuts, -0.22, 0.18) * array
    return jnp.clip(array, min=-reach, max=reach).astype(held_as)


def gaussian_with(key, extent, deviation, reach, pieces, heavy, kind=jnp.bfloat16):
    entries = deviation * jax.random.normal(key, extent, jnp.float32)
    if pieces:
        entries = entries * shard_levels(key, extent, pieces, -0.22, 0.18)
    return jnp.clip(raised(entries, jax.random.fold_in(key, 3), *heavy), -reach, reach).astype(kind)


def setup_inputs(seed: int = 0) -> dict:
    keys = jax.random.split(jax.random.key(seed), 14)
    return {
        "tokens": bell_draw(keys[0], (TOKENS, D), 1.0, 6.0, ((0, 32),)),
        "variate_ids": plant(jax.random.randint(keys[1], (TOKENS,), 0, 4), jax.random.fold_in(keys[1], 1), 0, 3).astype(jnp.int32),
        "time_ids": plant(jax.random.randint(keys[2], (TOKENS,), 0, 1024), jax.random.fold_in(keys[2], 1), 0, 1023).astype(jnp.int32),
        "lengths": jax.vmap(lambda own: uneven(own, NSEQ, UNITS_GRP, LONG, 2))(jax.random.split(keys[3], N_ROW)).reshape((N_ROW, NSEQ)).astype(jnp.int32),
        "deal": jax.vmap(lambda own: jax.random.permutation(own, N_COL))(jax.random.split(keys[4], N_ROW * N_COL)).reshape((N_ROW, N_COL, N_COL)).astype(jnp.int32),
        "w_qkv": bell_draw(keys[5], (D, 3 * D), D ** -0.5, 0.1875, ((0, 32),)),
        "w_out": bell_draw(keys[6], (D, D), (max(1, D * 8 // GROUP)) ** -0.5, 3.0, ((0, 32),)),
        "w_gate_up": bell_draw(keys[7], (D, 2 * FF), D ** -0.5, 0.1875, ((0, 32),)),
        "w_down": bell_draw(keys[8], (FF, D), FF ** -0.5, 0.09375, ((0, 32),)),
        "gain_attn": jnp.clip(1.0 + 0.1 * jax.random.normal(keys[9], (D,), jnp.float32), 0.5, 1.5).astype(jnp.bfloat16),
        "gain_ffn": jnp.clip(1.0 + 0.1 * jax.random.normal(keys[10], (D,), jnp.float32), 0.5, 1.5).astype(jnp.bfloat16),
        "var_bias": bell_draw(keys[11], (2, HEADS), 1.0, 3.0, (), jnp.float32),
        "cotangent": gaussian_with(keys[12], (TOKENS, D), 1.0, 6.0, ((0, 32),), (0, 1, 32, 2.75)),
    }


@jax.custom_vjp
def low(v):
    return lax.optimization_barrier(v.astype(jnp.bfloat16)).astype(jnp.float32)

@jax.custom_vjp
def low_back(v):
    return v

def low_keep(v):
    return (low(v), None)

def low_pass(kept, grad):
    return (grad,)

def back_keep(v):
    return (v, None)

def back_low(kept, grad):
    return (low(grad),)
low.defvjp(low_keep, low_pass)
low_back.defvjp(back_keep, back_low)
epsilon = 1e-05

def matmul(operand, factor):
    return jnp.dot(operand, factor, precision=lax.Precision.HIGHEST, preferred_element_type=jnp.float32)

def normalize(values):
    return values * lax.rsqrt(lax.optimization_barrier(jnp.mean(values * values, axis=-1, keepdims=True)) + epsilon)

def angles(time_ids):
    half_dim = HEAD_DIM // 2
    inverse_freq = jnp.exp(-math.log(10000.0) * jnp.arange(half_dim, dtype=jnp.float32) / half_dim)
    phases = time_ids.astype(jnp.float32)[:, None] * inverse_freq[None, :]
    return (jnp.cos(phases)[:, None, :], jnp.sin(phases)[:, None, :])

def rotate(tensor, cos_part, sin_part):
    half_dim = tensor.shape[-1] // 2
    former = tensor[..., :half_dim]
    latter = tensor[..., half_dim:]
    return jnp.concatenate([former * cos_part - latter * sin_part, latter * cos_part + former * sin_part], axis=-1)

def attend(queries, query_seq, query_var, keys_all, values_all, key_seq, key_var, var_bias):
    scores = low_back(jnp.einsum('qhd,khd->hqk', queries, keys_all, precision=lax.Precision.HIGHEST))
    matched = query_var[:, None] == key_var[None, :]
    scores = scores * 0.125 + jnp.where(matched[None], var_bias[0][:, None, None], var_bias[1][:, None, None])
    within = query_seq[:, None] == key_seq[None, :]
    weights = jnp.where(within[None], jnp.exp(scores), 0.0)
    denominator = lax.optimization_barrier(jnp.sum(weights, axis=-1))
    numerator = low_back(jnp.einsum('hqk,khd->qhd', low(weights), values_all, precision=lax.Precision.HIGHEST))
    return numerator / denominator.T[:, :, None]

def group_layer(tokens_f, w_qkv, w_out, w_gate_up, w_down, gain_attn, gain_ffn, var_bias, seq_ids, var_ids, cos_part, sin_part):
    group_size = tokens_f.shape[0]
    model_width = tokens_f.shape[1]
    head_count = model_width // HEAD_DIM
    scaled_one = low(normalize(tokens_f) * gain_attn)
    projected = low_back(matmul(scaled_one, w_qkv))
    shaped = projected.reshape(group_size, 3, head_count, HEAD_DIM)
    queries = low(rotate(shaped[:, 0], cos_part, sin_part))
    keys_all = low(rotate(shaped[:, 1], cos_part, sin_part))
    values_all = low(shaped[:, 2])
    stride = min(512, group_size)

    def one_span(number):
        offset = number * stride
        return attend(lax.dynamic_slice_in_dim(queries, offset, stride, 0), lax.dynamic_slice_in_dim(seq_ids, offset, stride, 0), lax.dynamic_slice_in_dim(var_ids, offset, stride, 0), keys_all, values_all, seq_ids, var_ids, var_bias)
    attended = lax.map(jax.checkpoint(one_span), jnp.arange(group_size // stride, dtype=jnp.int32))
    attn_low = low(attended.reshape(group_size, model_width))
    hidden_state = tokens_f + low_back(matmul(attn_low, w_out))
    scaled_two = low(normalize(hidden_state) * gain_ffn)
    gate_up = low_back(matmul(scaled_two, w_gate_up))
    hidden_units = w_down.shape[0]
    inner_act = low(jax.nn.silu(gate_up[:, :hidden_units]) * gate_up[:, hidden_units:])
    return hidden_state + low_back(matmul(inner_act, w_down))

def reference(tokens, variate_ids, time_ids, lengths, deal, w_qkv, w_out, w_gate_up, w_down, gain_attn, gain_ffn, var_bias, cotangent):
    group_size = N_COL * TOK_DEV
    piece_len = TOK_DEV // N_COL
    model_width = tokens.shape[1]
    places = jnp.arange(group_size, dtype=jnp.int32)
    source = (places // TOK_DEV).astype(jnp.int32)
    piece_num = (places % TOK_DEV // piece_len).astype(jnp.int32)
    in_piece = (places % piece_len).astype(jnp.int32)
    weights_f = (w_qkv.astype(jnp.float32), w_out.astype(jnp.float32), w_gate_up.astype(jnp.float32), w_down.astype(jnp.float32), gain_attn.astype(jnp.float32), gain_ffn.astype(jnp.float32), var_bias.astype(jnp.float32))

    def one_group(totals, batch):
        tokens_g, cotangent_g, variate_g, time_g, lengths_g, deal_g = batch
        bounds = (jnp.cumsum(lengths_g) * UNIT).astype(jnp.int32)
        seq_ids = lax.optimization_barrier(jnp.sum((places[:, None] >= bounds[None, :]).astype(jnp.int32), axis=1)).astype(jnp.int32)
        dealt = (deal_g[source, piece_num] * TOK_DEV + source * piece_len + in_piece).astype(jnp.int32)
        cos_part, sin_part = angles(time_g)
        layer = partial(group_layer, seq_ids=seq_ids, var_ids=variate_g, cos_part=cos_part, sin_part=sin_part)
        result, pullback = jax.vjp(layer, tokens_g.astype(jnp.float32), *weights_f)
        grads = pullback(cotangent_g.astype(jnp.float32)[dealt])
        inverse = jnp.argsort(dealt).astype(jnp.int32)
        totals = tuple((before + after for before, after in zip(totals, grads[1:])))
        return (totals, (result[inverse].astype(jnp.bfloat16), grads[0].astype(jnp.bfloat16)))
    batches = (tokens.reshape(N_ROW, group_size, model_width), cotangent.reshape(N_ROW, group_size, model_width), variate_ids.reshape(N_ROW, group_size), time_ids.reshape(N_ROW, group_size), lengths, deal)
    start_totals = tuple((jnp.zeros_like(matrix) for matrix in weights_f))
    totals, outputs = lax.scan(one_group, start_totals, batches)
    output = outputs[0].reshape(N_ROW * group_size, model_width)
    grad_tokens = outputs[1].reshape(N_ROW * group_size, model_width)
    return (output, grad_tokens, totals[0], totals[1], totals[2], totals[3], totals[4], totals[5], totals[6])
```

```python
import math

import jax
import jax.numpy as jnp
from jax import lax
from jax.experimental import pallas as pl
from jax.experimental.pallas import tpu as pltpu
from jax.sharding import PartitionSpec as P

HEAD_DIM = 64
UNIT = 128
KEY_BLOCK = 1024
NSEQ = 6


epsilon = 1e-05


def contract_rows(operand, factor):
    return lax.dot_general(
        operand, factor, (((0,), (0,)), ((), ())), preferred_element_type=jnp.float32
    )


def contract_cols(operand, factor):
    return lax.dot_general(
        operand, factor, (((1,), (1,)), ((), ())), preferred_element_type=jnp.float32
    )


def angles(time_ids):
    half_dim = HEAD_DIM // 2
    inverse_freq = jnp.exp(-math.log(10000.0) * jnp.arange(half_dim, dtype=jnp.float32) / half_dim)
    phases = time_ids.astype(jnp.float32)[:, None] * inverse_freq[None, :]
    return (jnp.cos(phases)[:, None, :], jnp.sin(phases)[:, None, :])


def rotate(tensor, cos_part, sin_part):
    half_dim = tensor.shape[-1] // 2
    former = tensor[..., :half_dim]
    latter = tensor[..., half_dim:]
    return jnp.concatenate(
        [former * cos_part - latter * sin_part, latter * cos_part + former * sin_part], axis=-1
    )


def unrotate(tensor, cos_part, sin_part):
    half_dim = tensor.shape[-1] // 2
    former = tensor[..., :half_dim]
    latter = tensor[..., half_dim:]
    return jnp.concatenate(
        [former * cos_part + latter * sin_part, latter * cos_part - former * sin_part], axis=-1
    )


def norm_scale(values):
    return lax.rsqrt(jnp.mean(values * values, axis=-1, keepdims=True) + epsilon)


def norm_back(d_normed, normed, scale):
    return scale * (d_normed - normed * jnp.mean(d_normed * normed, axis=-1, keepdims=True))


def score_weights(queries, query_seq, query_var, key_block, seq_block, var_block, var_bias):
    scores = (
        jnp.einsum("qhd,khd->hqk", queries, key_block, preferred_element_type=jnp.float32) * 0.125
    )
    matched = query_var[:, None] == var_block[None, :]
    scores = scores + jnp.where(
        matched[None], var_bias[0][:, None, None], var_bias[1][:, None, None]
    )
    within = query_seq[:, None] == seq_block[None, :]
    return (jnp.where(within[None], jnp.exp(scores), 0.0), matched)


def shards(
    tokens,
    variate_ids,
    time_ids,
    lengths,
    deal,
    w_qkv,
    w_out,
    w_gate_up,
    w_down,
    gain_attn,
    gain_ffn,
    var_bias,
    cotangent,
):
    tok_rows, model_width = tokens.shape
    n_col = lax.axis_size("col")
    col_index = lax.axis_index("col")
    piece_len = tok_rows // n_col
    head_count = model_width // HEAD_DIM
    bounds = jnp.cumsum(lengths[0]) * UNIT
    position = col_index * tok_rows + jnp.arange(tok_rows, dtype=jnp.int32)
    seq_own = jnp.sum((position[:, None] >= bounds[None, :]).astype(jnp.int32), axis=1)
    target = deal[0, 0]
    slots = jnp.arange(n_col, dtype=jnp.int32)
    inverse = jnp.sum(
        slots[:, None] * (target[:, None] == slots[None, :]).astype(jnp.int32), axis=0
    )
    send_rows = jnp.take(tokens.reshape(n_col, piece_len, model_width), inverse, axis=0)
    labels = jnp.stack(
        [
            seq_own.reshape(n_col, piece_len),
            variate_ids.reshape(n_col, piece_len),
            time_ids.reshape(n_col, piece_len),
        ],
        axis=1,
    )
    send_labels = jnp.take(labels, inverse, axis=0)
    got_rows, got_labels = (
        lax.all_to_all(send_rows, "col", split_axis=0, concat_axis=0, tiled=True),
        lax.all_to_all(send_labels, "col", split_axis=0, concat_axis=0, tiled=True),
    )
    inputs = got_rows.reshape(tok_rows, model_width).astype(jnp.float32)
    seq_q = got_labels[:, 0, :].reshape(tok_rows)
    var_q = got_labels[:, 1, :].reshape(tok_rows)
    cos_part, sin_part = angles(got_labels[:, 2, :].reshape(tok_rows))
    qkv_full, out_full, gate_up_full, down_full, gain_one, gain_two = (
        lax.all_gather(w_qkv, ("row", "col"), axis=0, tiled=True),
        lax.all_gather(w_out, ("row", "col"), axis=0, tiled=True),
        lax.all_gather(w_gate_up, ("row", "col"), axis=0, tiled=True),
        lax.all_gather(w_down, ("row", "col"), axis=0, tiled=True),
        lax.all_gather(gain_attn, ("row", "col"), axis=0, tiled=True),
        lax.all_gather(gain_ffn, ("row", "col"), axis=0, tiled=True),
    )
    scale_one = norm_scale(inputs)
    normed_one = inputs * scale_one
    scaled_one = (normed_one * gain_one.astype(jnp.float32)).astype(jnp.bfloat16)
    projected = jnp.dot(scaled_one, qkv_full, preferred_element_type=jnp.float32)
    shaped = projected.reshape(tok_rows, 3, head_count, HEAD_DIM)
    queries = rotate(shaped[:, 0], cos_part, sin_part).astype(jnp.bfloat16)
    key_own = (
        rotate(shaped[:, 1], cos_part, sin_part).astype(jnp.bfloat16).reshape(tok_rows, model_width)
    )
    value_own = projected[:, 2 * model_width :].astype(jnp.bfloat16)
    keys_all, values_all, seq_k, var_k = (
        lax.all_gather(key_own, "col", axis=0, tiled=True),
        lax.all_gather(value_own, "col", axis=0, tiled=True),
        lax.all_gather(seq_q, "col", axis=0, tiled=True),
        lax.all_gather(var_q, "col", axis=0, tiled=True),
    )
    group_size = keys_all.shape[0]
    stride = min(KEY_BLOCK, group_size)
    block_count = group_size // stride

    def split_blocks(key_rows, value_rows, key_seq, key_var):
        return (
            key_rows.reshape(block_count, stride, head_count, HEAD_DIM),
            value_rows.reshape(block_count, stride, head_count, HEAD_DIM),
            key_seq.reshape(block_count, stride),
            key_var.reshape(block_count, stride),
        )

    def forward_step(running, block_data):
        denominator, numerator = running
        key_block, value_block, seq_block, var_block = block_data
        weights = score_weights(queries, seq_q, var_q, key_block, seq_block, var_block, var_bias)[0]
        denominator = denominator + jnp.sum(weights, axis=-1)
        numerator = numerator + jnp.einsum(
            "hqk,khd->qhd",
            weights.astype(jnp.bfloat16),
            value_block,
            preferred_element_type=jnp.float32,
        )
        return ((denominator, numerator), None)

    (denominator, numerator), unused = lax.scan(
        forward_step,
        (
            jnp.zeros((head_count, tok_rows), jnp.float32),
            jnp.zeros((tok_rows, head_count, HEAD_DIM), jnp.float32),
        ),
        split_blocks(keys_all, values_all, seq_k, var_k),
    )
    attended = numerator / denominator.T[:, :, None]
    attn_low = attended.reshape(tok_rows, model_width).astype(jnp.bfloat16)
    hidden_state = inputs + jnp.dot(attn_low, out_full, preferred_element_type=jnp.float32)
    scale_two = norm_scale(hidden_state)
    normed_two = hidden_state * scale_two
    scaled_two = (normed_two * gain_two.astype(jnp.float32)).astype(jnp.bfloat16)
    gate_up = jnp.dot(scaled_two, gate_up_full, preferred_element_type=jnp.float32)
    hidden_units = gate_up_full.shape[1] // 2
    gate_part = gate_up[:, :hidden_units]
    upper_part = gate_up[:, hidden_units:]
    sigmoid_gate = jax.nn.sigmoid(gate_part)
    active = gate_part * sigmoid_gate
    inner_act = (active * upper_part).astype(jnp.bfloat16)
    ffn_branch = jnp.dot(inner_act, down_full, preferred_element_type=jnp.float32)
    output = (hidden_state + ffn_branch).astype(jnp.bfloat16)
    qkv_back, out_back, gate_up_back, down_back, gain_one_back, gain_two_back = (
        lax.all_gather(w_qkv, ("row", "col"), axis=0, tiled=True),
        lax.all_gather(w_out, ("row", "col"), axis=0, tiled=True),
        lax.all_gather(w_gate_up, ("row", "col"), axis=0, tiled=True),
        lax.all_gather(w_down, ("row", "col"), axis=0, tiled=True),
        lax.all_gather(gain_attn, ("row", "col"), axis=0, tiled=True),
        lax.all_gather(gain_ffn, ("row", "col"), axis=0, tiled=True),
    )
    d_inner = contract_cols(cotangent, down_back)
    d_gate = (
        d_inner * upper_part * sigmoid_gate * (1.0 + gate_part * (1.0 - sigmoid_gate))
    ).astype(jnp.bfloat16)
    d_upper = (d_inner * active).astype(jnp.bfloat16)
    d_gate_up = jnp.concatenate([d_gate, d_upper], axis=1)
    d_scaled_two = contract_cols(d_gate_up, gate_up_back)
    term_gain_two = jnp.sum(d_scaled_two * normed_two, axis=0)
    term_gate_up = contract_rows(scaled_two, d_gate_up)
    term_down = contract_rows(inner_act, cotangent)
    d_hidden = cotangent.astype(jnp.float32) + norm_back(
        d_scaled_two * gain_two_back.astype(jnp.float32), normed_two, scale_two
    )
    d_branch = d_hidden.astype(jnp.bfloat16)
    term_out = contract_rows(attn_low, d_branch)
    d_attended = contract_cols(d_branch, out_back).reshape(tok_rows, head_count, HEAD_DIM)
    d_numerator = (d_attended / denominator.T[:, :, None]).astype(jnp.bfloat16)
    centre = (jnp.sum(d_attended * attended, axis=-1) / denominator.T).T
    back_keys = (
        lax.all_gather(key_own, "col", axis=0, tiled=True),
        lax.all_gather(value_own, "col", axis=0, tiled=True),
        lax.all_gather(seq_q, "col", axis=0, tiled=True),
        lax.all_gather(var_q, "col", axis=0, tiled=True),
    )

    def query_step(running, block_data):
        d_queries, same_sum, other_sum = running
        key_block, value_block, seq_block, var_block = block_data
        weights, matched = score_weights(
            queries, seq_q, var_q, key_block, seq_block, var_block, var_bias
        )
        d_probs = jnp.einsum(
            "qhd,khd->hqk", d_numerator, value_block, preferred_element_type=jnp.float32
        )
        d_scores = weights * (d_probs - centre[:, :, None])
        same_sum = same_sum + jnp.sum(jnp.where(matched[None], d_scores, 0.0), axis=(1, 2))
        other_sum = other_sum + jnp.sum(jnp.where(matched[None], 0.0, d_scores), axis=(1, 2))
        d_rounded = d_scores.astype(jnp.bfloat16)
        d_queries = d_queries + jnp.einsum(
            "hqk,khd->qhd", d_rounded, key_block, preferred_element_type=jnp.float32
        )
        return ((d_queries, same_sum, other_sum), (d_rounded, weights.astype(jnp.bfloat16)))

    def query_and_key_step(running, block_data):
        running, rounded = query_step(running, block_data)
        d_rounded, weights_low = rounded
        d_keys = (
            jnp.einsum("hqk,qhd->khd", d_rounded, queries, preferred_element_type=jnp.float32)
            * 0.125
        )
        d_values = jnp.einsum(
            "hqk,qhd->khd", weights_low, d_numerator, preferred_element_type=jnp.float32
        )
        return (running, (d_keys, d_values))

    start_running = (
        jnp.zeros((tok_rows, head_count, HEAD_DIM), jnp.float32),
        jnp.zeros((head_count,), jnp.float32),
        jnp.zeros((head_count,), jnp.float32),
    )
    (d_queries, same_sum, other_sum), (d_keys, d_values) = lax.scan(
        query_and_key_step,
        start_running,
        split_blocks(back_keys[0], back_keys[1], back_keys[2], back_keys[3]),
    )
    key_grad, value_grad = (
        lax.psum_scatter(
            d_keys.reshape(group_size, model_width).astype(jnp.bfloat16),
            "col",
            scatter_dimension=0,
            tiled=True,
        ).astype(jnp.float32),
        lax.psum_scatter(
            d_values.reshape(group_size, model_width).astype(jnp.bfloat16),
            "col",
            scatter_dimension=0,
            tiled=True,
        ).astype(jnp.float32),
    )
    d_query_pre = unrotate(d_queries * 0.125, cos_part, sin_part).reshape(tok_rows, model_width)
    d_key_pre = unrotate(
        key_grad.reshape(tok_rows, head_count, HEAD_DIM), cos_part, sin_part
    ).reshape(tok_rows, model_width)
    d_projected = jnp.concatenate([d_query_pre, d_key_pre, value_grad], axis=1).astype(jnp.bfloat16)
    d_scaled_one = contract_cols(d_projected, qkv_back)
    term_qkv = contract_rows(scaled_one, d_projected)
    term_gain_one = jnp.sum(d_scaled_one * normed_one, axis=0)
    grad_w_qkv, grad_w_out, grad_w_gate_up, grad_w_down, grad_gain_attn, grad_gain_ffn = (
        lax.psum_scatter(term_qkv, ("row", "col"), scatter_dimension=0, tiled=True),
        lax.psum_scatter(term_out, ("row", "col"), scatter_dimension=0, tiled=True),
        lax.psum_scatter(term_gate_up, ("row", "col"), scatter_dimension=0, tiled=True),
        lax.psum_scatter(term_down, ("row", "col"), scatter_dimension=0, tiled=True),
        lax.psum_scatter(term_gain_one, ("row", "col"), scatter_dimension=0, tiled=True),
        lax.psum_scatter(term_gain_two, ("row", "col"), scatter_dimension=0, tiled=True),
    )
    grad_var_bias = lax.psum(jnp.stack([same_sum, other_sum], axis=0), ("row", "col"))
    d_inputs = d_hidden + norm_back(
        d_scaled_one * gain_one_back.astype(jnp.float32), normed_one, scale_one
    )
    returned = lax.all_to_all(
        d_inputs.astype(jnp.bfloat16).reshape(n_col, piece_len, model_width),
        "col",
        split_axis=0,
        concat_axis=0,
        tiled=True,
    )
    grad_tokens = jnp.take(returned, target, axis=0).reshape(tok_rows, model_width)
    return (
        output,
        grad_tokens,
        grad_w_qkv,
        grad_w_out,
        grad_w_gate_up,
        grad_w_down,
        grad_gain_attn,
        grad_gain_ffn,
        grad_var_bias,
    )


PLANES = 4
QUAD = 4
MEMBERS = 8
WINDOW = 512
AUG = 128
f32 = jnp.float32
bf16 = jnp.bfloat16
VM = pl.BlockSpec(memory_space=pltpu.VMEM)
SM = pl.BlockSpec(memory_space=pltpu.SMEM)


def mm(a, b):
    return lax.dot_general(a, b, (((1,), (0,)), ((), ())), preferred_element_type=f32)


def mm_nt(a, b):
    return lax.dot_general(a, b, (((1,), (1,)), ((), ())), preferred_element_type=f32)


def mm_tn(a, b):
    return lax.dot_general(a, b, (((0,), (0,)), ((), ())), preferred_element_type=f32)


def flip(value, bits):
    for bit in (1, 2, 4, 8, 16):
        if bits & bit:
            value = value + bit * (1 - 2 * ((value // bit) % 2))
    return value


def places():
    row = lax.axis_index("row")
    col = lax.axis_index("col")
    return row, col, col // QUAD, row * QUAD + col % QUAD


def in_plane(row, col, bits):
    return flip(row, bits // QUAD), flip(col, bits % QUAD)


def on_line(row, col, bits):
    return row, flip(col, bits * QUAD)


def anyone(row, col, bits):
    return flip(row, bits // 16), flip(col, bits % 16)


def push(source, target, send, recv, device):
    return pltpu.make_async_remote_copy(
        src_ref=source,
        dst_ref=target,
        send_sem=send,
        recv_sem=recv,
        device_id={"row": device[0], "col": device[1]},
        device_id_type=pl.DeviceIdType.MESH,
    )


def meet(devices):
    barrier = pltpu.get_barrier_semaphore()
    for device in devices:
        pl.semaphore_signal(
            barrier,
            1,
            device_id={"row": device[0], "col": device[1]},
            device_id_type=pl.DeviceIdType.MESH,
        )
    pl.semaphore_wait(barrier, len(devices))


NEAR = (2, 4, 6, 1)


def plane_near(row, col):
    return [in_plane(row, col, bits) for bits in NEAR]


def line_all(row, col):
    return [on_line(row, col, bits) for bits in (1, 2, 3)]


def gather_start(source, target, send, recv, row, col, place):
    copies = {}
    for bits in NEAR:
        copies[bits] = push(
            source, target.at[place], send.at[bits], recv.at[bits], in_plane(row, col, bits)
        )
        copies[bits].start()
    return copies


def gather_finish(copies, target, send, recv, row, col, place):
    onward = []
    for bits in (2, 4, 6):
        copies[bits].wait_recv()
        slot = target.at[flip(place, bits)]
        copy = push(slot, slot, send.at[bits + 1], recv.at[bits + 1], in_plane(row, col, 1))
        copy.start()
        onward.append(copy)
    copies[1].wait_recv()
    for copy in onward:
        copy.wait_recv()
    for copy in list(copies.values()) + onward:
        copy.wait_send()


def scatter_start(part, inbox, send, recv, row, col):
    other = 1 - col % 2
    copies = []
    for i in range(4):
        copy = push(
            part.at[2 * i + other], inbox.at[i], send.at[i], recv.at[i], in_plane(row, col, 1)
        )
        copy.start()
        copies.append(copy)
    return copies


def scatter_middle(copies, part, inbox, outbox, second, send, recv, row, col, place):
    core = col % 2
    for copy in copies:
        copy.wait_recv()
    sent = []
    for bits in (1, 2, 3):
        i = flip(place // 2, bits)
        outbox[bits - 1] = (part[2 * i + core].astype(f32) + inbox[i].astype(f32)).astype(bf16)
        copy = push(
            outbox.at[bits - 1],
            second.at[bits - 1],
            send.at[3 + bits],
            recv.at[3 + bits],
            in_plane(row, col, 2 * bits),
        )
        copy.start()
        sent.append(copy)
    return sent


def scatter_finish(copies, sent, part, inbox, second, place):
    for copy in sent:
        copy.wait_recv()
    total = part[place].astype(f32) + inbox[place // 2].astype(f32)
    for i in range(3):
        total = total + second[i].astype(f32)
    for copy in copies + sent:
        copy.wait_send()
    return total


def scatter_scratch(rows, width):
    return [
        pltpu.VMEM((4, rows, width), bf16),
        pltpu.VMEM((3, rows, width), bf16),
        pltpu.VMEM((3, rows, width), bf16),
        pltpu.SemaphoreType.DMA((7,)),
        pltpu.SemaphoreType.DMA((7,)),
    ]


def gather_body(
    x, wq, wo, wg, cot, tile,
    xp, wqp, wop, wgp, cotr, tiles, gains, times, labels,
    wqs, wgs, sx, rx, sq, rq, st, rt, sw, rw, sg, rg, sc, rc,
):
    row, col, z, place = places()
    me = row * 16 + col
    meet([anyone(row, col, bits) for bits in range(1, 32)])
    for p in range(MEMBERS):
        for part in range(3):
            wqs[p, :, part * 128 : part * 128 + 128] = wq[
                :, part * 1024 + p * 128 : part * 1024 + p * 128 + 128
            ]
    first = gather_start(x, xp, sx, rx, row, col, place)
    spread = []
    for bits in range(1, 32):
        there = anyone(row, col, bits)
        member = there[0] * QUAD + there[1] % QUAD
        copy = push(wqs.at[member], wqp.at[me], sq.at[bits], rq.at[bits], there)
        copy.start()
        spread.append(copy)
        copy = push(tile, tiles.at[me], st.at[bits], rt.at[bits], there)
        copy.start()
        spread.append(copy)
    xp[place] = x[...]
    wqp[me] = wqs[place]
    tiles[me] = tile[...]
    for p in range(MEMBERS):
        for half in range(2):
            for plane in range(PLANES):
                unit = (p // QUAD) * 16 + plane * QUAD + p % QUAD
                at = half * 512 + plane * 128
                start = half * 4096 + unit * 128
                wgs[p, :, at : at + 128] = wg[:, start : start + 128]
    for bits in range(1, 8):
        there = in_plane(row, col, bits)
        copy = push(wgs.at[flip(place, bits)], wgp.at[place], sg.at[bits], rg.at[bits], there)
        copy.start()
        spread.append(copy)
    wgp[place] = wgs[place]
    for bits in range(1, 16):
        there = (row, flip(col, bits))
        copy = push(cot.at[there[1]], cotr.at[col], sc.at[bits], rc.at[bits], there)
        copy.start()
        spread.append(copy)
    cotr[col] = cot[col]
    quarter = col % QUAD
    for plane in range(PLANES):
        there = (row, plane * QUAD + z)
        mine = jnp.logical_and(z == plane, quarter == z)

        @pl.when(jnp.logical_not(mine))
        def _():
            push(wo, wop.at[quarter], sw.at[plane], rw.at[quarter], there).start()

        @pl.when(mine)
        def _():
            wop[quarter] = wo[...]

    gather_finish(first, xp, sx, rx, row, col, place)
    for copy in spread:
        copy.wait_recv()
    for j in range(4):
        mine = jnp.logical_and(quarter == z, quarter == j)

        @pl.when(jnp.logical_not(mine))
        def _():
            push(wo, wop.at[j], sw.at[j], rw.at[j], (row, quarter * QUAD + j)).wait_recv()

    for k in range(8):
        lanes = slice(k * 128, k * 128 + 128)
        gains[:, lanes] = (tiles[4 * k] + tiles[4 * k + 1]) + (tiles[4 * k + 2] + tiles[4 * k + 3])
        times[:, lanes] = tiles[(k // QUAD) * 16 + z * QUAD + k % QUAD]
    for k in range(16):
        labels[:, k * 128 : k * 128 + 128] = tiles[(z // 2) * 16 + k]
    for copy in spread:
        copy.wait_send()
    for plane in range(PLANES):
        there = (row, plane * QUAD + z)
        mine = jnp.logical_and(z == plane, quarter == z)

        @pl.when(jnp.logical_not(mine))
        def _():
            push(wo, wop.at[quarter], sw.at[plane], rw.at[quarter], there).wait_send()


def project_body(
    xp, wqp, gains, times, freq, cot,
    s1, qkvt, cotp,
    wt, box, cs, sn, sa, ra, sz, rz,
):
    row, col, z, place = places()
    meet(plane_near(row, col) + line_all(row, col))
    first = gather_start(cot, cotp, sa, ra, row, col, place)
    cotp[place] = cot[...]
    wt[...] = jnp.transpose(wqp[...])
    phases = times[3:4, :] * freq[...]
    cs[...] = jnp.cos(phases)
    sn[...] = jnp.sin(phases)
    gain = gains[0:1, :]

    def step(t, unused):
        rows = pl.ds(pl.multiple_of(t * 256, 256), 256)
        values = xp[rows, :].astype(f32)
        normed = values * norm_scale(values)
        scaled = (normed * gain).astype(bf16)
        s1[rows, :] = scaled
        out = mm_nt(wt[...], scaled)
        cos_part, sin_part = cs[:, rows], sn[:, rows]
        lanes = pl.ds(pl.multiple_of((t % 2) * 256, 256), 256)
        for head in range(2):
            pair = (t // 2) * 2 + head
            for part in range(2):
                base = part * 128 + head * 64
                former, latter = out[base : base + 32], out[base + 32 : base + 64]
                factor = 0.125 if part == 0 else 1.0
                turned = former * cos_part - latter * sin_part
                other = latter * cos_part + former * sin_part
                box[pair, part * 64 : part * 64 + 32, lanes] = (turned * factor).astype(bf16)
                box[pair, part * 64 + 32 : part * 64 + 64, lanes] = (other * factor).astype(bf16)
            box[pair, 128:192, lanes] = out[256 + head * 64 : 256 + head * 64 + 64].astype(bf16)
        return unused

    lax.fori_loop(0, 4, step, 0)
    mine = pl.ds(pl.multiple_of(z * 512, 512), 512)
    copies = []
    for bits in (3, 2, 1):
        copy = push(
            box.at[flip(z, bits)], qkvt.at[:, mine], sz.at[bits], rz.at[bits], on_line(row, col, bits)
        )
        copy.start()
        copies.append(copy)
    qkvt[:, mine] = box[z]
    gather_finish(first, cotp, sa, ra, row, col, place)
    for copy in copies:
        copy.wait()


def split_three(value):
    high = value.astype(bf16).astype(f32)
    middle = (value - high).astype(bf16).astype(f32)
    return high, middle, (value - high - middle).astype(bf16).astype(f32)


def window_queries(qa, lanes, first, limit):
    place = first + lax.broadcasted_iota(jnp.int32, (16, WINDOW), 1)
    line = lax.broadcasted_iota(jnp.int32, (16, WINDOW), 0)
    extra = jnp.where(
        jnp.logical_and(line == 12, place >= limit), -1e30, qa[64:80, lanes].astype(f32)
    )
    return jnp.concatenate(
        [qa[0:64, lanes], extra.astype(bf16), jnp.zeros((AUG - 80, WINDOW), bf16)], axis=0
    )


def attend_body(info, bias, qkvt, labels, att, den, low, qa, ka, kt):
    size = qkvt.shape[1]
    variate = labels[2:3, :]
    line = lax.broadcasted_iota(jnp.int32, (16, size), 0)
    same = (variate == (line % 4).astype(f32)).astype(f32)
    same_pieces = split_three(jnp.full((16, size), bias[0] - bias[1], f32))
    other_pieces = split_three(jnp.full((16, size), bias[1], f32))

    def choose(pieces, number):
        return jnp.where(number == 0, pieces[0], jnp.where(number == 1, pieces[1], pieces[2]))

    extra_q = jnp.where(line < 12, same, jnp.where(line == 12, 0.0, 1.0))
    extra_k = jnp.where(
        line < 12,
        same * choose(same_pieces, line // 4),
        jnp.where(line == 12, 1.0, choose(other_pieces, line - 13)),
    )
    qa[0:64, 0:size] = qkvt[0:64, :]
    qa[64:80, 0:size] = extra_q.astype(bf16)
    qa[80:AUG, 0:size] = jnp.zeros((AUG - 80, size), bf16)
    qa[:, size:] = jnp.zeros((AUG, WINDOW), bf16)
    kt[0:64, :] = qkvt[64:128, :]
    kt[64:80, :] = extra_k.astype(bf16)
    kt[80:AUG, :] = jnp.zeros((AUG - 80, size), bf16)
    ka[...] = jnp.transpose(kt[...])

    def sequence(number, start):
        length = info[number]
        limit = (start + length) * 128

        def window(j, unused):
            first = (start + 4 * j) * 128
            lanes = pl.ds(pl.multiple_of(first, 128), WINDOW)
            queries = window_queries(qa, lanes, first, limit)

            def key(k, running):
                total, numerator = running
                rows = pl.ds(pl.multiple_of((start + k) * 128, 128), 128)
                weights = jnp.exp(mm(ka[rows, :], queries))
                total = total + jnp.sum(weights, axis=0, keepdims=True)
                numerator = numerator + mm(qkvt[128:192, rows], weights.astype(bf16))
                return total, numerator

            total, numerator = lax.fori_loop(
                0, length, key, (jnp.zeros((1, WINDOW), f32), jnp.zeros((64, WINDOW), f32))
            )
            attended = numerator / total
            att[:, lanes] = attended
            den[:, lanes] = jnp.broadcast_to(total, (8, WINDOW))
            low[:, lanes] = attended.astype(bf16)
            return unused

        lax.fori_loop(0, (length + 3) // 4, window, 0)
        return start + length

    lax.fori_loop(0, NSEQ, sequence, 0)


def attend_back_body(
    info, qkvt, qa, ka, labels, freq, grad, att, den,
    dproj, bias_tile,
    dn, cw, vn, dq, dk, dv,
):
    size = qkvt.shape[1]
    lanes_all = slice(0, size)
    inverse = 1.0 / den[0:1, lanes_all]
    d_att = grad[...].astype(f32)
    dn[:, lanes_all] = (d_att * inverse).astype(bf16)
    dn[:, size:] = jnp.zeros((64, WINDOW), bf16)
    cw[:, lanes_all] = jnp.broadcast_to(
        jnp.sum(d_att * att[:, lanes_all], axis=0, keepdims=True) * inverse, (8, size)
    )
    cw[:, size:] = jnp.zeros((8, WINDOW), f32)
    vn[...] = jnp.transpose(qkvt[128:192, :])
    dk[...] = jnp.zeros_like(dk)
    dv[...] = jnp.zeros_like(dv)

    def sequence(number, start):
        length = info[number]
        limit = (start + length) * 128

        def window(j, unused):
            first = (start + 4 * j) * 128
            lanes = pl.ds(pl.multiple_of(first, 128), WINDOW)
            queries = window_queries(qa, lanes, first, limit)
            upstream = dn[:, lanes]
            centre = cw[0:1, lanes]

            def key(k, running):
                rows = pl.ds(pl.multiple_of((start + k) * 128, 128), 128)
                weights = jnp.exp(mm(ka[rows, :], queries))
                d_scores = weights * (mm(vn[rows, :], upstream) - centre)
                rounded = d_scores.astype(bf16)
                dk[:, rows] += mm_nt(queries, rounded)
                dv[:, rows] += mm_nt(upstream, weights.astype(bf16))
                return running + mm(qkvt[64:128, rows], rounded)

            dq[:, lanes] = lax.fori_loop(0, length, key, jnp.zeros((64, WINDOW), f32))
            return unused

        lax.fori_loop(0, (length + 3) // 4, window, 0)
        return start + length

    lax.fori_loop(0, NSEQ, sequence, 0)
    phases = labels[3:4, :] * freq[...]
    cos_part, sin_part = jnp.cos(phases), jnp.sin(phases)
    for part, source, factor in ((0, dq, 0.125), (1, dk, 1.0)):
        former, latter = source[0:32, lanes_all], source[32:64, lanes_all]
        dproj[part * 64 : part * 64 + 32, :] = (
            (former * cos_part + latter * sin_part) * factor
        ).astype(bf16)
        dproj[part * 64 + 32 : part * 64 + 64, :] = (
            (latter * cos_part - former * sin_part) * factor
        ).astype(bf16)
    dproj[128:192, :] = dv[...].astype(bf16)
    variate = labels[2:3, :]
    line = lax.broadcasted_iota(jnp.int32, (16, size), 0)
    match = jnp.logical_and(variate == line.astype(f32), line < 4)
    near = jnp.sum(jnp.where(match, dk[64:80, :], 0.0))
    every = jnp.sum(dk[77:78, :])
    lane = lax.broadcasted_iota(jnp.int32, (8, 128), 1)
    line8 = lax.broadcasted_iota(jnp.int32, (8, 128), 0)
    here = lane == info[NSEQ]
    bias_tile[...] = jnp.where(
        jnp.logical_and(here, line8 == 2),
        near,
        jnp.where(jnp.logical_and(here, line8 == 3), every - near, 0.0),
    )


def branch_body(
    low, wop, x, gains,
    atp, hidden, s2p,
    atn, part, mine, sz, rz, inbox, outbox, second, ss, rs, sa, ra,
):
    row, col, z, place = places()
    meet(plane_near(row, col) + line_all(row, col))
    rows = pl.ds(pl.multiple_of((z % 2) * 64, 64), 64)
    lanes = pl.ds(pl.multiple_of((z // 2) * 512, 512), 512)
    copies = []
    for bits in (3, 2, 1):
        theirs = pl.ds(pl.multiple_of(flip(z, bits) * 512, 512), 512)
        copy = push(
            low.at[:, theirs], atp.at[rows, lanes], sz.at[bits], rz.at[bits], on_line(row, col, bits)
        )
        copy.start()
        copies.append(copy)
    atp[rows, lanes] = low[:, pl.ds(pl.multiple_of(z * 512, 512), 512)]
    for copy in copies:
        copy.wait()
    atn[...] = jnp.transpose(atp[...])
    for q in range(MEMBERS):
        part[q] = mm(atn[q * 128 : q * 128 + 128, :], wop[...]).astype(bf16)
    first = scatter_start(part, inbox, ss, rs, row, col)
    sent = scatter_middle(first, part, inbox, outbox, second, ss, rs, row, col, place)
    total = scatter_finish(first, sent, part, inbox, second, place)
    state = x[...].astype(f32) + total
    hidden[...] = state
    mine[...] = (state * norm_scale(state) * gains[1:2, :]).astype(bf16)
    spread = gather_start(mine, s2p, sa, ra, row, col, place)
    s2p[place] = mine[...]
    gather_finish(spread, s2p, sa, ra, row, col, place)


def ffn_body(s2, cot, wg, wd, out_part, d_part, gwd, gwg, wgs, inner_s, dgu):
    for plane in range(PLANES):
        for r in range(2):
            at = (r * PLANES + plane) * 128
            wgs[at : at + 128, :] = wg[plane * 2 + r]

    def step(t, unused):
        rows = pl.ds(pl.multiple_of(t * 256, 256), 256)
        both = mm(s2[rows, :], wgs[...])
        gate, upper = both[:, 0:512], both[:, 512:1024]
        sig = jax.nn.sigmoid(gate)
        active = gate * sig
        inner = (active * upper).astype(bf16)
        inner_s[rows, :] = inner
        out_part[rows, :] = mm(inner, wd[...]).astype(bf16)
        d_inner = mm_nt(cot[rows, :], wd[...])
        dgu[rows, 0:512] = (d_inner * upper * sig * (1.0 + gate * (1.0 - sig))).astype(bf16)
        dgu[rows, 512:1024] = (d_inner * active).astype(bf16)
        d_part[rows, :] = mm_nt(dgu[rows, :], wgs[...]).astype(bf16)
        return unused

    lax.fori_loop(0, 4, step, 0)
    for k in range(2):
        cols = slice(k * 256, k * 256 + 256)
        gwd[cols, :] = mm_tn(inner_s[:, cols], cot[...]).astype(bf16)
    for f in range(8):
        cols = slice(f * 128, f * 128 + 128)
        gwg[(f % PLANES) * 2 + f // PLANES] = mm_tn(s2[:, cols], dgu[...]).astype(bf16)


def hidden_back_body(
    d_part, out_part, cot, hidden, gains, wop, atp,
    grad, d_hidden, out, gwo, gain_term,
    low, dbp, dat, ia, oa, na, sa, ra, ib, ob, nb, sb, rb, sg, rg, sz, rz,
):
    row, col, z, place = places()
    meet(plane_near(row, col) + line_all(row, col))
    first = scatter_start(d_part, ia, sa, ra, row, col)
    sent = scatter_middle(first, d_part, ia, oa, na, sa, ra, row, col, place)
    d_scaled = scatter_finish(first, sent, d_part, ia, na, place)
    state = hidden[...]
    scale = norm_scale(state)
    normed = state * scale
    gain_term[...] = jnp.broadcast_to(jnp.sum(d_scaled * normed, axis=0, keepdims=True), (8, 1024))
    d_state = cot[...].astype(f32) + norm_back(d_scaled * gains[1:2, :], normed, scale)
    d_hidden[...] = d_state
    low[...] = d_state.astype(bf16)
    spread = gather_start(low, dbp, sg, rg, row, col, place)
    dbp[place] = low[...]
    other_first = scatter_start(out_part, ib, sb, rb, row, col)
    gather_finish(spread, dbp, sg, rg, row, col, place)
    for q in range(MEMBERS):
        dat[:, q * 128 : q * 128 + 128] = mm_nt(wop[...], dbp[q]).astype(bf16)
    mine = pl.ds(pl.multiple_of(z * 512, 512), 512)
    copies = []
    for bits in (3, 2, 1):
        pair = flip(z, bits)
        rows = pl.ds(pl.multiple_of((pair % 2) * 64, 64), 64)
        lanes = pl.ds(pl.multiple_of((pair // 2) * 512, 512), 512)
        copy = push(
            dat.at[rows, lanes], grad.at[:, mine], sz.at[bits], rz.at[bits], on_line(row, col, bits)
        )
        copy.start()
        copies.append(copy)
    grad[:, mine] = dat[
        pl.ds(pl.multiple_of((z % 2) * 64, 64), 64),
        pl.ds(pl.multiple_of((z // 2) * 512, 512), 512),
    ]
    other_sent = scatter_middle(other_first, out_part, ib, ob, nb, sb, rb, row, col, place)
    total = mm(atp[:, 0:128], dbp[0])
    for q in range(1, MEMBERS):
        total = total + mm(atp[:, q * 128 : q * 128 + 128], dbp[q])
    gwo[...] = total.astype(bf16)
    branch = scatter_finish(other_first, other_sent, out_part, ib, nb, place)
    out[...] = (state + branch).astype(bf16)
    for copy in copies:
        copy.wait()


def last_body(
    dproj, wqp, s1, xp, gains, d_hidden, gwo, slots, gwg, gain_two, bias_tile,
    grad_tokens, grad_q, grad_o, out, gwg_in, tile,
    dpt, dpn, part, gq, gqin, goin, pack, tiles,
    sz, rz, inbox, outbox, second, ss, rs, sq, rq, st, rt, sw, rw, sg, rg, sc, rc,
):
    row, col, z, place = places()
    me = row * 16 + col
    quarter = col % QUAD
    meet([anyone(row, col, bits) for bits in range(1, 32)])
    copies = []
    lanes = pl.ds(pl.multiple_of((z // 2) * 512, 512), 512)
    for bits in (3, 2, 1):
        theirs = pl.ds(pl.multiple_of(flip(z, bits) * 512, 512), 512)
        for kind in range(3):
            rows = pl.ds(pl.multiple_of(kind * 128 + (z % 2) * 64, 64), 64)
            copy = push(
                dproj.at[kind * 64 : kind * 64 + 64, theirs],
                dpt.at[rows, lanes],
                sz.at[bits, kind],
                rz.at[bits, kind],
                on_line(row, col, bits),
            )
            copy.start()
            copies.append(copy)
    for kind in range(3):
        rows = pl.ds(pl.multiple_of(kind * 128 + (z % 2) * 64, 64), 64)
        dpt[rows, lanes] = dproj[
            kind * 64 : kind * 64 + 64, pl.ds(pl.multiple_of(z * 512, 512), 512)
        ]
    spread = []
    for bits in range(1, 8):
        there = in_plane(row, col, bits)
        copy = push(gwg.at[flip(place, bits)], gwg_in.at[place], sg.at[bits], rg.at[bits], there)
        copy.start()
        spread.append(copy)
    gwg_in[place] = gwg[place]
    for bits in range(1, 16):
        there = (row, flip(col, bits))
        copy = push(slots.at[there[1]], out.at[col], sc.at[bits], rc.at[bits], there)
        copy.start()
        spread.append(copy)
    out[col] = slots[col]
    for j in range(4):
        there = (row, quarter * QUAD + j)
        mine = jnp.logical_and(quarter == z, quarter == j)

        @pl.when(jnp.logical_not(mine))
        def _():
            push(gwo.at[j], goin.at[z], sw.at[j], rw.at[z], there).start()

        @pl.when(mine)
        def _():
            goin[z] = gwo[j]

    for copy in copies:
        copy.wait()
    dpn[...] = jnp.transpose(dpt[...])
    gain_one = gains[0:1, :]
    term = jnp.zeros((1, 1024), f32)
    for q in range(MEMBERS):
        values = xp[q].astype(f32)
        d_scaled = mm_nt(dpn[q * 128 : q * 128 + 128, :], wqp[...])
        term = term + jnp.sum(d_scaled * (values * norm_scale(values)), axis=0, keepdims=True)
        part[q] = d_scaled.astype(bf16)
    first = scatter_start(part, inbox, ss, rs, row, col)
    for k in range(8):
        pack[k] = bias_tile[...]
        pack[k, 0:1, :] = term[:, k * 128 : k * 128 + 128]
        pack[k, 1:2, :] = gain_two[0:1, k * 128 : k * 128 + 128]
    for f in range(8):
        chunk = mm_tn(s1[:, f * 128 : f * 128 + 128], dpn[...]).astype(bf16)
        for j in range(4):
            gq[f * 4 + j] = chunk[j * 32 : j * 32 + 32, :]
    sent = scatter_middle(first, part, inbox, outbox, second, ss, rs, row, col, place)
    for bits in range(1, 32):
        there = anyone(row, col, bits)
        number = there[0] * 16 + there[1]
        copy = push(gq.at[number], gqin.at[me], sq.at[bits], rq.at[bits], there)
        copy.start()
        spread.append(copy)
        copy = push(pack.at[number // 4], tiles.at[me], st.at[bits], rt.at[bits], there)
        copy.start()
        spread.append(copy)
    gqin[me] = gq[me]
    tiles[me] = pack[me // 4]
    d_one = scatter_finish(first, sent, part, inbox, second, place)
    own = xp[place].astype(f32)
    scale = norm_scale(own)
    grad_tokens[...] = (
        d_hidden[...] + norm_back(d_one * gain_one, own * scale, scale)
    ).astype(bf16)
    for copy in spread:
        copy.wait_recv()
    for plane in range(PLANES):
        mine = jnp.logical_and(quarter == z, z == plane)

        @pl.when(jnp.logical_not(mine))
        def _():
            push(
                gwo.at[0], goin.at[plane], sw.at[plane], rw.at[plane], (row, plane * QUAD + z)
            ).wait_recv()

    grad_o[...] = (goin[0].astype(f32) + goin[1].astype(f32)) + (
        goin[2].astype(f32) + goin[3].astype(f32)
    )
    for p in range(MEMBERS):
        total = jnp.zeros((32, 384), f32)
        for plane in range(PLANES):
            total = total + gqin[(p // QUAD) * 16 + plane * QUAD + p % QUAD].astype(f32)
        for kind in range(3):
            at = kind * 1024 + p * 128
            grad_q[:, at : at + 128] = total[:, kind * 128 : kind * 128 + 128]
    total = tiles[0]
    for k in range(1, 32):
        total = total + tiles[k]
    tile[...] = total
    for copy in spread:
        copy.wait_send()
    for j in range(4):
        there = (row, quarter * QUAD + j)
        mine = jnp.logical_and(quarter == z, quarter == j)

        @pl.when(jnp.logical_not(mine))
        def _():
            push(gwo.at[j], goin.at[z], sw.at[j], rw.at[z], there).wait_send()


def sds(shape, dtype):
    return jax.ShapeDtypeStruct(shape, dtype)


def dma(*shape):
    return pltpu.SemaphoreType.DMA(shape)


def kernel(body, name, specs, outs, scratch, number=None, cost=0):
    params = dict(vmem_limit_bytes=56 << 20)
    if number is not None:
        params.update(collective_id=number, has_side_effects=True)
    return pl.pallas_call(
        body,
        name=name,
        in_specs=specs,
        out_shape=outs,
        out_specs=[VM] * len(outs),
        scratch_shapes=scratch,
        compiler_params=pltpu.CompilerParams(**params),
        cost_estimate=pl.CostEstimate(flops=cost, bytes_accessed=cost // 300, transcendentals=0),
    )


def plane_shards(
    tokens, variate_ids, time_ids, lengths, deal, w_qkv, w_out, w_gate_up, w_down,
    gain_attn, gain_ffn, var_bias, cotangent,
):
    row = lax.axis_index("row")
    col = lax.axis_index("col")
    z, q = col // QUAD, col % QUAD
    place = row * QUAD + q
    rows, width = tokens.shape
    lines = [[plane * QUAD + k for plane in range(PLANES)] for k in range(QUAD)]
    down = lax.all_gather(w_down, "col", axis=0, tiled=True, axis_index_groups=lines)
    spot = (q * 32 + jnp.arange(32, dtype=jnp.int32))[:, None] == jnp.arange(128)[None, :]
    gain_rows = jnp.sum(
        jnp.where(
            spot[None], jnp.stack([gain_attn, gain_ffn]).astype(f32)[:, :, None], 0.0
        ),
        axis=1,
    )
    tile = jnp.concatenate(
        [
            gain_rows,
            variate_ids.astype(f32)[None],
            time_ids.astype(f32)[None],
            jnp.pad(lengths[0].astype(f32), (0, 128 - lengths.shape[1]))[None],
            jnp.zeros((3, 128), f32),
        ],
        axis=0,
    )
    freq = jnp.exp(-math.log(10000.0) * jnp.arange(32, dtype=f32) / 32)[:, None]

    xp, wqp, wop, wgp, cotr, tiles, gains, times, labels = kernel(
        gather_body,
        "gather_all",
        [VM] * 6,
        [
            sds((8, rows, width), bf16),
            sds((32, 32, 384), bf16),
            sds((4, 32, 1024), bf16),
            sds((8, 32, 1024), bf16),
            sds((16, 8, width), bf16),
            sds((32, 8, 128), f32),
            sds((8, 1024), f32),
            sds((8, 1024), f32),
            sds((8, 2048), f32),
        ],
        [pltpu.VMEM((8, 32, 384), bf16), pltpu.VMEM((8, 32, 1024), bf16)]
        + [dma(8), dma(8), dma(32), dma(32), dma(32), dma(32), dma(4), dma(4)]
        + [dma(8), dma(8), dma(16), dma(16)],
        number=1,
    )(tokens, w_qkv, w_out, w_gate_up, cotangent.reshape(16, 8, width), tile)

    gate_up = lax.all_gather(
        wgp.reshape(256, 1024), "col", axis=0, tiled=True, axis_index_groups=lines
    )
    wqp = wqp.reshape(1024, 384)
    wop = wop.reshape(128, 1024)
    target = deal[0, 0]
    cot = jnp.take(cotr, target, axis=0).reshape(rows, width)

    s1, qkvt, cotp = kernel(
        project_body,
        "project",
        [VM] * 6,
        [sds((1024, width), bf16), sds((192, 2048), bf16), sds((8, rows, width), bf16)],
        [
            pltpu.VMEM((384, 1024), bf16),
            pltpu.VMEM((4, 192, 512), bf16),
            pltpu.VMEM((32, 1024), f32),
            pltpu.VMEM((32, 1024), f32),
            dma(8), dma(8), dma(4), dma(4),
        ],
        number=2,
    )(xp.reshape(1024, width), wqp, gains, times, freq, cot)

    head = place * 2 + z % 2
    info = jnp.concatenate(
        [labels[4, :NSEQ].astype(jnp.int32), head[None].astype(jnp.int32), jnp.zeros((1,), jnp.int32)]
    )
    bias = lax.dynamic_slice_in_dim(var_bias, head, 1, 1)[:, 0]
    wide = 2048 + WINDOW
    att, den, low, qa, ka = kernel(
        attend_body,
        "attend",
        [SM, SM, VM, VM],
        [
            sds((64, wide), f32),
            sds((8, wide), f32),
            sds((64, wide), bf16),
            sds((AUG, wide), bf16),
            sds((2048, AUG), bf16),
        ],
        [pltpu.VMEM((AUG, 2048), bf16)],
        cost=2 * 10**9,
    )(info, bias, qkvt, labels)

    atp, hidden, s2p = kernel(
        branch_body,
        "branch",
        [VM] * 4,
        [sds((128, 1024), bf16), sds((rows, width), f32), sds((8, rows, width), bf16)],
        [
            pltpu.VMEM((1024, 128), bf16),
            pltpu.VMEM((8, rows, width), bf16),
            pltpu.VMEM((rows, width), bf16),
            dma(4), dma(4),
        ]
        + scatter_scratch(rows, width)
        + [dma(8), dma(8)],
        number=3,
    )(low, wop, tokens, gains)

    out_part, d_part, gwd, gwg = kernel(
        ffn_body,
        "ffn",
        [VM] * 4,
        [
            sds((1024, width), bf16),
            sds((1024, width), bf16),
            sds((512, width), bf16),
            sds((8, 128, 1024), bf16),
        ],
        [
            pltpu.VMEM((1024, 1024), bf16),
            pltpu.VMEM((1024, 512), bf16),
            pltpu.VMEM((1024, 1024), bf16),
        ],
        cost=10**10,
    )(s2p.reshape(1024, width), cotp.reshape(1024, width), gate_up.reshape(8, 128, 1024), down)

    grad_down = lax.psum_scatter(
        gwd, "col", scatter_dimension=0, tiled=True, axis_index_groups=lines
    )
    gate_up_sum = lax.psum_scatter(
        gwg.reshape(1024, 1024), "col", scatter_dimension=0, tiled=True, axis_index_groups=lines
    )

    grad, d_hidden, out_rows, gwo, gain_two = kernel(
        hidden_back_body,
        "hidden_back",
        [VM] * 7,
        [
            sds((64, 2048), bf16),
            sds((rows, width), f32),
            sds((rows, width), bf16),
            sds((128, 1024), bf16),
            sds((8, 1024), f32),
        ],
        [
            pltpu.VMEM((rows, width), bf16),
            pltpu.VMEM((8, rows, width), bf16),
            pltpu.VMEM((128, 1024), bf16),
        ]
        + scatter_scratch(rows, width)
        + scatter_scratch(rows, width)
        + [dma(8), dma(8), dma(4), dma(4)],
        number=4,
    )(
        d_part.reshape(8, rows, width), out_part.reshape(8, rows, width), cot, hidden, gains, wop, atp
    )

    slot = jnp.arange(16, dtype=jnp.int32)
    inverse = jnp.sum(slot[:, None] * (target[:, None] == slot[None, :]).astype(jnp.int32), axis=0)
    slots = jnp.take(out_rows.reshape(16, 8, width), inverse, axis=0)

    dproj, bias_tile = kernel(
        attend_back_body,
        "attend_back",
        [SM] + [VM] * 8,
        [sds((192, 2048), bf16), sds((8, 128), f32)],
        [
            pltpu.VMEM((64, wide), bf16),
            pltpu.VMEM((8, wide), f32),
            pltpu.VMEM((2048, 64), bf16),
            pltpu.VMEM((64, wide), f32),
            pltpu.VMEM((AUG, 2048), f32),
            pltpu.VMEM((64, 2048), f32),
        ],
        cost=5 * 10**9,
    )(info, qkvt, qa, ka, labels, freq, grad, att, den)

    grad_tokens, grad_q, grad_o, out, gwg_in, sums = kernel(
        last_body,
        "last",
        [VM] * 11,
        [
            sds((rows, width), bf16),
            sds((32, 3072), f32),
            sds((32, 1024), f32),
            sds((16, 8, width), bf16),
            sds((8, 32, 1024), bf16),
            sds((8, 128), f32),
        ],
        [
            pltpu.VMEM((384, 1024), bf16),
            pltpu.VMEM((1024, 384), bf16),
            pltpu.VMEM((8, rows, width), bf16),
            pltpu.VMEM((32, 32, 384), bf16),
            pltpu.VMEM((32, 32, 384), bf16),
            pltpu.VMEM((4, 32, 1024), bf16),
            pltpu.VMEM((8, 8, 128), f32),
            pltpu.VMEM((32, 8, 128), f32),
            dma(4, 3), dma(4, 3),
        ]
        + scatter_scratch(rows, width)
        + [dma(32), dma(32), dma(32), dma(32), dma(4), dma(4), dma(8), dma(8), dma(16), dma(16)],
        number=5,
    )(
        dproj, wqp, s1, xp, gains, d_hidden, gwo.reshape(4, 32, 1024), slots,
        gate_up_sum.reshape(8, 32, 1024), gain_two, bias_tile,
    )
    grad_gate_up = (
        gwg_in.reshape(2, QUAD, 32, 2, PLANES, 128)
        .transpose(2, 3, 0, 4, 1, 5)
        .reshape(32, 8192)
        .astype(f32)
    )
    gain_grads = lax.dynamic_slice_in_dim(sums[0:2], q * 32, 32, 1)
    return (
        out.reshape(rows, width),
        grad_tokens,
        grad_q,
        grad_o,
        grad_gate_up,
        grad_down.astype(f32),
        gain_grads[0],
        gain_grads[1],
        sums[2:4, :16],
    )


def solution(mesh):
    planes = mesh.shape["row"] == 2 and mesh.shape["col"] == PLANES * QUAD
    return jax.shard_map(
        plane_shards if planes else shards,
        mesh=mesh,
        in_specs=(
            P(("row", "col"), None),
            P(("row", "col")),
            P(("row", "col")),
            P("row", None),
            P("row", "col", None),
            P(("row", "col"), None),
            P(("row", "col"), None),
            P(("row", "col"), None),
            P(("row", "col"), None),
            P(("row", "col")),
            P(("row", "col")),
            P(),
            P(("row", "col"), None),
        ),
        out_specs=(
            P(("row", "col"), None),
            P(("row", "col"), None),
            P(("row", "col"), None),
            P(("row", "col"), None),
            P(("row", "col"), None),
            P(("row", "col"), None),
            P(("row", "col")),
            P(("row", "col")),
            P(),
        ),
        check_vma=False,
    )
```

```python
import math

import jax
import jax.numpy as jnp
from jax import lax
from jax.experimental import pallas as pl
from jax.experimental.pallas import tpu as pltpu
from jax.sharding import PartitionSpec as P

HEAD_DIM = 64
UNIT = 128
KEY_BLOCK = 1024
NSEQ = 6


epsilon = 1e-05


def contract_rows(operand, factor):
    return lax.dot_general(
        operand, factor, (((0,), (0,)), ((), ())), preferred_element_type=jnp.float32
    )


def contract_cols(operand, factor):
    return lax.dot_general(
        operand, factor, (((1,), (1,)), ((), ())), preferred_element_type=jnp.float32
    )


def angles(time_ids):
    half_dim = HEAD_DIM // 2
    inverse_freq = jnp.exp(-math.log(10000.0) * jnp.arange(half_dim, dtype=jnp.float32) / half_dim)
    phases = time_ids.astype(jnp.float32)[:, None] * inverse_freq[None, :]
    return (jnp.cos(phases)[:, None, :], jnp.sin(phases)[:, None, :])


def rotate(tensor, cos_part, sin_part):
    half_dim = tensor.shape[-1] // 2
    former = tensor[..., :half_dim]
    latter = tensor[..., half_dim:]
    return jnp.concatenate(
        [former * cos_part - latter * sin_part, latter * cos_part + former * sin_part], axis=-1
    )


def unrotate(tensor, cos_part, sin_part):
    half_dim = tensor.shape[-1] // 2
    former = tensor[..., :half_dim]
    latter = tensor[..., half_dim:]
    return jnp.concatenate(
        [former * cos_part + latter * sin_part, latter * cos_part - former * sin_part], axis=-1
    )


def norm_scale(values):
    return lax.rsqrt(jnp.mean(values * values, axis=-1, keepdims=True) + epsilon)


def norm_back(d_normed, normed, scale):
    return scale * (d_normed - normed * jnp.mean(d_normed * normed, axis=-1, keepdims=True))


def score_weights(queries, query_seq, query_var, key_block, seq_block, var_block, var_bias):
    scores = (
        jnp.einsum("qhd,khd->hqk", queries, key_block, preferred_element_type=jnp.float32) * 0.125
    )
    matched = query_var[:, None] == var_block[None, :]
    scores = scores + jnp.where(
        matched[None], var_bias[0][:, None, None], var_bias[1][:, None, None]
    )
    within = query_seq[:, None] == seq_block[None, :]
    return (jnp.where(within[None], jnp.exp(scores), 0.0), matched)


def shards(
    tokens,
    variate_ids,
    time_ids,
    lengths,
    deal,
    w_qkv,
    w_out,
    w_gate_up,
    w_down,
    gain_attn,
    gain_ffn,
    var_bias,
    cotangent,
):
    tok_rows, model_width = tokens.shape
    n_col = lax.axis_size("col")
    col_index = lax.axis_index("col")
    piece_len = tok_rows // n_col
    head_count = model_width // HEAD_DIM
    bounds = jnp.cumsum(lengths[0]) * UNIT
    position = col_index * tok_rows + jnp.arange(tok_rows, dtype=jnp.int32)
    seq_own = jnp.sum((position[:, None] >= bounds[None, :]).astype(jnp.int32), axis=1)
    target = deal[0, 0]
    slots = jnp.arange(n_col, dtype=jnp.int32)
    inverse = jnp.sum(
        slots[:, None] * (target[:, None] == slots[None, :]).astype(jnp.int32), axis=0
    )
    send_rows = jnp.take(tokens.reshape(n_col, piece_len, model_width), inverse, axis=0)
    labels = jnp.stack(
        [
            seq_own.reshape(n_col, piece_len),
            variate_ids.reshape(n_col, piece_len),
            time_ids.reshape(n_col, piece_len),
        ],
        axis=1,
    )
    send_labels = jnp.take(labels, inverse, axis=0)
    got_rows, got_labels = (
        lax.all_to_all(send_rows, "col", split_axis=0, concat_axis=0, tiled=True),
        lax.all_to_all(send_labels, "col", split_axis=0, concat_axis=0, tiled=True),
    )
    inputs = got_rows.reshape(tok_rows, model_width).astype(jnp.float32)
    seq_q = got_labels[:, 0, :].reshape(tok_rows)
    var_q = got_labels[:, 1, :].reshape(tok_rows)
    cos_part, sin_part = angles(got_labels[:, 2, :].reshape(tok_rows))
    qkv_full, out_full, gate_up_full, down_full, gain_one, gain_two = (
        lax.all_gather(w_qkv, ("row", "col"), axis=0, tiled=True),
        lax.all_gather(w_out, ("row", "col"), axis=0, tiled=True),
        lax.all_gather(w_gate_up, ("row", "col"), axis=0, tiled=True),
        lax.all_gather(w_down, ("row", "col"), axis=0, tiled=True),
        lax.all_gather(gain_attn, ("row", "col"), axis=0, tiled=True),
        lax.all_gather(gain_ffn, ("row", "col"), axis=0, tiled=True),
    )
    scale_one = norm_scale(inputs)
    normed_one = inputs * scale_one
    scaled_one = (normed_one * gain_one.astype(jnp.float32)).astype(jnp.bfloat16)
    projected = jnp.dot(scaled_one, qkv_full, preferred_element_type=jnp.float32)
    shaped = projected.reshape(tok_rows, 3, head_count, HEAD_DIM)
    queries = rotate(shaped[:, 0], cos_part, sin_part).astype(jnp.bfloat16)
    key_own = (
        rotate(shaped[:, 1], cos_part, sin_part).astype(jnp.bfloat16).reshape(tok_rows, model_width)
    )
    value_own = projected[:, 2 * model_width :].astype(jnp.bfloat16)
    keys_all, values_all, seq_k, var_k = (
        lax.all_gather(key_own, "col", axis=0, tiled=True),
        lax.all_gather(value_own, "col", axis=0, tiled=True),
        lax.all_gather(seq_q, "col", axis=0, tiled=True),
        lax.all_gather(var_q, "col", axis=0, tiled=True),
    )
    group_size = keys_all.shape[0]
    stride = min(KEY_BLOCK, group_size)
    block_count = group_size // stride

    def split_blocks(key_rows, value_rows, key_seq, key_var):
        return (
            key_rows.reshape(block_count, stride, head_count, HEAD_DIM),
            value_rows.reshape(block_count, stride, head_count, HEAD_DIM),
            key_seq.reshape(block_count, stride),
            key_var.reshape(block_count, stride),
        )

    def forward_step(running, block_data):
        denominator, numerator = running
        key_block, value_block, seq_block, var_block = block_data
        weights = score_weights(queries, seq_q, var_q, key_block, seq_block, var_block, var_bias)[0]
        denominator = denominator + jnp.sum(weights, axis=-1)
        numerator = numerator + jnp.einsum(
            "hqk,khd->qhd",
            weights.astype(jnp.bfloat16),
            value_block,
            preferred_element_type=jnp.float32,
        )
        return ((denominator, numerator), None)

    (denominator, numerator), unused = lax.scan(
        forward_step,
        (
            jnp.zeros((head_count, tok_rows), jnp.float32),
            jnp.zeros((tok_rows, head_count, HEAD_DIM), jnp.float32),
        ),
        split_blocks(keys_all, values_all, seq_k, var_k),
    )
    attended = numerator / denominator.T[:, :, None]
    attn_low = attended.reshape(tok_rows, model_width).astype(jnp.bfloat16)
    hidden_state = inputs + jnp.dot(attn_low, out_full, preferred_element_type=jnp.float32)
    scale_two = norm_scale(hidden_state)
    normed_two = hidden_state * scale_two
    scaled_two = (normed_two * gain_two.astype(jnp.float32)).astype(jnp.bfloat16)
    gate_up = jnp.dot(scaled_two, gate_up_full, preferred_element_type=jnp.float32)
    hidden_units = gate_up_full.shape[1] // 2
    gate_part = gate_up[:, :hidden_units]
    upper_part = gate_up[:, hidden_units:]
    sigmoid_gate = jax.nn.sigmoid(gate_part)
    active = gate_part * sigmoid_gate
    inner_act = (active * upper_part).astype(jnp.bfloat16)
    ffn_branch = jnp.dot(inner_act, down_full, preferred_element_type=jnp.float32)
    output = (hidden_state + ffn_branch).astype(jnp.bfloat16)
    qkv_back, out_back, gate_up_back, down_back, gain_one_back, gain_two_back = (
        lax.all_gather(w_qkv, ("row", "col"), axis=0, tiled=True),
        lax.all_gather(w_out, ("row", "col"), axis=0, tiled=True),
        lax.all_gather(w_gate_up, ("row", "col"), axis=0, tiled=True),
        lax.all_gather(w_down, ("row", "col"), axis=0, tiled=True),
        lax.all_gather(gain_attn, ("row", "col"), axis=0, tiled=True),
        lax.all_gather(gain_ffn, ("row", "col"), axis=0, tiled=True),
    )
    d_inner = contract_cols(cotangent, down_back)
    d_gate = (
        d_inner * upper_part * sigmoid_gate * (1.0 + gate_part * (1.0 - sigmoid_gate))
    ).astype(jnp.bfloat16)
    d_upper = (d_inner * active).astype(jnp.bfloat16)
    d_gate_up = jnp.concatenate([d_gate, d_upper], axis=1)
    d_scaled_two = contract_cols(d_gate_up, gate_up_back)
    term_gain_two = jnp.sum(d_scaled_two * normed_two, axis=0)
    term_gate_up = contract_rows(scaled_two, d_gate_up)
    term_down = contract_rows(inner_act, cotangent)
    d_hidden = cotangent.astype(jnp.float32) + norm_back(
        d_scaled_two * gain_two_back.astype(jnp.float32), normed_two, scale_two
    )
    d_branch = d_hidden.astype(jnp.bfloat16)
    term_out = contract_rows(attn_low, d_branch)
    d_attended = contract_cols(d_branch, out_back).reshape(tok_rows, head_count, HEAD_DIM)
    d_numerator = (d_attended / denominator.T[:, :, None]).astype(jnp.bfloat16)
    centre = (jnp.sum(d_attended * attended, axis=-1) / denominator.T).T
    back_keys = (
        lax.all_gather(key_own, "col", axis=0, tiled=True),
        lax.all_gather(value_own, "col", axis=0, tiled=True),
        lax.all_gather(seq_q, "col", axis=0, tiled=True),
        lax.all_gather(var_q, "col", axis=0, tiled=True),
    )

    def query_step(running, block_data):
        d_queries, same_sum, other_sum = running
        key_block, value_block, seq_block, var_block = block_data
        weights, matched = score_weights(
            queries, seq_q, var_q, key_block, seq_block, var_block, var_bias
        )
        d_probs = jnp.einsum(
            "qhd,khd->hqk", d_numerator, value_block, preferred_element_type=jnp.float32
        )
        d_scores = weights * (d_probs - centre[:, :, None])
        same_sum = same_sum + jnp.sum(jnp.where(matched[None], d_scores, 0.0), axis=(1, 2))
        other_sum = other_sum + jnp.sum(jnp.where(matched[None], 0.0, d_scores), axis=(1, 2))
        d_rounded = d_scores.astype(jnp.bfloat16)
        d_queries = d_queries + jnp.einsum(
            "hqk,khd->qhd", d_rounded, key_block, preferred_element_type=jnp.float32
        )
        return ((d_queries, same_sum, other_sum), (d_rounded, weights.astype(jnp.bfloat16)))

    def query_and_key_step(running, block_data):
        running, rounded = query_step(running, block_data)
        d_rounded, weights_low = rounded
        d_keys = (
            jnp.einsum("hqk,qhd->khd", d_rounded, queries, preferred_element_type=jnp.float32)
            * 0.125
        )
        d_values = jnp.einsum(
            "hqk,qhd->khd", weights_low, d_numerator, preferred_element_type=jnp.float32
        )
        return (running, (d_keys, d_values))

    start_running = (
        jnp.zeros((tok_rows, head_count, HEAD_DIM), jnp.float32),
        jnp.zeros((head_count,), jnp.float32),
        jnp.zeros((head_count,), jnp.float32),
    )
    (d_queries, same_sum, other_sum), (d_keys, d_values) = lax.scan(
        query_and_key_step,
        start_running,
        split_blocks(back_keys[0], back_keys[1], back_keys[2], back_keys[3]),
    )
    key_grad, value_grad = (
        lax.psum_scatter(
            d_keys.reshape(group_size, model_width).astype(jnp.bfloat16),
            "col",
            scatter_dimension=0,
            tiled=True,
        ).astype(jnp.float32),
        lax.psum_scatter(
            d_values.reshape(group_size, model_width).astype(jnp.bfloat16),
            "col",
            scatter_dimension=0,
            tiled=True,
        ).astype(jnp.float32),
    )
    d_query_pre = unrotate(d_queries * 0.125, cos_part, sin_part).reshape(tok_rows, model_width)
    d_key_pre = unrotate(
        key_grad.reshape(tok_rows, head_count, HEAD_DIM), cos_part, sin_part
    ).reshape(tok_rows, model_width)
    d_projected = jnp.concatenate([d_query_pre, d_key_pre, value_grad], axis=1).astype(jnp.bfloat16)
    d_scaled_one = contract_cols(d_projected, qkv_back)
    term_qkv = contract_rows(scaled_one, d_projected)
    term_gain_one = jnp.sum(d_scaled_one * normed_one, axis=0)
    grad_w_qkv, grad_w_out, grad_w_gate_up, grad_w_down, grad_gain_attn, grad_gain_ffn = (
        lax.psum_scatter(term_qkv, ("row", "col"), scatter_dimension=0, tiled=True),
        lax.psum_scatter(term_out, ("row", "col"), scatter_dimension=0, tiled=True),
        lax.psum_scatter(term_gate_up, ("row", "col"), scatter_dimension=0, tiled=True),
        lax.psum_scatter(term_down, ("row", "col"), scatter_dimension=0, tiled=True),
        lax.psum_scatter(term_gain_one, ("row", "col"), scatter_dimension=0, tiled=True),
        lax.psum_scatter(term_gain_two, ("row", "col"), scatter_dimension=0, tiled=True),
    )
    grad_var_bias = lax.psum(jnp.stack([same_sum, other_sum], axis=0), ("row", "col"))
    d_inputs = d_hidden + norm_back(
        d_scaled_one * gain_one_back.astype(jnp.float32), normed_one, scale_one
    )
    returned = lax.all_to_all(
        d_inputs.astype(jnp.bfloat16).reshape(n_col, piece_len, model_width),
        "col",
        split_axis=0,
        concat_axis=0,
        tiled=True,
    )
    grad_tokens = jnp.take(returned, target, axis=0).reshape(tok_rows, model_width)
    return (
        output,
        grad_tokens,
        grad_w_qkv,
        grad_w_out,
        grad_w_gate_up,
        grad_w_down,
        grad_gain_attn,
        grad_gain_ffn,
        grad_var_bias,
    )


PLANES = 4
QUAD = 4
MEMBERS = 8
WINDOW = 512
AUG = 128
f32 = jnp.float32
bf16 = jnp.bfloat16
VM = pl.BlockSpec(memory_space=pltpu.VMEM)
SM = pl.BlockSpec(memory_space=pltpu.SMEM)
ANY = pl.BlockSpec(memory_space=pl.ANY)


def mm(a, b):
    return lax.dot_general(a, b, (((1,), (0,)), ((), ())), preferred_element_type=f32)


def mm_nt(a, b):
    return lax.dot_general(a, b, (((1,), (1,)), ((), ())), preferred_element_type=f32)


def mm_tn(a, b):
    return lax.dot_general(a, b, (((0,), (0,)), ((), ())), preferred_element_type=f32)


def flip(value, bits):
    for bit in (1, 2, 4, 8, 16):
        if bits & bit:
            value = value + bit * (1 - 2 * ((value // bit) % 2))
    return value


def places():
    row = lax.axis_index("row")
    col = lax.axis_index("col")
    return row, col, col // QUAD, row * QUAD + col % QUAD


def in_plane(row, col, bits):
    return flip(row, bits // QUAD), flip(col, bits % QUAD)


def on_line(row, col, bits):
    return row, flip(col, bits * QUAD)


def anyone(row, col, bits):
    return flip(row, bits // 16), flip(col, bits % 16)


def push(source, target, send, recv, device):
    return pltpu.make_async_remote_copy(
        src_ref=source,
        dst_ref=target,
        send_sem=send,
        recv_sem=recv,
        device_id={"row": device[0], "col": device[1]},
        device_id_type=pl.DeviceIdType.MESH,
    )


def meet(devices):
    barrier = pltpu.get_barrier_semaphore()
    for device in devices:
        pl.semaphore_signal(
            barrier,
            1,
            device_id={"row": device[0], "col": device[1]},
            device_id_type=pl.DeviceIdType.MESH,
        )
    pl.semaphore_wait(barrier, len(devices))


NEAR = (2, 4, 6, 1)


def plane_near(row, col):
    return [in_plane(row, col, bits) for bits in NEAR]


def line_all(row, col):
    return [on_line(row, col, bits) for bits in (1, 2, 3)]


class Gather:
    def __init__(self, target, send, recv):
        self.target, self.send, self.recv = target, send, recv
        self.row, self.col, _, self.place = places()
        self.copies, self.onward = {}, {}

    def start(self, source):
        for bits in NEAR:
            self.copies[bits] = push(
                source,
                self.target.at[self.place],
                self.send.at[bits],
                self.recv.at[bits],
                in_plane(self.row, self.col, bits),
            )
            self.copies[bits].start()

    def forward(self, bits):
        self.copies[bits].wait_recv()
        slot = self.target.at[flip(self.place, bits)]
        self.onward[bits] = push(
            slot,
            slot,
            self.send.at[bits + 1],
            self.recv.at[bits + 1],
            in_plane(self.row, self.col, 1),
        )
        self.onward[bits].start()

    def arrived(self, bits):
        (self.onward[bits] if bits else self.copies[1]).wait_recv()

    def close(self):
        for copy in list(self.copies.values()) + list(self.onward.values()):
            copy.wait_send()

    def finish(self):
        for bits in (2, 4, 6):
            self.forward(bits)
        for bits in (0, 2, 4, 6):
            self.arrived(bits)


class Scatter:
    def __init__(self, part, inbox, outbox, second, send, recv):
        self.part, self.inbox, self.outbox, self.second = part, inbox, outbox, second
        self.send, self.recv = send, recv
        self.row, self.col, _, self.place = places()
        self.core = self.col % 2
        self.copies, self.sent = [], []

    def near(self, chip, number):
        copy = push(
            self.part.at[2 * chip + 1 - self.core],
            self.inbox.at[number],
            self.send.at[number],
            self.recv.at[number],
            in_plane(self.row, self.col, 1),
        )
        copy.start()
        self.copies.append(copy)

    def far(self, bits):
        self.copies[bits].wait_recv()
        chip = flip(self.place // 2, bits)
        total = self.part[2 * chip + self.core].astype(f32) + self.inbox[bits].astype(f32)
        self.outbox[bits - 1] = total.astype(bf16)
        copy = push(
            self.outbox.at[bits - 1],
            self.second.at[bits - 1],
            self.send.at[3 + bits],
            self.recv.at[3 + bits],
            in_plane(self.row, self.col, 2 * bits),
        )
        copy.start()
        self.sent.append(copy)

    def near_all(self):
        for bits in range(4):
            self.near(flip(self.place // 2, bits), bits)

    def far_all(self):
        for bits in (3, 2, 1):
            self.far(bits)

    def finish(self):
        self.copies[0].wait_recv()
        total = self.part[self.place].astype(f32) + self.inbox[0].astype(f32)
        for copy in self.sent:
            copy.wait_recv()
        for i in range(3):
            total = total + self.second[i].astype(f32)
        return total

    def close(self):
        for copy in self.copies + self.sent:
            copy.wait_send()


def scatter_scratch(rows, width):
    return [
        pltpu.VMEM((4, rows, width), bf16),
        pltpu.VMEM((3, rows, width), bf16),
        pltpu.VMEM((3, rows, width), bf16),
        pltpu.SemaphoreType.DMA((7,)),
        pltpu.SemaphoreType.DMA((7,)),
    ]


def fetch(source, target, semaphore):
    copy = pltpu.make_async_copy(source, target, semaphore)
    copy.start()
    return copy


def block(number, size):
    return pl.ds(pl.multiple_of(number * size, size), size)


def enter_body(
    x, wq, wo, wg, cot, ga, gf, variate, time, lengths, deal, freq,
    xp_out, wqp_out, wop, wgp, cotp_out, s1_out, qkvt, gains, labels,
    xp, wqp, cotp, s1, keep, wqs, wgs, cotr, cots, tile, tl, tiles, wt, box, cs, sn, times,
    sx, rx, sq, rq, st, rt, su, ru, sw, rw, sg, rg, sc, rc, sa, ra, sz, rz,
):
    row, col, z, place = places()
    me = row * 16 + col
    quarter = col % QUAD
    lane = lax.broadcasted_iota(jnp.int32, (1, 128), 1)
    for line, gain in ((0, ga), (1, gf)):
        wide = gain[...].astype(f32)
        wide = jnp.concatenate([wide] * 4, axis=1)
        tile[line : line + 1, :] = jnp.where(lane // 32 == quarter, wide, 0.0)
    tile[2:3, :] = variate[...].astype(f32)
    tile[3:4, :] = time[...].astype(f32)
    numbers = jnp.zeros((1, 128), jnp.int32)
    for i in range(NSEQ):
        numbers = jnp.where(lane == i, lengths[0, i], numbers)
    tile[4:5, :] = numbers.astype(f32)
    tile[5:8, :] = jnp.zeros((3, 128), f32)
    meet([anyone(row, col, bits) for bits in range(1, 32)])
    rows_in = Gather(xp, sx, rx)
    rows_in.start(x)
    first = []
    for bits in (1, 2, 3):
        first.append(push(tile, tl.at[z], st.at[bits], rt.at[bits], on_line(row, col, bits)))
        first[-1].start()
    for p in range(MEMBERS):
        for part in range(3):
            at = part * 1024 + p * 128
            wqs[p, :, part * 128 : part * 128 + 128] = wq[:, at : at + 128]
    weights = []
    for bits in range(1, 32):
        there = anyone(row, col, bits)
        member = there[0] * QUAD + there[1] % QUAD
        weights.append(push(wqs.at[member], wqp.at[me], sq.at[bits], rq.at[bits], there))
        weights[-1].start()
    pieces = []
    for bits in range(1, 16):
        there = (row, flip(col, bits))
        pieces.append(push(cot.at[there[1]], cotr.at[col], sc.at[bits], rc.at[bits], there))
        pieces[-1].start()
    xp[place] = x[...]
    wqp[me] = wqs[place]
    tl[z] = tile[...]
    cotr[col] = cot[col]
    for copy in first:
        copy.wait_recv()
    second = []
    for bits in range(1, 8):
        there = in_plane(row, col, bits)
        second.append(push(tl, tiles.at[place], su.at[bits], ru.at[bits], there))
        second[-1].start()
    tiles[place] = tl[...]
    for p in range(MEMBERS):
        for half in range(2):
            for plane in range(PLANES):
                unit = (p // QUAD) * 16 + plane * QUAD + p % QUAD
                at = half * 512 + plane * 128
                start = half * 4096 + unit * 128
                wgs[p, :, at : at + 128] = wg[:, start : start + 128]
    for copy in second:
        copy.wait_recv()
    for k in range(8):
        lanes = slice(k * 128, k * 128 + 128)
        r, plane = k // PLANES, k % PLANES
        gains[:, lanes] = (tiles[r * QUAD, plane] + tiles[r * QUAD + 1, plane]) + (
            tiles[r * QUAD + 2, plane] + tiles[r * QUAD + 3, plane]
        )
        times[:, lanes] = tiles[k, z]
    for k in range(16):
        labels[:, k * 128 : k * 128 + 128] = tiles[(z // 2) * QUAD + k % QUAD, k // QUAD]
    phases = times[3:4, :] * freq[...]
    cs[...] = jnp.cos(phases)
    sn[...] = jnp.sin(phases)
    gain = gains[0:1, :]
    rows_in.finish()

    def scale(t, unused):
        values = xp[t].astype(f32)
        s1[t] = (values * norm_scale(values) * gain).astype(bf16)
        return unused

    lax.fori_loop(0, MEMBERS, scale, 0)
    kept = [fetch(xp, xp_out, keep.at[0]), fetch(s1, s1_out, keep.at[1])]
    for copy in pieces:
        copy.wait_recv()
    for j in range(16):
        cots[j * 8 : j * 8 + 8, :] = cotr[jnp.clip(deal[j], 0, 15)]
    cot_in = Gather(cotp, sa, ra)
    cot_in.start(cots)
    cotp[place] = cots[...]
    for copy in weights:
        copy.wait_recv()
    kept.append(fetch(wqp, wqp_out, keep.at[2]))
    for plane in range(PLANES):
        there = (row, plane * QUAD + z)
        mine = jnp.logical_and(z == plane, quarter == z)

        @pl.when(jnp.logical_not(mine))
        def _():
            push(wo, wop.at[quarter], sw.at[plane], rw.at[quarter], there).start()

        @pl.when(mine)
        def _():
            wop[quarter] = wo[...]

    blocks = []
    for bits in range(1, 8):
        there = in_plane(row, col, bits)
        blocks.append(
            push(wgs.at[flip(place, bits)], wgp.at[place], sg.at[bits], rg.at[bits], there)
        )
        blocks[-1].start()
    wgp[place] = wgs[place]
    for k in range(8):
        wt[:, k * 128 : k * 128 + 128] = jnp.transpose(
            jnp.concatenate([wqp[4 * k + j] for j in range(4)], axis=0)
        )
    for group in range(2):

        def project(t, unused):
            number = group * 4 + 2 * t
            rows = block(2 * group + t, 256)
            scaled = jnp.concatenate([s1[number], s1[number + 1]], axis=0)
            out = mm_nt(wt[...], scaled)
            cos_part, sin_part = cs[:, rows], sn[:, rows]
            lanes = block(t, 256)
            for head in range(2):
                pair = group * 2 + head
                for part in range(2):
                    base = part * 128 + head * 64
                    former, latter = out[base : base + 32], out[base + 32 : base + 64]
                    factor = 0.125 if part == 0 else 1.0
                    turned = former * cos_part - latter * sin_part
                    other = latter * cos_part + former * sin_part
                    at = part * 64
                    box[pair, at : at + 32, lanes] = (turned * factor).astype(bf16)
                    box[pair, at + 32 : at + 64, lanes] = (other * factor).astype(bf16)
                at = 256 + head * 64
                box[pair, 128:192, lanes] = out[at : at + 64].astype(bf16)
            return unused

        lax.fori_loop(0, 2, project, 0)
        for head in range(2):
            pair = group * 2 + head

            @pl.when(z != pair)
            def _():
                push(
                    box.at[pair], qkvt.at[:, block(z, 512)], sz.at[pair], rz.at[z],
                    (row, pair * QUAD + quarter),
                ).start()

            @pl.when(z == pair)
            def _():
                qkvt[:, block(z, 512)] = box[pair]

    cot_in.finish()
    kept.append(fetch(cotp, cotp_out, keep.at[3]))
    for copy in blocks:
        copy.wait_recv()
    for j in range(4):
        mine = jnp.logical_and(quarter == z, quarter == j)

        @pl.when(jnp.logical_not(mine))
        def _():
            push(wo, wop.at[j], sw.at[j], rw.at[j], (row, quarter * QUAD + j)).wait_recv()

    for plane in range(PLANES):
        there = (row, plane * QUAD + z)
        mine = jnp.logical_and(z == plane, quarter == z)

        @pl.when(jnp.logical_not(mine))
        def _():
            push(wo, wop.at[quarter], sw.at[plane], rw.at[quarter], there).wait_send()

    for pair in range(4):

        @pl.when(z != pair)
        def _():
            copy = push(
                box.at[pair], qkvt.at[:, block(pair, 512)], sz.at[pair], rz.at[pair],
                (row, pair * QUAD + quarter),
            )
            copy.wait_send()
            copy.wait_recv()

    rows_in.close()
    cot_in.close()
    for copy in first + second + weights + pieces + blocks:
        copy.wait_send()
    for copy in kept:
        copy.wait()


def split_three(value):
    high = value.astype(bf16).astype(f32)
    middle = (value - high).astype(bf16).astype(f32)
    return high, middle, (value - high - middle).astype(bf16).astype(f32)


def window_queries(qa, lanes, first, limit):
    place = first + lax.broadcasted_iota(jnp.int32, (16, WINDOW), 1)
    line = lax.broadcasted_iota(jnp.int32, (16, WINDOW), 0)
    extra = jnp.where(
        jnp.logical_and(line == 12, place >= limit), -1e30, qa[64:80, lanes].astype(f32)
    )
    return jnp.concatenate(
        [qa[0:64, lanes], extra.astype(bf16), jnp.zeros((AUG - 80, WINDOW), bf16)], axis=0
    )


def attend_body(info, bias, qkvt, labels, att, den, low, qa, ka, kt):
    size = qkvt.shape[1]
    variate = labels[2:3, :]
    line = lax.broadcasted_iota(jnp.int32, (16, size), 0)
    same = (variate == (line % 4).astype(f32)).astype(f32)
    same_pieces = split_three(jnp.full((16, size), bias[0] - bias[1], f32))
    other_pieces = split_three(jnp.full((16, size), bias[1], f32))

    def choose(pieces, number):
        return jnp.where(number == 0, pieces[0], jnp.where(number == 1, pieces[1], pieces[2]))

    extra_q = jnp.where(line < 12, same, jnp.where(line == 12, 0.0, 1.0))
    extra_k = jnp.where(
        line < 12,
        same * choose(same_pieces, line // 4),
        jnp.where(line == 12, 1.0, choose(other_pieces, line - 13)),
    )
    qa[0:64, 0:size] = qkvt[0:64, :]
    qa[64:80, 0:size] = extra_q.astype(bf16)
    qa[80:AUG, 0:size] = jnp.zeros((AUG - 80, size), bf16)
    qa[:, size:] = jnp.zeros((AUG, WINDOW), bf16)
    kt[0:64, :] = qkvt[64:128, :]
    kt[64:80, :] = extra_k.astype(bf16)
    kt[80:AUG, :] = jnp.zeros((AUG - 80, size), bf16)
    ka[...] = jnp.transpose(kt[...])

    def sequence(number, start):
        length = info[number]
        limit = (start + length) * 128

        def window(j, unused):
            first = (start + 4 * j) * 128
            lanes = pl.ds(pl.multiple_of(first, 128), WINDOW)
            queries = window_queries(qa, lanes, first, limit)

            def key(k, running):
                total, numerator = running
                rows = pl.ds(pl.multiple_of((start + k) * 128, 128), 128)
                weights = jnp.exp(mm(ka[rows, :], queries))
                total = total + jnp.sum(weights, axis=0, keepdims=True)
                numerator = numerator + mm(qkvt[128:192, rows], weights.astype(bf16))
                return total, numerator

            total, numerator = lax.fori_loop(
                0, length, key, (jnp.zeros((1, WINDOW), f32), jnp.zeros((64, WINDOW), f32))
            )
            attended = numerator / total
            att[:, lanes] = attended
            den[:, lanes] = jnp.broadcast_to(total, (8, WINDOW))
            low[:, lanes] = attended.astype(bf16)
            return unused

        lax.fori_loop(0, (length + 3) // 4, window, 0)
        return start + length

    lax.fori_loop(0, NSEQ, sequence, 0)


def attend_back_body(
    info, qkvt, qa, ka, labels, freq, grad, att, den,
    dproj, bias_tile,
    dn, cw, vn, dq, dk, dv,
):
    size = qkvt.shape[1]
    lanes_all = slice(0, size)
    inverse = 1.0 / den[0:1, lanes_all]
    d_att = grad[...].astype(f32)
    dn[:, lanes_all] = (d_att * inverse).astype(bf16)
    dn[:, size:] = jnp.zeros((64, WINDOW), bf16)
    cw[:, lanes_all] = jnp.broadcast_to(
        jnp.sum(d_att * att[:, lanes_all], axis=0, keepdims=True) * inverse, (8, size)
    )
    cw[:, size:] = jnp.zeros((8, WINDOW), f32)
    vn[...] = jnp.transpose(qkvt[128:192, :])
    dk[...] = jnp.zeros_like(dk)
    dv[...] = jnp.zeros_like(dv)

    def sequence(number, start):
        length = info[number]
        limit = (start + length) * 128

        def window(j, unused):
            first = (start + 4 * j) * 128
            lanes = pl.ds(pl.multiple_of(first, 128), WINDOW)
            queries = window_queries(qa, lanes, first, limit)
            upstream = dn[:, lanes]
            centre = cw[0:1, lanes]

            def key(k, running):
                rows = pl.ds(pl.multiple_of((start + k) * 128, 128), 128)
                weights = jnp.exp(mm(ka[rows, :], queries))
                d_scores = weights * (mm(vn[rows, :], upstream) - centre)
                rounded = d_scores.astype(bf16)
                dk[:, rows] += mm_nt(queries, rounded)
                dv[:, rows] += mm_nt(upstream, weights.astype(bf16))
                return running + mm(qkvt[64:128, rows], rounded)

            dq[:, lanes] = lax.fori_loop(0, length, key, jnp.zeros((64, WINDOW), f32))
            return unused

        lax.fori_loop(0, (length + 3) // 4, window, 0)
        return start + length

    lax.fori_loop(0, NSEQ, sequence, 0)
    phases = labels[3:4, :] * freq[...]
    cos_part, sin_part = jnp.cos(phases), jnp.sin(phases)
    for part, source, factor in ((0, dq, 0.125), (1, dk, 1.0)):
        former, latter = source[0:32, lanes_all], source[32:64, lanes_all]
        dproj[part * 64 : part * 64 + 32, :] = (
            (former * cos_part + latter * sin_part) * factor
        ).astype(bf16)
        dproj[part * 64 + 32 : part * 64 + 64, :] = (
            (latter * cos_part - former * sin_part) * factor
        ).astype(bf16)
    dproj[128:192, :] = dv[...].astype(bf16)
    variate = labels[2:3, :]
    line = lax.broadcasted_iota(jnp.int32, (16, size), 0)
    match = jnp.logical_and(variate == line.astype(f32), line < 4)
    near = jnp.sum(jnp.where(match, dk[64:80, :], 0.0))
    every = jnp.sum(dk[77:78, :])
    lane = lax.broadcasted_iota(jnp.int32, (8, 128), 1)
    line8 = lax.broadcasted_iota(jnp.int32, (8, 128), 0)
    here = lane == info[NSEQ]
    bias_tile[...] = jnp.where(
        jnp.logical_and(here, line8 == 2),
        near,
        jnp.where(jnp.logical_and(here, line8 == 3), every - near, 0.0),
    )


def branch_body(
    low, wop, x, gains,
    atp, hidden, s2,
    atn, part, sz, rz, inbox, outbox, second, ss, rs,
):
    row, col, z, place = places()
    meet(plane_near(row, col) + line_all(row, col))
    rows, lanes = block(z % 2, 64), block(z // 2, 512)
    copies = []
    for bits in (3, 2, 1):
        copy = push(
            low.at[:, block(flip(z, bits), 512)],
            atp.at[rows, lanes],
            sz.at[bits],
            rz.at[bits],
            on_line(row, col, bits),
        )
        copy.start()
        copies.append(copy)
    atp[rows, lanes] = low[:, block(z, 512)]
    for copy in copies:
        copy.wait()
    atn[...] = jnp.transpose(atp[...])
    total = Scatter(part, inbox, outbox, second, ss, rs)
    core = col % 2
    for bits in (3, 2, 1, 0):
        chip = flip(place // 2, bits)
        part[2 * chip + 1 - core] = mm(atn[block(2 * chip + 1 - core, 128), :], wop[...]).astype(bf16)
    for bits in range(4):
        total.near(flip(place // 2, bits), bits)
    for bits in (3, 2, 1, 0):
        chip = flip(place // 2, bits)
        part[2 * chip + core] = mm(atn[block(2 * chip + core, 128), :], wop[...]).astype(bf16)
    total.far_all()
    state = x[...].astype(f32) + total.finish()
    hidden[...] = state
    s2[...] = (state * norm_scale(state) * gains[1:2, :]).astype(bf16)
    total.close()


def ffn_body(
    s2, cotp_in, wg_in, w_down, hidden, gains,
    out_keep, down_in, gwg_out, d_hidden, low, gain_term,
    cotp, wg, s2p, wgs, wd, actives, factors, inner_s, dgu, d_part, out_part, gwd, gwg,
    keep, sa, ra, sw, rw, sd, rd, inbox, outbox, second, ss, rs,
):
    row, col, z, place = places()
    loads = [fetch(wg_in, wg, keep.at[0]), fetch(cotp_in, cotp, keep.at[1])]
    meet(plane_near(row, col) + line_all(row, col))
    rows_in = Gather(s2p, sa, ra)
    rows_in.start(s2)
    s2p[place] = s2[...]
    downs = []
    for bits in (3, 2, 1):
        downs.append(
            push(w_down, wd.at[block(z, 128), :], sw.at[bits], rw.at[bits], on_line(row, col, bits))
        )
        downs[-1].start()
    wd[block(z, 128), :] = w_down[...]
    loads[0].wait()
    for plane in range(PLANES):
        for r in range(2):
            at = (r * PLANES + plane) * 128
            wgs[at : at + 128, :] = wg[plane * 2 + r]
    for k in range(4):
        chip = flip(place // 2, k)
        if k:
            rows_in.forward(2 * k)
        rows_in.arrived(2 * k)
        rows = block(chip, 256)
        scaled = jnp.concatenate([s2p[2 * chip], s2p[2 * chip + 1]], axis=0)
        both = mm(scaled, wgs[...])
        gate, upper = both[:, 0:512], both[:, 512:1024]
        sig = jax.nn.sigmoid(gate)
        active = gate * sig
        inner_s[rows, :] = (active * upper).astype(bf16)
        actives[rows, :] = active
        factors[rows, :] = upper * sig * (1.0 + gate * (1.0 - sig))
    loads[1].wait()
    cot_all = jnp.concatenate([cotp[t] for t in range(MEMBERS)], axis=0)
    for k in range(4):
        cols = slice(k * 128, k * 128 + 128)
        gwd[k] = mm_tn(inner_s[:, cols], cot_all).astype(bf16)
    grads = []
    for bits in (3, 2, 1):
        grads.append(
            push(gwd.at[flip(z, bits)], down_in.at[z], sd.at[bits], rd.at[bits], on_line(row, col, bits))
        )
        grads[-1].start()
    down_in[z] = gwd[z]
    total = Scatter(d_part, inbox, outbox, second, ss, rs)
    for copy in downs:
        copy.wait_recv()
    for k in range(4):
        chip = flip(place // 2, k)
        rows = block(chip, 256)
        upstream = jnp.concatenate([cotp[2 * chip], cotp[2 * chip + 1]], axis=0)
        d_inner = mm_nt(upstream, wd[...])
        dgu[rows, 0:512] = (d_inner * factors[rows, :]).astype(bf16)
        dgu[rows, 512:1024] = (d_inner * actives[rows, :]).astype(bf16)
        tile = mm_nt(dgu[rows, :], wgs[...]).astype(bf16)
        d_part[2 * chip] = tile[0:128]
        d_part[2 * chip + 1] = tile[128:256]
        total.near(chip, k)
        if k > 1:
            total.far(k - 1)
    for k in range(4):
        chip = flip(place // 2, k)
        tile = mm(inner_s[block(chip, 256), :], wd[...]).astype(bf16)
        out_part[2 * chip] = tile[0:128]
        out_part[2 * chip + 1] = tile[128:256]
        if k == 0:
            total.far(3)
    kept = [fetch(out_part, out_keep, keep.at[10])]
    for f in range(8):
        cols = slice(f * 128, f * 128 + 128)
        lhs = jnp.concatenate([s2p[t, :, cols] for t in range(MEMBERS)], axis=0)
        at = (f % PLANES) * 2 + f // PLANES
        gwg[at] = mm_tn(lhs, dgu[...]).astype(bf16)
        kept.append(fetch(gwg.at[at], gwg_out.at[at], keep.at[2 + f]))
    d_scaled = total.finish()
    state = hidden[...]
    scale = norm_scale(state)
    normed = state * scale
    gain_term[...] = jnp.broadcast_to(jnp.sum(d_scaled * normed, axis=0, keepdims=True), (8, 1024))
    d_state = cotp[place].astype(f32) + norm_back(d_scaled * gains[1:2, :], normed, scale)
    d_hidden[...] = d_state
    low[...] = d_state.astype(bf16)
    rows_in.close()
    total.close()
    for copy in grads:
        copy.wait_recv()
    for copy in downs + grads:
        copy.wait_send()
    for copy in kept:
        copy.wait()


def attended_back_body(
    low, wop, atp,
    grad, gwo,
    dbp, dat, sg, rg, sz, rz,
):
    row, col, z, place = places()
    meet(plane_near(row, col) + line_all(row, col))
    quarter = col % QUAD
    rows_in = Gather(dbp, sg, rg)
    rows_in.start(low)
    dbp[place] = low[...]
    for k in range(4):
        chip = flip(place // 2, k)
        if k:
            rows_in.forward(2 * k)
        rows_in.arrived(2 * k)
        for core in range(2):
            dat[:, block(2 * chip + core, 128)] = mm_nt(wop[...], dbp[2 * chip + core]).astype(bf16)
        if k % 2 == 0:
            continue
        group = row if k == 1 else 1 - row
        for head in range(2):
            pair = group * 2 + head
            source = dat.at[head * 64 : head * 64 + 64, block(group, 512)]

            @pl.when(z != pair)
            def _():
                push(
                    source, grad.at[:, block(z, 512)], sz.at[pair], rz.at[z],
                    (row, pair * QUAD + quarter),
                ).start()

            @pl.when(z == pair)
            def _():
                grad[:, block(z, 512)] = source[...]

    total = mm(atp[:, 0:128], dbp[0])
    for q in range(1, MEMBERS):
        total = total + mm(atp[:, q * 128 : q * 128 + 128], dbp[q])
    gwo[...] = total.astype(bf16)
    for pair in range(4):

        @pl.when(z != pair)
        def _():
            copy = push(
                dat.at[0:64, 0:512], grad.at[:, block(pair, 512)], sz.at[pair], rz.at[pair],
                (row, pair * QUAD + quarter),
            )
            copy.wait_send()
            copy.wait_recv()

    rows_in.close()


def last_body(
    dproj, wqp_in, s1_in, xp_in, out_in, gains, d_hidden, hidden, gwo, gwg, gain_two, bias_tile, deal,
    grad_tokens, gqin, goin, gwg_in, sums, out,
    wqp, s1, xp, out_part, pieces, slots, keep, dpt, dpn, part, gq, pack, packs, packed,
    sz, rz, inbox, outbox, second, ss, rs,
    sq, rq, st, rt, su, ru, sw, rw, sg, rg, sc, rc, inbox2, outbox2, second2, ss2, rs2,
):
    row, col, z, place = places()
    me = row * 16 + col
    quarter = col % QUAD
    core = col % 2
    loads = [
        fetch(out_in, out_part, keep.at[3]),
        fetch(s1_in, s1, keep.at[0]),
        fetch(xp_in, xp, keep.at[1]),
        fetch(wqp_in, wqp, keep.at[2]),
    ]
    meet([anyone(row, col, bits) for bits in range(1, 32)])
    copies = []
    lanes = block(z // 2, 512)
    for bits in (3, 2, 1):
        for kind in range(3):
            copy = push(
                dproj.at[kind * 64 : kind * 64 + 64, block(flip(z, bits), 512)],
                dpt.at[pl.ds(pl.multiple_of(kind * 128 + (z % 2) * 64, 64), 64), lanes],
                sz.at[bits, kind],
                rz.at[bits, kind],
                on_line(row, col, bits),
            )
            copy.start()
            copies.append(copy)
    for kind in range(3):
        rows = pl.ds(pl.multiple_of(kind * 128 + (z % 2) * 64, 64), 64)
        dpt[rows, lanes] = dproj[kind * 64 : kind * 64 + 64, block(z, 512)]
    loads[0].wait()
    output = Scatter(out_part, inbox2, outbox2, second2, ss2, rs2)
    output.near_all()
    output.far_all()
    spread = []
    for bits in range(1, 8):
        there = in_plane(row, col, bits)
        copy = push(gwg.at[flip(place, bits)], gwg_in.at[place], sg.at[bits], rg.at[bits], there)
        copy.start()
        spread.append(copy)
    gwg_in[place] = gwg[place]
    for copy in loads[1:]:
        copy.wait()
    rows_out = (hidden[...] + output.finish()).astype(bf16)
    for j in range(16):
        pieces[j] = rows_out[j * 8 : j * 8 + 8, :]
    for d in range(16):
        number = 0
        for j in range(1, 16):
            number = jnp.where(deal[j] == d, j, number)
        slots[d] = pieces[number]
    for copy in copies:
        copy.wait_recv()
    for bits in range(1, 16):
        there = (row, flip(col, bits))
        copy = push(slots.at[there[1]], out.at[col], sc.at[bits], rc.at[bits], there)
        copy.start()
        spread.append(copy)
    out[col] = slots[col]
    for j in range(4):
        there = (row, quarter * QUAD + j)
        mine = jnp.logical_and(quarter == z, quarter == j)

        @pl.when(jnp.logical_not(mine))
        def _():
            push(gwo.at[j], goin.at[z], sw.at[j], rw.at[z], there).start()

        @pl.when(mine)
        def _():
            goin[z] = gwo[j]

    dpn[...] = jnp.transpose(dpt[...])
    for f in range(8):
        lhs = jnp.concatenate([s1[t, :, f * 128 : f * 128 + 128] for t in range(MEMBERS)], axis=0)
        chunk = mm_tn(lhs, dpn[...]).astype(bf16)
        for j in range(4):
            gq[f * 4 + j] = chunk[j * 32 : j * 32 + 32, :]
    for bits in range(31, 0, -1):
        there = anyone(row, col, bits)
        number = there[0] * 16 + there[1]
        copy = push(gq.at[number], gqin.at[me], sq.at[bits], rq.at[bits], there)
        copy.start()
        spread.append(copy)
    gqin[me] = gq[me]
    gain_one = gains[0:1, :]
    total = Scatter(part, inbox, outbox, second, ss, rs)
    term = jnp.zeros((1, 1024), f32)
    for own in range(2):
        for bits in (3, 2, 1, 0):
            number = 2 * flip(place // 2, bits) + (core if own else 1 - core)
            values = xp[number].astype(f32)
            d_scaled = mm_nt(dpn[block(number, 128), :], wqp[...])
            term = term + jnp.sum(d_scaled * (values * norm_scale(values)), axis=0, keepdims=True)
            part[number] = d_scaled.astype(bf16)
        if own == 0:
            total.near_all()
    total.far_all()
    for k in range(8):
        pack[k] = bias_tile[...]
        pack[k, 0:1, :] = term[:, k * 128 : k * 128 + 128]
        pack[k, 1:2, :] = gain_two[0:1, k * 128 : k * 128 + 128]
    first = []
    for bits in range(1, 8):
        there = in_plane(row, col, bits)
        copy = push(
            pack.at[pl.ds(there[0] * PLANES, PLANES)], packs.at[place], st.at[bits], rt.at[bits], there
        )
        copy.start()
        first.append(copy)
    packs[place] = pack[pl.ds(row * PLANES, PLANES)]
    for copy in first:
        copy.wait_recv()
    summed = packs[0]
    for p in range(1, MEMBERS):
        summed = summed + packs[p]
    packed[...] = summed
    for bits in (1, 2, 3):
        copy = push(
            packed.at[flip(z, bits)], sums.at[z], su.at[bits], ru.at[bits], on_line(row, col, bits)
        )
        copy.start()
        spread.append(copy)
    sums[z] = packed[z]
    d_one = total.finish()
    own_rows = xp[place].astype(f32)
    scale = norm_scale(own_rows)
    grad_tokens[...] = (
        d_hidden[...] + norm_back(d_one * gain_one, own_rows * scale, scale)
    ).astype(bf16)
    for copy in spread:
        copy.wait_recv()
    for plane in range(PLANES):
        mine = jnp.logical_and(quarter == z, z == plane)

        @pl.when(jnp.logical_not(mine))
        def _():
            push(
                gwo.at[0], goin.at[plane], sw.at[plane], rw.at[plane], (row, plane * QUAD + z)
            ).wait_recv()

    for j in range(4):
        there = (row, quarter * QUAD + j)
        mine = jnp.logical_and(quarter == z, quarter == j)

        @pl.when(jnp.logical_not(mine))
        def _():
            push(gwo.at[j], goin.at[z], sw.at[j], rw.at[z], there).wait_send()

    for copy in copies + first + spread:
        copy.wait_send()
    total.close()
    output.close()


def finish_body(
    place_info, grad_tokens_in, gqin, goin, out_in, gwg, gwd, tiles,
    out, grad_tokens, grad_q, grad_o, grad_gu, grad_d, grad_gains, grad_bias,
):
    grad_tokens[...] = grad_tokens_in[...]
    out[...] = out_in[...]
    grad_o[...] = (goin[0].astype(f32) + goin[1].astype(f32)) + (
        goin[2].astype(f32) + goin[3].astype(f32)
    )
    grad_d[...] = (gwd[0].astype(f32) + gwd[1].astype(f32)) + (
        gwd[2].astype(f32) + gwd[3].astype(f32)
    )
    for p in range(MEMBERS):
        total = jnp.zeros((32, 384), f32)
        for plane in range(PLANES):
            total = total + gqin[(p // QUAD) * 16 + plane * QUAD + p % QUAD].astype(f32)
        for kind in range(3):
            at = kind * 1024 + p * 128
            grad_q[:, at : at + 128] = total[:, kind * 128 : kind * 128 + 128]
        for half in range(2):
            for plane in range(PLANES):
                unit = (p // QUAD) * 16 + plane * QUAD + p % QUAD
                at = half * 512 + plane * 128
                start = half * 4096 + unit * 128
                grad_gu[:, start : start + 128] = gwg[p, :, at : at + 128].astype(f32)
    total = (tiles[0] + tiles[1]) + (tiles[2] + tiles[3])
    quarter = place_info[0]
    chosen = jnp.zeros((2, 32), f32)
    for k in range(4):
        chosen = chosen + jnp.where(quarter == k, total[0:2, k * 32 : k * 32 + 32], 0.0)
    grad_gains[...] = chosen
    grad_bias[...] = total[2:4, 0:16]


def sds(shape, dtype):
    return jax.ShapeDtypeStruct(shape, dtype)


def dma(*shape):
    return pltpu.SemaphoreType.DMA(shape)


def kernel(body, name, specs, outs, scratch, number=None, cost=0, places_out=None):
    params = dict(vmem_limit_bytes=56 << 20)
    if number is not None:
        params.update(collective_id=number, has_side_effects=True)
    return pl.pallas_call(
        body,
        name=name,
        in_specs=specs,
        out_shape=outs,
        out_specs=places_out or [VM] * len(outs),
        scratch_shapes=scratch,
        compiler_params=pltpu.CompilerParams(**params),
        cost_estimate=pl.CostEstimate(flops=cost, bytes_accessed=cost // 300, transcendentals=0),
    )


def plane_shards(
    tokens, variate_ids, time_ids, lengths, deal, w_qkv, w_out, w_gate_up, w_down,
    gain_attn, gain_ffn, var_bias, cotangent,
):
    row = lax.axis_index("row")
    col = lax.axis_index("col")
    z, q = col // QUAD, col % QUAD
    place = row * QUAD + q
    rows, width = tokens.shape
    lines = [[plane * QUAD + k for plane in range(PLANES)] for k in range(QUAD)]
    freq = jnp.exp(-math.log(10000.0) * jnp.arange(32, dtype=f32) / 32)[:, None]
    target = deal[0, 0]

    xp, wqp, wop, wgp, cotp, s1, qkvt, gains, labels = kernel(
        enter_body,
        "enter",
        [VM] * 9 + [SM, SM, VM],
        [
            sds((8, rows, width), bf16),
            sds((32, 32, 384), bf16),
            sds((4, 32, 1024), bf16),
            sds((8, 32, 1024), bf16),
            sds((8, rows, width), bf16),
            sds((8, rows, width), bf16),
            sds((192, 2048), bf16),
            sds((8, 1024), f32),
            sds((8, 2048), f32),
        ],
        [
            pltpu.VMEM((8, rows, width), bf16),
            pltpu.VMEM((32, 32, 384), bf16),
            pltpu.VMEM((8, rows, width), bf16),
            pltpu.VMEM((8, rows, width), bf16),
            dma(4),
            pltpu.VMEM((8, 32, 384), bf16),
            pltpu.VMEM((8, 32, 1024), bf16),
            pltpu.VMEM((16, 8, width), bf16),
            pltpu.VMEM((rows, width), bf16),
            pltpu.VMEM((8, 128), f32),
            pltpu.VMEM((4, 8, 128), f32),
            pltpu.VMEM((8, 4, 8, 128), f32),
            pltpu.VMEM((384, 1024), bf16),
            pltpu.VMEM((4, 192, 512), bf16),
            pltpu.VMEM((32, 1024), f32),
            pltpu.VMEM((32, 1024), f32),
            pltpu.VMEM((8, 1024), f32),
        ]
        + [dma(8), dma(8), dma(32), dma(32), dma(4), dma(4), dma(8), dma(8), dma(4), dma(4)]
        + [dma(8), dma(8), dma(16), dma(16), dma(8), dma(8), dma(4), dma(4)],
        number=1,
        places_out=[ANY, ANY, VM, VM, ANY, ANY, VM, VM, VM],
    )(
        tokens, w_qkv, w_out, w_gate_up, cotangent.reshape(16, 8, width), gain_attn[None],
        gain_ffn[None], variate_ids[None], time_ids[None], lengths, target, freq,
    )

    gate_up = lax.all_gather(
        wgp.reshape(256, 1024), "col", axis=0, tiled=True, axis_index_groups=lines
    )
    wqp = wqp.reshape(1024, 384)
    wop = wop.reshape(128, 1024)

    head = place * 2 + z % 2
    info = jnp.concatenate(
        [labels[4, :NSEQ].astype(jnp.int32), head[None].astype(jnp.int32), jnp.zeros((1,), jnp.int32)]
    )
    bias = lax.dynamic_slice_in_dim(var_bias, head, 1, 1)[:, 0]
    wide = 2048 + WINDOW
    att, den, low, qa, ka = kernel(
        attend_body,
        "attend",
        [SM, SM, VM, VM],
        [
            sds((64, wide), f32),
            sds((8, wide), f32),
            sds((64, wide), bf16),
            sds((AUG, wide), bf16),
            sds((2048, AUG), bf16),
        ],
        [pltpu.VMEM((AUG, 2048), bf16)],
        cost=2 * 10**9,
    )(info, bias, qkvt, labels)

    atp, hidden, s2 = kernel(
        branch_body,
        "branch",
        [VM] * 4,
        [sds((128, 1024), bf16), sds((rows, width), f32), sds((rows, width), bf16)],
        [
            pltpu.VMEM((1024, 128), bf16),
            pltpu.VMEM((8, rows, width), bf16),
            dma(4), dma(4),
        ]
        + scatter_scratch(rows, width),
        number=2,
    )(low, wop, tokens, gains)

    out_part, down_in, gwg, d_hidden, d_branch, gain_two = kernel(
        ffn_body,
        "ffn",
        [VM, ANY, ANY, VM, VM, VM],
        [
            sds((8, rows, width), bf16),
            sds((4, rows, width), bf16),
            sds((8, 128, 1024), bf16),
            sds((rows, width), f32),
            sds((rows, width), bf16),
            sds((8, 1024), f32),
        ],
        [
            pltpu.VMEM((8, rows, width), bf16),
            pltpu.VMEM((8, 128, 1024), bf16),
            pltpu.VMEM((8, rows, width), bf16),
            pltpu.VMEM((1024, 1024), bf16),
            pltpu.VMEM((512, width), bf16),
            pltpu.VMEM((1024, 512), f32),
            pltpu.VMEM((1024, 512), f32),
            pltpu.VMEM((1024, 512), bf16),
            pltpu.VMEM((1024, 1024), bf16),
            pltpu.VMEM((8, rows, width), bf16),
            pltpu.VMEM((8, rows, width), bf16),
            pltpu.VMEM((4, rows, width), bf16),
            pltpu.VMEM((8, 128, 1024), bf16),
            dma(11), dma(8), dma(8), dma(4), dma(4), dma(4), dma(4),
        ]
        + scatter_scratch(rows, width),
        number=3,
        cost=10**10,
        places_out=[ANY, VM, ANY, VM, VM, VM],
    )(s2, cotp, gate_up.reshape(8, 128, 1024), w_down, hidden, gains)

    gate_up_sum = lax.psum_scatter(
        gwg.reshape(1024, 1024), "col", scatter_dimension=0, tiled=True, axis_index_groups=lines
    )

    grad, gwo = kernel(
        attended_back_body,
        "attended_back",
        [VM] * 3,
        [sds((64, 2048), bf16), sds((128, 1024), bf16)],
        [
            pltpu.VMEM((8, rows, width), bf16),
            pltpu.VMEM((128, 1024), bf16),
            dma(8), dma(8), dma(4), dma(4),
        ],
        number=4,
    )(d_branch, wop, atp)

    dproj, bias_tile = kernel(
        attend_back_body,
        "attend_back",
        [SM] + [VM] * 8,
        [sds((192, 2048), bf16), sds((8, 128), f32)],
        [
            pltpu.VMEM((64, wide), bf16),
            pltpu.VMEM((8, wide), f32),
            pltpu.VMEM((2048, 64), bf16),
            pltpu.VMEM((64, wide), f32),
            pltpu.VMEM((AUG, 2048), f32),
            pltpu.VMEM((64, 2048), f32),
        ],
        cost=5 * 10**9,
    )(info, qkvt, qa, ka, labels, freq, grad, att, den)

    grad_tokens, gqin, goin, gwg_in, sums, out = kernel(
        last_body,
        "last",
        [VM] + [ANY] * 4 + [VM] * 7 + [SM],
        [
            sds((rows, width), bf16),
            sds((32, 32, 384), bf16),
            sds((4, 32, 1024), bf16),
            sds((8, 32, 1024), bf16),
            sds((4, 8, 128), f32),
            sds((16, 8, width), bf16),
        ],
        [
            pltpu.VMEM((1024, 384), bf16),
            pltpu.VMEM((8, rows, width), bf16),
            pltpu.VMEM((8, rows, width), bf16),
            pltpu.VMEM((8, rows, width), bf16),
            pltpu.VMEM((16, 8, width), bf16),
            pltpu.VMEM((16, 8, width), bf16),
            dma(4),
            pltpu.VMEM((384, 1024), bf16),
            pltpu.VMEM((1024, 384), bf16),
            pltpu.VMEM((8, rows, width), bf16),
            pltpu.VMEM((32, 32, 384), bf16),
            pltpu.VMEM((8, 8, 128), f32),
            pltpu.VMEM((8, 4, 8, 128), f32),
            pltpu.VMEM((4, 8, 128), f32),
            dma(4, 3), dma(4, 3),
        ]
        + scatter_scratch(rows, width)
        + [dma(32), dma(32), dma(8), dma(8), dma(4), dma(4), dma(4), dma(4), dma(8), dma(8)]
        + [dma(16), dma(16)]
        + scatter_scratch(rows, width),
        number=5,
    )(
        dproj, wqp, s1, xp, out_part, gains, d_hidden, hidden, gwo.reshape(4, 32, 1024),
        gate_up_sum.reshape(8, 32, 1024), gain_two, bias_tile, target,
    )
    out, grad_tokens, grad_q, grad_o, grad_gate_up, grad_down, gain_grads, bias_grads = kernel(
        finish_body,
        "finish",
        [SM] + [VM] * 7,
        [
            sds((rows, width), bf16),
            sds((rows, width), bf16),
            sds((32, 3072), f32),
            sds((32, 1024), f32),
            sds((32, 8192), f32),
            sds((rows, width), f32),
            sds((2, 32), f32),
            sds((2, 16), f32),
        ],
        [],
    )(
        q[None].astype(jnp.int32), grad_tokens, gqin, goin, out.reshape(rows, width), gwg_in,
        down_in, sums,
    )
    return (
        out,
        grad_tokens,
        grad_q,
        grad_o,
        grad_gate_up,
        grad_down,
        gain_grads[0],
        gain_grads[1],
        bias_grads,
    )


def solution(mesh):
    planes = mesh.shape["row"] == 2 and mesh.shape["col"] == PLANES * QUAD
    return jax.shard_map(
        plane_shards if planes else shards,
        mesh=mesh,
        in_specs=(
            P(("row", "col"), None),
            P(("row", "col")),
            P(("row", "col")),
            P("row", None),
            P("row", "col", None),
            P(("row", "col"), None),
            P(("row", "col"), None),
            P(("row", "col"), None),
            P(("row", "col"), None),
            P(("row", "col")),
            P(("row", "col")),
            P(),
            P(("row", "col"), None),
        ),
        out_specs=(
            P(("row", "col"), None),
            P(("row", "col"), None),
            P(("row", "col"), None),
            P(("row", "col"), None),
            P(("row", "col"), None),
            P(("row", "col"), None),
            P(("row", "col")),
            P(("row", "col")),
            P(),
        ),
        check_vma=False,
    )
```

```python
import math

import jax
import jax.numpy as jnp
import numpy as np
from jax import lax
from jax.experimental import pallas as pl
from jax.experimental.pallas import tpu as pltpu
from jax.sharding import PartitionSpec as P

HEAD_DIM = 64
UNIT = 128
KEY_BLOCK = 1024
NSEQ = 6


epsilon = 1e-05


def contract_rows(operand, factor):
    return lax.dot_general(
        operand, factor, (((0,), (0,)), ((), ())), preferred_element_type=jnp.float32
    )


def contract_cols(operand, factor):
    return lax.dot_general(
        operand, factor, (((1,), (1,)), ((), ())), preferred_element_type=jnp.float32
    )


def angles(time_ids):
    half_dim = HEAD_DIM // 2
    inverse_freq = jnp.exp(-math.log(10000.0) * jnp.arange(half_dim, dtype=jnp.float32) / half_dim)
    phases = time_ids.astype(jnp.float32)[:, None] * inverse_freq[None, :]
    return (jnp.cos(phases)[:, None, :], jnp.sin(phases)[:, None, :])


def rotate(tensor, cos_part, sin_part):
    half_dim = tensor.shape[-1] // 2
    former = tensor[..., :half_dim]
    latter = tensor[..., half_dim:]
    return jnp.concatenate(
        [former * cos_part - latter * sin_part, latter * cos_part + former * sin_part], axis=-1
    )


def unrotate(tensor, cos_part, sin_part):
    half_dim = tensor.shape[-1] // 2
    former = tensor[..., :half_dim]
    latter = tensor[..., half_dim:]
    return jnp.concatenate(
        [former * cos_part + latter * sin_part, latter * cos_part - former * sin_part], axis=-1
    )


def norm_scale(values):
    return lax.rsqrt(jnp.mean(values * values, axis=-1, keepdims=True) + epsilon)


def norm_back(d_normed, normed, scale):
    return scale * (d_normed - normed * jnp.mean(d_normed * normed, axis=-1, keepdims=True))


def score_weights(queries, query_seq, query_var, key_block, seq_block, var_block, var_bias):
    scores = (
        jnp.einsum("qhd,khd->hqk", queries, key_block, preferred_element_type=jnp.float32) * 0.125
    )
    matched = query_var[:, None] == var_block[None, :]
    scores = scores + jnp.where(
        matched[None], var_bias[0][:, None, None], var_bias[1][:, None, None]
    )
    within = query_seq[:, None] == seq_block[None, :]
    return (jnp.where(within[None], jnp.exp(scores), 0.0), matched)


def shards(
    tokens,
    variate_ids,
    time_ids,
    lengths,
    deal,
    w_qkv,
    w_out,
    w_gate_up,
    w_down,
    gain_attn,
    gain_ffn,
    var_bias,
    cotangent,
):
    tok_rows, model_width = tokens.shape
    n_col = lax.axis_size("col")
    col_index = lax.axis_index("col")
    piece_len = tok_rows // n_col
    head_count = model_width // HEAD_DIM
    bounds = jnp.cumsum(lengths[0]) * UNIT
    position = col_index * tok_rows + jnp.arange(tok_rows, dtype=jnp.int32)
    seq_own = jnp.sum((position[:, None] >= bounds[None, :]).astype(jnp.int32), axis=1)
    target = deal[0, 0]
    slots = jnp.arange(n_col, dtype=jnp.int32)
    inverse = jnp.sum(
        slots[:, None] * (target[:, None] == slots[None, :]).astype(jnp.int32), axis=0
    )
    send_rows = jnp.take(tokens.reshape(n_col, piece_len, model_width), inverse, axis=0)
    labels = jnp.stack(
        [
            seq_own.reshape(n_col, piece_len),
            variate_ids.reshape(n_col, piece_len),
            time_ids.reshape(n_col, piece_len),
        ],
        axis=1,
    )
    send_labels = jnp.take(labels, inverse, axis=0)
    got_rows, got_labels = (
        lax.all_to_all(send_rows, "col", split_axis=0, concat_axis=0, tiled=True),
        lax.all_to_all(send_labels, "col", split_axis=0, concat_axis=0, tiled=True),
    )
    inputs = got_rows.reshape(tok_rows, model_width).astype(jnp.float32)
    seq_q = got_labels[:, 0, :].reshape(tok_rows)
    var_q = got_labels[:, 1, :].reshape(tok_rows)
    cos_part, sin_part = angles(got_labels[:, 2, :].reshape(tok_rows))
    qkv_full, out_full, gate_up_full, down_full, gain_one, gain_two = (
        lax.all_gather(w_qkv, ("row", "col"), axis=0, tiled=True),
        lax.all_gather(w_out, ("row", "col"), axis=0, tiled=True),
        lax.all_gather(w_gate_up, ("row", "col"), axis=0, tiled=True),
        lax.all_gather(w_down, ("row", "col"), axis=0, tiled=True),
        lax.all_gather(gain_attn, ("row", "col"), axis=0, tiled=True),
        lax.all_gather(gain_ffn, ("row", "col"), axis=0, tiled=True),
    )
    scale_one = norm_scale(inputs)
    normed_one = inputs * scale_one
    scaled_one = (normed_one * gain_one.astype(jnp.float32)).astype(jnp.bfloat16)
    projected = jnp.dot(scaled_one, qkv_full, preferred_element_type=jnp.float32)
    shaped = projected.reshape(tok_rows, 3, head_count, HEAD_DIM)
    queries = rotate(shaped[:, 0], cos_part, sin_part).astype(jnp.bfloat16)
    key_own = (
        rotate(shaped[:, 1], cos_part, sin_part).astype(jnp.bfloat16).reshape(tok_rows, model_width)
    )
    value_own = projected[:, 2 * model_width :].astype(jnp.bfloat16)
    keys_all, values_all, seq_k, var_k = (
        lax.all_gather(key_own, "col", axis=0, tiled=True),
        lax.all_gather(value_own, "col", axis=0, tiled=True),
        lax.all_gather(seq_q, "col", axis=0, tiled=True),
        lax.all_gather(var_q, "col", axis=0, tiled=True),
    )
    group_size = keys_all.shape[0]
    stride = min(KEY_BLOCK, group_size)
    block_count = group_size // stride

    def split_blocks(key_rows, value_rows, key_seq, key_var):
        return (
            key_rows.reshape(block_count, stride, head_count, HEAD_DIM),
            value_rows.reshape(block_count, stride, head_count, HEAD_DIM),
            key_seq.reshape(block_count, stride),
            key_var.reshape(block_count, stride),
        )

    def forward_step(running, block_data):
        denominator, numerator = running
        key_block, value_block, seq_block, var_block = block_data
        weights = score_weights(queries, seq_q, var_q, key_block, seq_block, var_block, var_bias)[0]
        denominator = denominator + jnp.sum(weights, axis=-1)
        numerator = numerator + jnp.einsum(
            "hqk,khd->qhd",
            weights.astype(jnp.bfloat16),
            value_block,
            preferred_element_type=jnp.float32,
        )
        return ((denominator, numerator), None)

    (denominator, numerator), unused = lax.scan(
        forward_step,
        (
            jnp.zeros((head_count, tok_rows), jnp.float32),
            jnp.zeros((tok_rows, head_count, HEAD_DIM), jnp.float32),
        ),
        split_blocks(keys_all, values_all, seq_k, var_k),
    )
    attended = numerator / denominator.T[:, :, None]
    attn_low = attended.reshape(tok_rows, model_width).astype(jnp.bfloat16)
    hidden_state = inputs + jnp.dot(attn_low, out_full, preferred_element_type=jnp.float32)
    scale_two = norm_scale(hidden_state)
    normed_two = hidden_state * scale_two
    scaled_two = (normed_two * gain_two.astype(jnp.float32)).astype(jnp.bfloat16)
    gate_up = jnp.dot(scaled_two, gate_up_full, preferred_element_type=jnp.float32)
    hidden_units = gate_up_full.shape[1] // 2
    gate_part = gate_up[:, :hidden_units]
    upper_part = gate_up[:, hidden_units:]
    sigmoid_gate = jax.nn.sigmoid(gate_part)
    active = gate_part * sigmoid_gate
    inner_act = (active * upper_part).astype(jnp.bfloat16)
    ffn_branch = jnp.dot(inner_act, down_full, preferred_element_type=jnp.float32)
    output = (hidden_state + ffn_branch).astype(jnp.bfloat16)
    qkv_back, out_back, gate_up_back, down_back, gain_one_back, gain_two_back = (
        lax.all_gather(w_qkv, ("row", "col"), axis=0, tiled=True),
        lax.all_gather(w_out, ("row", "col"), axis=0, tiled=True),
        lax.all_gather(w_gate_up, ("row", "col"), axis=0, tiled=True),
        lax.all_gather(w_down, ("row", "col"), axis=0, tiled=True),
        lax.all_gather(gain_attn, ("row", "col"), axis=0, tiled=True),
        lax.all_gather(gain_ffn, ("row", "col"), axis=0, tiled=True),
    )
    d_inner = contract_cols(cotangent, down_back)
    d_gate = (
        d_inner * upper_part * sigmoid_gate * (1.0 + gate_part * (1.0 - sigmoid_gate))
    ).astype(jnp.bfloat16)
    d_upper = (d_inner * active).astype(jnp.bfloat16)
    d_gate_up = jnp.concatenate([d_gate, d_upper], axis=1)
    d_scaled_two = contract_cols(d_gate_up, gate_up_back)
    term_gain_two = jnp.sum(d_scaled_two * normed_two, axis=0)
    term_gate_up = contract_rows(scaled_two, d_gate_up)
    term_down = contract_rows(inner_act, cotangent)
    d_hidden = cotangent.astype(jnp.float32) + norm_back(
        d_scaled_two * gain_two_back.astype(jnp.float32), normed_two, scale_two
    )
    d_branch = d_hidden.astype(jnp.bfloat16)
    term_out = contract_rows(attn_low, d_branch)
    d_attended = contract_cols(d_branch, out_back).reshape(tok_rows, head_count, HEAD_DIM)
    d_numerator = (d_attended / denominator.T[:, :, None]).astype(jnp.bfloat16)
    centre = (jnp.sum(d_attended * attended, axis=-1) / denominator.T).T
    back_keys = (
        lax.all_gather(key_own, "col", axis=0, tiled=True),
        lax.all_gather(value_own, "col", axis=0, tiled=True),
        lax.all_gather(seq_q, "col", axis=0, tiled=True),
        lax.all_gather(var_q, "col", axis=0, tiled=True),
    )

    def query_step(running, block_data):
        d_queries, same_sum, other_sum = running
        key_block, value_block, seq_block, var_block = block_data
        weights, matched = score_weights(
            queries, seq_q, var_q, key_block, seq_block, var_block, var_bias
        )
        d_probs = jnp.einsum(
            "qhd,khd->hqk", d_numerator, value_block, preferred_element_type=jnp.float32
        )
        d_scores = weights * (d_probs - centre[:, :, None])
        same_sum = same_sum + jnp.sum(jnp.where(matched[None], d_scores, 0.0), axis=(1, 2))
        other_sum = other_sum + jnp.sum(jnp.where(matched[None], 0.0, d_scores), axis=(1, 2))
        d_rounded = d_scores.astype(jnp.bfloat16)
        d_queries = d_queries + jnp.einsum(
            "hqk,khd->qhd", d_rounded, key_block, preferred_element_type=jnp.float32
        )
        return ((d_queries, same_sum, other_sum), (d_rounded, weights.astype(jnp.bfloat16)))

    def query_and_key_step(running, block_data):
        running, rounded = query_step(running, block_data)
        d_rounded, weights_low = rounded
        d_keys = (
            jnp.einsum("hqk,qhd->khd", d_rounded, queries, preferred_element_type=jnp.float32)
            * 0.125
        )
        d_values = jnp.einsum(
            "hqk,qhd->khd", weights_low, d_numerator, preferred_element_type=jnp.float32
        )
        return (running, (d_keys, d_values))

    start_running = (
        jnp.zeros((tok_rows, head_count, HEAD_DIM), jnp.float32),
        jnp.zeros((head_count,), jnp.float32),
        jnp.zeros((head_count,), jnp.float32),
    )
    (d_queries, same_sum, other_sum), (d_keys, d_values) = lax.scan(
        query_and_key_step,
        start_running,
        split_blocks(back_keys[0], back_keys[1], back_keys[2], back_keys[3]),
    )
    key_grad, value_grad = (
        lax.psum_scatter(
            d_keys.reshape(group_size, model_width).astype(jnp.bfloat16),
            "col",
            scatter_dimension=0,
            tiled=True,
        ).astype(jnp.float32),
        lax.psum_scatter(
            d_values.reshape(group_size, model_width).astype(jnp.bfloat16),
            "col",
            scatter_dimension=0,
            tiled=True,
        ).astype(jnp.float32),
    )
    d_query_pre = unrotate(d_queries * 0.125, cos_part, sin_part).reshape(tok_rows, model_width)
    d_key_pre = unrotate(
        key_grad.reshape(tok_rows, head_count, HEAD_DIM), cos_part, sin_part
    ).reshape(tok_rows, model_width)
    d_projected = jnp.concatenate([d_query_pre, d_key_pre, value_grad], axis=1).astype(jnp.bfloat16)
    d_scaled_one = contract_cols(d_projected, qkv_back)
    term_qkv = contract_rows(scaled_one, d_projected)
    term_gain_one = jnp.sum(d_scaled_one * normed_one, axis=0)
    grad_w_qkv, grad_w_out, grad_w_gate_up, grad_w_down, grad_gain_attn, grad_gain_ffn = (
        lax.psum_scatter(term_qkv, ("row", "col"), scatter_dimension=0, tiled=True),
        lax.psum_scatter(term_out, ("row", "col"), scatter_dimension=0, tiled=True),
        lax.psum_scatter(term_gate_up, ("row", "col"), scatter_dimension=0, tiled=True),
        lax.psum_scatter(term_down, ("row", "col"), scatter_dimension=0, tiled=True),
        lax.psum_scatter(term_gain_one, ("row", "col"), scatter_dimension=0, tiled=True),
        lax.psum_scatter(term_gain_two, ("row", "col"), scatter_dimension=0, tiled=True),
    )
    grad_var_bias = lax.psum(jnp.stack([same_sum, other_sum], axis=0), ("row", "col"))
    d_inputs = d_hidden + norm_back(
        d_scaled_one * gain_one_back.astype(jnp.float32), normed_one, scale_one
    )
    returned = lax.all_to_all(
        d_inputs.astype(jnp.bfloat16).reshape(n_col, piece_len, model_width),
        "col",
        split_axis=0,
        concat_axis=0,
        tiled=True,
    )
    grad_tokens = jnp.take(returned, target, axis=0).reshape(tok_rows, model_width)
    return (
        output,
        grad_tokens,
        grad_w_qkv,
        grad_w_out,
        grad_w_gate_up,
        grad_w_down,
        grad_gain_attn,
        grad_gain_ffn,
        grad_var_bias,
    )


PLANES = 4
QUAD = 4
MEMBERS = 8
WINDOW = 512
AUG = 128
f32 = jnp.float32
bf16 = jnp.bfloat16
VM = pl.BlockSpec(memory_space=pltpu.VMEM)
SM = pl.BlockSpec(memory_space=pltpu.SMEM)
ANY = pl.BlockSpec(memory_space=pl.ANY)


def mm(a, b):
    return lax.dot_general(a, b, (((1,), (0,)), ((), ())), preferred_element_type=f32)


def mm_nt(a, b):
    return lax.dot_general(a, b, (((1,), (1,)), ((), ())), preferred_element_type=f32)


def mm_tn(a, b):
    return lax.dot_general(a, b, (((0,), (0,)), ((), ())), preferred_element_type=f32)


def flip(value, bits):
    for bit in (1, 2, 4, 8, 16):
        if bits & bit:
            value = value + bit * (1 - 2 * ((value // bit) % 2))
    return value


def places():
    row = lax.axis_index("row")
    col = lax.axis_index("col")
    return row, col, col // QUAD, row * QUAD + col % QUAD


def in_plane(row, col, bits):
    return flip(row, bits // QUAD), flip(col, bits % QUAD)


def in_line(row, col, bits):
    return row, flip(col, bits // 2 * QUAD + bits % 2)


def on_line(row, col, bits):
    return row, flip(col, bits * QUAD)


def anyone(row, col, bits):
    return flip(row, bits // 16), flip(col, bits % 16)


def push(source, target, send, recv, device):
    return pltpu.make_async_remote_copy(
        src_ref=source,
        dst_ref=target,
        send_sem=send,
        recv_sem=recv,
        device_id={"row": device[0], "col": device[1]},
        device_id_type=pl.DeviceIdType.MESH,
    )


def meet(devices):
    barrier = pltpu.get_barrier_semaphore()
    for device in devices:
        pl.semaphore_signal(
            barrier,
            1,
            device_id={"row": device[0], "col": device[1]},
            device_id_type=pl.DeviceIdType.MESH,
        )
    pl.semaphore_wait(barrier, len(devices))


NEAR = (2, 4, 6, 1)


def plane_near(row, col):
    return [in_plane(row, col, bits) for bits in NEAR]


def line_all(row, col):
    return [on_line(row, col, bits) for bits in (1, 2, 3)]


def column_all(row, col):
    return [
        (flip(row, bits // 4), flip(col, bits % 4 * QUAD)) for bits in (1, 2, 3, 5, 6, 7)
    ]


class Gather:
    def __init__(self, target, send, recv, peer=in_plane, place=None):
        self.target, self.send, self.recv, self.peer = target, send, recv, peer
        self.row, self.col, _, self.place = places()
        if place is not None:
            self.place = place
        self.copies, self.onward = {}, {}

    def start(self, source):
        for bits in NEAR:
            self.copies[bits] = push(
                source,
                self.target.at[self.place],
                self.send.at[bits],
                self.recv.at[bits],
                self.peer(self.row, self.col, bits),
            )
            self.copies[bits].start()

    def forward(self, bits):
        self.copies[bits].wait_recv()
        slot = self.target.at[flip(self.place, bits)]
        self.onward[bits] = push(
            slot,
            slot,
            self.send.at[bits + 1],
            self.recv.at[bits + 1],
            self.peer(self.row, self.col, 1),
        )
        self.onward[bits].start()

    def arrived(self, bits):
        (self.onward[bits] if bits else self.copies[1]).wait_recv()

    def close(self):
        for copy in list(self.copies.values()) + list(self.onward.values()):
            copy.wait_send()

    def finish(self):
        for bits in (2, 4, 6):
            self.forward(bits)
        for bits in (0, 2, 4, 6):
            self.arrived(bits)


class LineGather(Gather):
    def __init__(self, target, send, recv):
        row, col, z, _ = places()
        super().__init__(target, send, recv, in_line, z * 2 + col % 2)
        self.inner = jnp.logical_or(z == 1, z == 2)

    def start(self, source):
        for bits in (4, 2, 6, 1):
            self.copies[bits] = push(
                source,
                self.target.at[self.place],
                self.send.at[bits],
                self.recv.at[bits],
                in_line(self.row, self.col, bits),
            )
            if bits != 6:
                self.copies[bits].start()
        slot = self.target.at[flip(self.place, 4)]
        self.passing = push(
            slot, slot, self.send.at[0], self.recv.at[6], in_line(self.row, self.col, 2)
        )

        @pl.when(self.inner)
        def _():
            self.copies[6].start()

    def forward(self, bits):
        super().forward(bits)
        if bits == 4:

            @pl.when(self.inner)
            def _():
                self.passing.start()

    def close(self):
        for bits in (4, 2, 1):
            self.copies[bits].wait_send()
        for copy in self.onward.values():
            copy.wait_send()

        @pl.when(self.inner)
        def _():
            self.copies[6].wait_send()
            self.passing.wait_send()


class Scatter:
    def __init__(self, part, inbox, outbox, second, send, recv, peer=in_plane, place=None):
        self.part, self.inbox, self.outbox, self.second = part, inbox, outbox, second
        self.send, self.recv, self.peer = send, recv, peer
        self.row, self.col, _, self.place = places()
        if place is not None:
            self.place = place
        self.core = self.col % 2
        self.copies, self.sent = [], []

    def near(self, chip, number):
        copy = push(
            self.part.at[2 * chip + 1 - self.core],
            self.inbox.at[number],
            self.send.at[number],
            self.recv.at[number],
            self.peer(self.row, self.col, 1),
        )
        copy.start()
        self.copies.append(copy)

    def far(self, bits):
        self.copies[bits].wait_recv()
        chip = flip(self.place // 2, bits)
        total = self.part[2 * chip + self.core].astype(f32) + self.inbox[bits].astype(f32)
        self.outbox[bits - 1] = total.astype(bf16)
        copy = push(
            self.outbox.at[bits - 1],
            self.second.at[bits - 1],
            self.send.at[3 + bits],
            self.recv.at[3 + bits],
            self.peer(self.row, self.col, 2 * bits),
        )
        copy.start()
        self.sent.append(copy)

    def near_all(self):
        for bits in range(4):
            self.near(flip(self.place // 2, bits), bits)

    def far_all(self):
        for bits in (3, 2, 1):
            self.far(bits)

    def finish(self):
        self.copies[0].wait_recv()
        total = self.part[self.place].astype(f32) + self.inbox[0].astype(f32)
        for copy in self.sent:
            copy.wait_recv()
        for i in range(3):
            total = total + self.second[i].astype(f32)
        return total

    def close(self):
        for copy in self.copies + self.sent:
            copy.wait_send()


class LineScatter(Scatter):
    def __init__(self, part, inbox, outbox, second, send, recv, passed, sems):
        row, col, z, _ = places()
        super().__init__(part, inbox, outbox, second, send, recv, in_line, z * 2 + col % 2)
        self.passed, self.sems = passed, sems
        self.inner = jnp.logical_or(z == 1, z == 2)
        self.end = jnp.logical_not(self.inner)

    def sum_for(self, bits):
        self.copies[bits].wait_recv()
        chip = flip(self.place // 2, bits)
        return self.part[2 * chip + self.core].astype(f32) + self.inbox[bits].astype(f32)

    def to(self, bits):
        return push(
            self.outbox.at[bits - 1],
            self.second.at[bits - 1],
            self.send.at[3 + bits],
            self.recv.at[3 + bits],
            in_line(self.row, self.col, 2 * bits),
        )

    def far_all(self):
        self.outbox[2] = self.sum_for(3).astype(bf16)
        self.across = self.to(3)
        self.passing = push(
            self.outbox.at[2],
            self.passed,
            self.sems.at[0],
            self.sems.at[1],
            in_line(self.row, self.col, 2),
        )

        @pl.when(self.end)
        def _():
            self.passing.start()
            self.second[2] = jnp.zeros(self.second.shape[1:], bf16)

        @pl.when(self.inner)
        def _():
            self.across.start()

        total = self.sum_for(2)
        self.sent = [self.to(2), self.to(1)]

        @pl.when(self.end)
        def _():
            self.outbox[1] = total.astype(bf16)
            self.sent[0].start()

        self.outbox[0] = self.sum_for(1).astype(bf16)
        self.sent[1].start()

        @pl.when(self.inner)
        def _():
            self.passing.wait_recv()
            self.outbox[1] = (total + self.passed[...].astype(f32)).astype(bf16)
            self.sent[0].start()

    def finish(self):
        @pl.when(self.inner)
        def _():
            self.across.wait_recv()

        return super().finish()

    def close(self):
        super().close()

        @pl.when(self.inner)
        def _():
            self.across.wait_send()

        @pl.when(self.end)
        def _():
            self.passing.wait_send()


def scatter_scratch(rows, width):
    return [
        pltpu.VMEM((4, rows, width), bf16),
        pltpu.VMEM((3, rows, width), bf16),
        pltpu.VMEM((3, rows, width), bf16),
        pltpu.SemaphoreType.DMA((7,)),
        pltpu.SemaphoreType.DMA((7,)),
    ]


def fetch(source, target, semaphore):
    copy = pltpu.make_async_copy(source, target, semaphore)
    copy.start()
    return copy


def block(number, size):
    return pl.ds(pl.multiple_of(number * size, size), size)


def enter_body(
    x, wq, wo, wg, cot, ga, gf, variate, time, lengths, deal, freq,
    xp_out, wt_out, wop, wgp, cotp_out, s1_out, qkvt, gains, labels,
    xp, cotp, s1, keep, wqs, wline, wqp, wgs, cotr, cots, tile, tl, tiles, wt, box, cs, sn, times,
    sx, rx, sq, rq, sv, rv, st, rt, su, ru, sw, rw, sg, rg, sc, rc, sa, ra, sz, rz,
):
    row, col, z, place = places()
    quarter = col % QUAD
    y, core = col // 2 % 2, col % 2
    member = z * 2 + core
    lane = lax.broadcasted_iota(jnp.int32, (1, 128), 1)
    for line, gain in ((0, ga), (1, gf)):
        wide = gain[...].astype(f32)
        wide = jnp.concatenate([wide] * 4, axis=1)
        tile[line : line + 1, :] = jnp.where(lane // 32 == quarter, wide, 0.0)
    tile[2:3, :] = variate[...].astype(f32)
    tile[3:4, :] = time[...].astype(f32)
    numbers = jnp.zeros((1, 128), jnp.int32)
    for i in range(NSEQ):
        numbers = jnp.where(lane == i, lengths[0, i], numbers)
    tile[4:5, :] = numbers.astype(f32)
    tile[5:8, :] = jnp.zeros((3, 128), f32)
    for p in range(MEMBERS):
        for part in range(3):
            at = part * 1024 + p * 128
            wqs[p, :, part * 128 : part * 128 + 128] = wq[:, at : at + 128]
    meet([anyone(row, col, bits) for bits in range(1, 32)])
    first = []
    for bits in range(1, 8):
        there = in_line(row, col, bits)
        first.append(push(wqs.at[flip(member, bits)], wline.at[member], sq.at[bits], rq.at[bits], there))
        first[-1].start()
    for bits in (1, 2, 3):
        first.append(push(tile, tl.at[z], st.at[bits], rt.at[bits], on_line(row, col, bits)))
        first[-1].start()
    pieces = []
    for bits in range(1, 16):
        there = (row, flip(col, bits))
        pieces.append(push(cot.at[there[1]], cotr.at[col], sc.at[bits], rc.at[bits], there))
        pieces[-1].start()
    rows_in = LineGather(xp, sx, rx)
    rows_in.start(x)
    xp[member] = x[...]
    wline[member] = wqs[member]
    tl[z] = tile[...]
    cotr[col] = cot[col]
    for p in range(MEMBERS):
        for half in range(2):
            for plane in range(PLANES):
                unit = (p // QUAD) * 16 + plane * QUAD + p % QUAD
                at = half * 512 + plane * 128
                start = half * 4096 + unit * 128
                wgs[p, :, at : at + 128] = wg[:, start : start + 128]
    for copy in first:
        copy.wait_recv()
    column = row * 2 + y
    second = []
    for bits in (1, 2, 3):
        there = (flip(row, bits // 2), flip(col, bits % 2 * 2))
        second.append(push(wline, wqp.at[column], sv.at[bits], rv.at[bits], there))
        second[-1].start()
    wqp[column] = wline[...]
    for bits in range(1, 8):
        there = in_plane(row, col, bits)
        second.append(push(tl, tiles.at[place], su.at[bits], ru.at[bits], there))
        second[-1].start()
    tiles[place] = tl[...]
    blocks = []
    for bits in range(1, 8):
        there = in_plane(row, col, bits)
        blocks.append(
            push(wgs.at[flip(place, bits)], wgp.at[place], sg.at[bits], rg.at[bits], there)
        )
        blocks[-1].start()
    wgp[place] = wgs[place]
    for copy in pieces:
        copy.wait_recv()
    for j in range(16):
        cots[j * 8 : j * 8 + 8, :] = cotr[jnp.clip(deal[j], 0, 15)]
    cot_in = Gather(cotp, sa, ra)
    cot_in.start(cots)
    cotp[place] = cots[...]
    for copy in second:
        copy.wait_recv()
    for k in range(8):
        lanes = slice(k * 128, k * 128 + 128)
        r, plane = k // PLANES, k % PLANES
        gains[:, lanes] = (tiles[r * QUAD, plane] + tiles[r * QUAD + 1, plane]) + (
            tiles[r * QUAD + 2, plane] + tiles[r * QUAD + 3, plane]
        )
        times[:, lanes] = tiles[row * QUAD + y * 2 + k % 2, k // 2]
        wt[:, lanes] = jnp.transpose(
            jnp.concatenate(
                [wqp[r * 2 + j // 2, plane * 2 + j % 2] for j in range(4)], axis=0
            )
        )
    for k in range(16):
        labels[:, k * 128 : k * 128 + 128] = tiles[row * QUAD + k % QUAD, k // QUAD]
    phases = times[3:4, :] * freq[...]
    cs[...] = jnp.cos(phases)
    sn[...] = jnp.sin(phases)
    gain = gains[0:1, :]
    kept = [fetch(wt, wt_out, keep.at[2])]

    def project(chip):
        rows = block(chip, 256)
        values = jnp.concatenate([xp[2 * chip], xp[2 * chip + 1]], axis=0).astype(f32)
        scaled = (values * norm_scale(values) * gain).astype(bf16)
        s1[2 * chip] = scaled[0:128]
        s1[2 * chip + 1] = scaled[128:256]
        out = mm_nt(wt[...], scaled)
        cos_part, sin_part = cs[:, rows], sn[:, rows]
        for head in range(2):
            for part in range(2):
                base = part * 128 + head * 64
                former, latter = out[base : base + 32], out[base + 32 : base + 64]
                factor = 0.125 if part == 0 else 1.0
                turned = former * cos_part - latter * sin_part
                other = latter * cos_part + former * sin_part
                at = part * 64
                box[head, at : at + 32, rows] = (turned * factor).astype(bf16)
                box[head, at + 32 : at + 64, rows] = (other * factor).astype(bf16)
            at = 256 + head * 64
            box[head, 128:192, rows] = out[at : at + 64].astype(bf16)

    turned = []

    def exchange(chip, number):
        lanes = pl.ds(pl.multiple_of(chip * 512 + y * 256, 256), 256)
        copy = push(
            box.at[1 - y, :, block(chip, 256)],
            qkvt.at[:, lanes],
            sz.at[number],
            rz.at[number],
            (row, flip(col, 2)),
        )
        copy.start()
        turned.append(copy)
        qkvt[:, lanes] = box[y, :, block(chip, 256)]

    for k, bits in enumerate((0, 4, 2, 6)):
        if bits:
            rows_in.forward(bits)
        if bits == 4:
            cot_in.forward(2)
            cot_in.forward(4)
            cot_in.forward(6)
        rows_in.arrived(bits)
        chip = flip(z, bits // 2)
        project(chip)
        exchange(chip, k)
        if bits == 2:
            target = col // 2 % 2 * 2 + col // 4 % 2
            slot = col // 8 * 2 + col % 2
            for plane in range(PLANES):
                there = (row, plane * QUAD + target)
                mine = jnp.logical_and(z == plane, quarter == target)

                @pl.when(jnp.logical_not(mine))
                def _():
                    push(wo, wop.at[slot], sw.at[plane], rw.at[slot], there).start()

                @pl.when(mine)
                def _():
                    wop[slot] = wo[...]

    kept.append(fetch(xp, xp_out, keep.at[0]))
    kept.append(fetch(s1, s1_out, keep.at[1]))
    for bits in (0, 2, 4, 6):
        cot_in.arrived(bits)
    kept.append(fetch(cotp, cotp_out, keep.at[3]))
    for copy in blocks:
        copy.wait_recv()
    for j in range(4):
        source = j // 2 * 8 + core * 4 + y * 2 + j % 2
        mine = col == source

        @pl.when(jnp.logical_not(mine))
        def _():
            push(wo, wop.at[j], sw.at[j], rw.at[j], (row, source)).wait_recv()

    target = col // 2 % 2 * 2 + col // 4 % 2
    slot = col // 8 * 2 + col % 2
    for plane in range(PLANES):
        there = (row, plane * QUAD + target)
        mine = jnp.logical_and(z == plane, quarter == target)

        @pl.when(jnp.logical_not(mine))
        def _():
            push(wo, wop.at[slot], sw.at[plane], rw.at[slot], there).wait_send()

    for copy in turned:
        copy.wait()
    rows_in.close()
    cot_in.close()
    for copy in first + second + pieces + blocks:
        copy.wait_send()
    for copy in kept:
        copy.wait()


def split_three(value):
    high = value.astype(bf16).astype(f32)
    middle = (value - high).astype(bf16).astype(f32)
    return high, middle, (value - high - middle).astype(bf16).astype(f32)


def window_queries(qa, lanes, first, limit):
    place = first + lax.broadcasted_iota(jnp.int32, (16, WINDOW), 1)
    line = lax.broadcasted_iota(jnp.int32, (16, WINDOW), 0)
    extra = jnp.where(
        jnp.logical_and(line == 12, place >= limit), -1e30, qa[64:80, lanes].astype(f32)
    )
    return jnp.concatenate(
        [qa[0:64, lanes], extra.astype(bf16), jnp.zeros((AUG - 80, WINDOW), bf16)], axis=0
    )


def head_of():
    row, col, z, place = places()
    return (z * 2 + col % 2) * 2 + col // 2 % 2


def read_lengths(labels, info):
    lane = lax.broadcasted_iota(jnp.int32, (1, 128), 1)
    numbers = labels[4:5, 0:128]
    for i in range(NSEQ):
        info[i] = jnp.sum(jnp.where(lane == i, numbers, 0.0)).astype(jnp.int32)


def over_keys(start, length, step, carry):
    carry = lax.fori_loop(
        0, length // 2, lambda k, c: step((start + 2 * k) * 128, 256, c), carry
    )
    return lax.fori_loop(
        0, length % 2, lambda k, c: step((start + length - 1) * 128, 128, c), carry
    )


def attend_body(bias_all, qkvt, labels, att, den, low, qa, ka, kt, info):
    size = qkvt.shape[1]
    head = head_of()
    bias = (bias_all[0, head], bias_all[1, head])
    variate = labels[2:3, :]
    line = lax.broadcasted_iota(jnp.int32, (16, size), 0)
    same = (variate == (line % 4).astype(f32)).astype(f32)
    same_pieces = split_three(jnp.full((16, size), bias[0] - bias[1], f32))
    other_pieces = split_three(jnp.full((16, size), bias[1], f32))

    def choose(pieces, number):
        return jnp.where(number == 0, pieces[0], jnp.where(number == 1, pieces[1], pieces[2]))

    extra_q = jnp.where(line < 12, same, jnp.where(line == 12, 0.0, 1.0))
    extra_k = jnp.where(
        line < 12,
        same * choose(same_pieces, line // 4),
        jnp.where(line == 12, 1.0, choose(other_pieces, line - 13)),
    )
    qa[0:64, 0:size] = qkvt[0:64, :]
    qa[64:80, 0:size] = extra_q.astype(bf16)
    qa[80:AUG, 0:size] = jnp.zeros((AUG - 80, size), bf16)
    qa[:, size:] = jnp.zeros((AUG, WINDOW), bf16)
    kt[0:64, :] = qkvt[64:128, :]
    kt[64:80, :] = extra_k.astype(bf16)
    kt[80:AUG, :] = jnp.zeros((AUG - 80, size), bf16)
    ka[...] = jnp.transpose(kt[...])
    read_lengths(labels, info)

    def sequence(number, start):
        length = info[number]
        limit = (start + length) * 128

        def window(j, unused):
            first = (start + 4 * j) * 128
            lanes = pl.ds(pl.multiple_of(first, 128), WINDOW)
            queries = window_queries(qa, lanes, first, limit)

            def keys(first_key, count, running):
                total, numerator = running
                rows = pl.ds(pl.multiple_of(first_key, 128), count)
                weights = jnp.exp(mm(ka[rows, :], queries))
                total = total + jnp.sum(weights, axis=0, keepdims=True)
                numerator = numerator + mm(qkvt[128:192, rows], weights.astype(bf16))
                return total, numerator

            total, numerator = over_keys(
                start, length, keys, (jnp.zeros((1, WINDOW), f32), jnp.zeros((64, WINDOW), f32))
            )
            attended = numerator / total
            att[:, lanes] = attended
            den[:, lanes] = jnp.broadcast_to(total, (8, WINDOW))
            low[:, lanes] = attended.astype(bf16)
            return unused

        lax.fori_loop(0, (length + 3) // 4, window, 0)
        return start + length

    lax.fori_loop(0, NSEQ, sequence, 0)


def attend_back_body(
    qkvt, qa, ka, labels, freq, grad, att, den,
    dproj, bias_tile,
    dn, cw, vn, dq, dk, dv, info,
):
    size = qkvt.shape[1]
    lanes_all = slice(0, size)
    inverse = 1.0 / den[0:1, lanes_all]
    d_att = grad[...].astype(f32)
    dn[:, lanes_all] = (d_att * inverse).astype(bf16)
    dn[:, size:] = jnp.zeros((64, WINDOW), bf16)
    cw[:, lanes_all] = jnp.broadcast_to(
        jnp.sum(d_att * att[:, lanes_all], axis=0, keepdims=True) * inverse, (8, size)
    )
    cw[:, size:] = jnp.zeros((8, WINDOW), f32)
    vn[...] = jnp.transpose(qkvt[128:192, :])
    dk[...] = jnp.zeros_like(dk)
    dv[...] = jnp.zeros_like(dv)

    read_lengths(labels, info)

    def sequence(number, start):
        length = info[number]
        limit = (start + length) * 128

        def window(j, unused):
            first = (start + 4 * j) * 128
            lanes = pl.ds(pl.multiple_of(first, 128), WINDOW)
            queries = window_queries(qa, lanes, first, limit)
            upstream = dn[:, lanes]
            centre = cw[0:1, lanes]

            def keys(first_key, count, running):
                rows = pl.ds(pl.multiple_of(first_key, 128), count)
                weights = jnp.exp(mm(ka[rows, :], queries))
                d_scores = weights * (mm(vn[rows, :], upstream) - centre)
                rounded = d_scores.astype(bf16)
                dk[:, rows] += mm_nt(queries, rounded)
                dv[:, rows] += mm_nt(upstream, weights.astype(bf16))
                return running + mm(qkvt[64:128, rows], rounded)

            dq[:, lanes] = over_keys(start, length, keys, jnp.zeros((64, WINDOW), f32))
            return unused

        lax.fori_loop(0, (length + 3) // 4, window, 0)
        return start + length

    lax.fori_loop(0, NSEQ, sequence, 0)

    phases = labels[3:4, :] * freq[...]
    cos_part, sin_part = jnp.cos(phases), jnp.sin(phases)
    for part, source, factor in ((0, dq, 0.125), (1, dk, 1.0)):
        former, latter = source[0:32, lanes_all], source[32:64, lanes_all]
        dproj[part * 64 : part * 64 + 32, :] = (
            (former * cos_part + latter * sin_part) * factor
        ).astype(bf16)
        dproj[part * 64 + 32 : part * 64 + 64, :] = (
            (latter * cos_part - former * sin_part) * factor
        ).astype(bf16)
    dproj[128:192, :] = dv[...].astype(bf16)
    variate = labels[2:3, :]
    line = lax.broadcasted_iota(jnp.int32, (16, size), 0)
    match = jnp.logical_and(variate == line.astype(f32), line < 4)
    near = jnp.sum(jnp.where(match, dk[64:80, :], 0.0))
    every = jnp.sum(dk[77:78, :])
    lane = lax.broadcasted_iota(jnp.int32, (8, 128), 1)
    line8 = lax.broadcasted_iota(jnp.int32, (8, 128), 0)
    here = lane == head_of()
    bias_tile[...] = jnp.where(
        jnp.logical_and(here, line8 == 2),
        near,
        jnp.where(jnp.logical_and(here, line8 == 3), every - near, 0.0),
    )


def branch_body(
    low, wop, x, gains,
    atp, hidden, s2,
    atn, part, sz, rz, inbox, outbox, second, ss, rs,
):
    row, col, z, place = places()
    quarter = col % QUAD
    meet(plane_near(row, col) + column_all(row, col))
    rows, lanes = block(z % 2, 64), block(row, 512)
    for plane in range(PLANES):
        mine = jnp.logical_and(row == z // 2, z == plane)

        @pl.when(jnp.logical_not(mine))
        def _():
            push(
                low.at[:, plane * 512 : plane * 512 + 512], atp.at[rows, lanes],
                sz.at[plane], rz.at[row * 2 + z % 2], (z // 2, plane * QUAD + quarter),
            ).start()

        @pl.when(mine)
        def _():
            atp[rows, lanes] = low[:, plane * 512 : plane * 512 + 512]

    for j in range(4):
        source = (j // 2, (2 * row + j % 2) * QUAD + quarter)
        mine = jnp.logical_and(row == j // 2, z == 2 * row + j % 2)

        @pl.when(jnp.logical_not(mine))
        def _():
            push(
                low.at[:, 0:512], atp.at[0:64, 0:512], sz.at[j], rz.at[j], source
            ).wait_recv()

    for plane in range(PLANES):
        mine = jnp.logical_and(row == z // 2, z == plane)

        @pl.when(jnp.logical_not(mine))
        def _():
            push(
                low.at[:, plane * 512 : plane * 512 + 512], atp.at[rows, lanes],
                sz.at[plane], rz.at[row * 2 + z % 2], (z // 2, plane * QUAD + quarter),
            ).wait_send()

    atn[...] = jnp.transpose(atp[...])
    total = Scatter(part, inbox, outbox, second, ss, rs)
    core = col % 2
    for bits in (3, 2, 1, 0):
        chip = flip(place // 2, bits)
        part[2 * chip + 1 - core] = mm(atn[block(2 * chip + 1 - core, 128), :], wop[...]).astype(bf16)
    for bits in range(4):
        total.near(flip(place // 2, bits), bits)
    for bits in (3, 2, 1, 0):
        chip = flip(place // 2, bits)
        part[2 * chip + core] = mm(atn[block(2 * chip + core, 128), :], wop[...]).astype(bf16)
    total.far_all()
    state = x[...].astype(f32) + total.finish()
    hidden[...] = state
    s2[...] = (state * norm_scale(state) * gains[1:2, :]).astype(bf16)
    total.close()


def ffn_body(
    s2, cotp_in, wg_in, w_down, hidden, gains,
    out_keep, down_in, gwg_out, d_hidden, low, gain_term,
    cotp, wg, s2p, wgs, wd, actives, factors, inner_s, dgu, d_part, out_part, gwd, gwg, relayed, both_terms,
    keep, sa, ra, sw, rw, sd, rd, inbox, outbox, second, ss, rs,
):
    row, col, z, place = places()
    loads = [fetch(wg_in, wg, keep.at[0]), fetch(cotp_in, cotp, keep.at[1])]
    meet(plane_near(row, col) + line_all(row, col))
    rows_in = Gather(s2p, sa, ra)
    rows_in.start(s2)
    s2p[place] = s2[...]
    inner = jnp.logical_or(z == 1, z == 2)
    end = jnp.logical_not(inner)
    downs = {
        bits: push(
            w_down, wd.at[block(z, 128), :], sw.at[bits], rw.at[bits], on_line(row, col, bits)
        )
        for bits in (2, 1, 3)
    }
    passed = wd.at[block(flip(z, 2), 128), :]
    downs[0] = push(passed, passed, sw.at[0], rw.at[3], on_line(row, col, 1))
    downs[2].start()

    @pl.when(inner)
    def _():
        downs[3].start()

    downs[1].start()
    wd[block(z, 128), :] = w_down[...]
    loads[0].wait()
    for plane in range(PLANES):
        for r in range(2):
            at = (r * PLANES + plane) * 128
            wgs[at : at + 128, :] = wg[plane * 2 + r]
    for k in range(4):
        chip = flip(place // 2, k)
        if k:
            rows_in.forward(2 * k)
        rows_in.arrived(2 * k)
        if k == 1:
            downs[2].wait_recv()

            @pl.when(inner)
            def _():
                downs[0].start()

        rows = block(chip, 256)
        scaled = jnp.concatenate([s2p[2 * chip], s2p[2 * chip + 1]], axis=0)
        both = mm(scaled, wgs[...])
        gate, upper = both[:, 0:512], both[:, 512:1024]
        sig = jax.nn.sigmoid(gate)
        active = gate * sig
        inner_s[rows, :] = (active * upper).astype(bf16)
        actives[rows, :] = active
        factors[rows, :] = upper * sig * (1.0 + gate * (1.0 - sig))
    loads[1].wait()
    cot_all = jnp.concatenate([cotp[t] for t in range(MEMBERS)], axis=0)
    for k in range(4):
        cols = slice(k * 128, k * 128 + 128)
        gwd[k] = mm_tn(inner_s[:, cols], cot_all).astype(bf16)
    grads = {
        bits: push(
            gwd.at[flip(z, bits)], down_in.at[bits], sd.at[bits], rd.at[bits], on_line(row, col, bits)
        )
        for bits in (1, 3)
    }
    grads[2] = push(both_terms, down_in.at[2], sd.at[2], rd.at[2], on_line(row, col, 2))
    grads[0] = push(gwd.at[flip(z, 3)], relayed, sd.at[0], rd.at[0], on_line(row, col, 1))

    @pl.when(end)
    def _():
        grads[0].start()
        both_terms[...] = gwd[flip(z, 2)]
        grads[2].start()
        down_in[3] = jnp.zeros(down_in.shape[1:], bf16)

    @pl.when(inner)
    def _():
        grads[3].start()

    grads[1].start()
    down_in[0] = gwd[z]
    total = Scatter(d_part, inbox, outbox, second, ss, rs)
    downs[1].wait_recv()
    downs[3].wait_recv()
    for k in range(4):
        chip = flip(place // 2, k)
        rows = block(chip, 256)
        upstream = jnp.concatenate([cotp[2 * chip], cotp[2 * chip + 1]], axis=0)
        d_inner = mm_nt(upstream, wd[...])
        dgu[rows, 0:512] = (d_inner * factors[rows, :]).astype(bf16)
        dgu[rows, 512:1024] = (d_inner * actives[rows, :]).astype(bf16)
        tile = mm_nt(dgu[rows, :], wgs[...]).astype(bf16)
        d_part[2 * chip] = tile[0:128]
        d_part[2 * chip + 1] = tile[128:256]
        total.near(chip, k)
        if k > 1:
            total.far(k - 1)
        if k == 1:

            @pl.when(inner)
            def _():
                grads[0].wait_recv()
                both_terms[...] = (
                    gwd[flip(z, 2)].astype(f32) + relayed[...].astype(f32)
                ).astype(bf16)
                grads[2].start()

    for k in range(4):
        chip = flip(place // 2, k)
        tile = mm(inner_s[block(chip, 256), :], wd[...]).astype(bf16)
        out_part[2 * chip] = tile[0:128]
        out_part[2 * chip + 1] = tile[128:256]
        if k == 0:
            total.far(3)
    kept = [fetch(out_part, out_keep, keep.at[10])]
    for f in range(8):
        cols = slice(f * 128, f * 128 + 128)
        lhs = jnp.concatenate([s2p[t, :, cols] for t in range(MEMBERS)], axis=0)
        at = (f % PLANES) * 2 + f // PLANES
        gwg[at] = mm_tn(lhs, dgu[...]).astype(bf16)
        kept.append(fetch(gwg.at[at], gwg_out.at[at], keep.at[2 + f]))
    d_scaled = total.finish()
    state = hidden[...]
    scale = norm_scale(state)
    normed = state * scale
    gain_term[...] = jnp.broadcast_to(jnp.sum(d_scaled * normed, axis=0, keepdims=True), (8, 1024))
    d_state = cotp[place].astype(f32) + norm_back(d_scaled * gains[1:2, :], normed, scale)
    d_hidden[...] = d_state
    low[...] = d_state.astype(bf16)
    rows_in.close()
    total.close()
    grads[1].wait_recv()
    grads[2].wait_recv()
    for copy in (downs[1], downs[2], grads[1], grads[2]):
        copy.wait_send()

    @pl.when(inner)
    def _():
        grads[3].wait_recv()
        for copy in (downs[3], downs[0], grads[3]):
            copy.wait_send()

    @pl.when(end)
    def _():
        grads[0].wait_send()

    for copy in kept:
        copy.wait()


def attended_back_body(
    low, wop, atp,
    grad, gwo,
    dbp, dat, sg, rg, sz, rz,
):
    row, col, z, place = places()
    meet(plane_near(row, col) + column_all(row, col))
    quarter = col % QUAD
    rows_in = Gather(dbp, sg, rg)
    rows_in.start(low)
    dbp[place] = low[...]
    for k in range(4):
        chip = flip(place // 2, k)
        if k:
            rows_in.forward(2 * k)
        rows_in.arrived(2 * k)
        for core in range(2):
            dat[:, block(2 * chip + core, 128)] = mm_nt(wop[...], dbp[2 * chip + core]).astype(bf16)
        if k % 2 == 0:
            continue
        group = row if k == 1 else 1 - row
        for head in range(2):
            plane = 2 * row + head
            source = dat.at[head * 64 : head * 64 + 64, block(group, 512)]
            if k == 1:

                @pl.when(z != plane)
                def _():
                    push(
                        source, grad.at[:, block(z, 512)], sz.at[head], rz.at[z],
                        (group, plane * QUAD + quarter),
                    ).start()

                @pl.when(z == plane)
                def _():
                    grad[:, block(z, 512)] = source[...]

            else:
                push(
                    source, grad.at[:, block(z, 512)], sz.at[2 + head], rz.at[z],
                    (group, plane * QUAD + quarter),
                ).start()

    total = mm(atp[:, 0:128], dbp[0])
    for q in range(1, MEMBERS):
        total = total + mm(atp[:, q * 128 : q * 128 + 128], dbp[q])
    gwo[...] = total.astype(bf16)
    for plane in range(PLANES):
        mine = jnp.logical_and(row == z // 2, z == plane)

        @pl.when(jnp.logical_not(mine))
        def _():
            push(
                dat.at[0:64, 0:512], grad.at[:, plane * 512 : plane * 512 + 512], sz.at[0],
                rz.at[plane], (z // 2, plane * QUAD + quarter),
            ).wait_recv()

    for head in range(2):
        plane = 2 * row + head

        @pl.when(z != plane)
        def _():
            push(
                dat.at[0:64, 0:512], grad.at[:, 0:512], sz.at[head], rz.at[z],
                (row, plane * QUAD + quarter),
            ).wait_send()

        push(
            dat.at[0:64, 0:512], grad.at[:, 0:512], sz.at[2 + head], rz.at[z],
            (1 - row, plane * QUAD + quarter),
        ).wait_send()

    rows_in.close()


def last_body(
    dproj, wt_in, s1_in, xp_in, out_in, gains, d_hidden, hidden, gwo, gwg, gain_two, bias_tile, deal,
    grad_tokens, gqin, goin, gwg_in, sums, out,
    wt, s1, xp, out_part, pieces, slots, keep, dpt, dpn, part, gq, gqcol, gqsum, pack, packs, packed,
    passed, sz, rz, inbox, outbox, second, ss, rs, sp,
    sq, rq, sv, rv, st, rt, su, ru, sw, rw, sg, rg, sc, rc, inbox2, outbox2, second2, ss2, rs2,
):
    row, col, z, place = places()
    quarter = col % QUAD
    y, core = col // 2 % 2, col % 2
    member = z * 2 + core
    column = row * 2 + y
    loads = [
        fetch(out_in, out_part, keep.at[3]),
        fetch(s1_in, s1, keep.at[0]),
        fetch(xp_in, xp, keep.at[1]),
        fetch(wt_in, wt, keep.at[2]),
    ]
    meet([anyone(row, col, bits) for bits in range(1, 32)])
    copies = []
    for plane in range(PLANES):
        ours = pl.ds(pl.multiple_of(plane * 512 + y * 256, 256), 256)
        theirs = pl.ds(pl.multiple_of(plane * 512 + (1 - y) * 256, 256), 256)
        lanes = slice(plane * 256, plane * 256 + 256)
        copy = push(
            dproj.at[:, theirs], dpt.at[y, :, lanes], sz.at[plane], rz.at[plane], (row, flip(col, 2))
        )
        copy.start()
        copies.append(copy)
        dpt[y, :, lanes] = dproj[:, ours]
    owner = core * 4 + y * 2
    for j in range(4):
        there = (row, j // 2 * 8 + owner + j % 2)
        mine = col == there[1]

        @pl.when(jnp.logical_not(mine))
        def _():
            push(gwo.at[j], goin.at[z], sw.at[j], rw.at[z], there).start()

        @pl.when(mine)
        def _():
            goin[z] = gwo[j]

    loads[0].wait()
    output = Scatter(out_part, inbox2, outbox2, second2, ss2, rs2)
    output.near_all()
    output.far_all()
    spread = []
    for bits in range(1, 8):
        there = in_plane(row, col, bits)
        copy = push(gwg.at[flip(place, bits)], gwg_in.at[place], sg.at[bits], rg.at[bits], there)
        copy.start()
        spread.append(copy)
    gwg_in[place] = gwg[place]
    for copy in loads[1:]:
        copy.wait()
    for copy in copies:
        copy.wait_recv()
    for plane in range(PLANES):
        lanes = slice(plane * 256, plane * 256 + 256)
        for kind in range(3):
            both = jnp.concatenate(
                [dpt[head, kind * 64 : kind * 64 + 64, lanes] for head in range(2)], axis=0
            )
            dpn[lanes, kind * 128 : kind * 128 + 128] = jnp.transpose(both)
    total = LineScatter(part, inbox, outbox, second, ss, rs, passed, sp)
    term = jnp.zeros((1, 1024), f32)
    for own in range(2):
        for bits in (3, 2, 1, 0):
            number = 2 * flip(z, bits) + (core if own else 1 - core)
            values = xp[number].astype(f32)
            d_scaled = mm(dpn[block(number, 128), :], wt[...])
            term = term + jnp.sum(d_scaled * (values * norm_scale(values)), axis=0, keepdims=True)
            part[number] = d_scaled.astype(bf16)
        if own == 0:
            for bits in range(4):
                total.near(flip(z, bits), bits)
    total.far_all()
    for f in range(8):
        lhs = jnp.concatenate([s1[t, :, f * 128 : f * 128 + 128] for t in range(MEMBERS)], axis=0)
        chunk = mm_tn(lhs, dpn[...]).astype(bf16)
        for j in range(4):
            gq[f // PLANES * 2 + j // 2, f % PLANES * 2 + j % 2] = chunk[j * 32 : j * 32 + 32, :]
    columns = []
    for bits in (3, 2, 1):
        there = (flip(row, bits // 2), flip(col, bits % 2 * 2))
        copy = push(
            gq.at[flip(column, bits)], gqcol.at[bits - 1], sv.at[bits], rv.at[bits], there
        )
        copy.start()
        columns.append(copy)
    for k in range(8):
        pack[k] = bias_tile[...]
        pack[k, 0:1, :] = term[:, k * 128 : k * 128 + 128]
        pack[k, 1:2, :] = gain_two[0:1, k * 128 : k * 128 + 128]
    first = []
    for bits in range(1, 8):
        there = in_plane(row, col, bits)
        copy = push(
            pack.at[pl.ds(there[0] * PLANES, PLANES)], packs.at[place], st.at[bits], rt.at[bits], there
        )
        copy.start()
        first.append(copy)
    packs[place] = pack[pl.ds(row * PLANES, PLANES)]
    rows_out = (hidden[...] + output.finish()).astype(bf16)
    for j in range(16):
        pieces[j] = rows_out[j * 8 : j * 8 + 8, :]
    for d in range(16):
        number = 0
        for j in range(1, 16):
            number = jnp.where(deal[j] == d, j, number)
        slots[d] = pieces[number]
    for bits in range(1, 16):
        there = (row, flip(col, bits))
        copy = push(slots.at[there[1]], out.at[col], sc.at[bits], rc.at[bits], there)
        copy.start()
        spread.append(copy)
    out[col] = slots[col]
    for copy in first:
        copy.wait_recv()
    summed = packs[0]
    for p in range(1, MEMBERS):
        summed = summed + packs[p]
    packed[...] = summed
    for bits in (1, 2, 3):
        copy = push(
            packed.at[flip(z, bits)], sums.at[z], su.at[bits], ru.at[bits], on_line(row, col, bits)
        )
        copy.start()
        spread.append(copy)
    sums[z] = packed[z]
    for copy in columns:
        copy.wait_recv()
    for m in range(MEMBERS):
        gqsum[m] = (
            (gq[column, m].astype(f32) + gqcol[0, m].astype(f32))
            + (gqcol[1, m].astype(f32) + gqcol[2, m].astype(f32))
        ).astype(bf16)
    for bits in range(7, 0, -1):
        there = in_line(row, col, bits)
        copy = push(gqsum.at[flip(member, bits)], gqin.at[member], sq.at[bits], rq.at[bits], there)
        copy.start()
        spread.append(copy)
    gqin[member] = gqsum[member]
    d_one = total.finish()
    own_rows = xp[member].astype(f32)
    scale = norm_scale(own_rows)
    grad_tokens[...] = (
        d_hidden[...] + norm_back(d_one * gains[0:1, :], own_rows * scale, scale)
    ).astype(bf16)
    for copy in spread:
        copy.wait_recv()
    senders = col // 2 % 2 * 2 + col // 4 % 2
    for plane in range(PLANES):
        mine = jnp.logical_and(quarter == senders, z == plane)

        @pl.when(jnp.logical_not(mine))
        def _():
            push(
                gwo.at[0], goin.at[plane], sw.at[0], rw.at[plane], (row, plane * QUAD + senders)
            ).wait_recv()

    for j in range(4):
        there = (row, j // 2 * 8 + owner + j % 2)
        mine = col == there[1]

        @pl.when(jnp.logical_not(mine))
        def _():
            push(gwo.at[j], goin.at[z], sw.at[j], rw.at[z], there).wait_send()

    for copy in copies + columns + first + spread:
        copy.wait_send()
    total.close()
    output.close()


def finish_body(
    grad_tokens_in, gqin, goin, out_in, gwg, gwd, tiles,
    out, grad_tokens, grad_q, grad_o, grad_gu, grad_d, grad_gains, grad_bias,
):
    grad_tokens[...] = grad_tokens_in[...]
    out[...] = out_in[...]
    grad_o[...] = (goin[0].astype(f32) + goin[1].astype(f32)) + (
        goin[2].astype(f32) + goin[3].astype(f32)
    )
    grad_d[...] = (gwd[0].astype(f32) + gwd[1].astype(f32)) + (
        gwd[2].astype(f32) + gwd[3].astype(f32)
    )
    for p in range(MEMBERS):
        total = gqin[p].astype(f32)
        for kind in range(3):
            at = kind * 1024 + p * 128
            grad_q[:, at : at + 128] = total[:, kind * 128 : kind * 128 + 128]
        for half in range(2):
            for plane in range(PLANES):
                unit = (p // QUAD) * 16 + plane * QUAD + p % QUAD
                at = half * 512 + plane * 128
                start = half * 4096 + unit * 128
                grad_gu[:, start : start + 128] = gwg[p, :, at : at + 128].astype(f32)
    total = (tiles[0] + tiles[1]) + (tiles[2] + tiles[3])
    quarter = lax.axis_index("col") % QUAD
    chosen = jnp.zeros((2, 32), f32)
    for k in range(4):
        chosen = chosen + jnp.where(quarter == k, total[0:2, k * 32 : k * 32 + 32], 0.0)
    grad_gains[...] = chosen
    grad_bias[...] = total[2:4, 0:16]


def sds(shape, dtype):
    return jax.ShapeDtypeStruct(shape, dtype)


def dma(*shape):
    return pltpu.SemaphoreType.DMA(shape)


def kernel(body, name, specs, outs, scratch, number=None, cost=0, places_out=None):
    params = dict(vmem_limit_bytes=56 << 20)
    if number is not None:
        params.update(collective_id=number, has_side_effects=True)
    return pl.pallas_call(
        body,
        name=name,
        in_specs=specs,
        out_shape=outs,
        out_specs=places_out or [VM] * len(outs),
        scratch_shapes=scratch,
        compiler_params=pltpu.CompilerParams(**params),
        cost_estimate=pl.CostEstimate(flops=cost, bytes_accessed=cost // 300, transcendentals=0),
    )


def plane_shards(
    tokens, variate_ids, time_ids, lengths, deal, w_qkv, w_out, w_gate_up, w_down,
    gain_attn, gain_ffn, var_bias, cotangent,
):
    rows, width = tokens.shape
    lines = [[plane * QUAD + k for plane in range(PLANES)] for k in range(QUAD)]
    freq = jnp.asarray(np.exp(-math.log(10000.0) * np.arange(32) / 32).astype(np.float32)[:, None])
    target = deal[0, 0]

    xp, wt, wop, wgp, cotp, s1, qkvt, gains, labels = kernel(
        enter_body,
        "enter",
        [VM] * 9 + [SM, SM, VM],
        [
            sds((8, rows, width), bf16),
            sds((384, 1024), bf16),
            sds((4, 32, 1024), bf16),
            sds((8, 32, 1024), bf16),
            sds((8, rows, width), bf16),
            sds((8, rows, width), bf16),
            sds((192, 2048), bf16),
            sds((8, 1024), f32),
            sds((8, 2048), f32),
        ],
        [
            pltpu.VMEM((8, rows, width), bf16),
            pltpu.VMEM((8, rows, width), bf16),
            pltpu.VMEM((8, rows, width), bf16),
            dma(4),
            pltpu.VMEM((8, 32, 384), bf16),
            pltpu.VMEM((8, 32, 384), bf16),
            pltpu.VMEM((4, 8, 32, 384), bf16),
            pltpu.VMEM((8, 32, 1024), bf16),
            pltpu.VMEM((16, 8, width), bf16),
            pltpu.VMEM((rows, width), bf16),
            pltpu.VMEM((8, 128), f32),
            pltpu.VMEM((4, 8, 128), f32),
            pltpu.VMEM((8, 4, 8, 128), f32),
            pltpu.VMEM((384, 1024), bf16),
            pltpu.VMEM((2, 192, 1024), bf16),
            pltpu.VMEM((32, 1024), f32),
            pltpu.VMEM((32, 1024), f32),
            pltpu.VMEM((8, 1024), f32),
        ]
        + [dma(8), dma(8), dma(8), dma(8), dma(4), dma(4), dma(4), dma(4), dma(8), dma(8)]
        + [dma(4), dma(4), dma(8), dma(8), dma(16), dma(16), dma(8), dma(8), dma(4), dma(4)],
        number=1,
        places_out=[ANY, ANY, VM, VM, ANY, ANY, VM, VM, VM],
    )(
        tokens, w_qkv, w_out, w_gate_up, cotangent.reshape(16, 8, width), gain_attn[None],
        gain_ffn[None], variate_ids[None], time_ids[None], lengths, target, freq,
    )

    gate_up = lax.all_gather(
        wgp.reshape(256, 1024), "col", axis=0, tiled=True, axis_index_groups=lines
    )
    wop = wop.reshape(128, 1024)

    wide = 2048 + WINDOW
    att, den, low, qa, ka = kernel(
        attend_body,
        "attend",
        [SM, VM, VM],
        [
            sds((64, wide), f32),
            sds((8, wide), f32),
            sds((64, wide), bf16),
            sds((AUG, wide), bf16),
            sds((2048, AUG), bf16),
        ],
        [pltpu.VMEM((AUG, 2048), bf16), pltpu.SMEM((8,), jnp.int32)],
        cost=2 * 10**9,
    )(var_bias, qkvt, labels)

    atp, hidden, s2 = kernel(
        branch_body,
        "branch",
        [VM] * 4,
        [sds((128, 1024), bf16), sds((rows, width), f32), sds((rows, width), bf16)],
        [
            pltpu.VMEM((1024, 128), bf16),
            pltpu.VMEM((8, rows, width), bf16),
            dma(4), dma(4),
        ]
        + scatter_scratch(rows, width),
        number=2,
    )(low, wop, tokens, gains)

    out_part, down_in, gwg, d_hidden, d_branch, gain_two = kernel(
        ffn_body,
        "ffn",
        [VM, ANY, ANY, VM, VM, VM],
        [
            sds((8, rows, width), bf16),
            sds((4, rows, width), bf16),
            sds((8, 128, 1024), bf16),
            sds((rows, width), f32),
            sds((rows, width), bf16),
            sds((8, 1024), f32),
        ],
        [
            pltpu.VMEM((8, rows, width), bf16),
            pltpu.VMEM((8, 128, 1024), bf16),
            pltpu.VMEM((8, rows, width), bf16),
            pltpu.VMEM((1024, 1024), bf16),
            pltpu.VMEM((512, width), bf16),
            pltpu.VMEM((1024, 512), f32),
            pltpu.VMEM((1024, 512), f32),
            pltpu.VMEM((1024, 512), bf16),
            pltpu.VMEM((1024, 1024), bf16),
            pltpu.VMEM((8, rows, width), bf16),
            pltpu.VMEM((8, rows, width), bf16),
            pltpu.VMEM((4, rows, width), bf16),
            pltpu.VMEM((8, 128, 1024), bf16),
            pltpu.VMEM((rows, width), bf16),
            pltpu.VMEM((rows, width), bf16),
            dma(11), dma(8), dma(8), dma(4), dma(4), dma(4), dma(4),
        ]
        + scatter_scratch(rows, width),
        number=3,
        cost=10**10,
        places_out=[ANY, VM, ANY, VM, VM, VM],
    )(s2, cotp, gate_up.reshape(8, 128, 1024), w_down, hidden, gains)

    gate_up_sum = lax.psum_scatter(
        gwg.reshape(1024, 1024), "col", scatter_dimension=0, tiled=True, axis_index_groups=lines
    )

    grad, gwo = kernel(
        attended_back_body,
        "attended_back",
        [VM] * 3,
        [sds((64, 2048), bf16), sds((128, 1024), bf16)],
        [
            pltpu.VMEM((8, rows, width), bf16),
            pltpu.VMEM((128, 1024), bf16),
            dma(8), dma(8), dma(4), dma(4),
        ],
        number=4,
    )(d_branch, wop, atp)

    dproj, bias_tile = kernel(
        attend_back_body,
        "attend_back",
        [VM] * 8,
        [sds((192, 2048), bf16), sds((8, 128), f32)],
        [
            pltpu.VMEM((64, wide), bf16),
            pltpu.VMEM((8, wide), f32),
            pltpu.VMEM((2048, 64), bf16),
            pltpu.VMEM((64, wide), f32),
            pltpu.VMEM((AUG, 2048), f32),
            pltpu.VMEM((64, 2048), f32),
            pltpu.SMEM((8,), jnp.int32),
        ],
        cost=5 * 10**9,
    )(qkvt, qa, ka, labels, freq, grad, att, den)

    grad_tokens, gqin, goin, gwg_in, sums, out = kernel(
        last_body,
        "last",
        [VM] + [ANY] * 4 + [VM] * 7 + [SM],
        [
            sds((rows, width), bf16),
            sds((8, 32, 384), bf16),
            sds((4, 32, 1024), bf16),
            sds((8, 32, 1024), bf16),
            sds((4, 8, 128), f32),
            sds((16, 8, width), bf16),
        ],
        [
            pltpu.VMEM((384, 1024), bf16),
            pltpu.VMEM((8, rows, width), bf16),
            pltpu.VMEM((8, rows, width), bf16),
            pltpu.VMEM((8, rows, width), bf16),
            pltpu.VMEM((16, 8, width), bf16),
            pltpu.VMEM((16, 8, width), bf16),
            dma(4),
            pltpu.VMEM((2, 192, 1024), bf16),
            pltpu.VMEM((1024, 384), bf16),
            pltpu.VMEM((8, rows, width), bf16),
            pltpu.VMEM((4, 8, 32, 384), bf16),
            pltpu.VMEM((3, 8, 32, 384), bf16),
            pltpu.VMEM((8, 32, 384), bf16),
            pltpu.VMEM((8, 8, 128), f32),
            pltpu.VMEM((8, 4, 8, 128), f32),
            pltpu.VMEM((4, 8, 128), f32),
            pltpu.VMEM((rows, width), bf16),
            dma(4), dma(4),
        ]
        + scatter_scratch(rows, width)
        + [dma(2), dma(8), dma(8), dma(4), dma(4), dma(8), dma(8), dma(4), dma(4)]
        + [dma(4), dma(4), dma(8), dma(8), dma(16), dma(16)]
        + scatter_scratch(rows, width),
        number=5,
    )(
        dproj, wt, s1, xp, out_part, gains, d_hidden, hidden, gwo.reshape(4, 32, 1024),
        gate_up_sum.reshape(8, 32, 1024), gain_two, bias_tile, target,
    )
    out, grad_tokens, grad_q, grad_o, grad_gate_up, grad_down, gain_grads, bias_grads = kernel(
        finish_body,
        "finish",
        [VM] * 7,
        [
            sds((rows, width), bf16),
            sds((rows, width), bf16),
            sds((32, 3072), f32),
            sds((32, 1024), f32),
            sds((32, 8192), f32),
            sds((rows, width), f32),
            sds((2, 32), f32),
            sds((2, 16), f32),
        ],
        [],
    )(
        grad_tokens, gqin, goin, out.reshape(rows, width), gwg_in,
        down_in, sums,
    )
    return (
        out,
        grad_tokens,
        grad_q,
        grad_o,
        grad_gate_up,
        grad_down,
        gain_grads[0],
        gain_grads[1],
        bias_grads,
    )


def solution(mesh):
    planes = mesh.shape["row"] == 2 and mesh.shape["col"] == PLANES * QUAD
    return jax.shard_map(
        plane_shards if planes else shards,
        mesh=mesh,
        in_specs=(
            P(("row", "col"), None),
            P(("row", "col")),
            P(("row", "col")),
            P("row", None),
            P("row", "col", None),
            P(("row", "col"), None),
            P(("row", "col"), None),
            P(("row", "col"), None),
            P(("row", "col"), None),
            P(("row", "col")),
            P(("row", "col")),
            P(),
            P(("row", "col"), None),
        ),
        out_specs=(
            P(("row", "col"), None),
            P(("row", "col"), None),
            P(("row", "col"), None),
            P(("row", "col"), None),
            P(("row", "col"), None),
            P(("row", "col"), None),
            P(("row", "col")),
            P(("row", "col")),
            P(),
        ),
        check_vma=False,
    )
```

```python
import math

import jax
import jax.numpy as jnp
import numpy as np
from jax import lax
from jax.experimental import pallas as pl
from jax.experimental.pallas import tpu as pltpu
from jax.sharding import PartitionSpec as P

HEAD_DIM = 64
UNIT = 128
KEY_BLOCK = 1024
NSEQ = 6


epsilon = 1e-05


def contract_rows(operand, factor):
    return lax.dot_general(
        operand, factor, (((0,), (0,)), ((), ())), preferred_element_type=jnp.float32
    )


def contract_cols(operand, factor):
    return lax.dot_general(
        operand, factor, (((1,), (1,)), ((), ())), preferred_element_type=jnp.float32
    )


def angles(time_ids):
    half_dim = HEAD_DIM // 2
    inverse_freq = jnp.exp(-math.log(10000.0) * jnp.arange(half_dim, dtype=jnp.float32) / half_dim)
    phases = time_ids.astype(jnp.float32)[:, None] * inverse_freq[None, :]
    return (jnp.cos(phases)[:, None, :], jnp.sin(phases)[:, None, :])


def rotate(tensor, cos_part, sin_part):
    half_dim = tensor.shape[-1] // 2
    former = tensor[..., :half_dim]
    latter = tensor[..., half_dim:]
    return jnp.concatenate(
        [former * cos_part - latter * sin_part, latter * cos_part + former * sin_part], axis=-1
    )


def unrotate(tensor, cos_part, sin_part):
    half_dim = tensor.shape[-1] // 2
    former = tensor[..., :half_dim]
    latter = tensor[..., half_dim:]
    return jnp.concatenate(
        [former * cos_part + latter * sin_part, latter * cos_part - former * sin_part], axis=-1
    )


def norm_scale(values):
    return lax.rsqrt(jnp.mean(values * values, axis=-1, keepdims=True) + epsilon)


def norm_back(d_normed, normed, scale):
    return scale * (d_normed - normed * jnp.mean(d_normed * normed, axis=-1, keepdims=True))


def score_weights(queries, query_seq, query_var, key_block, seq_block, var_block, var_bias):
    scores = (
        jnp.einsum("qhd,khd->hqk", queries, key_block, preferred_element_type=jnp.float32) * 0.125
    )
    matched = query_var[:, None] == var_block[None, :]
    scores = scores + jnp.where(
        matched[None], var_bias[0][:, None, None], var_bias[1][:, None, None]
    )
    within = query_seq[:, None] == seq_block[None, :]
    return (jnp.where(within[None], jnp.exp(scores), 0.0), matched)


def shards(
    tokens,
    variate_ids,
    time_ids,
    lengths,
    deal,
    w_qkv,
    w_out,
    w_gate_up,
    w_down,
    gain_attn,
    gain_ffn,
    var_bias,
    cotangent,
):
    tok_rows, model_width = tokens.shape
    n_col = lax.axis_size("col")
    col_index = lax.axis_index("col")
    piece_len = tok_rows // n_col
    head_count = model_width // HEAD_DIM
    bounds = jnp.cumsum(lengths[0]) * UNIT
    position = col_index * tok_rows + jnp.arange(tok_rows, dtype=jnp.int32)
    seq_own = jnp.sum((position[:, None] >= bounds[None, :]).astype(jnp.int32), axis=1)
    target = deal[0, 0]
    slots = jnp.arange(n_col, dtype=jnp.int32)
    inverse = jnp.sum(
        slots[:, None] * (target[:, None] == slots[None, :]).astype(jnp.int32), axis=0
    )
    send_rows = jnp.take(tokens.reshape(n_col, piece_len, model_width), inverse, axis=0)
    labels = jnp.stack(
        [
            seq_own.reshape(n_col, piece_len),
            variate_ids.reshape(n_col, piece_len),
            time_ids.reshape(n_col, piece_len),
        ],
        axis=1,
    )
    send_labels = jnp.take(labels, inverse, axis=0)
    got_rows, got_labels = (
        lax.all_to_all(send_rows, "col", split_axis=0, concat_axis=0, tiled=True),
        lax.all_to_all(send_labels, "col", split_axis=0, concat_axis=0, tiled=True),
    )
    inputs = got_rows.reshape(tok_rows, model_width).astype(jnp.float32)
    seq_q = got_labels[:, 0, :].reshape(tok_rows)
    var_q = got_labels[:, 1, :].reshape(tok_rows)
    cos_part, sin_part = angles(got_labels[:, 2, :].reshape(tok_rows))
    qkv_full, out_full, gate_up_full, down_full, gain_one, gain_two = (
        lax.all_gather(w_qkv, ("row", "col"), axis=0, tiled=True),
        lax.all_gather(w_out, ("row", "col"), axis=0, tiled=True),
        lax.all_gather(w_gate_up, ("row", "col"), axis=0, tiled=True),
        lax.all_gather(w_down, ("row", "col"), axis=0, tiled=True),
        lax.all_gather(gain_attn, ("row", "col"), axis=0, tiled=True),
        lax.all_gather(gain_ffn, ("row", "col"), axis=0, tiled=True),
    )
    scale_one = norm_scale(inputs)
    normed_one = inputs * scale_one
    scaled_one = (normed_one * gain_one.astype(jnp.float32)).astype(jnp.bfloat16)
    projected = jnp.dot(scaled_one, qkv_full, preferred_element_type=jnp.float32)
    shaped = projected.reshape(tok_rows, 3, head_count, HEAD_DIM)
    queries = rotate(shaped[:, 0], cos_part, sin_part).astype(jnp.bfloat16)
    key_own = (
        rotate(shaped[:, 1], cos_part, sin_part).astype(jnp.bfloat16).reshape(tok_rows, model_width)
    )
    value_own = projected[:, 2 * model_width :].astype(jnp.bfloat16)
    keys_all, values_all, seq_k, var_k = (
        lax.all_gather(key_own, "col", axis=0, tiled=True),
        lax.all_gather(value_own, "col", axis=0, tiled=True),
        lax.all_gather(seq_q, "col", axis=0, tiled=True),
        lax.all_gather(var_q, "col", axis=0, tiled=True),
    )
    group_size = keys_all.shape[0]
    stride = min(KEY_BLOCK, group_size)
    block_count = group_size // stride

    def split_blocks(key_rows, value_rows, key_seq, key_var):
        return (
            key_rows.reshape(block_count, stride, head_count, HEAD_DIM),
            value_rows.reshape(block_count, stride, head_count, HEAD_DIM),
            key_seq.reshape(block_count, stride),
            key_var.reshape(block_count, stride),
        )

    def forward_step(running, block_data):
        denominator, numerator = running
        key_block, value_block, seq_block, var_block = block_data
        weights = score_weights(queries, seq_q, var_q, key_block, seq_block, var_block, var_bias)[0]
        denominator = denominator + jnp.sum(weights, axis=-1)
        numerator = numerator + jnp.einsum(
            "hqk,khd->qhd",
            weights.astype(jnp.bfloat16),
            value_block,
            preferred_element_type=jnp.float32,
        )
        return ((denominator, numerator), None)

    (denominator, numerator), unused = lax.scan(
        forward_step,
        (
            jnp.zeros((head_count, tok_rows), jnp.float32),
            jnp.zeros((tok_rows, head_count, HEAD_DIM), jnp.float32),
        ),
        split_blocks(keys_all, values_all, seq_k, var_k),
    )
    attended = numerator / denominator.T[:, :, None]
    attn_low = attended.reshape(tok_rows, model_width).astype(jnp.bfloat16)
    hidden_state = inputs + jnp.dot(attn_low, out_full, preferred_element_type=jnp.float32)
    scale_two = norm_scale(hidden_state)
    normed_two = hidden_state * scale_two
    scaled_two = (normed_two * gain_two.astype(jnp.float32)).astype(jnp.bfloat16)
    gate_up = jnp.dot(scaled_two, gate_up_full, preferred_element_type=jnp.float32)
    hidden_units = gate_up_full.shape[1] // 2
    gate_part = gate_up[:, :hidden_units]
    upper_part = gate_up[:, hidden_units:]
    sigmoid_gate = jax.nn.sigmoid(gate_part)
    active = gate_part * sigmoid_gate
    inner_act = (active * upper_part).astype(jnp.bfloat16)
    ffn_branch = jnp.dot(inner_act, down_full, preferred_element_type=jnp.float32)
    output = (hidden_state + ffn_branch).astype(jnp.bfloat16)
    qkv_back, out_back, gate_up_back, down_back, gain_one_back, gain_two_back = (
        lax.all_gather(w_qkv, ("row", "col"), axis=0, tiled=True),
        lax.all_gather(w_out, ("row", "col"), axis=0, tiled=True),
        lax.all_gather(w_gate_up, ("row", "col"), axis=0, tiled=True),
        lax.all_gather(w_down, ("row", "col"), axis=0, tiled=True),
        lax.all_gather(gain_attn, ("row", "col"), axis=0, tiled=True),
        lax.all_gather(gain_ffn, ("row", "col"), axis=0, tiled=True),
    )
    d_inner = contract_cols(cotangent, down_back)
    d_gate = (
        d_inner * upper_part * sigmoid_gate * (1.0 + gate_part * (1.0 - sigmoid_gate))
    ).astype(jnp.bfloat16)
    d_upper = (d_inner * active).astype(jnp.bfloat16)
    d_gate_up = jnp.concatenate([d_gate, d_upper], axis=1)
    d_scaled_two = contract_cols(d_gate_up, gate_up_back)
    term_gain_two = jnp.sum(d_scaled_two * normed_two, axis=0)
    term_gate_up = contract_rows(scaled_two, d_gate_up)
    term_down = contract_rows(inner_act, cotangent)
    d_hidden = cotangent.astype(jnp.float32) + norm_back(
        d_scaled_two * gain_two_back.astype(jnp.float32), normed_two, scale_two
    )
    d_branch = d_hidden.astype(jnp.bfloat16)
    term_out = contract_rows(attn_low, d_branch)
    d_attended = contract_cols(d_branch, out_back).reshape(tok_rows, head_count, HEAD_DIM)
    d_numerator = (d_attended / denominator.T[:, :, None]).astype(jnp.bfloat16)
    centre = (jnp.sum(d_attended * attended, axis=-1) / denominator.T).T
    back_keys = (
        lax.all_gather(key_own, "col", axis=0, tiled=True),
        lax.all_gather(value_own, "col", axis=0, tiled=True),
        lax.all_gather(seq_q, "col", axis=0, tiled=True),
        lax.all_gather(var_q, "col", axis=0, tiled=True),
    )

    def query_step(running, block_data):
        d_queries, same_sum, other_sum = running
        key_block, value_block, seq_block, var_block = block_data
        weights, matched = score_weights(
            queries, seq_q, var_q, key_block, seq_block, var_block, var_bias
        )
        d_probs = jnp.einsum(
            "qhd,khd->hqk", d_numerator, value_block, preferred_element_type=jnp.float32
        )
        d_scores = weights * (d_probs - centre[:, :, None])
        same_sum = same_sum + jnp.sum(jnp.where(matched[None], d_scores, 0.0), axis=(1, 2))
        other_sum = other_sum + jnp.sum(jnp.where(matched[None], 0.0, d_scores), axis=(1, 2))
        d_rounded = d_scores.astype(jnp.bfloat16)
        d_queries = d_queries + jnp.einsum(
            "hqk,khd->qhd", d_rounded, key_block, preferred_element_type=jnp.float32
        )
        return ((d_queries, same_sum, other_sum), (d_rounded, weights.astype(jnp.bfloat16)))

    def query_and_key_step(running, block_data):
        running, rounded = query_step(running, block_data)
        d_rounded, weights_low = rounded
        d_keys = (
            jnp.einsum("hqk,qhd->khd", d_rounded, queries, preferred_element_type=jnp.float32)
            * 0.125
        )
        d_values = jnp.einsum(
            "hqk,qhd->khd", weights_low, d_numerator, preferred_element_type=jnp.float32
        )
        return (running, (d_keys, d_values))

    start_running = (
        jnp.zeros((tok_rows, head_count, HEAD_DIM), jnp.float32),
        jnp.zeros((head_count,), jnp.float32),
        jnp.zeros((head_count,), jnp.float32),
    )
    (d_queries, same_sum, other_sum), (d_keys, d_values) = lax.scan(
        query_and_key_step,
        start_running,
        split_blocks(back_keys[0], back_keys[1], back_keys[2], back_keys[3]),
    )
    key_grad, value_grad = (
        lax.psum_scatter(
            d_keys.reshape(group_size, model_width).astype(jnp.bfloat16),
            "col",
            scatter_dimension=0,
            tiled=True,
        ).astype(jnp.float32),
        lax.psum_scatter(
            d_values.reshape(group_size, model_width).astype(jnp.bfloat16),
            "col",
            scatter_dimension=0,
            tiled=True,
        ).astype(jnp.float32),
    )
    d_query_pre = unrotate(d_queries * 0.125, cos_part, sin_part).reshape(tok_rows, model_width)
    d_key_pre = unrotate(
        key_grad.reshape(tok_rows, head_count, HEAD_DIM), cos_part, sin_part
    ).reshape(tok_rows, model_width)
    d_projected = jnp.concatenate([d_query_pre, d_key_pre, value_grad], axis=1).astype(jnp.bfloat16)
    d_scaled_one = contract_cols(d_projected, qkv_back)
    term_qkv = contract_rows(scaled_one, d_projected)
    term_gain_one = jnp.sum(d_scaled_one * normed_one, axis=0)
    grad_w_qkv, grad_w_out, grad_w_gate_up, grad_w_down, grad_gain_attn, grad_gain_ffn = (
        lax.psum_scatter(term_qkv, ("row", "col"), scatter_dimension=0, tiled=True),
        lax.psum_scatter(term_out, ("row", "col"), scatter_dimension=0, tiled=True),
        lax.psum_scatter(term_gate_up, ("row", "col"), scatter_dimension=0, tiled=True),
        lax.psum_scatter(term_down, ("row", "col"), scatter_dimension=0, tiled=True),
        lax.psum_scatter(term_gain_one, ("row", "col"), scatter_dimension=0, tiled=True),
        lax.psum_scatter(term_gain_two, ("row", "col"), scatter_dimension=0, tiled=True),
    )
    grad_var_bias = lax.psum(jnp.stack([same_sum, other_sum], axis=0), ("row", "col"))
    d_inputs = d_hidden + norm_back(
        d_scaled_one * gain_one_back.astype(jnp.float32), normed_one, scale_one
    )
    returned = lax.all_to_all(
        d_inputs.astype(jnp.bfloat16).reshape(n_col, piece_len, model_width),
        "col",
        split_axis=0,
        concat_axis=0,
        tiled=True,
    )
    grad_tokens = jnp.take(returned, target, axis=0).reshape(tok_rows, model_width)
    return (
        output,
        grad_tokens,
        grad_w_qkv,
        grad_w_out,
        grad_w_gate_up,
        grad_w_down,
        grad_gain_attn,
        grad_gain_ffn,
        grad_var_bias,
    )


PLANES = 4
QUAD = 4
MEMBERS = 8
WINDOW = 512
AUG = 128
f32 = jnp.float32
bf16 = jnp.bfloat16
VM = pl.BlockSpec(memory_space=pltpu.VMEM)
SM = pl.BlockSpec(memory_space=pltpu.SMEM)
ANY = pl.BlockSpec(memory_space=pl.ANY)


def mm(a, b):
    return lax.dot_general(a, b, (((1,), (0,)), ((), ())), preferred_element_type=f32)


def mm_nt(a, b):
    return lax.dot_general(a, b, (((1,), (1,)), ((), ())), preferred_element_type=f32)


def mm_tn(a, b):
    return lax.dot_general(a, b, (((0,), (0,)), ((), ())), preferred_element_type=f32)


def flip(value, bits):
    for bit in (1, 2, 4, 8, 16):
        if bits & bit:
            value = value + bit * (1 - 2 * ((value // bit) % 2))
    return value


def places():
    row = lax.axis_index("row")
    col = lax.axis_index("col")
    return row, col, col // QUAD, row * QUAD + col % QUAD


def in_plane(row, col, bits):
    return flip(row, bits // QUAD), flip(col, bits % QUAD)


def in_line(row, col, bits):
    return row, flip(col, bits // 2 * QUAD + bits % 2)


def on_line(row, col, bits):
    return row, flip(col, bits * QUAD)


def anyone(row, col, bits):
    return flip(row, bits // 16), flip(col, bits % 16)


def push(source, target, send, recv, device):
    return pltpu.make_async_remote_copy(
        src_ref=source,
        dst_ref=target,
        send_sem=send,
        recv_sem=recv,
        device_id={"row": device[0], "col": device[1]},
        device_id_type=pl.DeviceIdType.MESH,
    )


def meet(devices):
    barrier = pltpu.get_barrier_semaphore()
    for device in devices:
        pl.semaphore_signal(
            barrier,
            1,
            device_id={"row": device[0], "col": device[1]},
            device_id_type=pl.DeviceIdType.MESH,
        )
    pl.semaphore_wait(barrier, len(devices))


NEAR = (2, 4, 6, 1)


def plane_near(row, col):
    return [in_plane(row, col, bits) for bits in NEAR]


def line_all(row, col):
    return [on_line(row, col, bits) for bits in (1, 2, 3)]


def column_all(row, col):
    return [
        (flip(row, bits // 4), flip(col, bits % 4 * QUAD)) for bits in (1, 2, 3, 5, 6, 7)
    ]


class Gather:
    def __init__(self, target, send, recv, peer=in_plane, place=None):
        self.target, self.send, self.recv, self.peer = target, send, recv, peer
        self.row, self.col, _, self.place = places()
        if place is not None:
            self.place = place
        self.copies, self.onward = {}, {}

    def start(self, source):
        for bits in NEAR:
            self.copies[bits] = push(
                source,
                self.target.at[self.place],
                self.send.at[bits],
                self.recv.at[bits],
                self.peer(self.row, self.col, bits),
            )
            self.copies[bits].start()

    def forward(self, bits):
        self.copies[bits].wait_recv()
        slot = self.target.at[flip(self.place, bits)]
        self.onward[bits] = push(
            slot,
            slot,
            self.send.at[bits + 1],
            self.recv.at[bits + 1],
            self.peer(self.row, self.col, 1),
        )
        self.onward[bits].start()

    def arrived(self, bits):
        (self.onward[bits] if bits else self.copies[1]).wait_recv()

    def close(self):
        for copy in list(self.copies.values()) + list(self.onward.values()):
            copy.wait_send()

    def finish(self):
        for bits in (2, 4, 6):
            self.forward(bits)
        for bits in (0, 2, 4, 6):
            self.arrived(bits)


class LineGather(Gather):
    def __init__(self, target, send, recv):
        row, col, z, _ = places()
        super().__init__(target, send, recv, in_line, z * 2 + col % 2)
        self.inner = jnp.logical_or(z == 1, z == 2)

    def start(self, source):
        for bits in (4, 2, 6, 1):
            self.copies[bits] = push(
                source,
                self.target.at[self.place],
                self.send.at[bits],
                self.recv.at[bits],
                in_line(self.row, self.col, bits),
            )
            if bits != 6:
                self.copies[bits].start()
        slot = self.target.at[flip(self.place, 4)]
        self.passing = push(
            slot, slot, self.send.at[0], self.recv.at[6], in_line(self.row, self.col, 2)
        )

        @pl.when(self.inner)
        def _():
            self.copies[6].start()

    def forward(self, bits):
        super().forward(bits)
        if bits == 4:

            @pl.when(self.inner)
            def _():
                self.passing.start()

    def close(self):
        for bits in (4, 2, 1):
            self.copies[bits].wait_send()
        for copy in self.onward.values():
            copy.wait_send()

        @pl.when(self.inner)
        def _():
            self.copies[6].wait_send()
            self.passing.wait_send()


class Scatter:
    def __init__(self, part, inbox, outbox, second, send, recv, peer=in_plane, place=None):
        self.part, self.inbox, self.outbox, self.second = part, inbox, outbox, second
        self.send, self.recv, self.peer = send, recv, peer
        self.row, self.col, _, self.place = places()
        if place is not None:
            self.place = place
        self.core = self.col % 2
        self.copies, self.sent = {}, []

    def near(self, chip, number):
        copy = push(
            self.part.at[2 * chip + 1 - self.core],
            self.inbox.at[number],
            self.send.at[number],
            self.recv.at[number],
            self.peer(self.row, self.col, 1),
        )
        copy.start()
        self.copies[number] = copy

    def far(self, bits):
        self.copies[bits].wait_recv()
        chip = flip(self.place // 2, bits)
        total = self.part[2 * chip + self.core].astype(f32) + self.inbox[bits].astype(f32)
        self.outbox[bits - 1] = total.astype(bf16)
        copy = push(
            self.outbox.at[bits - 1],
            self.second.at[bits - 1],
            self.send.at[3 + bits],
            self.recv.at[3 + bits],
            self.peer(self.row, self.col, 2 * bits),
        )
        copy.start()
        self.sent.append(copy)

    def near_all(self):
        for bits in range(4):
            self.near(flip(self.place // 2, bits), bits)

    def far_all(self):
        for bits in (3, 2, 1):
            self.far(bits)

    def finish(self):
        self.copies[0].wait_recv()
        total = self.part[self.place].astype(f32) + self.inbox[0].astype(f32)
        for copy in self.sent:
            copy.wait_recv()
        for i in range(3):
            total = total + self.second[i].astype(f32)
        return total

    def close(self):
        for copy in list(self.copies.values()) + self.sent:
            copy.wait_send()


class RoundScatter(Scatter):
    def __init__(self, part, inbox, outbox, second, send, recv, passed, sems):
        super().__init__(part, inbox, outbox, second, send, recv)
        self.passed, self.sems = passed, sems

    def sum_for(self, bits):
        self.copies[bits].wait_recv()
        chip = flip(self.place // 2, bits)
        return self.part[2 * chip + self.core].astype(f32) + self.inbox[bits].astype(f32)

    def far_first(self):
        self.outbox[2] = self.sum_for(3).astype(bf16)
        across = in_plane(self.row, self.col, 4)
        self.passing = push(
            self.outbox.at[2], self.passed, self.sems.at[0], self.sems.at[1], across
        )
        self.passing.start()
        self.outbox[1] = self.sum_for(2).astype(bf16)
        self.sent.append(
            push(self.outbox.at[1], self.second.at[1], self.send.at[5], self.recv.at[5], across)
        )
        self.sent[0].start()

    def far_second(self):
        total = self.sum_for(1)
        self.passing.wait_recv()
        self.outbox[0] = (total + self.passed[...].astype(f32)).astype(bf16)
        self.sent.append(
            push(
                self.outbox.at[0],
                self.second.at[0],
                self.send.at[4],
                self.recv.at[4],
                in_plane(self.row, self.col, 2),
            )
        )
        self.sent[1].start()

    def finish(self):
        self.copies[0].wait_recv()
        total = self.part[self.place].astype(f32) + self.inbox[0].astype(f32)
        for copy in self.sent:
            copy.wait_recv()
        return total + (self.second[0].astype(f32) + self.second[1].astype(f32))

    def close(self):
        super().close()
        self.passing.wait_send()


class LineScatter(Scatter):
    def __init__(self, part, inbox, outbox, second, send, recv, passed, sems):
        row, col, z, _ = places()
        super().__init__(part, inbox, outbox, second, send, recv, in_line, z * 2 + col % 2)
        self.passed, self.sems = passed, sems
        self.inner = jnp.logical_or(z == 1, z == 2)
        self.end = jnp.logical_not(self.inner)

    def sum_for(self, bits):
        self.copies[bits].wait_recv()
        chip = flip(self.place // 2, bits)
        return self.part[2 * chip + self.core].astype(f32) + self.inbox[bits].astype(f32)

    def sum_again(self, bits):
        chip = flip(self.place // 2, bits)
        return self.part[2 * chip + self.core].astype(f32) + self.inbox[bits].astype(f32)

    def to(self, bits):
        return push(
            self.outbox.at[bits - 1],
            self.second.at[bits - 1],
            self.send.at[3 + bits],
            self.recv.at[3 + bits],
            in_line(self.row, self.col, 2 * bits),
        )

    def far(self, bits):
        self.outbox[bits - 1] = self.sum_for(bits).astype(bf16)
        if bits == 1:
            self.sent.append(self.to(1))
            self.sent[-1].start()
        if bits == 2:
            self.added = self.to(2)
            self.sent.append(self.added)

            @pl.when(self.end)
            def _():
                self.added.start()

        if bits == 3:
            self.across = self.to(3)
            self.passing = push(
                self.outbox.at[2],
                self.passed,
                self.sems.at[0],
                self.sems.at[1],
                in_line(self.row, self.col, 2),
            )

            @pl.when(self.end)
            def _():
                self.passing.start()
                self.second[2] = jnp.zeros(self.second.shape[1:], bf16)

            @pl.when(self.inner)
            def _():
                self.across.start()

    def far_second(self):
        @pl.when(self.inner)
        def _():
            self.passing.wait_recv()
            total = self.sum_again(2) + self.passed[...].astype(f32)
            self.outbox[1] = total.astype(bf16)
            self.added.start()

    def finish(self):
        @pl.when(self.inner)
        def _():
            self.across.wait_recv()

        return super().finish()

    def close(self):
        super().close()

        @pl.when(self.inner)
        def _():
            self.across.wait_send()

        @pl.when(self.end)
        def _():
            self.passing.wait_send()


def scatter_scratch(rows, width):
    return [
        pltpu.VMEM((4, rows, width), bf16),
        pltpu.VMEM((3, rows, width), bf16),
        pltpu.VMEM((3, rows, width), bf16),
        pltpu.SemaphoreType.DMA((7,)),
        pltpu.SemaphoreType.DMA((7,)),
    ]


def fetch(source, target, semaphore):
    copy = pltpu.make_async_copy(source, target, semaphore)
    copy.start()
    return copy


def block(number, size):
    return pl.ds(pl.multiple_of(number * size, size), size)


def enter_body(
    x, wq, wo, wg, ga, gf, variate, time, lengths, freq,
    xp_out, wt_out, wop, wgp, s1_out, qkvt, gains, labels,
    xp, s1, keep, wqs, wline, wqp, wgs, tile, tl, tiles, wt, box, cs, sn, times,
    sx, rx, sq, rq, sv, rv, st, rt, su, ru, sw, rw, sg, rg, sz, rz,
):
    row, col, z, place = places()
    quarter = col % QUAD
    y, core = col // 2 % 2, col % 2
    member = z * 2 + core
    lane = lax.broadcasted_iota(jnp.int32, (1, 128), 1)
    for line, gain in ((0, ga), (1, gf)):
        wide = gain[...].astype(f32)
        wide = jnp.concatenate([wide] * 4, axis=1)
        tile[line : line + 1, :] = jnp.where(lane // 32 == quarter, wide, 0.0)
    tile[2:3, :] = variate[...].astype(f32)
    tile[3:4, :] = time[...].astype(f32)
    numbers = jnp.zeros((1, 128), jnp.int32)
    for i in range(NSEQ):
        numbers = jnp.where(lane == i, lengths[0, i], numbers)
    tile[4:5, :] = numbers.astype(f32)
    tile[5:8, :] = jnp.zeros((3, 128), f32)
    for p in range(MEMBERS):
        for part in range(3):
            at = part * 1024 + p * 128
            wqs[p, :, part * 128 : part * 128 + 128] = wq[:, at : at + 128]
    meet([anyone(row, col, bits) for bits in range(1, 32)])
    first = []
    for bits in range(1, 8):
        there = in_line(row, col, bits)
        first.append(push(wqs.at[flip(member, bits)], wline.at[member], sq.at[bits], rq.at[bits], there))
        first[-1].start()
    for bits in (1, 2, 3):
        first.append(push(tile, tl.at[z], st.at[bits], rt.at[bits], on_line(row, col, bits)))
        first[-1].start()
    rows_in = LineGather(xp, sx, rx)
    xp[member] = x[...]
    wline[member] = wqs[member]
    tl[z] = tile[...]
    for p in range(MEMBERS):
        for half in range(2):
            for plane in range(PLANES):
                unit = (p // QUAD) * 16 + plane * QUAD + p % QUAD
                at = half * 512 + plane * 128
                start = half * 4096 + unit * 128
                wgs[p, :, at : at + 128] = wg[:, start : start + 128]
    blocks = []
    for bits in range(1, 8):
        there = in_plane(row, col, bits)
        blocks.append(
            push(wgs.at[flip(place, bits)], wgp.at[place], sg.at[bits], rg.at[bits], there)
        )
        blocks[-1].start()
    wgp[place] = wgs[place]
    for copy in first:
        copy.wait_recv()
    rows_in.start(x)
    column = row * 2 + y
    beside, across = (row, flip(col, 2)), (flip(row, 1), col)
    ways = [
        push(wline, wqp.at[column], sv.at[1], rv.at[1], beside),
        push(wline, wqp.at[column], sv.at[2], rv.at[2], across),
    ]
    for copy in ways:
        copy.start()
    wqp[column] = wline[...]
    second = []
    for bits in range(1, 8):
        there = in_plane(row, col, bits)
        second.append(push(tl, tiles.at[place], su.at[bits], ru.at[bits], there))
        second[-1].start()
    tiles[place] = tl[...]
    ways[0].wait_recv()
    slot = wqp.at[flip(column, 1)]
    ways.append(push(slot, slot, sv.at[3], rv.at[3], across))
    ways[2].start()
    for copy in second:
        copy.wait_recv()
    rows_in.forward(4)
    rows_in.forward(2)
    for copy in ways[1:]:
        copy.wait_recv()
    for k in range(8):
        lanes = slice(k * 128, k * 128 + 128)
        r, plane = k // PLANES, k % PLANES
        gains[:, lanes] = (tiles[r * QUAD, plane] + tiles[r * QUAD + 1, plane]) + (
            tiles[r * QUAD + 2, plane] + tiles[r * QUAD + 3, plane]
        )
        times[:, lanes] = tiles[row * QUAD + y * 2 + k % 2, k // 2]
        wt[:, lanes] = jnp.transpose(
            jnp.concatenate(
                [wqp[r * 2 + j // 2, plane * 2 + j % 2] for j in range(4)], axis=0
            )
        )
    for k in range(16):
        labels[:, k * 128 : k * 128 + 128] = tiles[row * QUAD + k % QUAD, k // QUAD]
    phases = times[3:4, :] * freq[...]
    cs[...] = jnp.cos(phases)
    sn[...] = jnp.sin(phases)
    gain = gains[0:1, :]
    kept = [fetch(wt, wt_out, keep.at[2])]

    def project(chip):
        rows = block(chip, 256)
        values = jnp.concatenate([xp[2 * chip], xp[2 * chip + 1]], axis=0).astype(f32)
        scaled = (values * norm_scale(values) * gain).astype(bf16)
        s1[2 * chip] = scaled[0:128]
        s1[2 * chip + 1] = scaled[128:256]
        out = mm_nt(wt[...], scaled)
        cos_part, sin_part = cs[:, rows], sn[:, rows]
        for head in range(2):
            for part in range(2):
                base = part * 128 + head * 64
                former, latter = out[base : base + 32], out[base + 32 : base + 64]
                factor = 0.125 if part == 0 else 1.0
                turned = former * cos_part - latter * sin_part
                other = latter * cos_part + former * sin_part
                at = part * 64
                box[head, at : at + 32, rows] = (turned * factor).astype(bf16)
                box[head, at + 32 : at + 64, rows] = (other * factor).astype(bf16)
            at = 256 + head * 64
            box[head, 128:192, rows] = out[at : at + 64].astype(bf16)

    turned = []

    def exchange(chip, number):
        lanes = pl.ds(pl.multiple_of(chip * 512 + y * 256, 256), 256)
        copy = push(
            box.at[1 - y, :, block(chip, 256)],
            qkvt.at[:, lanes],
            sz.at[number],
            rz.at[number],
            (row, flip(col, 2)),
        )
        copy.start()
        turned.append(copy)
        qkvt[:, lanes] = box[y, :, block(chip, 256)]

    for k, bits in enumerate((0, 4, 2, 6)):
        if bits == 6:
            rows_in.forward(6)
        rows_in.arrived(bits)
        chip = flip(z, bits // 2)
        project(chip)
        exchange(chip, k)
        if bits == 2:
            target = col // 2 % 2 * 2 + col // 4 % 2
            slot = row * 2 + col % 2
            for plane in range(PLANES):
                there = (col // 8, plane * QUAD + target)
                mine = jnp.logical_and(row * 16 + col == there[0] * 16 + there[1], z == plane)

                @pl.when(jnp.logical_not(mine))
                def _():
                    push(wo, wop.at[slot], sw.at[plane], rw.at[slot], there).start()

                @pl.when(mine)
                def _():
                    wop[slot] = wo[...]

    kept.append(fetch(xp, xp_out, keep.at[0]))
    kept.append(fetch(s1, s1_out, keep.at[1]))
    for copy in blocks:
        copy.wait_recv()
    for j in range(4):
        source = (j // 2, row * 8 + core * 4 + y * 2 + j % 2)
        mine = jnp.logical_and(row == source[0], col == source[1])

        @pl.when(jnp.logical_not(mine))
        def _():
            push(wo, wop.at[j], sw.at[j], rw.at[j], source).wait_recv()

    target = col // 2 % 2 * 2 + col // 4 % 2
    slot = row * 2 + col % 2
    for plane in range(PLANES):
        there = (col // 8, plane * QUAD + target)
        mine = jnp.logical_and(row * 16 + col == there[0] * 16 + there[1], z == plane)

        @pl.when(jnp.logical_not(mine))
        def _():
            push(wo, wop.at[slot], sw.at[plane], rw.at[slot], there).wait_send()

    for copy in turned:
        copy.wait()
    rows_in.close()
    for copy in first + second + blocks + ways:
        copy.wait_send()
    for copy in kept:
        copy.wait()


def split_three(value):
    high = value.astype(bf16).astype(f32)
    middle = (value - high).astype(bf16).astype(f32)
    return high, middle, (value - high - middle).astype(bf16).astype(f32)


def window_queries(qa, lanes, first, limit):
    place = first + lax.broadcasted_iota(jnp.int32, (16, WINDOW), 1)
    line = lax.broadcasted_iota(jnp.int32, (16, WINDOW), 0)
    extra = jnp.where(
        jnp.logical_and(line == 12, place >= limit), -1e30, qa[64:80, lanes].astype(f32)
    )
    return jnp.concatenate(
        [qa[0:64, lanes], extra.astype(bf16), jnp.zeros((AUG - 80, WINDOW), bf16)], axis=0
    )


def head_of():
    row, col, z, place = places()
    return (z * 2 + col % 2) * 2 + col // 2 % 2


def read_lengths(labels, info):
    lane = lax.broadcasted_iota(jnp.int32, (1, 128), 1)
    numbers = labels[4:5, 0:128]
    for i in range(NSEQ):
        info[i] = jnp.sum(jnp.where(lane == i, numbers, 0.0)).astype(jnp.int32)


def over_keys(start, length, step, carry):
    carry = lax.fori_loop(
        0, length // 2, lambda k, c: step((start + 2 * k) * 128, 256, c), carry
    )
    return lax.fori_loop(
        0, length % 2, lambda k, c: step((start + length - 1) * 128, 128, c), carry
    )


def attend_body(bias_all, qkvt, labels, att, den, low, qa, ka, kt, info):
    size = qkvt.shape[1]
    head = head_of()
    bias = (bias_all[0, head], bias_all[1, head])
    variate = labels[2:3, :]
    line = lax.broadcasted_iota(jnp.int32, (16, size), 0)
    same = (variate == (line % 4).astype(f32)).astype(f32)
    same_pieces = split_three(jnp.full((16, size), bias[0] - bias[1], f32))
    other_pieces = split_three(jnp.full((16, size), bias[1], f32))

    def choose(pieces, number):
        return jnp.where(number == 0, pieces[0], jnp.where(number == 1, pieces[1], pieces[2]))

    extra_q = jnp.where(line < 12, same, jnp.where(line == 12, 0.0, 1.0))
    extra_k = jnp.where(
        line < 12,
        same * choose(same_pieces, line // 4),
        jnp.where(line == 12, 1.0, choose(other_pieces, line - 13)),
    )
    qa[0:64, 0:size] = qkvt[0:64, :]
    qa[64:80, 0:size] = extra_q.astype(bf16)
    qa[80:AUG, 0:size] = jnp.zeros((AUG - 80, size), bf16)
    qa[:, size:] = jnp.zeros((AUG, WINDOW), bf16)
    kt[0:64, :] = qkvt[64:128, :]
    kt[64:80, :] = extra_k.astype(bf16)
    kt[80:AUG, :] = jnp.zeros((AUG - 80, size), bf16)
    ka[...] = jnp.transpose(kt[...])
    read_lengths(labels, info)

    def sequence(number, start):
        length = info[number]
        limit = (start + length) * 128

        def window(j, unused):
            first = (start + 4 * j) * 128
            lanes = pl.ds(pl.multiple_of(first, 128), WINDOW)
            queries = window_queries(qa, lanes, first, limit)

            def keys(first_key, count, running):
                total, numerator = running
                rows = pl.ds(pl.multiple_of(first_key, 128), count)
                weights = jnp.exp(mm(ka[rows, :], queries))
                total = total + jnp.sum(weights, axis=0, keepdims=True)
                numerator = numerator + mm(qkvt[128:192, rows], weights.astype(bf16))
                return total, numerator

            total, numerator = over_keys(
                start, length, keys, (jnp.zeros((1, WINDOW), f32), jnp.zeros((64, WINDOW), f32))
            )
            attended = numerator / total
            att[:, lanes] = attended
            den[:, lanes] = jnp.broadcast_to(total, (8, WINDOW))
            low[:, lanes] = attended.astype(bf16)
            return unused

        lax.fori_loop(0, (length + 3) // 4, window, 0)
        return start + length

    lax.fori_loop(0, NSEQ, sequence, 0)


def attend_back_body(
    qkvt, qa, ka, labels, freq, grad, att, den,
    dproj, bias_tile,
    dn, cw, vn, dq, dk, dv, info,
):
    size = qkvt.shape[1]
    lanes_all = slice(0, size)
    inverse = 1.0 / den[0:1, lanes_all]
    d_att = grad[...].astype(f32)
    dn[:, lanes_all] = (d_att * inverse).astype(bf16)
    dn[:, size:] = jnp.zeros((64, WINDOW), bf16)
    cw[:, lanes_all] = jnp.broadcast_to(
        jnp.sum(d_att * att[:, lanes_all], axis=0, keepdims=True) * inverse, (8, size)
    )
    cw[:, size:] = jnp.zeros((8, WINDOW), f32)
    vn[...] = jnp.transpose(qkvt[128:192, :])
    dk[...] = jnp.zeros_like(dk)
    dv[...] = jnp.zeros_like(dv)

    read_lengths(labels, info)

    def sequence(number, start):
        length = info[number]
        limit = (start + length) * 128

        def window(j, unused):
            first = (start + 4 * j) * 128
            lanes = pl.ds(pl.multiple_of(first, 128), WINDOW)
            queries = window_queries(qa, lanes, first, limit)
            upstream = dn[:, lanes]
            centre = cw[0:1, lanes]

            def keys(first_key, count, running):
                rows = pl.ds(pl.multiple_of(first_key, 128), count)
                weights = jnp.exp(mm(ka[rows, :], queries))
                d_scores = weights * (mm(vn[rows, :], upstream) - centre)
                rounded = d_scores.astype(bf16)
                dk[:, rows] += mm_nt(queries, rounded)
                dv[:, rows] += mm_nt(upstream, weights.astype(bf16))
                return running + mm(qkvt[64:128, rows], rounded)

            dq[:, lanes] = over_keys(start, length, keys, jnp.zeros((64, WINDOW), f32))
            return unused

        lax.fori_loop(0, (length + 3) // 4, window, 0)
        return start + length

    lax.fori_loop(0, NSEQ, sequence, 0)

    phases = labels[3:4, :] * freq[...]
    cos_part, sin_part = jnp.cos(phases), jnp.sin(phases)
    for part, source, factor in ((0, dq, 0.125), (1, dk, 1.0)):
        former, latter = source[0:32, lanes_all], source[32:64, lanes_all]
        dproj[part * 64 : part * 64 + 32, :] = (
            (former * cos_part + latter * sin_part) * factor
        ).astype(bf16)
        dproj[part * 64 + 32 : part * 64 + 64, :] = (
            (latter * cos_part - former * sin_part) * factor
        ).astype(bf16)
    dproj[128:192, :] = dv[...].astype(bf16)
    variate = labels[2:3, :]
    line = lax.broadcasted_iota(jnp.int32, (16, size), 0)
    match = jnp.logical_and(variate == line.astype(f32), line < 4)
    near = jnp.sum(jnp.where(match, dk[64:80, :], 0.0))
    every = jnp.sum(dk[77:78, :])
    lane = lax.broadcasted_iota(jnp.int32, (8, 128), 1)
    line8 = lax.broadcasted_iota(jnp.int32, (8, 128), 0)
    here = lane == head_of()
    bias_tile[...] = jnp.where(
        jnp.logical_and(here, line8 == 2),
        near,
        jnp.where(jnp.logical_and(here, line8 == 3), every - near, 0.0),
    )


def branch_body(
    low, wop, x, gains, cot, deal,
    atp, hidden, s2, cotp_out,
    cotp, cotr, cots, keep, atn, part, sz, rz, sc, rc, sa, ra, inbox, outbox, second, ss, rs,
):
    row, col, z, place = places()
    quarter = col % QUAD
    dealt = [(row, flip(col, bits)) for bits in range(1, 16)]
    others = [(flip(row, 1), flip(col, bits)) for bits in (0, 2, 4, 8, 12)]
    meet(dealt + others)
    rows, lanes = block(z // 2, 64), block(row, 512)
    for plane in range(PLANES):
        mine = jnp.logical_and(row == z % 2, z == plane)

        @pl.when(jnp.logical_not(mine))
        def _():
            push(
                low.at[:, plane * 512 : plane * 512 + 512], atp.at[rows, lanes],
                sz.at[plane], rz.at[row * 2 + z // 2], (z % 2, plane * QUAD + quarter),
            ).start()

        @pl.when(mine)
        def _():
            atp[rows, lanes] = low[:, plane * 512 : plane * 512 + 512]

    pieces = []
    for bits in range(1, 16):
        there = dealt[bits - 1]
        pieces.append(push(cot.at[there[1]], cotr.at[col], sc.at[bits], rc.at[bits], there))
        pieces[-1].start()
    cotr[col] = cot[col]
    for j in range(4):
        source = (j // 2, (row + 2 * (j % 2)) * QUAD + quarter)
        mine = jnp.logical_and(row == j // 2, z == row + 2 * (j % 2))

        @pl.when(jnp.logical_not(mine))
        def _():
            push(
                low.at[:, 0:512], atp.at[0:64, 0:512], sz.at[j], rz.at[j], source
            ).wait_recv()

    for plane in range(PLANES):
        mine = jnp.logical_and(row == z % 2, z == plane)

        @pl.when(jnp.logical_not(mine))
        def _():
            push(
                low.at[:, plane * 512 : plane * 512 + 512], atp.at[rows, lanes],
                sz.at[plane], rz.at[row * 2 + z // 2], (z % 2, plane * QUAD + quarter),
            ).wait_send()

    atn[...] = jnp.transpose(atp[...])
    total = Scatter(part, inbox, outbox, second, ss, rs)
    core = col % 2
    for bits in (3, 2, 1, 0):
        chip = flip(place // 2, bits)
        part[2 * chip + 1 - core] = mm(atn[block(2 * chip + 1 - core, 128), :], wop[...]).astype(bf16)
    for bits in range(4):
        total.near(flip(place // 2, bits), bits)
    for bits in (3, 2, 1, 0):
        chip = flip(place // 2, bits)
        part[2 * chip + core] = mm(atn[block(2 * chip + core, 128), :], wop[...]).astype(bf16)
    total.far_all()
    for copy in pieces:
        copy.wait_recv()
    for j in range(16):
        cots[j * 8 : j * 8 + 8, :] = cotr[jnp.clip(deal[j], 0, 15)]
    cot_in = Gather(cotp, sa, ra)
    cot_in.start(cots)
    cotp[place] = cots[...]
    state = x[...].astype(f32) + total.finish()
    hidden[...] = state
    s2[...] = (state * norm_scale(state) * gains[1:2, :]).astype(bf16)
    cot_in.finish()
    kept = fetch(cotp, cotp_out, keep.at[0])
    for copy in pieces:
        copy.wait_send()
    total.close()
    cot_in.close()
    kept.wait()


def ffn_body(
    s2, cotp_in, wg_in, w_down, hidden, gains,
    out_keep, down_in, gwg_out, d_hidden, low, gain_term,
    cotp, wg, s2p, wgs, wd, actives, factors, inner_s, dgu, d_part, out_part, gwd, gwg, relayed, both_terms,
    keep, sa, ra, sw, rw, sd, rd, inbox, outbox, second, ss, rs,
):
    row, col, z, place = places()
    loads = [fetch(wg_in, wg, keep.at[0]), fetch(cotp_in, cotp, keep.at[1])]
    meet(plane_near(row, col) + line_all(row, col))
    rows_in = Gather(s2p, sa, ra)
    rows_in.start(s2)
    s2p[place] = s2[...]
    inner = jnp.logical_or(z == 1, z == 2)
    end = jnp.logical_not(inner)
    downs = {
        bits: push(
            w_down, wd.at[block(z, 128), :], sw.at[bits], rw.at[bits], on_line(row, col, bits)
        )
        for bits in (2, 1, 3)
    }
    passed = wd.at[block(flip(z, 2), 128), :]
    downs[0] = push(passed, passed, sw.at[0], rw.at[3], on_line(row, col, 1))
    downs[2].start()

    @pl.when(inner)
    def _():
        downs[3].start()

    downs[1].start()
    wd[block(z, 128), :] = w_down[...]
    loads[0].wait()
    for plane in range(PLANES):
        for r in range(2):
            at = (r * PLANES + plane) * 128
            wgs[at : at + 128, :] = wg[plane * 2 + r]
    for k in range(4):
        chip = flip(place // 2, k)
        if k:
            rows_in.forward(2 * k)
        rows_in.arrived(2 * k)
        if k == 1:
            downs[2].wait_recv()

            @pl.when(inner)
            def _():
                downs[0].start()

        rows = block(chip, 256)
        scaled = jnp.concatenate([s2p[2 * chip], s2p[2 * chip + 1]], axis=0)
        both = mm(scaled, wgs[...])
        gate, upper = both[:, 0:512], both[:, 512:1024]
        sig = jax.nn.sigmoid(gate)
        active = gate * sig
        inner_s[rows, :] = (active * upper).astype(bf16)
        actives[rows, :] = active
        factors[rows, :] = upper * sig * (1.0 + gate * (1.0 - sig))
    loads[1].wait()
    cot_all = jnp.concatenate([cotp[t] for t in range(MEMBERS)], axis=0)
    for k in range(4):
        cols = slice(k * 128, k * 128 + 128)
        gwd[k] = mm_tn(inner_s[:, cols], cot_all).astype(bf16)
    grads = {
        bits: push(
            gwd.at[flip(z, bits)], down_in.at[bits], sd.at[bits], rd.at[bits], on_line(row, col, bits)
        )
        for bits in (1, 3)
    }
    grads[2] = push(both_terms, down_in.at[2], sd.at[2], rd.at[2], on_line(row, col, 2))
    grads[0] = push(gwd.at[flip(z, 3)], relayed, sd.at[0], rd.at[0], on_line(row, col, 1))

    @pl.when(end)
    def _():
        grads[0].start()
        both_terms[...] = gwd[flip(z, 2)]
        grads[2].start()
        down_in[3] = jnp.zeros(down_in.shape[1:], bf16)

    @pl.when(inner)
    def _():
        grads[3].start()

    grads[1].start()
    down_in[0] = gwd[z]
    total = Scatter(d_part, inbox, outbox, second, ss, rs)
    downs[1].wait_recv()
    downs[3].wait_recv()
    for k in range(4):
        chip = flip(place // 2, k)
        rows = block(chip, 256)
        upstream = jnp.concatenate([cotp[2 * chip], cotp[2 * chip + 1]], axis=0)
        d_inner = mm_nt(upstream, wd[...])
        dgu[rows, 0:512] = (d_inner * factors[rows, :]).astype(bf16)
        dgu[rows, 512:1024] = (d_inner * actives[rows, :]).astype(bf16)
        tile = mm_nt(dgu[rows, :], wgs[...]).astype(bf16)
        d_part[2 * chip] = tile[0:128]
        d_part[2 * chip + 1] = tile[128:256]
        total.near(chip, k)
        if k > 1:
            total.far(k - 1)
        if k == 1:

            @pl.when(inner)
            def _():
                grads[0].wait_recv()
                both_terms[...] = (
                    gwd[flip(z, 2)].astype(f32) + relayed[...].astype(f32)
                ).astype(bf16)
                grads[2].start()

    for k in range(4):
        chip = flip(place // 2, k)
        tile = mm(inner_s[block(chip, 256), :], wd[...]).astype(bf16)
        out_part[2 * chip] = tile[0:128]
        out_part[2 * chip + 1] = tile[128:256]
        if k == 0:
            total.far(3)
    kept = [fetch(out_part, out_keep, keep.at[10])]
    for f in range(8):
        cols = slice(f * 128, f * 128 + 128)
        lhs = jnp.concatenate([s2p[t, :, cols] for t in range(MEMBERS)], axis=0)
        at = (f % PLANES) * 2 + f // PLANES
        gwg[at] = mm_tn(lhs, dgu[...]).astype(bf16)
        kept.append(fetch(gwg.at[at], gwg_out.at[at], keep.at[2 + f]))
    d_scaled = total.finish()
    state = hidden[...]
    scale = norm_scale(state)
    normed = state * scale
    gain_term[...] = jnp.broadcast_to(jnp.sum(d_scaled * normed, axis=0, keepdims=True), (8, 1024))
    d_state = cotp[place].astype(f32) + norm_back(d_scaled * gains[1:2, :], normed, scale)
    d_hidden[...] = d_state
    low[...] = d_state.astype(bf16)
    rows_in.close()
    total.close()
    grads[1].wait_recv()
    grads[2].wait_recv()
    for copy in (downs[1], downs[2], grads[1], grads[2]):
        copy.wait_send()

    @pl.when(inner)
    def _():
        grads[3].wait_recv()
        for copy in (downs[3], downs[0], grads[3]):
            copy.wait_send()

    @pl.when(end)
    def _():
        grads[0].wait_send()

    for copy in kept:
        copy.wait()


def attended_back_body(
    low, wop, atp,
    grad, gwo,
    dbp, dat, sg, rg, sz, rz,
):
    row, col, z, place = places()
    meet(plane_near(row, col) + column_all(row, col))
    quarter = col % QUAD
    rows_in = Gather(dbp, sg, rg)
    rows_in.start(low)
    dbp[place] = low[...]
    for k in range(4):
        chip = flip(place // 2, k)
        if k:
            rows_in.forward(2 * k)
        rows_in.arrived(2 * k)
        for core in range(2):
            dat[:, block(2 * chip + core, 128)] = mm_nt(wop[...], dbp[2 * chip + core]).astype(bf16)
        if k % 2 == 0:
            continue
        group = row if k == 1 else 1 - row
        for head in range(2):
            plane = row + 2 * head
            source = dat.at[head * 64 : head * 64 + 64, block(group, 512)]
            if k == 1:

                @pl.when(z != plane)
                def _():
                    push(
                        source, grad.at[:, block(z, 512)], sz.at[head], rz.at[z],
                        (group, plane * QUAD + quarter),
                    ).start()

                @pl.when(z == plane)
                def _():
                    grad[:, block(z, 512)] = source[...]

            else:
                push(
                    source, grad.at[:, block(z, 512)], sz.at[2 + head], rz.at[z],
                    (group, plane * QUAD + quarter),
                ).start()

    total = mm(atp[:, 0:128], dbp[0])
    for q in range(1, MEMBERS):
        total = total + mm(atp[:, q * 128 : q * 128 + 128], dbp[q])
    gwo[...] = total.astype(bf16)
    for plane in range(PLANES):
        mine = jnp.logical_and(row == z % 2, z == plane)

        @pl.when(jnp.logical_not(mine))
        def _():
            push(
                dat.at[0:64, 0:512], grad.at[:, plane * 512 : plane * 512 + 512], sz.at[0],
                rz.at[plane], (z % 2, plane * QUAD + quarter),
            ).wait_recv()

    for head in range(2):
        plane = row + 2 * head

        @pl.when(z != plane)
        def _():
            push(
                dat.at[0:64, 0:512], grad.at[:, 0:512], sz.at[head], rz.at[z],
                (row, plane * QUAD + quarter),
            ).wait_send()

        push(
            dat.at[0:64, 0:512], grad.at[:, 0:512], sz.at[2 + head], rz.at[z],
            (1 - row, plane * QUAD + quarter),
        ).wait_send()

    rows_in.close()


def last_body(
    dproj, wt_in, s1_in, xp_in, out_in, gains, d_hidden, hidden, gwo, gwg, gain_two, bias_tile, deal,
    grad_tokens, gqin, goin, gwg_in, sums, out,
    wt, s1, xp, out_part, pieces, slots, keep, dpt, dpn, part, gq, gqcol, gqout, gqsum, pack, packs, packed,
    passed, sz, rz, inbox, outbox, second, ss, rs, sp,
    sq, rq, sv, rv, st, rt, su, ru, sw, rw, sg, rg, sc, rc, passed2, sp2, inbox2, outbox2, second2, ss2, rs2,
):
    row, col, z, place = places()
    quarter = col % QUAD
    y, core = col // 2 % 2, col % 2
    member = z * 2 + core
    column = row * 2 + y
    loads = [
        fetch(out_in, out_part, keep.at[3]),
        fetch(s1_in, s1, keep.at[0]),
        fetch(xp_in, xp, keep.at[1]),
        fetch(wt_in, wt, keep.at[2]),
    ]
    meet([anyone(row, col, bits) for bits in range(1, 32)])
    copies = {}
    for bits in (3, 2, 1, 0):
        chip = flip(z, bits)
        ours = pl.ds(pl.multiple_of(chip * 512 + y * 256, 256), 256)
        theirs = pl.ds(pl.multiple_of(chip * 512 + (1 - y) * 256, 256), 256)
        copies[bits] = push(
            dproj.at[:, theirs], dpt.at[y, :, block(chip, 256)], sz.at[bits], rz.at[bits],
            (row, flip(col, 2)),
        )
        copies[bits].start()
        dpt[y, :, block(chip, 256)] = dproj[:, ours]
    owner = core * 4 + y * 2
    for j in range(4):
        there = (j // 2, row * 8 + owner + j % 2)
        mine = jnp.logical_and(row == there[0], col == there[1])

        @pl.when(jnp.logical_not(mine))
        def _():
            push(gwo.at[j], goin.at[z], sw.at[j], rw.at[z], there).start()

        @pl.when(mine)
        def _():
            goin[z] = gwo[j]

    loads[0].wait()
    output = RoundScatter(out_part, inbox2, outbox2, second2, ss2, rs2, passed2, sp2)
    output.near_all()
    output.far_first()
    spread = []
    for bits in range(1, 8):
        there = in_plane(row, col, bits)
        copy = push(gwg.at[flip(place, bits)], gwg_in.at[place], sg.at[bits], rg.at[bits], there)
        copy.start()
        spread.append(copy)
    gwg_in[place] = gwg[place]
    for copy in loads[1:]:
        copy.wait()
    total = LineScatter(part, inbox, outbox, second, ss, rs, passed, sp)
    term = jnp.zeros((1, 1024), f32)
    for bits in (3, 2, 1, 0):
        chip = flip(z, bits)
        lanes = block(chip, 256)
        copies[bits].wait_recv()
        for kind in range(3):
            both = jnp.concatenate(
                [dpt[head, kind * 64 : kind * 64 + 64, lanes] for head in range(2)], axis=0
            )
            dpn[lanes, kind * 128 : kind * 128 + 128] = jnp.transpose(both)
        d_scaled = mm(dpn[lanes, :], wt[...])
        values = jnp.concatenate([xp[2 * chip], xp[2 * chip + 1]], axis=0).astype(f32)
        term = term + jnp.sum(d_scaled * (values * norm_scale(values)), axis=0, keepdims=True)
        part[2 * chip] = d_scaled[0:128].astype(bf16)
        part[2 * chip + 1] = d_scaled[128:256].astype(bf16)
        total.near(chip, bits)
        if bits < 3:
            total.far(bits + 1)
    output.far_second()
    for f in range(8):
        if f == 4:
            total.far_second()
        lhs = jnp.concatenate([s1[t, :, f * 128 : f * 128 + 128] for t in range(MEMBERS)], axis=0)
        chunk = mm_tn(lhs, dpn[...]).astype(bf16)
        for j in range(4):
            gq[f // PLANES * 2 + j // 2, f % PLANES * 2 + j % 2] = chunk[j * 32 : j * 32 + 32, :]
    beside, across = (row, flip(col, 2)), (flip(row, 1), col)
    columns = [
        push(gq.at[flip(column, 3)], gqcol.at[1], sv.at[3], rv.at[3], across),
        push(gq.at[flip(column, 2)], gqcol.at[0], sv.at[2], rv.at[2], across),
    ]
    for copy in columns:
        copy.start()
    for k in range(8):
        pack[k] = bias_tile[...]
        pack[k, 0:1, :] = term[:, k * 128 : k * 128 + 128]
        pack[k, 1:2, :] = gain_two[0:1, k * 128 : k * 128 + 128]
    first = []
    for bits in range(1, 8):
        there = in_plane(row, col, bits)
        copy = push(
            pack.at[pl.ds(there[0] * PLANES, PLANES)], packs.at[place], st.at[bits], rt.at[bits], there
        )
        copy.start()
        first.append(copy)
    packs[place] = pack[pl.ds(row * PLANES, PLANES)]
    rows_out = (hidden[...] + output.finish()).astype(bf16)
    for j in range(16):
        pieces[j] = rows_out[j * 8 : j * 8 + 8, :]
    for d in range(16):
        number = 0
        for j in range(1, 16):
            number = jnp.where(deal[j] == d, j, number)
        slots[d] = pieces[number]
    for bits in range(1, 16):
        there = (row, flip(col, bits))
        copy = push(slots.at[there[1]], out.at[col], sc.at[bits], rc.at[bits], there)
        copy.start()
        spread.append(copy)
    out[col] = slots[col]
    columns[0].wait_recv()
    nearby = flip(column, 1)
    for m in range(MEMBERS):
        gqout[m] = (gq[nearby, m].astype(f32) + gqcol[1, m].astype(f32)).astype(bf16)
    columns.append(push(gqout, gqcol.at[2], sv.at[1], rv.at[1], beside))
    columns[2].start()
    for copy in first:
        copy.wait_recv()
    summed = packs[0]
    for p in range(1, MEMBERS):
        summed = summed + packs[p]
    packed[...] = summed
    for bits in (1, 2, 3):
        copy = push(
            packed.at[flip(z, bits)], sums.at[z], su.at[bits], ru.at[bits], on_line(row, col, bits)
        )
        copy.start()
        spread.append(copy)
    sums[z] = packed[z]
    for copy in columns[1:]:
        copy.wait_recv()
    for m in range(MEMBERS):
        gqsum[m] = (
            (gq[column, m].astype(f32) + gqcol[0, m].astype(f32)) + gqcol[2, m].astype(f32)
        ).astype(bf16)
    for bits in range(7, 0, -1):
        there = in_line(row, col, bits)
        copy = push(gqsum.at[flip(member, bits)], gqin.at[member], sq.at[bits], rq.at[bits], there)
        copy.start()
        spread.append(copy)
    gqin[member] = gqsum[member]
    d_one = total.finish()
    own_rows = xp[member].astype(f32)
    scale = norm_scale(own_rows)
    grad_tokens[...] = (
        d_hidden[...] + norm_back(d_one * gains[0:1, :], own_rows * scale, scale)
    ).astype(bf16)
    for copy in spread:
        copy.wait_recv()
    senders = col // 2 % 2 * 2 + col // 4 % 2
    for plane in range(PLANES):
        mine = jnp.logical_and(row * 16 + col == (col // 8) * 16 + plane * QUAD + senders, z == plane)

        @pl.when(jnp.logical_not(mine))
        def _():
            push(
                gwo.at[0], goin.at[plane], sw.at[0], rw.at[plane],
                (col // 8, plane * QUAD + senders),
            ).wait_recv()

    for j in range(4):
        there = (j // 2, row * 8 + owner + j % 2)
        mine = jnp.logical_and(row == there[0], col == there[1])

        @pl.when(jnp.logical_not(mine))
        def _():
            push(gwo.at[j], goin.at[z], sw.at[j], rw.at[z], there).wait_send()

    for copy in list(copies.values()) + columns + first + spread:
        copy.wait_send()
    total.close()
    output.close()


def finish_body(
    grad_tokens_in, gqin, goin, out_in, gwg, gwd, tiles,
    out, grad_tokens, grad_q, grad_o, grad_gu, grad_d, grad_gains, grad_bias,
):
    grad_tokens[...] = grad_tokens_in[...]
    out[...] = out_in[...]
    grad_o[...] = (goin[0].astype(f32) + goin[1].astype(f32)) + (
        goin[2].astype(f32) + goin[3].astype(f32)
    )
    grad_d[...] = (gwd[0].astype(f32) + gwd[1].astype(f32)) + (
        gwd[2].astype(f32) + gwd[3].astype(f32)
    )
    for p in range(MEMBERS):
        total = gqin[p].astype(f32)
        for kind in range(3):
            at = kind * 1024 + p * 128
            grad_q[:, at : at + 128] = total[:, kind * 128 : kind * 128 + 128]
        for half in range(2):
            for plane in range(PLANES):
                unit = (p // QUAD) * 16 + plane * QUAD + p % QUAD
                at = half * 512 + plane * 128
                start = half * 4096 + unit * 128
                grad_gu[:, start : start + 128] = gwg[p, :, at : at + 128].astype(f32)
    total = (tiles[0] + tiles[1]) + (tiles[2] + tiles[3])
    quarter = lax.axis_index("col") % QUAD
    chosen = jnp.zeros((2, 32), f32)
    for k in range(4):
        chosen = chosen + jnp.where(quarter == k, total[0:2, k * 32 : k * 32 + 32], 0.0)
    grad_gains[...] = chosen
    grad_bias[...] = total[2:4, 0:16]


def sds(shape, dtype):
    return jax.ShapeDtypeStruct(shape, dtype)


def dma(*shape):
    return pltpu.SemaphoreType.DMA(shape)


def kernel(body, name, specs, outs, scratch, number=None, cost=0, places_out=None):
    params = dict(vmem_limit_bytes=56 << 20)
    if number is not None:
        params.update(collective_id=number, has_side_effects=True)
    return pl.pallas_call(
        body,
        name=name,
        in_specs=specs,
        out_shape=outs,
        out_specs=places_out or [VM] * len(outs),
        scratch_shapes=scratch,
        compiler_params=pltpu.CompilerParams(**params),
        cost_estimate=pl.CostEstimate(flops=cost, bytes_accessed=cost // 300, transcendentals=0),
    )


def plane_shards(
    tokens, variate_ids, time_ids, lengths, deal, w_qkv, w_out, w_gate_up, w_down,
    gain_attn, gain_ffn, var_bias, cotangent,
):
    rows, width = tokens.shape
    lines = [[plane * QUAD + k for plane in range(PLANES)] for k in range(QUAD)]
    freq = jnp.asarray(np.exp(-math.log(10000.0) * np.arange(32) / 32).astype(np.float32)[:, None])
    target = deal[0, 0]

    xp, wt, wop, wgp, s1, qkvt, gains, labels = kernel(
        enter_body,
        "enter",
        [VM] * 8 + [SM, VM],
        [
            sds((8, rows, width), bf16),
            sds((384, 1024), bf16),
            sds((4, 32, 1024), bf16),
            sds((8, 32, 1024), bf16),
            sds((8, rows, width), bf16),
            sds((192, 2048), bf16),
            sds((8, 1024), f32),
            sds((8, 2048), f32),
        ],
        [
            pltpu.VMEM((8, rows, width), bf16),
            pltpu.VMEM((8, rows, width), bf16),
            dma(4),
            pltpu.VMEM((8, 32, 384), bf16),
            pltpu.VMEM((8, 32, 384), bf16),
            pltpu.VMEM((4, 8, 32, 384), bf16),
            pltpu.VMEM((8, 32, 1024), bf16),
            pltpu.VMEM((8, 128), f32),
            pltpu.VMEM((4, 8, 128), f32),
            pltpu.VMEM((8, 4, 8, 128), f32),
            pltpu.VMEM((384, 1024), bf16),
            pltpu.VMEM((2, 192, 1024), bf16),
            pltpu.VMEM((32, 1024), f32),
            pltpu.VMEM((32, 1024), f32),
            pltpu.VMEM((8, 1024), f32),
        ]
        + [dma(8), dma(8), dma(8), dma(8), dma(4), dma(4), dma(4), dma(4), dma(8), dma(8)]
        + [dma(4), dma(4), dma(8), dma(8), dma(4), dma(4)],
        number=1,
        places_out=[ANY, ANY, VM, VM, ANY, VM, VM, VM],
    )(
        tokens, w_qkv, w_out, w_gate_up, gain_attn[None], gain_ffn[None], variate_ids[None],
        time_ids[None], lengths, freq,
    )

    gate_up = lax.all_gather(
        wgp.reshape(256, 1024), "col", axis=0, tiled=True, axis_index_groups=lines
    )
    wop = wop.reshape(128, 1024)

    wide = 2048 + WINDOW
    att, den, low, qa, ka = kernel(
        attend_body,
        "attend",
        [SM, VM, VM],
        [
            sds((64, wide), f32),
            sds((8, wide), f32),
            sds((64, wide), bf16),
            sds((AUG, wide), bf16),
            sds((2048, AUG), bf16),
        ],
        [pltpu.VMEM((AUG, 2048), bf16), pltpu.SMEM((8,), jnp.int32)],
        cost=2 * 10**9,
    )(var_bias, qkvt, labels)

    atp, hidden, s2, cotp = kernel(
        branch_body,
        "branch",
        [VM] * 5 + [SM],
        [
            sds((128, 1024), bf16),
            sds((rows, width), f32),
            sds((rows, width), bf16),
            sds((8, rows, width), bf16),
        ],
        [
            pltpu.VMEM((8, rows, width), bf16),
            pltpu.VMEM((16, 8, width), bf16),
            pltpu.VMEM((rows, width), bf16),
            dma(1),
            pltpu.VMEM((1024, 128), bf16),
            pltpu.VMEM((8, rows, width), bf16),
            dma(4), dma(4), dma(16), dma(16), dma(8), dma(8),
        ]
        + scatter_scratch(rows, width),
        number=2,
        places_out=[VM, VM, VM, ANY],
    )(low, wop, tokens, gains, cotangent.reshape(16, 8, width), target)

    out_part, down_in, gwg, d_hidden, d_branch, gain_two = kernel(
        ffn_body,
        "ffn",
        [VM, ANY, ANY, VM, VM, VM],
        [
            sds((8, rows, width), bf16),
            sds((4, rows, width), bf16),
            sds((8, 128, 1024), bf16),
            sds((rows, width), f32),
            sds((rows, width), bf16),
            sds((8, 1024), f32),
        ],
        [
            pltpu.VMEM((8, rows, width), bf16),
            pltpu.VMEM((8, 128, 1024), bf16),
            pltpu.VMEM((8, rows, width), bf16),
            pltpu.VMEM((1024, 1024), bf16),
            pltpu.VMEM((512, width), bf16),
            pltpu.VMEM((1024, 512), f32),
            pltpu.VMEM((1024, 512), f32),
            pltpu.VMEM((1024, 512), bf16),
            pltpu.VMEM((1024, 1024), bf16),
            pltpu.VMEM((8, rows, width), bf16),
            pltpu.VMEM((8, rows, width), bf16),
            pltpu.VMEM((4, rows, width), bf16),
            pltpu.VMEM((8, 128, 1024), bf16),
            pltpu.VMEM((rows, width), bf16),
            pltpu.VMEM((rows, width), bf16),
            dma(11), dma(8), dma(8), dma(4), dma(4), dma(4), dma(4),
        ]
        + scatter_scratch(rows, width),
        number=3,
        cost=10**10,
        places_out=[ANY, VM, ANY, VM, VM, VM],
    )(s2, cotp, gate_up.reshape(8, 128, 1024), w_down, hidden, gains)

    gate_up_sum = lax.psum_scatter(
        gwg.reshape(1024, 1024), "col", scatter_dimension=0, tiled=True, axis_index_groups=lines
    )

    grad, gwo = kernel(
        attended_back_body,
        "attended_back",
        [VM] * 3,
        [sds((64, 2048), bf16), sds((128, 1024), bf16)],
        [
            pltpu.VMEM((8, rows, width), bf16),
            pltpu.VMEM((128, 1024), bf16),
            dma(8), dma(8), dma(4), dma(4),
        ],
        number=4,
    )(d_branch, wop, atp)

    dproj, bias_tile = kernel(
        attend_back_body,
        "attend_back",
        [VM] * 8,
        [sds((192, 2048), bf16), sds((8, 128), f32)],
        [
            pltpu.VMEM((64, wide), bf16),
            pltpu.VMEM((8, wide), f32),
            pltpu.VMEM((2048, 64), bf16),
            pltpu.VMEM((64, wide), f32),
            pltpu.VMEM((AUG, 2048), f32),
            pltpu.VMEM((64, 2048), f32),
            pltpu.SMEM((8,), jnp.int32),
        ],
        cost=5 * 10**9,
    )(qkvt, qa, ka, labels, freq, grad, att, den)

    grad_tokens, gqin, goin, gwg_in, sums, out = kernel(
        last_body,
        "last",
        [VM] + [ANY] * 4 + [VM] * 7 + [SM],
        [
            sds((rows, width), bf16),
            sds((8, 32, 384), bf16),
            sds((4, 32, 1024), bf16),
            sds((8, 32, 1024), bf16),
            sds((4, 8, 128), f32),
            sds((16, 8, width), bf16),
        ],
        [
            pltpu.VMEM((384, 1024), bf16),
            pltpu.VMEM((8, rows, width), bf16),
            pltpu.VMEM((8, rows, width), bf16),
            pltpu.VMEM((8, rows, width), bf16),
            pltpu.VMEM((16, 8, width), bf16),
            pltpu.VMEM((16, 8, width), bf16),
            dma(4),
            pltpu.VMEM((2, 192, 1024), bf16),
            pltpu.VMEM((1024, 384), bf16),
            pltpu.VMEM((8, rows, width), bf16),
            pltpu.VMEM((4, 8, 32, 384), bf16),
            pltpu.VMEM((3, 8, 32, 384), bf16),
            pltpu.VMEM((8, 32, 384), bf16),
            pltpu.VMEM((8, 32, 384), bf16),
            pltpu.VMEM((8, 8, 128), f32),
            pltpu.VMEM((8, 4, 8, 128), f32),
            pltpu.VMEM((4, 8, 128), f32),
            pltpu.VMEM((rows, width), bf16),
            dma(4), dma(4),
        ]
        + scatter_scratch(rows, width)
        + [dma(2), dma(8), dma(8), dma(4), dma(4), dma(8), dma(8), dma(4), dma(4)]
        + [dma(4), dma(4), dma(8), dma(8), dma(16), dma(16)]
        + [pltpu.VMEM((rows, width), bf16), dma(2)]
        + scatter_scratch(rows, width),
        number=5,
    )(
        dproj, wt, s1, xp, out_part, gains, d_hidden, hidden, gwo.reshape(4, 32, 1024),
        gate_up_sum.reshape(8, 32, 1024), gain_two, bias_tile, target,
    )
    out, grad_tokens, grad_q, grad_o, grad_gate_up, grad_down, gain_grads, bias_grads = kernel(
        finish_body,
        "finish",
        [VM] * 7,
        [
            sds((rows, width), bf16),
            sds((rows, width), bf16),
            sds((32, 3072), f32),
            sds((32, 1024), f32),
            sds((32, 8192), f32),
            sds((rows, width), f32),
            sds((2, 32), f32),
            sds((2, 16), f32),
        ],
        [],
    )(
        grad_tokens, gqin, goin, out.reshape(rows, width), gwg_in,
        down_in, sums,
    )
    return (
        out,
        grad_tokens,
        grad_q,
        grad_o,
        grad_gate_up,
        grad_down,
        gain_grads[0],
        gain_grads[1],
        bias_grads,
    )


def solution(mesh):
    planes = mesh.shape["row"] == 2 and mesh.shape["col"] == PLANES * QUAD
    return jax.shard_map(
        plane_shards if planes else shards,
        mesh=mesh,
        in_specs=(
            P(("row", "col"), None),
            P(("row", "col")),
            P(("row", "col")),
            P("row", None),
            P("row", "col", None),
            P(("row", "col"), None),
            P(("row", "col"), None),
            P(("row", "col"), None),
            P(("row", "col"), None),
            P(("row", "col")),
            P(("row", "col")),
            P(),
            P(("row", "col"), None),
        ),
        out_specs=(
            P(("row", "col"), None),
            P(("row", "col"), None),
            P(("row", "col"), None),
            P(("row", "col"), None),
            P(("row", "col"), None),
            P(("row", "col"), None),
            P(("row", "col")),
            P(("row", "col")),
            P(),
        ),
        check_vma=False,
    )
```

```python
import math

import jax
import jax.numpy as jnp
import numpy as np
from jax import lax
from jax.experimental import pallas as pl
from jax.experimental.pallas import tpu as pltpu
from jax.sharding import PartitionSpec as P

HEAD_DIM = 64
UNIT = 128
KEY_BLOCK = 1024
NSEQ = 6


epsilon = 1e-05


def contract_rows(operand, factor):
    return lax.dot_general(
        operand, factor, (((0,), (0,)), ((), ())), preferred_element_type=jnp.float32
    )


def contract_cols(operand, factor):
    return lax.dot_general(
        operand, factor, (((1,), (1,)), ((), ())), preferred_element_type=jnp.float32
    )


def angles(time_ids):
    half_dim = HEAD_DIM // 2
    inverse_freq = jnp.exp(-math.log(10000.0) * jnp.arange(half_dim, dtype=jnp.float32) / half_dim)
    phases = time_ids.astype(jnp.float32)[:, None] * inverse_freq[None, :]
    return (jnp.cos(phases)[:, None, :], jnp.sin(phases)[:, None, :])


def rotate(tensor, cos_part, sin_part):
    half_dim = tensor.shape[-1] // 2
    former = tensor[..., :half_dim]
    latter = tensor[..., half_dim:]
    return jnp.concatenate(
        [former * cos_part - latter * sin_part, latter * cos_part + former * sin_part], axis=-1
    )


def unrotate(tensor, cos_part, sin_part):
    half_dim = tensor.shape[-1] // 2
    former = tensor[..., :half_dim]
    latter = tensor[..., half_dim:]
    return jnp.concatenate(
        [former * cos_part + latter * sin_part, latter * cos_part - former * sin_part], axis=-1
    )


def norm_scale(values):
    return lax.rsqrt(jnp.mean(values * values, axis=-1, keepdims=True) + epsilon)


def norm_back(d_normed, normed, scale):
    return scale * (d_normed - normed * jnp.mean(d_normed * normed, axis=-1, keepdims=True))


def score_weights(queries, query_seq, query_var, key_block, seq_block, var_block, var_bias):
    scores = (
        jnp.einsum("qhd,khd->hqk", queries, key_block, preferred_element_type=jnp.float32) * 0.125
    )
    matched = query_var[:, None] == var_block[None, :]
    scores = scores + jnp.where(
        matched[None], var_bias[0][:, None, None], var_bias[1][:, None, None]
    )
    within = query_seq[:, None] == seq_block[None, :]
    return (jnp.where(within[None], jnp.exp(scores), 0.0), matched)


def shards(
    tokens,
    variate_ids,
    time_ids,
    lengths,
    deal,
    w_qkv,
    w_out,
    w_gate_up,
    w_down,
    gain_attn,
    gain_ffn,
    var_bias,
    cotangent,
):
    tok_rows, model_width = tokens.shape
    n_col = lax.axis_size("col")
    col_index = lax.axis_index("col")
    piece_len = tok_rows // n_col
    head_count = model_width // HEAD_DIM
    bounds = jnp.cumsum(lengths[0]) * UNIT
    position = col_index * tok_rows + jnp.arange(tok_rows, dtype=jnp.int32)
    seq_own = jnp.sum((position[:, None] >= bounds[None, :]).astype(jnp.int32), axis=1)
    target = deal[0, 0]
    slots = jnp.arange(n_col, dtype=jnp.int32)
    inverse = jnp.sum(
        slots[:, None] * (target[:, None] == slots[None, :]).astype(jnp.int32), axis=0
    )
    send_rows = jnp.take(tokens.reshape(n_col, piece_len, model_width), inverse, axis=0)
    labels = jnp.stack(
        [
            seq_own.reshape(n_col, piece_len),
            variate_ids.reshape(n_col, piece_len),
            time_ids.reshape(n_col, piece_len),
        ],
        axis=1,
    )
    send_labels = jnp.take(labels, inverse, axis=0)
    got_rows, got_labels = (
        lax.all_to_all(send_rows, "col", split_axis=0, concat_axis=0, tiled=True),
        lax.all_to_all(send_labels, "col", split_axis=0, concat_axis=0, tiled=True),
    )
    inputs = got_rows.reshape(tok_rows, model_width).astype(jnp.float32)
    seq_q = got_labels[:, 0, :].reshape(tok_rows)
    var_q = got_labels[:, 1, :].reshape(tok_rows)
    cos_part, sin_part = angles(got_labels[:, 2, :].reshape(tok_rows))
    qkv_full, out_full, gate_up_full, down_full, gain_one, gain_two = (
        lax.all_gather(w_qkv, ("row", "col"), axis=0, tiled=True),
        lax.all_gather(w_out, ("row", "col"), axis=0, tiled=True),
        lax.all_gather(w_gate_up, ("row", "col"), axis=0, tiled=True),
        lax.all_gather(w_down, ("row", "col"), axis=0, tiled=True),
        lax.all_gather(gain_attn, ("row", "col"), axis=0, tiled=True),
        lax.all_gather(gain_ffn, ("row", "col"), axis=0, tiled=True),
    )
    scale_one = norm_scale(inputs)
    normed_one = inputs * scale_one
    scaled_one = (normed_one * gain_one.astype(jnp.float32)).astype(jnp.bfloat16)
    projected = jnp.dot(scaled_one, qkv_full, preferred_element_type=jnp.float32)
    shaped = projected.reshape(tok_rows, 3, head_count, HEAD_DIM)
    queries = rotate(shaped[:, 0], cos_part, sin_part).astype(jnp.bfloat16)
    key_own = (
        rotate(shaped[:, 1], cos_part, sin_part).astype(jnp.bfloat16).reshape(tok_rows, model_width)
    )
    value_own = projected[:, 2 * model_width :].astype(jnp.bfloat16)
    keys_all, values_all, seq_k, var_k = (
        lax.all_gather(key_own, "col", axis=0, tiled=True),
        lax.all_gather(value_own, "col", axis=0, tiled=True),
        lax.all_gather(seq_q, "col", axis=0, tiled=True),
        lax.all_gather(var_q, "col", axis=0, tiled=True),
    )
    group_size = keys_all.shape[0]
    stride = min(KEY_BLOCK, group_size)
    block_count = group_size // stride

    def split_blocks(key_rows, value_rows, key_seq, key_var):
        return (
            key_rows.reshape(block_count, stride, head_count, HEAD_DIM),
            value_rows.reshape(block_count, stride, head_count, HEAD_DIM),
            key_seq.reshape(block_count, stride),
            key_var.reshape(block_count, stride),
        )

    def forward_step(running, block_data):
        denominator, numerator = running
        key_block, value_block, seq_block, var_block = block_data
        weights = score_weights(queries, seq_q, var_q, key_block, seq_block, var_block, var_bias)[0]
        denominator = denominator + jnp.sum(weights, axis=-1)
        numerator = numerator + jnp.einsum(
            "hqk,khd->qhd",
            weights.astype(jnp.bfloat16),
            value_block,
            preferred_element_type=jnp.float32,
        )
        return ((denominator, numerator), None)

    (denominator, numerator), unused = lax.scan(
        forward_step,
        (
            jnp.zeros((head_count, tok_rows), jnp.float32),
            jnp.zeros((tok_rows, head_count, HEAD_DIM), jnp.float32),
        ),
        split_blocks(keys_all, values_all, seq_k, var_k),
    )
    attended = numerator / denominator.T[:, :, None]
    attn_low = attended.reshape(tok_rows, model_width).astype(jnp.bfloat16)
    hidden_state = inputs + jnp.dot(attn_low, out_full, preferred_element_type=jnp.float32)
    scale_two = norm_scale(hidden_state)
    normed_two = hidden_state * scale_two
    scaled_two = (normed_two * gain_two.astype(jnp.float32)).astype(jnp.bfloat16)
    gate_up = jnp.dot(scaled_two, gate_up_full, preferred_element_type=jnp.float32)
    hidden_units = gate_up_full.shape[1] // 2
    gate_part = gate_up[:, :hidden_units]
    upper_part = gate_up[:, hidden_units:]
    sigmoid_gate = jax.nn.sigmoid(gate_part)
    active = gate_part * sigmoid_gate
    inner_act = (active * upper_part).astype(jnp.bfloat16)
    ffn_branch = jnp.dot(inner_act, down_full, preferred_element_type=jnp.float32)
    output = (hidden_state + ffn_branch).astype(jnp.bfloat16)
    qkv_back, out_back, gate_up_back, down_back, gain_one_back, gain_two_back = (
        lax.all_gather(w_qkv, ("row", "col"), axis=0, tiled=True),
        lax.all_gather(w_out, ("row", "col"), axis=0, tiled=True),
        lax.all_gather(w_gate_up, ("row", "col"), axis=0, tiled=True),
        lax.all_gather(w_down, ("row", "col"), axis=0, tiled=True),
        lax.all_gather(gain_attn, ("row", "col"), axis=0, tiled=True),
        lax.all_gather(gain_ffn, ("row", "col"), axis=0, tiled=True),
    )
    d_inner = contract_cols(cotangent, down_back)
    d_gate = (
        d_inner * upper_part * sigmoid_gate * (1.0 + gate_part * (1.0 - sigmoid_gate))
    ).astype(jnp.bfloat16)
    d_upper = (d_inner * active).astype(jnp.bfloat16)
    d_gate_up = jnp.concatenate([d_gate, d_upper], axis=1)
    d_scaled_two = contract_cols(d_gate_up, gate_up_back)
    term_gain_two = jnp.sum(d_scaled_two * normed_two, axis=0)
    term_gate_up = contract_rows(scaled_two, d_gate_up)
    term_down = contract_rows(inner_act, cotangent)
    d_hidden = cotangent.astype(jnp.float32) + norm_back(
        d_scaled_two * gain_two_back.astype(jnp.float32), normed_two, scale_two
    )
    d_branch = d_hidden.astype(jnp.bfloat16)
    term_out = contract_rows(attn_low, d_branch)
    d_attended = contract_cols(d_branch, out_back).reshape(tok_rows, head_count, HEAD_DIM)
    d_numerator = (d_attended / denominator.T[:, :, None]).astype(jnp.bfloat16)
    centre = (jnp.sum(d_attended * attended, axis=-1) / denominator.T).T
    back_keys = (
        lax.all_gather(key_own, "col", axis=0, tiled=True),
        lax.all_gather(value_own, "col", axis=0, tiled=True),
        lax.all_gather(seq_q, "col", axis=0, tiled=True),
        lax.all_gather(var_q, "col", axis=0, tiled=True),
    )

    def query_step(running, block_data):
        d_queries, same_sum, other_sum = running
        key_block, value_block, seq_block, var_block = block_data
        weights, matched = score_weights(
            queries, seq_q, var_q, key_block, seq_block, var_block, var_bias
        )
        d_probs = jnp.einsum(
            "qhd,khd->hqk", d_numerator, value_block, preferred_element_type=jnp.float32
        )
        d_scores = weights * (d_probs - centre[:, :, None])
        same_sum = same_sum + jnp.sum(jnp.where(matched[None], d_scores, 0.0), axis=(1, 2))
        other_sum = other_sum + jnp.sum(jnp.where(matched[None], 0.0, d_scores), axis=(1, 2))
        d_rounded = d_scores.astype(jnp.bfloat16)
        d_queries = d_queries + jnp.einsum(
            "hqk,khd->qhd", d_rounded, key_block, preferred_element_type=jnp.float32
        )
        return ((d_queries, same_sum, other_sum), (d_rounded, weights.astype(jnp.bfloat16)))

    def query_and_key_step(running, block_data):
        running, rounded = query_step(running, block_data)
        d_rounded, weights_low = rounded
        d_keys = (
            jnp.einsum("hqk,qhd->khd", d_rounded, queries, preferred_element_type=jnp.float32)
            * 0.125
        )
        d_values = jnp.einsum(
            "hqk,qhd->khd", weights_low, d_numerator, preferred_element_type=jnp.float32
        )
        return (running, (d_keys, d_values))

    start_running = (
        jnp.zeros((tok_rows, head_count, HEAD_DIM), jnp.float32),
        jnp.zeros((head_count,), jnp.float32),
        jnp.zeros((head_count,), jnp.float32),
    )
    (d_queries, same_sum, other_sum), (d_keys, d_values) = lax.scan(
        query_and_key_step,
        start_running,
        split_blocks(back_keys[0], back_keys[1], back_keys[2], back_keys[3]),
    )
    key_grad, value_grad = (
        lax.psum_scatter(
            d_keys.reshape(group_size, model_width).astype(jnp.bfloat16),
            "col",
            scatter_dimension=0,
            tiled=True,
        ).astype(jnp.float32),
        lax.psum_scatter(
            d_values.reshape(group_size, model_width).astype(jnp.bfloat16),
            "col",
            scatter_dimension=0,
            tiled=True,
        ).astype(jnp.float32),
    )
    d_query_pre = unrotate(d_queries * 0.125, cos_part, sin_part).reshape(tok_rows, model_width)
    d_key_pre = unrotate(
        key_grad.reshape(tok_rows, head_count, HEAD_DIM), cos_part, sin_part
    ).reshape(tok_rows, model_width)
    d_projected = jnp.concatenate([d_query_pre, d_key_pre, value_grad], axis=1).astype(jnp.bfloat16)
    d_scaled_one = contract_cols(d_projected, qkv_back)
    term_qkv = contract_rows(scaled_one, d_projected)
    term_gain_one = jnp.sum(d_scaled_one * normed_one, axis=0)
    grad_w_qkv, grad_w_out, grad_w_gate_up, grad_w_down, grad_gain_attn, grad_gain_ffn = (
        lax.psum_scatter(term_qkv, ("row", "col"), scatter_dimension=0, tiled=True),
        lax.psum_scatter(term_out, ("row", "col"), scatter_dimension=0, tiled=True),
        lax.psum_scatter(term_gate_up, ("row", "col"), scatter_dimension=0, tiled=True),
        lax.psum_scatter(term_down, ("row", "col"), scatter_dimension=0, tiled=True),
        lax.psum_scatter(term_gain_one, ("row", "col"), scatter_dimension=0, tiled=True),
        lax.psum_scatter(term_gain_two, ("row", "col"), scatter_dimension=0, tiled=True),
    )
    grad_var_bias = lax.psum(jnp.stack([same_sum, other_sum], axis=0), ("row", "col"))
    d_inputs = d_hidden + norm_back(
        d_scaled_one * gain_one_back.astype(jnp.float32), normed_one, scale_one
    )
    returned = lax.all_to_all(
        d_inputs.astype(jnp.bfloat16).reshape(n_col, piece_len, model_width),
        "col",
        split_axis=0,
        concat_axis=0,
        tiled=True,
    )
    grad_tokens = jnp.take(returned, target, axis=0).reshape(tok_rows, model_width)
    return (
        output,
        grad_tokens,
        grad_w_qkv,
        grad_w_out,
        grad_w_gate_up,
        grad_w_down,
        grad_gain_attn,
        grad_gain_ffn,
        grad_var_bias,
    )


PLANES = 4
QUAD = 4
MEMBERS = 8
WINDOW = 512
AUG = 128
f32 = jnp.float32
bf16 = jnp.bfloat16
VM = pl.BlockSpec(memory_space=pltpu.VMEM)
SM = pl.BlockSpec(memory_space=pltpu.SMEM)
ANY = pl.BlockSpec(memory_space=pl.ANY)


def mm(a, b):
    return lax.dot_general(a, b, (((1,), (0,)), ((), ())), preferred_element_type=f32)


def mm_nt(a, b):
    return lax.dot_general(a, b, (((1,), (1,)), ((), ())), preferred_element_type=f32)


def mm_tn(a, b):
    return lax.dot_general(a, b, (((0,), (0,)), ((), ())), preferred_element_type=f32)


def flip(value, bits):
    for bit in (1, 2, 4, 8, 16):
        if bits & bit:
            value = value + bit * (1 - 2 * ((value // bit) % 2))
    return value


def places():
    row = lax.axis_index("row")
    col = lax.axis_index("col")
    return row, col, col // QUAD, row * QUAD + col % QUAD


def in_plane(row, col, bits):
    return flip(row, bits // QUAD), flip(col, bits % QUAD)


def in_line(row, col, bits):
    return row, flip(col, bits // 2 * QUAD + bits % 2)


def on_line(row, col, bits):
    return row, flip(col, bits * QUAD)


def anyone(row, col, bits):
    return flip(row, bits // 16), flip(col, bits % 16)


def push(source, target, send, recv, device):
    return pltpu.make_async_remote_copy(
        src_ref=source,
        dst_ref=target,
        send_sem=send,
        recv_sem=recv,
        device_id={"row": device[0], "col": device[1]},
        device_id_type=pl.DeviceIdType.MESH,
    )


def meet(devices):
    barrier = pltpu.get_barrier_semaphore()
    for device in devices:
        pl.semaphore_signal(
            barrier,
            1,
            device_id={"row": device[0], "col": device[1]},
            device_id_type=pl.DeviceIdType.MESH,
        )
    pl.semaphore_wait(barrier, len(devices))


NEAR = (2, 4, 6, 1)


def plane_near(row, col):
    return [in_plane(row, col, bits) for bits in NEAR]


def line_all(row, col):
    return [on_line(row, col, bits) for bits in (1, 2, 3)]


def column_all(row, col):
    return [
        (flip(row, bits // 4), flip(col, bits % 4 * QUAD)) for bits in (1, 2, 3, 5, 6, 7)
    ]


class Gather:
    def __init__(self, target, send, recv, peer=in_plane, place=None):
        self.target, self.send, self.recv, self.peer = target, send, recv, peer
        self.row, self.col, _, self.place = places()
        if place is not None:
            self.place = place
        self.copies, self.onward = {}, {}

    def start(self, source):
        for bits in NEAR:
            self.copies[bits] = push(
                source,
                self.target.at[self.place],
                self.send.at[bits],
                self.recv.at[bits],
                self.peer(self.row, self.col, bits),
            )
            self.copies[bits].start()

    def forward(self, bits):
        self.copies[bits].wait_recv()
        slot = self.target.at[flip(self.place, bits)]
        self.onward[bits] = push(
            slot,
            slot,
            self.send.at[bits + 1],
            self.recv.at[bits + 1],
            self.peer(self.row, self.col, 1),
        )
        self.onward[bits].start()

    def arrived(self, bits):
        (self.onward[bits] if bits else self.copies[1]).wait_recv()

    def close(self):
        for copy in list(self.copies.values()) + list(self.onward.values()):
            copy.wait_send()

    def finish(self):
        for bits in (2, 4, 6):
            self.forward(bits)
        for bits in (0, 2, 4, 6):
            self.arrived(bits)


class LineGather(Gather):
    def __init__(self, target, send, recv):
        row, col, z, _ = places()
        super().__init__(target, send, recv, in_line, z * 2 + col % 2)
        self.inner = jnp.logical_or(z == 1, z == 2)

    def start(self, source):
        for bits in (4, 2, 6, 1):
            self.copies[bits] = push(
                source,
                self.target.at[self.place],
                self.send.at[bits],
                self.recv.at[bits],
                in_line(self.row, self.col, bits),
            )
            if bits != 6:
                self.copies[bits].start()
        slot = self.target.at[flip(self.place, 4)]
        self.passing = push(
            slot, slot, self.send.at[0], self.recv.at[6], in_line(self.row, self.col, 2)
        )

        @pl.when(self.inner)
        def _():
            self.copies[6].start()

    def forward(self, bits):
        super().forward(bits)
        if bits == 4:

            @pl.when(self.inner)
            def _():
                self.passing.start()

    def close(self):
        for bits in (4, 2, 1):
            self.copies[bits].wait_send()
        for copy in self.onward.values():
            copy.wait_send()

        @pl.when(self.inner)
        def _():
            self.copies[6].wait_send()
            self.passing.wait_send()


class Scatter:
    def __init__(self, part, inbox, outbox, second, send, recv, peer=in_plane, place=None):
        self.part, self.inbox, self.outbox, self.second = part, inbox, outbox, second
        self.send, self.recv, self.peer = send, recv, peer
        self.row, self.col, _, self.place = places()
        if place is not None:
            self.place = place
        self.core = self.col % 2
        self.copies, self.sent = {}, []

    def near(self, chip, number):
        copy = push(
            self.part.at[2 * chip + 1 - self.core],
            self.inbox.at[number],
            self.send.at[number],
            self.recv.at[number],
            self.peer(self.row, self.col, 1),
        )
        copy.start()
        self.copies[number] = copy

    def far(self, bits):
        self.copies[bits].wait_recv()
        chip = flip(self.place // 2, bits)
        total = self.part[2 * chip + self.core].astype(f32) + self.inbox[bits].astype(f32)
        self.outbox[bits - 1] = total.astype(bf16)
        copy = push(
            self.outbox.at[bits - 1],
            self.second.at[bits - 1],
            self.send.at[3 + bits],
            self.recv.at[3 + bits],
            self.peer(self.row, self.col, 2 * bits),
        )
        copy.start()
        self.sent.append(copy)

    def near_all(self):
        for bits in range(4):
            self.near(flip(self.place // 2, bits), bits)

    def far_all(self):
        for bits in (3, 2, 1):
            self.far(bits)

    def finish(self):
        self.copies[0].wait_recv()
        total = self.part[self.place].astype(f32) + self.inbox[0].astype(f32)
        for copy in self.sent:
            copy.wait_recv()
        for i in range(3):
            total = total + self.second[i].astype(f32)
        return total

    def close(self):
        for copy in list(self.copies.values()) + self.sent:
            copy.wait_send()


class RoundScatter(Scatter):
    def __init__(self, part, inbox, outbox, second, send, recv, passed, sems):
        super().__init__(part, inbox, outbox, second, send, recv)
        self.passed, self.sems = passed, sems

    def sum_for(self, bits):
        self.copies[bits].wait_recv()
        chip = flip(self.place // 2, bits)
        return self.part[2 * chip + self.core].astype(f32) + self.inbox[bits].astype(f32)

    def far_first(self):
        self.outbox[2] = self.sum_for(3).astype(bf16)
        across = in_plane(self.row, self.col, 4)
        self.passing = push(
            self.outbox.at[2], self.passed, self.sems.at[0], self.sems.at[1], across
        )
        self.passing.start()
        self.outbox[1] = self.sum_for(2).astype(bf16)
        self.sent.append(
            push(self.outbox.at[1], self.second.at[1], self.send.at[5], self.recv.at[5], across)
        )
        self.sent[0].start()

    def far_second(self):
        total = self.sum_for(1)
        self.passing.wait_recv()
        self.outbox[0] = (total + self.passed[...].astype(f32)).astype(bf16)
        self.sent.append(
            push(
                self.outbox.at[0],
                self.second.at[0],
                self.send.at[4],
                self.recv.at[4],
                in_plane(self.row, self.col, 2),
            )
        )
        self.sent[1].start()

    def finish(self):
        self.copies[0].wait_recv()
        total = self.part[self.place].astype(f32) + self.inbox[0].astype(f32)
        for copy in self.sent:
            copy.wait_recv()
        return total + (self.second[0].astype(f32) + self.second[1].astype(f32))

    def close(self):
        super().close()
        self.passing.wait_send()


class LineScatter(Scatter):
    def __init__(self, part, inbox, outbox, second, send, recv, passed, sems):
        row, col, z, _ = places()
        super().__init__(part, inbox, outbox, second, send, recv, in_line, z * 2 + col % 2)
        self.passed, self.sems = passed, sems
        self.inner = jnp.logical_or(z == 1, z == 2)
        self.end = jnp.logical_not(self.inner)

    def sum_for(self, bits):
        self.copies[bits].wait_recv()
        chip = flip(self.place // 2, bits)
        return self.part[2 * chip + self.core].astype(f32) + self.inbox[bits].astype(f32)

    def sum_again(self, bits):
        chip = flip(self.place // 2, bits)
        return self.part[2 * chip + self.core].astype(f32) + self.inbox[bits].astype(f32)

    def to(self, bits):
        return push(
            self.outbox.at[bits - 1],
            self.second.at[bits - 1],
            self.send.at[3 + bits],
            self.recv.at[3 + bits],
            in_line(self.row, self.col, 2 * bits),
        )

    def far(self, bits):
        self.outbox[bits - 1] = self.sum_for(bits).astype(bf16)
        if bits == 1:
            self.sent.append(self.to(1))
            self.sent[-1].start()
        if bits == 2:
            self.added = self.to(2)
            self.sent.append(self.added)

            @pl.when(self.end)
            def _():
                self.added.start()

        if bits == 3:
            self.across = self.to(3)
            self.passing = push(
                self.outbox.at[2],
                self.passed,
                self.sems.at[0],
                self.sems.at[1],
                in_line(self.row, self.col, 2),
            )

            @pl.when(self.end)
            def _():
                self.passing.start()
                self.second[2] = jnp.zeros(self.second.shape[1:], bf16)

            @pl.when(self.inner)
            def _():
                self.across.start()

    def far_second(self):
        @pl.when(self.inner)
        def _():
            self.passing.wait_recv()
            total = self.sum_again(2) + self.passed[...].astype(f32)
            self.outbox[1] = total.astype(bf16)
            self.added.start()

    def finish(self):
        @pl.when(self.inner)
        def _():
            self.across.wait_recv()

        return super().finish()

    def close(self):
        super().close()

        @pl.when(self.inner)
        def _():
            self.across.wait_send()

        @pl.when(self.end)
        def _():
            self.passing.wait_send()


def scatter_scratch(rows, width):
    return [
        pltpu.VMEM((4, rows, width), bf16),
        pltpu.VMEM((3, rows, width), bf16),
        pltpu.VMEM((3, rows, width), bf16),
        pltpu.SemaphoreType.DMA((7,)),
        pltpu.SemaphoreType.DMA((7,)),
    ]


def fetch(source, target, semaphore):
    copy = pltpu.make_async_copy(source, target, semaphore)
    copy.start()
    return copy


def block(number, size):
    return pl.ds(pl.multiple_of(number * size, size), size)


def enter_body(
    x, wq, wo, wg, cot, ga, gf, variate, time, lengths, deal, freq,
    xp_out, wt_out, wop, wgp, s1_out, qkvt, gains, labels, cots,
    cotr, xp, s1, keep, wqs, wline, wqp, wgs, tile, tl, tiles, wt, box, cs, sn, times,
    sx, rx, sq, rq, sv, rv, st, rt, su, ru, sw, rw, sg, rg, sz, rz, sc, rc,
):
    row, col, z, place = places()
    quarter = col % QUAD
    y, core = col // 2 % 2, col % 2
    member = z * 2 + core
    lane = lax.broadcasted_iota(jnp.int32, (1, 128), 1)
    for line, gain in ((0, ga), (1, gf)):
        wide = gain[...].astype(f32)
        wide = jnp.concatenate([wide] * 4, axis=1)
        tile[line : line + 1, :] = jnp.where(lane // 32 == quarter, wide, 0.0)
    tile[2:3, :] = variate[...].astype(f32)
    tile[3:4, :] = time[...].astype(f32)
    numbers = jnp.zeros((1, 128), jnp.int32)
    for i in range(NSEQ):
        numbers = jnp.where(lane == i, lengths[0, i], numbers)
    tile[4:5, :] = numbers.astype(f32)
    tile[5:8, :] = jnp.zeros((3, 128), f32)
    for p in range(MEMBERS):
        for part in range(3):
            at = part * 1024 + p * 128
            wqs[p, :, part * 128 : part * 128 + 128] = wq[:, at : at + 128]
    meet([anyone(row, col, bits) for bits in range(1, 32)])
    first = []
    for bits in range(1, 8):
        there = in_line(row, col, bits)
        first.append(push(wqs.at[flip(member, bits)], wline.at[member], sq.at[bits], rq.at[bits], there))
        first[-1].start()
    for bits in (1, 2, 3):
        first.append(push(tile, tl.at[z], st.at[bits], rt.at[bits], on_line(row, col, bits)))
        first[-1].start()
    rows_in = LineGather(xp, sx, rx)
    xp[member] = x[...]
    wline[member] = wqs[member]
    tl[z] = tile[...]
    for p in range(MEMBERS):
        for half in range(2):
            for plane in range(PLANES):
                unit = (p // QUAD) * 16 + plane * QUAD + p % QUAD
                at = half * 512 + plane * 128
                start = half * 4096 + unit * 128
                wgs[p, :, at : at + 128] = wg[:, start : start + 128]
    blocks = []
    for bits in range(1, 8):
        there = in_plane(row, col, bits)
        blocks.append(
            push(wgs.at[flip(place, bits)], wgp.at[place], sg.at[bits], rg.at[bits], there)
        )
        blocks[-1].start()
    wgp[place] = wgs[place]
    for copy in first:
        copy.wait_recv()
    rows_in.start(x)
    column = row * 2 + y
    beside, across = (row, flip(col, 2)), (flip(row, 1), col)
    ways = [
        push(wline, wqp.at[column], sv.at[1], rv.at[1], beside),
        push(wline, wqp.at[column], sv.at[2], rv.at[2], across),
    ]
    for copy in ways:
        copy.start()
    wqp[column] = wline[...]
    second = []
    for bits in range(1, 8):
        there = in_plane(row, col, bits)
        second.append(push(tl, tiles.at[place], su.at[bits], ru.at[bits], there))
        second[-1].start()
    tiles[place] = tl[...]
    ways[0].wait_recv()
    slot = wqp.at[flip(column, 1)]
    ways.append(push(slot, slot, sv.at[3], rv.at[3], across))
    ways[2].start()
    for copy in second:
        copy.wait_recv()
    rows_in.forward(4)
    rows_in.forward(2)
    for copy in ways[1:]:
        copy.wait_recv()
    for k in range(8):
        lanes = slice(k * 128, k * 128 + 128)
        r, plane = k // PLANES, k % PLANES
        gains[:, lanes] = (tiles[r * QUAD, plane] + tiles[r * QUAD + 1, plane]) + (
            tiles[r * QUAD + 2, plane] + tiles[r * QUAD + 3, plane]
        )
        times[:, lanes] = tiles[row * QUAD + y * 2 + k % 2, k // 2]
        wt[:, lanes] = jnp.transpose(
            jnp.concatenate(
                [wqp[r * 2 + j // 2, plane * 2 + j % 2] for j in range(4)], axis=0
            )
        )
    for k in range(16):
        labels[:, k * 128 : k * 128 + 128] = tiles[row * QUAD + k % QUAD, k // QUAD]
    phases = times[3:4, :] * freq[...]
    cs[...] = jnp.cos(phases)
    sn[...] = jnp.sin(phases)
    gain = gains[0:1, :]
    kept = [fetch(wt, wt_out, keep.at[2])]

    def project(chip):
        rows = block(chip, 256)
        values = jnp.concatenate([xp[2 * chip], xp[2 * chip + 1]], axis=0).astype(f32)
        scaled = (values * norm_scale(values) * gain).astype(bf16)
        s1[2 * chip] = scaled[0:128]
        s1[2 * chip + 1] = scaled[128:256]
        out = mm_nt(wt[...], scaled)
        cos_part, sin_part = cs[:, rows], sn[:, rows]
        for head in range(2):
            for part in range(2):
                base = part * 128 + head * 64
                former, latter = out[base : base + 32], out[base + 32 : base + 64]
                factor = 0.125 if part == 0 else 1.0
                turned = former * cos_part - latter * sin_part
                other = latter * cos_part + former * sin_part
                at = part * 64
                box[head, at : at + 32, rows] = (turned * factor).astype(bf16)
                box[head, at + 32 : at + 64, rows] = (other * factor).astype(bf16)
            at = 256 + head * 64
            box[head, 128:192, rows] = out[at : at + 64].astype(bf16)

    pieces = []
    for bits in range(1, 16):
        there = (row, flip(col, bits))
        pieces.append(push(cot.at[there[1]], cotr.at[col], sc.at[bits], rc.at[bits], there))
        pieces[-1].start()
    cotr[col] = cot[col]
    turned = []

    def exchange(chip, number):
        lanes = pl.ds(pl.multiple_of(chip * 512 + y * 256, 256), 256)
        copy = push(
            box.at[1 - y, :, block(chip, 256)],
            qkvt.at[:, lanes],
            sz.at[number],
            rz.at[number],
            (row, flip(col, 2)),
        )
        copy.start()
        turned.append(copy)
        qkvt[:, lanes] = box[y, :, block(chip, 256)]

    for k, bits in enumerate((0, 4, 2, 6)):
        if bits == 6:
            rows_in.forward(6)
        rows_in.arrived(bits)
        chip = flip(z, bits // 2)
        project(chip)
        exchange(chip, k)
        if bits == 2:
            target = col // 2 % 2 * 2 + col // 4 % 2
            slot = row * 2 + col % 2
            for plane in range(PLANES):
                there = (col // 8, plane * QUAD + target)
                mine = jnp.logical_and(row * 16 + col == there[0] * 16 + there[1], z == plane)

                @pl.when(jnp.logical_not(mine))
                def _():
                    push(wo, wop.at[slot], sw.at[plane], rw.at[slot], there).start()

                @pl.when(mine)
                def _():
                    wop[slot] = wo[...]

    kept.append(fetch(xp, xp_out, keep.at[0]))
    kept.append(fetch(s1, s1_out, keep.at[1]))
    for copy in blocks:
        copy.wait_recv()
    for j in range(4):
        source = (j // 2, row * 8 + core * 4 + y * 2 + j % 2)
        mine = jnp.logical_and(row == source[0], col == source[1])

        @pl.when(jnp.logical_not(mine))
        def _():
            push(wo, wop.at[j], sw.at[j], rw.at[j], source).wait_recv()

    target = col // 2 % 2 * 2 + col // 4 % 2
    slot = row * 2 + col % 2
    for plane in range(PLANES):
        there = (col // 8, plane * QUAD + target)
        mine = jnp.logical_and(row * 16 + col == there[0] * 16 + there[1], z == plane)

        @pl.when(jnp.logical_not(mine))
        def _():
            push(wo, wop.at[slot], sw.at[plane], rw.at[slot], there).wait_send()

    for copy in pieces:
        copy.wait_recv()
    for j in range(16):
        cots[j * 8 : j * 8 + 8, :] = cotr[jnp.clip(deal[j], 0, 15)]
    for copy in turned:
        copy.wait()
    rows_in.close()
    for copy in first + second + blocks + ways + pieces:
        copy.wait_send()
    for copy in kept:
        copy.wait()


def split_three(value):
    high = value.astype(bf16).astype(f32)
    middle = (value - high).astype(bf16).astype(f32)
    return high, middle, (value - high - middle).astype(bf16).astype(f32)


def window_queries(qa, lanes, first, limit):
    place = first + lax.broadcasted_iota(jnp.int32, (16, WINDOW), 1)
    line = lax.broadcasted_iota(jnp.int32, (16, WINDOW), 0)
    extra = jnp.where(
        jnp.logical_and(line == 12, place >= limit), -1e30, qa[64:80, lanes].astype(f32)
    )
    return jnp.concatenate(
        [qa[0:64, lanes], extra.astype(bf16), jnp.zeros((AUG - 80, WINDOW), bf16)], axis=0
    )


def head_of():
    row, col, z, place = places()
    return (z * 2 + col % 2) * 2 + col // 2 % 2


def read_lengths(labels, info):
    lane = lax.broadcasted_iota(jnp.int32, (1, 128), 1)
    numbers = labels[4:5, 0:128]
    for i in range(NSEQ):
        info[i] = jnp.sum(jnp.where(lane == i, numbers, 0.0)).astype(jnp.int32)


def over_keys(start, length, step, carry):
    carry = lax.fori_loop(
        0, length // 2, lambda k, c: step((start + 2 * k) * 128, 256, c), carry
    )
    return lax.fori_loop(
        0, length % 2, lambda k, c: step((start + length - 1) * 128, 128, c), carry
    )


def attend_body(bias_all, qkvt, labels, att, den, low, qa, ka, kt, info):
    size = qkvt.shape[1]
    head = head_of()
    bias = (bias_all[0, head], bias_all[1, head])
    variate = labels[2:3, :]
    line = lax.broadcasted_iota(jnp.int32, (16, size), 0)
    same = (variate == (line % 4).astype(f32)).astype(f32)
    same_pieces = split_three(jnp.full((16, size), bias[0] - bias[1], f32))
    other_pieces = split_three(jnp.full((16, size), bias[1], f32))

    def choose(pieces, number):
        return jnp.where(number == 0, pieces[0], jnp.where(number == 1, pieces[1], pieces[2]))

    extra_q = jnp.where(line < 12, same, jnp.where(line == 12, 0.0, 1.0))
    extra_k = jnp.where(
        line < 12,
        same * choose(same_pieces, line // 4),
        jnp.where(line == 12, 1.0, choose(other_pieces, line - 13)),
    )
    qa[0:64, 0:size] = qkvt[0:64, :]
    qa[64:80, 0:size] = extra_q.astype(bf16)
    qa[80:AUG, 0:size] = jnp.zeros((AUG - 80, size), bf16)
    qa[:, size:] = jnp.zeros((AUG, WINDOW), bf16)
    kt[0:64, :] = qkvt[64:128, :]
    kt[64:80, :] = extra_k.astype(bf16)
    kt[80:AUG, :] = jnp.zeros((AUG - 80, size), bf16)
    ka[...] = jnp.transpose(kt[...])
    read_lengths(labels, info)

    def sequence(number, start):
        length = info[number]
        limit = (start + length) * 128

        def window(j, unused):
            first = (start + 4 * j) * 128
            lanes = pl.ds(pl.multiple_of(first, 128), WINDOW)
            queries = window_queries(qa, lanes, first, limit)

            def keys(first_key, count, running):
                total, numerator = running
                rows = pl.ds(pl.multiple_of(first_key, 128), count)
                weights = jnp.exp(mm(ka[rows, :], queries))
                total = total + jnp.sum(weights, axis=0, keepdims=True)
                numerator = numerator + mm(qkvt[128:192, rows], weights.astype(bf16))
                return total, numerator

            total, numerator = over_keys(
                start, length, keys, (jnp.zeros((1, WINDOW), f32), jnp.zeros((64, WINDOW), f32))
            )
            attended = numerator / total
            att[:, lanes] = attended
            den[:, lanes] = jnp.broadcast_to(total, (8, WINDOW))
            low[:, lanes] = attended.astype(bf16)
            return unused

        lax.fori_loop(0, (length + 3) // 4, window, 0)
        return start + length

    lax.fori_loop(0, NSEQ, sequence, 0)


def attend_back_body(
    qkvt, qa, ka, labels, freq, grad, att, den,
    dproj, bias_tile,
    dn, cw, vn, dq, dk, dv, info,
):
    size = qkvt.shape[1]
    lanes_all = slice(0, size)
    inverse = 1.0 / den[0:1, lanes_all]
    d_att = grad[...].astype(f32)
    dn[:, lanes_all] = (d_att * inverse).astype(bf16)
    dn[:, size:] = jnp.zeros((64, WINDOW), bf16)
    cw[:, lanes_all] = jnp.broadcast_to(
        jnp.sum(d_att * att[:, lanes_all], axis=0, keepdims=True) * inverse, (8, size)
    )
    cw[:, size:] = jnp.zeros((8, WINDOW), f32)
    vn[...] = jnp.transpose(qkvt[128:192, :])
    dk[...] = jnp.zeros_like(dk)
    dv[...] = jnp.zeros_like(dv)

    read_lengths(labels, info)

    def sequence(number, start):
        length = info[number]
        limit = (start + length) * 128

        def window(j, unused):
            first = (start + 4 * j) * 128
            lanes = pl.ds(pl.multiple_of(first, 128), WINDOW)
            queries = window_queries(qa, lanes, first, limit)
            upstream = dn[:, lanes]
            centre = cw[0:1, lanes]

            def keys(first_key, count, running):
                rows = pl.ds(pl.multiple_of(first_key, 128), count)
                weights = jnp.exp(mm(ka[rows, :], queries))
                d_scores = weights * (mm(vn[rows, :], upstream) - centre)
                rounded = d_scores.astype(bf16)
                dk[:, rows] += mm_nt(queries, rounded)
                dv[:, rows] += mm_nt(upstream, weights.astype(bf16))
                return running + mm(qkvt[64:128, rows], rounded)

            dq[:, lanes] = over_keys(start, length, keys, jnp.zeros((64, WINDOW), f32))
            return unused

        lax.fori_loop(0, (length + 3) // 4, window, 0)
        return start + length

    lax.fori_loop(0, NSEQ, sequence, 0)

    phases = labels[3:4, :] * freq[...]
    cos_part, sin_part = jnp.cos(phases), jnp.sin(phases)
    for part, source, factor in ((0, dq, 0.125), (1, dk, 1.0)):
        former, latter = source[0:32, lanes_all], source[32:64, lanes_all]
        dproj[part * 64 : part * 64 + 32, :] = (
            (former * cos_part + latter * sin_part) * factor
        ).astype(bf16)
        dproj[part * 64 + 32 : part * 64 + 64, :] = (
            (latter * cos_part - former * sin_part) * factor
        ).astype(bf16)
    dproj[128:192, :] = dv[...].astype(bf16)
    variate = labels[2:3, :]
    line = lax.broadcasted_iota(jnp.int32, (16, size), 0)
    match = jnp.logical_and(variate == line.astype(f32), line < 4)
    near = jnp.sum(jnp.where(match, dk[64:80, :], 0.0))
    every = jnp.sum(dk[77:78, :])
    lane = lax.broadcasted_iota(jnp.int32, (8, 128), 1)
    line8 = lax.broadcasted_iota(jnp.int32, (8, 128), 0)
    here = lane == head_of()
    bias_tile[...] = jnp.where(
        jnp.logical_and(here, line8 == 2),
        near,
        jnp.where(jnp.logical_and(here, line8 == 3), every - near, 0.0),
    )


def branch_body(
    low, wop, x, gains, cots,
    atp, hidden, s2, cotp_out,
    cotp, keep, atn, part, sz, rz, sa, ra, inbox, outbox, second, ss, rs,
):
    row, col, z, place = places()
    quarter = col % QUAD
    meet(plane_near(row, col) + column_all(row, col))
    rows, lanes = block(z // 2, 64), block(row, 512)
    for plane in range(PLANES):
        mine = jnp.logical_and(row == z % 2, z == plane)

        @pl.when(jnp.logical_not(mine))
        def _():
            push(
                low.at[:, plane * 512 : plane * 512 + 512], atp.at[rows, lanes],
                sz.at[plane], rz.at[row * 2 + z // 2], (z % 2, plane * QUAD + quarter),
            ).start()

        @pl.when(mine)
        def _():
            atp[rows, lanes] = low[:, plane * 512 : plane * 512 + 512]

    cot_in = Gather(cotp, sa, ra)
    cot_in.start(cots)
    cotp[place] = cots[...]
    for j in range(4):
        source = (j // 2, (row + 2 * (j % 2)) * QUAD + quarter)
        mine = jnp.logical_and(row == j // 2, z == row + 2 * (j % 2))

        @pl.when(jnp.logical_not(mine))
        def _():
            push(
                low.at[:, 0:512], atp.at[0:64, 0:512], sz.at[j], rz.at[j], source
            ).wait_recv()

    for plane in range(PLANES):
        mine = jnp.logical_and(row == z % 2, z == plane)

        @pl.when(jnp.logical_not(mine))
        def _():
            push(
                low.at[:, plane * 512 : plane * 512 + 512], atp.at[rows, lanes],
                sz.at[plane], rz.at[row * 2 + z // 2], (z % 2, plane * QUAD + quarter),
            ).wait_send()

    atn[...] = jnp.transpose(atp[...])
    total = Scatter(part, inbox, outbox, second, ss, rs)
    core = col % 2
    for bits in (3, 2, 1, 0):
        chip = flip(place // 2, bits)
        part[2 * chip + 1 - core] = mm(atn[block(2 * chip + 1 - core, 128), :], wop[...]).astype(bf16)
    for bits in range(4):
        total.near(flip(place // 2, bits), bits)
    for bits in (3, 2, 1, 0):
        chip = flip(place // 2, bits)
        part[2 * chip + core] = mm(atn[block(2 * chip + core, 128), :], wop[...]).astype(bf16)
    total.far_all()
    cot_in.finish()
    kept = fetch(cotp, cotp_out, keep.at[0])
    state = x[...].astype(f32) + total.finish()
    hidden[...] = state
    s2[...] = (state * norm_scale(state) * gains[1:2, :]).astype(bf16)
    total.close()
    cot_in.close()
    kept.wait()


def ffn_body(
    s2, cotp_in, wg_in, w_down, hidden, gains,
    out_keep, down_in, gwg_out, d_hidden, low, gain_term,
    cotp, wg, s2p, wgs, wd, actives, factors, inner_s, dgu, d_part, out_part, gwd, gwg, relayed, both_terms,
    keep, sa, ra, sw, rw, sd, rd, inbox, outbox, second, ss, rs,
):
    row, col, z, place = places()
    loads = [fetch(wg_in, wg, keep.at[0]), fetch(cotp_in, cotp, keep.at[1])]
    meet(plane_near(row, col) + line_all(row, col))
    rows_in = Gather(s2p, sa, ra)
    rows_in.start(s2)
    s2p[place] = s2[...]
    inner = jnp.logical_or(z == 1, z == 2)
    end = jnp.logical_not(inner)
    downs = {
        bits: push(
            w_down, wd.at[block(z, 128), :], sw.at[bits], rw.at[bits], on_line(row, col, bits)
        )
        for bits in (2, 1, 3)
    }
    passed = wd.at[block(flip(z, 2), 128), :]
    downs[0] = push(passed, passed, sw.at[0], rw.at[3], on_line(row, col, 1))
    downs[2].start()

    @pl.when(inner)
    def _():
        downs[3].start()

    downs[1].start()
    wd[block(z, 128), :] = w_down[...]
    loads[0].wait()
    for plane in range(PLANES):
        for r in range(2):
            at = (r * PLANES + plane) * 128
            wgs[at : at + 128, :] = wg[plane * 2 + r]
    for k in range(4):
        chip = flip(place // 2, k)
        if k:
            rows_in.forward(2 * k)
        rows_in.arrived(2 * k)
        if k == 1:
            downs[2].wait_recv()

            @pl.when(inner)
            def _():
                downs[0].start()

        rows = block(chip, 256)
        scaled = jnp.concatenate([s2p[2 * chip], s2p[2 * chip + 1]], axis=0)
        both = mm(scaled, wgs[...])
        gate, upper = both[:, 0:512], both[:, 512:1024]
        sig = jax.nn.sigmoid(gate)
        active = gate * sig
        inner_s[rows, :] = (active * upper).astype(bf16)
        actives[rows, :] = active
        factors[rows, :] = upper * sig * (1.0 + gate * (1.0 - sig))
    loads[1].wait()
    cot_all = jnp.concatenate([cotp[t] for t in range(MEMBERS)], axis=0)
    for k in range(4):
        cols = slice(k * 128, k * 128 + 128)
        gwd[k] = mm_tn(inner_s[:, cols], cot_all).astype(bf16)
    grads = {
        bits: push(
            gwd.at[flip(z, bits)], down_in.at[bits], sd.at[bits], rd.at[bits], on_line(row, col, bits)
        )
        for bits in (1, 3)
    }
    grads[2] = push(both_terms, down_in.at[2], sd.at[2], rd.at[2], on_line(row, col, 2))
    grads[0] = push(gwd.at[flip(z, 3)], relayed, sd.at[0], rd.at[0], on_line(row, col, 1))

    @pl.when(end)
    def _():
        grads[0].start()
        both_terms[...] = gwd[flip(z, 2)]
        grads[2].start()
        down_in[3] = jnp.zeros(down_in.shape[1:], bf16)

    @pl.when(inner)
    def _():
        grads[3].start()

    grads[1].start()
    down_in[0] = gwd[z]
    total = Scatter(d_part, inbox, outbox, second, ss, rs)
    downs[1].wait_recv()
    downs[3].wait_recv()
    for k in range(4):
        chip = flip(place // 2, k)
        rows = block(chip, 256)
        upstream = jnp.concatenate([cotp[2 * chip], cotp[2 * chip + 1]], axis=0)
        d_inner = mm_nt(upstream, wd[...])
        dgu[rows, 0:512] = (d_inner * factors[rows, :]).astype(bf16)
        dgu[rows, 512:1024] = (d_inner * actives[rows, :]).astype(bf16)
        tile = mm_nt(dgu[rows, :], wgs[...]).astype(bf16)
        d_part[2 * chip] = tile[0:128]
        d_part[2 * chip + 1] = tile[128:256]
        total.near(chip, k)
        if k > 1:
            total.far(k - 1)
        if k == 1:

            @pl.when(inner)
            def _():
                grads[0].wait_recv()
                both_terms[...] = (
                    gwd[flip(z, 2)].astype(f32) + relayed[...].astype(f32)
                ).astype(bf16)
                grads[2].start()

    for k in range(4):
        chip = flip(place // 2, k)
        tile = mm(inner_s[block(chip, 256), :], wd[...]).astype(bf16)
        out_part[2 * chip] = tile[0:128]
        out_part[2 * chip + 1] = tile[128:256]
        if k == 0:
            total.far(3)
    kept = [fetch(out_part, out_keep, keep.at[10])]
    for f in range(8):
        cols = slice(f * 128, f * 128 + 128)
        lhs = jnp.concatenate([s2p[t, :, cols] for t in range(MEMBERS)], axis=0)
        at = (f % PLANES) * 2 + f // PLANES
        gwg[at] = mm_tn(lhs, dgu[...]).astype(bf16)
        kept.append(fetch(gwg.at[at], gwg_out.at[at], keep.at[2 + f]))
    d_scaled = total.finish()
    state = hidden[...]
    scale = norm_scale(state)
    normed = state * scale
    gain_term[...] = jnp.broadcast_to(jnp.sum(d_scaled * normed, axis=0, keepdims=True), (8, 1024))
    d_state = cotp[place].astype(f32) + norm_back(d_scaled * gains[1:2, :], normed, scale)
    d_hidden[...] = d_state
    low[...] = d_state.astype(bf16)
    rows_in.close()
    total.close()
    grads[1].wait_recv()
    grads[2].wait_recv()
    for copy in (downs[1], downs[2], grads[1], grads[2]):
        copy.wait_send()

    @pl.when(inner)
    def _():
        grads[3].wait_recv()
        for copy in (downs[3], downs[0], grads[3]):
            copy.wait_send()

    @pl.when(end)
    def _():
        grads[0].wait_send()

    for copy in kept:
        copy.wait()


def attended_back_body(
    low, wop, atp,
    grad, gwo,
    dbp, dat, sg, rg, sz, rz,
):
    row, col, z, place = places()
    meet(plane_near(row, col) + column_all(row, col))
    quarter = col % QUAD
    rows_in = Gather(dbp, sg, rg)
    rows_in.start(low)
    dbp[place] = low[...]
    for k in range(4):
        chip = flip(place // 2, k)
        if k:
            rows_in.forward(2 * k)
        rows_in.arrived(2 * k)
        for core in range(2):
            dat[:, block(2 * chip + core, 128)] = mm_nt(wop[...], dbp[2 * chip + core]).astype(bf16)
        if k % 2 == 0:
            continue
        group = row if k == 1 else 1 - row
        for head in range(2):
            plane = row + 2 * head
            source = dat.at[head * 64 : head * 64 + 64, block(group, 512)]
            if k == 1:

                @pl.when(z != plane)
                def _():
                    push(
                        source, grad.at[:, block(z, 512)], sz.at[head], rz.at[z],
                        (group, plane * QUAD + quarter),
                    ).start()

                @pl.when(z == plane)
                def _():
                    grad[:, block(z, 512)] = source[...]

            else:
                push(
                    source, grad.at[:, block(z, 512)], sz.at[2 + head], rz.at[z],
                    (group, plane * QUAD + quarter),
                ).start()

    total = mm(atp[:, 0:128], dbp[0])
    for q in range(1, MEMBERS):
        total = total + mm(atp[:, q * 128 : q * 128 + 128], dbp[q])
    gwo[...] = total.astype(bf16)
    for plane in range(PLANES):
        mine = jnp.logical_and(row == z % 2, z == plane)

        @pl.when(jnp.logical_not(mine))
        def _():
            push(
                dat.at[0:64, 0:512], grad.at[:, plane * 512 : plane * 512 + 512], sz.at[0],
                rz.at[plane], (z % 2, plane * QUAD + quarter),
            ).wait_recv()

    for head in range(2):
        plane = row + 2 * head

        @pl.when(z != plane)
        def _():
            push(
                dat.at[0:64, 0:512], grad.at[:, 0:512], sz.at[head], rz.at[z],
                (row, plane * QUAD + quarter),
            ).wait_send()

        push(
            dat.at[0:64, 0:512], grad.at[:, 0:512], sz.at[2 + head], rz.at[z],
            (1 - row, plane * QUAD + quarter),
        ).wait_send()

    rows_in.close()


def last_body(
    dproj, wt_in, s1_in, xp_in, out_in, gains, d_hidden, hidden, gwo, gwg, gain_two, bias_tile, deal,
    grad_tokens, gqin, goin, gwg_in, sums, out,
    wt, s1, xp, out_part, pieces, slots, keep, dpt, dpn, part, gq, gqcol, gqout, gqsum, pack, packs, packed,
    passed, sz, rz, inbox, outbox, second, ss, rs, sp,
    sq, rq, sv, rv, st, rt, su, ru, sw, rw, sg, rg, sc, rc, passed2, sp2, inbox2, outbox2, second2, ss2, rs2,
):
    row, col, z, place = places()
    quarter = col % QUAD
    y, core = col // 2 % 2, col % 2
    member = z * 2 + core
    column = row * 2 + y
    loads = [
        fetch(out_in, out_part, keep.at[3]),
        fetch(s1_in, s1, keep.at[0]),
        fetch(xp_in, xp, keep.at[1]),
        fetch(wt_in, wt, keep.at[2]),
    ]
    meet([anyone(row, col, bits) for bits in range(1, 32)])
    copies = {}
    for bits in (3, 2, 1, 0):
        chip = flip(z, bits)
        ours = pl.ds(pl.multiple_of(chip * 512 + y * 256, 256), 256)
        theirs = pl.ds(pl.multiple_of(chip * 512 + (1 - y) * 256, 256), 256)
        copies[bits] = push(
            dproj.at[:, theirs], dpt.at[y, :, block(chip, 256)], sz.at[bits], rz.at[bits],
            (row, flip(col, 2)),
        )
        copies[bits].start()
        dpt[y, :, block(chip, 256)] = dproj[:, ours]
    owner = core * 4 + y * 2
    for j in range(4):
        there = (j // 2, row * 8 + owner + j % 2)
        mine = jnp.logical_and(row == there[0], col == there[1])

        @pl.when(jnp.logical_not(mine))
        def _():
            push(gwo.at[j], goin.at[z], sw.at[j], rw.at[z], there).start()

        @pl.when(mine)
        def _():
            goin[z] = gwo[j]

    loads[0].wait()
    output = RoundScatter(out_part, inbox2, outbox2, second2, ss2, rs2, passed2, sp2)
    output.near_all()
    output.far_first()
    spread = []
    for bits in range(1, 8):
        there = in_plane(row, col, bits)
        copy = push(gwg.at[flip(place, bits)], gwg_in.at[place], sg.at[bits], rg.at[bits], there)
        copy.start()
        spread.append(copy)
    gwg_in[place] = gwg[place]
    for copy in loads[1:]:
        copy.wait()
    total = LineScatter(part, inbox, outbox, second, ss, rs, passed, sp)
    term = jnp.zeros((1, 1024), f32)
    for bits in (3, 2, 1, 0):
        chip = flip(z, bits)
        lanes = block(chip, 256)
        copies[bits].wait_recv()
        for kind in range(3):
            both = jnp.concatenate(
                [dpt[head, kind * 64 : kind * 64 + 64, lanes] for head in range(2)], axis=0
            )
            dpn[lanes, kind * 128 : kind * 128 + 128] = jnp.transpose(both)
        d_scaled = mm(dpn[lanes, :], wt[...])
        values = jnp.concatenate([xp[2 * chip], xp[2 * chip + 1]], axis=0).astype(f32)
        term = term + jnp.sum(d_scaled * (values * norm_scale(values)), axis=0, keepdims=True)
        part[2 * chip] = d_scaled[0:128].astype(bf16)
        part[2 * chip + 1] = d_scaled[128:256].astype(bf16)
        total.near(chip, bits)
        if bits < 3:
            total.far(bits + 1)
    output.far_second()
    for f in range(8):
        if f == 4:
            total.far_second()
        lhs = jnp.concatenate([s1[t, :, f * 128 : f * 128 + 128] for t in range(MEMBERS)], axis=0)
        chunk = mm_tn(lhs, dpn[...]).astype(bf16)
        for j in range(4):
            gq[f // PLANES * 2 + j // 2, f % PLANES * 2 + j % 2] = chunk[j * 32 : j * 32 + 32, :]
    beside, across = (row, flip(col, 2)), (flip(row, 1), col)
    columns = [
        push(gq.at[flip(column, 3)], gqcol.at[1], sv.at[3], rv.at[3], across),
        push(gq.at[flip(column, 2)], gqcol.at[0], sv.at[2], rv.at[2], across),
    ]
    for copy in columns:
        copy.start()
    for k in range(8):
        pack[k] = bias_tile[...]
        pack[k, 0:1, :] = term[:, k * 128 : k * 128 + 128]
        pack[k, 1:2, :] = gain_two[0:1, k * 128 : k * 128 + 128]
    first = []
    for bits in range(1, 8):
        there = in_plane(row, col, bits)
        copy = push(
            pack.at[pl.ds(there[0] * PLANES, PLANES)], packs.at[place], st.at[bits], rt.at[bits], there
        )
        copy.start()
        first.append(copy)
    packs[place] = pack[pl.ds(row * PLANES, PLANES)]
    rows_out = (hidden[...] + output.finish()).astype(bf16)
    for j in range(16):
        pieces[j] = rows_out[j * 8 : j * 8 + 8, :]
    for d in range(16):
        number = 0
        for j in range(1, 16):
            number = jnp.where(deal[j] == d, j, number)
        slots[d] = pieces[number]
    for bits in range(1, 16):
        there = (row, flip(col, bits))
        copy = push(slots.at[there[1]], out.at[col], sc.at[bits], rc.at[bits], there)
        copy.start()
        spread.append(copy)
    out[col] = slots[col]
    columns[0].wait_recv()
    nearby = flip(column, 1)
    for m in range(MEMBERS):
        gqout[m] = (gq[nearby, m].astype(f32) + gqcol[1, m].astype(f32)).astype(bf16)
    columns.append(push(gqout, gqcol.at[2], sv.at[1], rv.at[1], beside))
    columns[2].start()
    for copy in first:
        copy.wait_recv()
    summed = packs[0]
    for p in range(1, MEMBERS):
        summed = summed + packs[p]
    packed[...] = summed
    for bits in (1, 2, 3):
        copy = push(
            packed.at[flip(z, bits)], sums.at[z], su.at[bits], ru.at[bits], on_line(row, col, bits)
        )
        copy.start()
        spread.append(copy)
    sums[z] = packed[z]
    for copy in columns[1:]:
        copy.wait_recv()
    for m in range(MEMBERS):
        gqsum[m] = (
            (gq[column, m].astype(f32) + gqcol[0, m].astype(f32)) + gqcol[2, m].astype(f32)
        ).astype(bf16)
    for bits in range(7, 0, -1):
        there = in_line(row, col, bits)
        copy = push(gqsum.at[flip(member, bits)], gqin.at[member], sq.at[bits], rq.at[bits], there)
        copy.start()
        spread.append(copy)
    gqin[member] = gqsum[member]
    d_one = total.finish()
    own_rows = xp[member].astype(f32)
    scale = norm_scale(own_rows)
    grad_tokens[...] = (
        d_hidden[...] + norm_back(d_one * gains[0:1, :], own_rows * scale, scale)
    ).astype(bf16)
    for copy in spread:
        copy.wait_recv()
    senders = col // 2 % 2 * 2 + col // 4 % 2
    for plane in range(PLANES):
        mine = jnp.logical_and(row * 16 + col == (col // 8) * 16 + plane * QUAD + senders, z == plane)

        @pl.when(jnp.logical_not(mine))
        def _():
            push(
                gwo.at[0], goin.at[plane], sw.at[0], rw.at[plane],
                (col // 8, plane * QUAD + senders),
            ).wait_recv()

    for j in range(4):
        there = (j // 2, row * 8 + owner + j % 2)
        mine = jnp.logical_and(row == there[0], col == there[1])

        @pl.when(jnp.logical_not(mine))
        def _():
            push(gwo.at[j], goin.at[z], sw.at[j], rw.at[z], there).wait_send()

    for copy in list(copies.values()) + columns + first + spread:
        copy.wait_send()
    total.close()
    output.close()


def finish_body(
    grad_tokens_in, gqin, goin, out_in, gwg, gwd, tiles,
    out, grad_tokens, grad_q, grad_o, grad_gu, grad_d, grad_gains, grad_bias,
):
    grad_tokens[...] = grad_tokens_in[...]
    out[...] = out_in[...]
    grad_o[...] = (goin[0].astype(f32) + goin[1].astype(f32)) + (
        goin[2].astype(f32) + goin[3].astype(f32)
    )
    grad_d[...] = (gwd[0].astype(f32) + gwd[1].astype(f32)) + (
        gwd[2].astype(f32) + gwd[3].astype(f32)
    )
    for p in range(MEMBERS):
        total = gqin[p].astype(f32)
        for kind in range(3):
            at = kind * 1024 + p * 128
            grad_q[:, at : at + 128] = total[:, kind * 128 : kind * 128 + 128]
        for half in range(2):
            for plane in range(PLANES):
                unit = (p // QUAD) * 16 + plane * QUAD + p % QUAD
                at = half * 512 + plane * 128
                start = half * 4096 + unit * 128
                grad_gu[:, start : start + 128] = gwg[p, :, at : at + 128].astype(f32)
    total = (tiles[0] + tiles[1]) + (tiles[2] + tiles[3])
    quarter = lax.axis_index("col") % QUAD
    chosen = jnp.zeros((2, 32), f32)
    for k in range(4):
        chosen = chosen + jnp.where(quarter == k, total[0:2, k * 32 : k * 32 + 32], 0.0)
    grad_gains[...] = chosen
    grad_bias[...] = total[2:4, 0:16]


def sds(shape, dtype):
    return jax.ShapeDtypeStruct(shape, dtype)


def dma(*shape):
    return pltpu.SemaphoreType.DMA(shape)


def kernel(body, name, specs, outs, scratch, number=None, cost=0, places_out=None):
    params = dict(vmem_limit_bytes=56 << 20)
    if number is not None:
        params.update(collective_id=number, has_side_effects=True)
    return pl.pallas_call(
        body,
        name=name,
        in_specs=specs,
        out_shape=outs,
        out_specs=places_out or [VM] * len(outs),
        scratch_shapes=scratch,
        compiler_params=pltpu.CompilerParams(**params),
        cost_estimate=pl.CostEstimate(flops=cost, bytes_accessed=cost // 300, transcendentals=0),
    )


def plane_shards(
    tokens, variate_ids, time_ids, lengths, deal, w_qkv, w_out, w_gate_up, w_down,
    gain_attn, gain_ffn, var_bias, cotangent,
):
    rows, width = tokens.shape
    lines = [[plane * QUAD + k for plane in range(PLANES)] for k in range(QUAD)]
    freq = jnp.asarray(np.exp(-math.log(10000.0) * np.arange(32) / 32).astype(np.float32)[:, None])
    target = deal[0, 0]

    xp, wt, wop, wgp, s1, qkvt, gains, labels, cot = kernel(
        enter_body,
        "enter",
        [VM] * 9 + [SM, SM, VM],
        [
            sds((8, rows, width), bf16),
            sds((384, 1024), bf16),
            sds((4, 32, 1024), bf16),
            sds((8, 32, 1024), bf16),
            sds((8, rows, width), bf16),
            sds((192, 2048), bf16),
            sds((8, 1024), f32),
            sds((8, 2048), f32),
            sds((rows, width), bf16),
        ],
        [
            pltpu.VMEM((16, 8, width), bf16),
            pltpu.VMEM((8, rows, width), bf16),
            pltpu.VMEM((8, rows, width), bf16),
            dma(4),
            pltpu.VMEM((8, 32, 384), bf16),
            pltpu.VMEM((8, 32, 384), bf16),
            pltpu.VMEM((4, 8, 32, 384), bf16),
            pltpu.VMEM((8, 32, 1024), bf16),
            pltpu.VMEM((8, 128), f32),
            pltpu.VMEM((4, 8, 128), f32),
            pltpu.VMEM((8, 4, 8, 128), f32),
            pltpu.VMEM((384, 1024), bf16),
            pltpu.VMEM((2, 192, 1024), bf16),
            pltpu.VMEM((32, 1024), f32),
            pltpu.VMEM((32, 1024), f32),
            pltpu.VMEM((8, 1024), f32),
        ]
        + [dma(8), dma(8), dma(8), dma(8), dma(4), dma(4), dma(4), dma(4), dma(8), dma(8)]
        + [dma(4), dma(4), dma(8), dma(8), dma(4), dma(4), dma(16), dma(16)],
        number=1,
        places_out=[ANY, ANY, VM, VM, ANY, VM, VM, VM, VM],
    )(
        tokens, w_qkv, w_out, w_gate_up, cotangent.reshape(16, 8, width), gain_attn[None],
        gain_ffn[None], variate_ids[None], time_ids[None], lengths, target, freq,
    )

    gate_up = lax.all_gather(
        wgp.reshape(256, 1024), "col", axis=0, tiled=True, axis_index_groups=lines
    )
    wop = wop.reshape(128, 1024)

    wide = 2048 + WINDOW
    att, den, low, qa, ka = kernel(
        attend_body,
        "attend",
        [SM, VM, VM],
        [
            sds((64, wide), f32),
            sds((8, wide), f32),
            sds((64, wide), bf16),
            sds((AUG, wide), bf16),
            sds((2048, AUG), bf16),
        ],
        [pltpu.VMEM((AUG, 2048), bf16), pltpu.SMEM((8,), jnp.int32)],
        cost=2 * 10**9,
    )(var_bias, qkvt, labels)

    atp, hidden, s2, cotp = kernel(
        branch_body,
        "branch",
        [VM] * 5,
        [
            sds((128, 1024), bf16),
            sds((rows, width), f32),
            sds((rows, width), bf16),
            sds((8, rows, width), bf16),
        ],
        [
            pltpu.VMEM((8, rows, width), bf16),
            dma(1),
            pltpu.VMEM((1024, 128), bf16),
            pltpu.VMEM((8, rows, width), bf16),
            dma(4), dma(4), dma(8), dma(8),
        ]
        + scatter_scratch(rows, width),
        number=2,
        places_out=[VM, VM, VM, ANY],
    )(low, wop, tokens, gains, cot)

    out_part, down_in, gwg, d_hidden, d_branch, gain_two = kernel(
        ffn_body,
        "ffn",
        [VM, ANY, ANY, VM, VM, VM],
        [
            sds((8, rows, width), bf16),
            sds((4, rows, width), bf16),
            sds((8, 128, 1024), bf16),
            sds((rows, width), f32),
            sds((rows, width), bf16),
            sds((8, 1024), f32),
        ],
        [
            pltpu.VMEM((8, rows, width), bf16),
            pltpu.VMEM((8, 128, 1024), bf16),
            pltpu.VMEM((8, rows, width), bf16),
            pltpu.VMEM((1024, 1024), bf16),
            pltpu.VMEM((512, width), bf16),
            pltpu.VMEM((1024, 512), f32),
            pltpu.VMEM((1024, 512), f32),
            pltpu.VMEM((1024, 512), bf16),
            pltpu.VMEM((1024, 1024), bf16),
            pltpu.VMEM((8, rows, width), bf16),
            pltpu.VMEM((8, rows, width), bf16),
            pltpu.VMEM((4, rows, width), bf16),
            pltpu.VMEM((8, 128, 1024), bf16),
            pltpu.VMEM((rows, width), bf16),
            pltpu.VMEM((rows, width), bf16),
            dma(11), dma(8), dma(8), dma(4), dma(4), dma(4), dma(4),
        ]
        + scatter_scratch(rows, width),
        number=3,
        cost=10**10,
        places_out=[ANY, VM, ANY, VM, VM, VM],
    )(s2, cotp, gate_up.reshape(8, 128, 1024), w_down, hidden, gains)

    gate_up_sum = lax.psum_scatter(
        gwg.reshape(1024, 1024), "col", scatter_dimension=0, tiled=True, axis_index_groups=lines
    )

    grad, gwo = kernel(
        attended_back_body,
        "attended_back",
        [VM] * 3,
        [sds((64, 2048), bf16), sds((128, 1024), bf16)],
        [
            pltpu.VMEM((8, rows, width), bf16),
            pltpu.VMEM((128, 1024), bf16),
            dma(8), dma(8), dma(4), dma(4),
        ],
        number=4,
    )(d_branch, wop, atp)

    dproj, bias_tile = kernel(
        attend_back_body,
        "attend_back",
        [VM] * 8,
        [sds((192, 2048), bf16), sds((8, 128), f32)],
        [
            pltpu.VMEM((64, wide), bf16),
            pltpu.VMEM((8, wide), f32),
            pltpu.VMEM((2048, 64), bf16),
            pltpu.VMEM((64, wide), f32),
            pltpu.VMEM((AUG, 2048), f32),
            pltpu.VMEM((64, 2048), f32),
            pltpu.SMEM((8,), jnp.int32),
        ],
        cost=5 * 10**9,
    )(qkvt, qa, ka, labels, freq, grad, att, den)

    grad_tokens, gqin, goin, gwg_in, sums, out = kernel(
        last_body,
        "last",
        [VM] + [ANY] * 4 + [VM] * 7 + [SM],
        [
            sds((rows, width), bf16),
            sds((8, 32, 384), bf16),
            sds((4, 32, 1024), bf16),
            sds((8, 32, 1024), bf16),
            sds((4, 8, 128), f32),
            sds((16, 8, width), bf16),
        ],
        [
            pltpu.VMEM((384, 1024), bf16),
            pltpu.VMEM((8, rows, width), bf16),
            pltpu.VMEM((8, rows, width), bf16),
            pltpu.VMEM((8, rows, width), bf16),
            pltpu.VMEM((16, 8, width), bf16),
            pltpu.VMEM((16, 8, width), bf16),
            dma(4),
            pltpu.VMEM((2, 192, 1024), bf16),
            pltpu.VMEM((1024, 384), bf16),
            pltpu.VMEM((8, rows, width), bf16),
            pltpu.VMEM((4, 8, 32, 384), bf16),
            pltpu.VMEM((3, 8, 32, 384), bf16),
            pltpu.VMEM((8, 32, 384), bf16),
            pltpu.VMEM((8, 32, 384), bf16),
            pltpu.VMEM((8, 8, 128), f32),
            pltpu.VMEM((8, 4, 8, 128), f32),
            pltpu.VMEM((4, 8, 128), f32),
            pltpu.VMEM((rows, width), bf16),
            dma(4), dma(4),
        ]
        + scatter_scratch(rows, width)
        + [dma(2), dma(8), dma(8), dma(4), dma(4), dma(8), dma(8), dma(4), dma(4)]
        + [dma(4), dma(4), dma(8), dma(8), dma(16), dma(16)]
        + [pltpu.VMEM((rows, width), bf16), dma(2)]
        + scatter_scratch(rows, width),
        number=5,
    )(
        dproj, wt, s1, xp, out_part, gains, d_hidden, hidden, gwo.reshape(4, 32, 1024),
        gate_up_sum.reshape(8, 32, 1024), gain_two, bias_tile, target,
    )
    out, grad_tokens, grad_q, grad_o, grad_gate_up, grad_down, gain_grads, bias_grads = kernel(
        finish_body,
        "finish",
        [VM] * 7,
        [
            sds((rows, width), bf16),
            sds((rows, width), bf16),
            sds((32, 3072), f32),
            sds((32, 1024), f32),
            sds((32, 8192), f32),
            sds((rows, width), f32),
            sds((2, 32), f32),
            sds((2, 16), f32),
        ],
        [],
    )(
        grad_tokens, gqin, goin, out.reshape(rows, width), gwg_in,
        down_in, sums,
    )
    return (
        out,
        grad_tokens,
        grad_q,
        grad_o,
        grad_gate_up,
        grad_down,
        gain_grads[0],
        gain_grads[1],
        bias_grads,
    )


def solution(mesh):
    planes = mesh.shape["row"] == 2 and mesh.shape["col"] == PLANES * QUAD
    return jax.shard_map(
        plane_shards if planes else shards,
        mesh=mesh,
        in_specs=(
            P(("row", "col"), None),
            P(("row", "col")),
            P(("row", "col")),
            P("row", None),
            P("row", "col", None),
            P(("row", "col"), None),
            P(("row", "col"), None),
            P(("row", "col"), None),
            P(("row", "col"), None),
            P(("row", "col")),
            P(("row", "col")),
            P(),
            P(("row", "col"), None),
        ),
        out_specs=(
            P(("row", "col"), None),
            P(("row", "col"), None),
            P(("row", "col"), None),
            P(("row", "col"), None),
            P(("row", "col"), None),
            P(("row", "col"), None),
            P(("row", "col")),
            P(("row", "col")),
            P(),
        ),
        check_vma=False,
    )
```

```python
import math

import jax
import jax.numpy as jnp
import numpy as np
from jax import lax
from jax.experimental import pallas as pl
from jax.experimental.pallas import tpu as pltpu
from jax.sharding import PartitionSpec as P

HEAD_DIM = 64
UNIT = 128
KEY_BLOCK = 1024
NSEQ = 6


epsilon = 1e-05


def contract_rows(operand, factor):
    return lax.dot_general(
        operand, factor, (((0,), (0,)), ((), ())), preferred_element_type=jnp.float32
    )


def contract_cols(operand, factor):
    return lax.dot_general(
        operand, factor, (((1,), (1,)), ((), ())), preferred_element_type=jnp.float32
    )


def angles(time_ids):
    half_dim = HEAD_DIM // 2
    inverse_freq = jnp.exp(-math.log(10000.0) * jnp.arange(half_dim, dtype=jnp.float32) / half_dim)
    phases = time_ids.astype(jnp.float32)[:, None] * inverse_freq[None, :]
    return (jnp.cos(phases)[:, None, :], jnp.sin(phases)[:, None, :])


def rotate(tensor, cos_part, sin_part):
    half_dim = tensor.shape[-1] // 2
    former = tensor[..., :half_dim]
    latter = tensor[..., half_dim:]
    return jnp.concatenate(
        [former * cos_part - latter * sin_part, latter * cos_part + former * sin_part], axis=-1
    )


def unrotate(tensor, cos_part, sin_part):
    half_dim = tensor.shape[-1] // 2
    former = tensor[..., :half_dim]
    latter = tensor[..., half_dim:]
    return jnp.concatenate(
        [former * cos_part + latter * sin_part, latter * cos_part - former * sin_part], axis=-1
    )


def norm_scale(values):
    return lax.rsqrt(jnp.mean(values * values, axis=-1, keepdims=True) + epsilon)


def norm_back(d_normed, normed, scale):
    return scale * (d_normed - normed * jnp.mean(d_normed * normed, axis=-1, keepdims=True))


def score_weights(queries, query_seq, query_var, key_block, seq_block, var_block, var_bias):
    scores = (
        jnp.einsum("qhd,khd->hqk", queries, key_block, preferred_element_type=jnp.float32) * 0.125
    )
    matched = query_var[:, None] == var_block[None, :]
    scores = scores + jnp.where(
        matched[None], var_bias[0][:, None, None], var_bias[1][:, None, None]
    )
    within = query_seq[:, None] == seq_block[None, :]
    return (jnp.where(within[None], jnp.exp(scores), 0.0), matched)


def shards(
    tokens,
    variate_ids,
    time_ids,
    lengths,
    deal,
    w_qkv,
    w_out,
    w_gate_up,
    w_down,
    gain_attn,
    gain_ffn,
    var_bias,
    cotangent,
):
    tok_rows, model_width = tokens.shape
    n_col = lax.axis_size("col")
    col_index = lax.axis_index("col")
    piece_len = tok_rows // n_col
    head_count = model_width // HEAD_DIM
    bounds = jnp.cumsum(lengths[0]) * UNIT
    position = col_index * tok_rows + jnp.arange(tok_rows, dtype=jnp.int32)
    seq_own = jnp.sum((position[:, None] >= bounds[None, :]).astype(jnp.int32), axis=1)
    target = deal[0, 0]
    slots = jnp.arange(n_col, dtype=jnp.int32)
    inverse = jnp.sum(
        slots[:, None] * (target[:, None] == slots[None, :]).astype(jnp.int32), axis=0
    )
    send_rows = jnp.take(tokens.reshape(n_col, piece_len, model_width), inverse, axis=0)
    labels = jnp.stack(
        [
            seq_own.reshape(n_col, piece_len),
            variate_ids.reshape(n_col, piece_len),
            time_ids.reshape(n_col, piece_len),
        ],
        axis=1,
    )
    send_labels = jnp.take(labels, inverse, axis=0)
    got_rows, got_labels = (
        lax.all_to_all(send_rows, "col", split_axis=0, concat_axis=0, tiled=True),
        lax.all_to_all(send_labels, "col", split_axis=0, concat_axis=0, tiled=True),
    )
    inputs = got_rows.reshape(tok_rows, model_width).astype(jnp.float32)
    seq_q = got_labels[:, 0, :].reshape(tok_rows)
    var_q = got_labels[:, 1, :].reshape(tok_rows)
    cos_part, sin_part = angles(got_labels[:, 2, :].reshape(tok_rows))
    qkv_full, out_full, gate_up_full, down_full, gain_one, gain_two = (
        lax.all_gather(w_qkv, ("row", "col"), axis=0, tiled=True),
        lax.all_gather(w_out, ("row", "col"), axis=0, tiled=True),
        lax.all_gather(w_gate_up, ("row", "col"), axis=0, tiled=True),
        lax.all_gather(w_down, ("row", "col"), axis=0, tiled=True),
        lax.all_gather(gain_attn, ("row", "col"), axis=0, tiled=True),
        lax.all_gather(gain_ffn, ("row", "col"), axis=0, tiled=True),
    )
    scale_one = norm_scale(inputs)
    normed_one = inputs * scale_one
    scaled_one = (normed_one * gain_one.astype(jnp.float32)).astype(jnp.bfloat16)
    projected = jnp.dot(scaled_one, qkv_full, preferred_element_type=jnp.float32)
    shaped = projected.reshape(tok_rows, 3, head_count, HEAD_DIM)
    queries = rotate(shaped[:, 0], cos_part, sin_part).astype(jnp.bfloat16)
    key_own = (
        rotate(shaped[:, 1], cos_part, sin_part).astype(jnp.bfloat16).reshape(tok_rows, model_width)
    )
    value_own = projected[:, 2 * model_width :].astype(jnp.bfloat16)
    keys_all, values_all, seq_k, var_k = (
        lax.all_gather(key_own, "col", axis=0, tiled=True),
        lax.all_gather(value_own, "col", axis=0, tiled=True),
        lax.all_gather(seq_q, "col", axis=0, tiled=True),
        lax.all_gather(var_q, "col", axis=0, tiled=True),
    )
    group_size = keys_all.shape[0]
    stride = min(KEY_BLOCK, group_size)
    block_count = group_size // stride

    def split_blocks(key_rows, value_rows, key_seq, key_var):
        return (
            key_rows.reshape(block_count, stride, head_count, HEAD_DIM),
            value_rows.reshape(block_count, stride, head_count, HEAD_DIM),
            key_seq.reshape(block_count, stride),
            key_var.reshape(block_count, stride),
        )

    def forward_step(running, block_data):
        denominator, numerator = running
        key_block, value_block, seq_block, var_block = block_data
        weights = score_weights(queries, seq_q, var_q, key_block, seq_block, var_block, var_bias)[0]
        denominator = denominator + jnp.sum(weights, axis=-1)
        numerator = numerator + jnp.einsum(
            "hqk,khd->qhd",
            weights.astype(jnp.bfloat16),
            value_block,
            preferred_element_type=jnp.float32,
        )
        return ((denominator, numerator), None)

    (denominator, numerator), unused = lax.scan(
        forward_step,
        (
            jnp.zeros((head_count, tok_rows), jnp.float32),
            jnp.zeros((tok_rows, head_count, HEAD_DIM), jnp.float32),
        ),
        split_blocks(keys_all, values_all, seq_k, var_k),
    )
    attended = numerator / denominator.T[:, :, None]
    attn_low = attended.reshape(tok_rows, model_width).astype(jnp.bfloat16)
    hidden_state = inputs + jnp.dot(attn_low, out_full, preferred_element_type=jnp.float32)
    scale_two = norm_scale(hidden_state)
    normed_two = hidden_state * scale_two
    scaled_two = (normed_two * gain_two.astype(jnp.float32)).astype(jnp.bfloat16)
    gate_up = jnp.dot(scaled_two, gate_up_full, preferred_element_type=jnp.float32)
    hidden_units = gate_up_full.shape[1] // 2
    gate_part = gate_up[:, :hidden_units]
    upper_part = gate_up[:, hidden_units:]
    sigmoid_gate = jax.nn.sigmoid(gate_part)
    active = gate_part * sigmoid_gate
    inner_act = (active * upper_part).astype(jnp.bfloat16)
    ffn_branch = jnp.dot(inner_act, down_full, preferred_element_type=jnp.float32)
    output = (hidden_state + ffn_branch).astype(jnp.bfloat16)
    qkv_back, out_back, gate_up_back, down_back, gain_one_back, gain_two_back = (
        lax.all_gather(w_qkv, ("row", "col"), axis=0, tiled=True),
        lax.all_gather(w_out, ("row", "col"), axis=0, tiled=True),
        lax.all_gather(w_gate_up, ("row", "col"), axis=0, tiled=True),
        lax.all_gather(w_down, ("row", "col"), axis=0, tiled=True),
        lax.all_gather(gain_attn, ("row", "col"), axis=0, tiled=True),
        lax.all_gather(gain_ffn, ("row", "col"), axis=0, tiled=True),
    )
    d_inner = contract_cols(cotangent, down_back)
    d_gate = (
        d_inner * upper_part * sigmoid_gate * (1.0 + gate_part * (1.0 - sigmoid_gate))
    ).astype(jnp.bfloat16)
    d_upper = (d_inner * active).astype(jnp.bfloat16)
    d_gate_up = jnp.concatenate([d_gate, d_upper], axis=1)
    d_scaled_two = contract_cols(d_gate_up, gate_up_back)
    term_gain_two = jnp.sum(d_scaled_two * normed_two, axis=0)
    term_gate_up = contract_rows(scaled_two, d_gate_up)
    term_down = contract_rows(inner_act, cotangent)
    d_hidden = cotangent.astype(jnp.float32) + norm_back(
        d_scaled_two * gain_two_back.astype(jnp.float32), normed_two, scale_two
    )
    d_branch = d_hidden.astype(jnp.bfloat16)
    term_out = contract_rows(attn_low, d_branch)
    d_attended = contract_cols(d_branch, out_back).reshape(tok_rows, head_count, HEAD_DIM)
    d_numerator = (d_attended / denominator.T[:, :, None]).astype(jnp.bfloat16)
    centre = (jnp.sum(d_attended * attended, axis=-1) / denominator.T).T
    back_keys = (
        lax.all_gather(key_own, "col", axis=0, tiled=True),
        lax.all_gather(value_own, "col", axis=0, tiled=True),
        lax.all_gather(seq_q, "col", axis=0, tiled=True),
        lax.all_gather(var_q, "col", axis=0, tiled=True),
    )

    def query_step(running, block_data):
        d_queries, same_sum, other_sum = running
        key_block, value_block, seq_block, var_block = block_data
        weights, matched = score_weights(
            queries, seq_q, var_q, key_block, seq_block, var_block, var_bias
        )
        d_probs = jnp.einsum(
            "qhd,khd->hqk", d_numerator, value_block, preferred_element_type=jnp.float32
        )
        d_scores = weights * (d_probs - centre[:, :, None])
        same_sum = same_sum + jnp.sum(jnp.where(matched[None], d_scores, 0.0), axis=(1, 2))
        other_sum = other_sum + jnp.sum(jnp.where(matched[None], 0.0, d_scores), axis=(1, 2))
        d_rounded = d_scores.astype(jnp.bfloat16)
        d_queries = d_queries + jnp.einsum(
            "hqk,khd->qhd", d_rounded, key_block, preferred_element_type=jnp.float32
        )
        return ((d_queries, same_sum, other_sum), (d_rounded, weights.astype(jnp.bfloat16)))

    def query_and_key_step(running, block_data):
        running, rounded = query_step(running, block_data)
        d_rounded, weights_low = rounded
        d_keys = (
            jnp.einsum("hqk,qhd->khd", d_rounded, queries, preferred_element_type=jnp.float32)
            * 0.125
        )
        d_values = jnp.einsum(
            "hqk,qhd->khd", weights_low, d_numerator, preferred_element_type=jnp.float32
        )
        return (running, (d_keys, d_values))

    start_running = (
        jnp.zeros((tok_rows, head_count, HEAD_DIM), jnp.float32),
        jnp.zeros((head_count,), jnp.float32),
        jnp.zeros((head_count,), jnp.float32),
    )
    (d_queries, same_sum, other_sum), (d_keys, d_values) = lax.scan(
        query_and_key_step,
        start_running,
        split_blocks(back_keys[0], back_keys[1], back_keys[2], back_keys[3]),
    )
    key_grad, value_grad = (
        lax.psum_scatter(
            d_keys.reshape(group_size, model_width).astype(jnp.bfloat16),
            "col",
            scatter_dimension=0,
            tiled=True,
        ).astype(jnp.float32),
        lax.psum_scatter(
            d_values.reshape(group_size, model_width).astype(jnp.bfloat16),
            "col",
            scatter_dimension=0,
            tiled=True,
        ).astype(jnp.float32),
    )
    d_query_pre = unrotate(d_queries * 0.125, cos_part, sin_part).reshape(tok_rows, model_width)
    d_key_pre = unrotate(
        key_grad.reshape(tok_rows, head_count, HEAD_DIM), cos_part, sin_part
    ).reshape(tok_rows, model_width)
    d_projected = jnp.concatenate([d_query_pre, d_key_pre, value_grad], axis=1).astype(jnp.bfloat16)
    d_scaled_one = contract_cols(d_projected, qkv_back)
    term_qkv = contract_rows(scaled_one, d_projected)
    term_gain_one = jnp.sum(d_scaled_one * normed_one, axis=0)
    grad_w_qkv, grad_w_out, grad_w_gate_up, grad_w_down, grad_gain_attn, grad_gain_ffn = (
        lax.psum_scatter(term_qkv, ("row", "col"), scatter_dimension=0, tiled=True),
        lax.psum_scatter(term_out, ("row", "col"), scatter_dimension=0, tiled=True),
        lax.psum_scatter(term_gate_up, ("row", "col"), scatter_dimension=0, tiled=True),
        lax.psum_scatter(term_down, ("row", "col"), scatter_dimension=0, tiled=True),
        lax.psum_scatter(term_gain_one, ("row", "col"), scatter_dimension=0, tiled=True),
        lax.psum_scatter(term_gain_two, ("row", "col"), scatter_dimension=0, tiled=True),
    )
    grad_var_bias = lax.psum(jnp.stack([same_sum, other_sum], axis=0), ("row", "col"))
    d_inputs = d_hidden + norm_back(
        d_scaled_one * gain_one_back.astype(jnp.float32), normed_one, scale_one
    )
    returned = lax.all_to_all(
        d_inputs.astype(jnp.bfloat16).reshape(n_col, piece_len, model_width),
        "col",
        split_axis=0,
        concat_axis=0,
        tiled=True,
    )
    grad_tokens = jnp.take(returned, target, axis=0).reshape(tok_rows, model_width)
    return (
        output,
        grad_tokens,
        grad_w_qkv,
        grad_w_out,
        grad_w_gate_up,
        grad_w_down,
        grad_gain_attn,
        grad_gain_ffn,
        grad_var_bias,
    )


PLANES = 4
QUAD = 4
MEMBERS = 8
WINDOW = 512
AUG = 128
f32 = jnp.float32
bf16 = jnp.bfloat16
VM = pl.BlockSpec(memory_space=pltpu.VMEM)
SM = pl.BlockSpec(memory_space=pltpu.SMEM)
ANY = pl.BlockSpec(memory_space=pl.ANY)


def mm(a, b):
    return lax.dot_general(a, b, (((1,), (0,)), ((), ())), preferred_element_type=f32)


def mm_nt(a, b):
    return lax.dot_general(a, b, (((1,), (1,)), ((), ())), preferred_element_type=f32)


def mm_tn(a, b):
    return lax.dot_general(a, b, (((0,), (0,)), ((), ())), preferred_element_type=f32)


def flip(value, bits):
    for bit in (1, 2, 4, 8, 16):
        if bits & bit:
            value = value + bit * (1 - 2 * ((value // bit) % 2))
    return value


def places():
    row = lax.axis_index("row")
    col = lax.axis_index("col")
    return row, col, col // QUAD, row * QUAD + col % QUAD


def in_plane(row, col, bits):
    return flip(row, bits // QUAD), flip(col, bits % QUAD)


def in_line(row, col, bits):
    return row, flip(col, bits // 2 * QUAD + bits % 2)


def on_line(row, col, bits):
    return row, flip(col, bits * QUAD)


def anyone(row, col, bits):
    return flip(row, bits // 16), flip(col, bits % 16)


def push(source, target, send, recv, device):
    return pltpu.make_async_remote_copy(
        src_ref=source,
        dst_ref=target,
        send_sem=send,
        recv_sem=recv,
        device_id={"row": device[0], "col": device[1]},
        device_id_type=pl.DeviceIdType.MESH,
    )


def greet(devices):
    barrier = pltpu.get_barrier_semaphore()
    for device in devices:
        pl.semaphore_signal(
            barrier,
            1,
            device_id={"row": device[0], "col": device[1]},
            device_id_type=pl.DeviceIdType.MESH,
        )
    return len(devices)


def wait_for(number):
    pl.semaphore_wait(pltpu.get_barrier_semaphore(), number)


NEAR = (2, 4, 6, 1)


def plane_near(row, col):
    return [in_plane(row, col, bits) for bits in NEAR]


def line_all(row, col):
    return [on_line(row, col, bits) for bits in (1, 2, 3)]


def column_all(row, col):
    return [
        (flip(row, bits // 4), flip(col, bits % 4 * QUAD)) for bits in (1, 2, 3, 5, 6, 7)
    ]


class Gather:
    def __init__(self, target, send, recv, peer=in_plane, place=None):
        self.target, self.send, self.recv, self.peer = target, send, recv, peer
        self.row, self.col, _, self.place = places()
        if place is not None:
            self.place = place
        self.copies, self.onward = {}, {}

    def start(self, source):
        for bits in NEAR:
            self.copies[bits] = push(
                source,
                self.target.at[self.place],
                self.send.at[bits],
                self.recv.at[bits],
                self.peer(self.row, self.col, bits),
            )
            self.copies[bits].start()

    def forward(self, bits):
        self.copies[bits].wait_recv()
        slot = self.target.at[flip(self.place, bits)]
        self.onward[bits] = push(
            slot,
            slot,
            self.send.at[bits + 1],
            self.recv.at[bits + 1],
            self.peer(self.row, self.col, 1),
        )
        self.onward[bits].start()

    def arrived(self, bits):
        (self.onward[bits] if bits else self.copies[1]).wait_recv()

    def close(self):
        for copy in list(self.copies.values()) + list(self.onward.values()):
            copy.wait_send()

    def finish(self):
        for bits in (2, 4, 6):
            self.forward(bits)
        for bits in (0, 2, 4, 6):
            self.arrived(bits)


class LineGather(Gather):
    def __init__(self, target, send, recv):
        row, col, z, _ = places()
        super().__init__(target, send, recv, in_line, z * 2 + col % 2)
        self.inner = jnp.logical_or(z == 1, z == 2)

    def start(self, source):
        for bits in (4, 2, 6, 1):
            self.copies[bits] = push(
                source,
                self.target.at[self.place],
                self.send.at[bits],
                self.recv.at[bits],
                in_line(self.row, self.col, bits),
            )
            if bits != 6:
                self.copies[bits].start()
        slot = self.target.at[flip(self.place, 4)]
        self.passing = push(
            slot, slot, self.send.at[0], self.recv.at[6], in_line(self.row, self.col, 2)
        )

        @pl.when(self.inner)
        def _():
            self.copies[6].start()

    def forward(self, bits):
        super().forward(bits)
        if bits == 4:

            @pl.when(self.inner)
            def _():
                self.passing.start()

    def close(self):
        for bits in (4, 2, 1):
            self.copies[bits].wait_send()
        for copy in self.onward.values():
            copy.wait_send()

        @pl.when(self.inner)
        def _():
            self.copies[6].wait_send()
            self.passing.wait_send()


class Scatter:
    def __init__(self, part, inbox, outbox, second, send, recv, peer=in_plane, place=None):
        self.part, self.inbox, self.outbox, self.second = part, inbox, outbox, second
        self.send, self.recv, self.peer = send, recv, peer
        self.row, self.col, _, self.place = places()
        if place is not None:
            self.place = place
        self.core = self.col % 2
        self.copies, self.sent = {}, []

    def near(self, chip, number):
        copy = push(
            self.part.at[2 * chip + 1 - self.core],
            self.inbox.at[number],
            self.send.at[number],
            self.recv.at[number],
            self.peer(self.row, self.col, 1),
        )
        copy.start()
        self.copies[number] = copy

    def far(self, bits):
        self.copies[bits].wait_recv()
        chip = flip(self.place // 2, bits)
        total = self.part[2 * chip + self.core].astype(f32) + self.inbox[bits].astype(f32)
        self.outbox[bits - 1] = total.astype(bf16)
        copy = push(
            self.outbox.at[bits - 1],
            self.second.at[bits - 1],
            self.send.at[3 + bits],
            self.recv.at[3 + bits],
            self.peer(self.row, self.col, 2 * bits),
        )
        copy.start()
        self.sent.append(copy)

    def near_all(self):
        for bits in range(4):
            self.near(flip(self.place // 2, bits), bits)

    def far_all(self):
        for bits in (3, 2, 1):
            self.far(bits)

    def finish(self):
        self.copies[0].wait_recv()
        total = self.part[self.place].astype(f32) + self.inbox[0].astype(f32)
        for copy in self.sent:
            copy.wait_recv()
        for i in range(3):
            total = total + self.second[i].astype(f32)
        return total

    def close(self):
        for copy in list(self.copies.values()) + self.sent:
            copy.wait_send()


class LineScatter(Scatter):
    def __init__(self, part, inbox, outbox, second, send, recv, passed, sems):
        row, col, z, _ = places()
        super().__init__(part, inbox, outbox, second, send, recv, in_line, z * 2 + col % 2)
        self.passed, self.sems = passed, sems
        self.inner = jnp.logical_or(z == 1, z == 2)
        self.end = jnp.logical_not(self.inner)

    def sum_for(self, bits):
        self.copies[bits].wait_recv()
        chip = flip(self.place // 2, bits)
        return self.part[2 * chip + self.core].astype(f32) + self.inbox[bits].astype(f32)

    def sum_again(self, bits):
        chip = flip(self.place // 2, bits)
        return self.part[2 * chip + self.core].astype(f32) + self.inbox[bits].astype(f32)

    def to(self, bits):
        return push(
            self.outbox.at[bits - 1],
            self.second.at[bits - 1],
            self.send.at[3 + bits],
            self.recv.at[3 + bits],
            in_line(self.row, self.col, 2 * bits),
        )

    def far(self, bits):
        self.outbox[bits - 1] = self.sum_for(bits).astype(bf16)
        if bits == 1:
            self.sent.append(self.to(1))
            self.sent[-1].start()
        if bits == 2:
            self.added = self.to(2)
            self.sent.append(self.added)

            @pl.when(self.end)
            def _():
                self.added.start()

        if bits == 3:
            self.across = self.to(3)
            self.passing = push(
                self.outbox.at[2],
                self.passed,
                self.sems.at[0],
                self.sems.at[1],
                in_line(self.row, self.col, 2),
            )

            @pl.when(self.end)
            def _():
                self.passing.start()
                self.second[2] = jnp.zeros(self.second.shape[1:], bf16)

            @pl.when(self.inner)
            def _():
                self.across.start()

    def far_second(self):
        @pl.when(self.inner)
        def _():
            self.passing.wait_recv()
            total = self.sum_again(2) + self.passed[...].astype(f32)
            self.outbox[1] = total.astype(bf16)
            self.added.start()

    def finish(self):
        @pl.when(self.inner)
        def _():
            self.across.wait_recv()

        return super().finish()

    def close(self):
        super().close()

        @pl.when(self.inner)
        def _():
            self.across.wait_send()

        @pl.when(self.end)
        def _():
            self.passing.wait_send()


def scatter_scratch(rows, width):
    return [
        pltpu.VMEM((4, rows, width), bf16),
        pltpu.VMEM((3, rows, width), bf16),
        pltpu.VMEM((3, rows, width), bf16),
        pltpu.SemaphoreType.DMA((7,)),
        pltpu.SemaphoreType.DMA((7,)),
    ]


def fetch(source, target, semaphore):
    copy = pltpu.make_async_copy(source, target, semaphore)
    copy.start()
    return copy


def block(number, size):
    return pl.ds(pl.multiple_of(number * size, size), size)


def enter_body(
    x, wq, wo, wg, cot, ga, gf, variate, time, lengths, deal, freq,
    xp_out, wt_out, wop, wgp, s1_out, qkvt, gains, labels, cots,
    cotr, xp, s1, keep, wqs, wline, wqp, wgs, tile, tl, tiles, wt, box, cs, sn, times,
    sx, rx, sq, rq, sv, rv, st, rt, su, ru, sw, rw, sg, rg, sz, rz, sc, rc,
):
    row, col, z, place = places()
    quarter = col % QUAD
    y, core = col // 2 % 2, col % 2
    member = z * 2 + core
    present = greet([anyone(row, col, bits) for bits in range(1, 32)])
    lane = lax.broadcasted_iota(jnp.int32, (1, 128), 1)
    for line, gain in ((0, ga), (1, gf)):
        wide = gain[...].astype(f32)
        wide = jnp.concatenate([wide] * 4, axis=1)
        tile[line : line + 1, :] = jnp.where(lane // 32 == quarter, wide, 0.0)
    tile[2:3, :] = variate[...].astype(f32)
    tile[3:4, :] = time[...].astype(f32)
    numbers = jnp.zeros((1, 128), jnp.int32)
    for i in range(NSEQ):
        numbers = jnp.where(lane == i, lengths[0, i], numbers)
    tile[4:5, :] = numbers.astype(f32)
    tile[5:8, :] = jnp.zeros((3, 128), f32)
    for p in range(MEMBERS):
        for part in range(3):
            at = part * 1024 + p * 128
            wqs[p, :, part * 128 : part * 128 + 128] = wq[:, at : at + 128]
    for p in range(MEMBERS):
        for half in range(2):
            for plane in range(PLANES):
                unit = (p // QUAD) * 16 + plane * QUAD + p % QUAD
                at = half * 512 + plane * 128
                start = half * 4096 + unit * 128
                wgs[p, :, at : at + 128] = wg[:, start : start + 128]
    xp[member] = x[...]
    wline[member] = wqs[member]
    tl[z] = tile[...]
    wait_for(present)
    first = []
    for bits in range(1, 8):
        there = in_line(row, col, bits)
        first.append(push(wqs.at[flip(member, bits)], wline.at[member], sq.at[bits], rq.at[bits], there))
        first[-1].start()
    for bits in (1, 2, 3):
        first.append(push(tile, tl.at[z], st.at[bits], rt.at[bits], on_line(row, col, bits)))
        first[-1].start()
    rows_in = LineGather(xp, sx, rx)
    blocks = []
    for bits in range(1, 8):
        there = in_plane(row, col, bits)
        blocks.append(
            push(wgs.at[flip(place, bits)], wgp.at[place], sg.at[bits], rg.at[bits], there)
        )
        blocks[-1].start()
    wgp[place] = wgs[place]
    for copy in first:
        copy.wait_recv()
    rows_in.start(x)
    column = row * 2 + y
    beside, across = (row, flip(col, 2)), (flip(row, 1), col)
    ways = [
        push(wline, wqp.at[column], sv.at[1], rv.at[1], beside),
        push(wline, wqp.at[column], sv.at[2], rv.at[2], across),
    ]
    for copy in ways:
        copy.start()
    wqp[column] = wline[...]
    second = []
    for bits in range(1, 8):
        there = in_plane(row, col, bits)
        second.append(push(tl, tiles.at[place], su.at[bits], ru.at[bits], there))
        second[-1].start()
    tiles[place] = tl[...]
    ways[0].wait_recv()
    slot = wqp.at[flip(column, 1)]
    ways.append(push(slot, slot, sv.at[3], rv.at[3], across))
    ways[2].start()
    for copy in second:
        copy.wait_recv()
    rows_in.forward(4)
    rows_in.forward(2)
    for copy in ways[1:]:
        copy.wait_recv()
    for k in range(8):
        lanes = slice(k * 128, k * 128 + 128)
        r, plane = k // PLANES, k % PLANES
        gains[:, lanes] = (tiles[r * QUAD, plane] + tiles[r * QUAD + 1, plane]) + (
            tiles[r * QUAD + 2, plane] + tiles[r * QUAD + 3, plane]
        )
        times[:, lanes] = tiles[row * QUAD + y * 2 + k % 2, k // 2]
        wt[:, lanes] = jnp.transpose(
            jnp.concatenate(
                [wqp[r * 2 + j // 2, plane * 2 + j % 2] for j in range(4)], axis=0
            )
        )
    for k in range(16):
        labels[:, k * 128 : k * 128 + 128] = tiles[row * QUAD + k % QUAD, k // QUAD]
    phases = times[3:4, :] * freq[...]
    cs[...] = jnp.cos(phases)
    sn[...] = jnp.sin(phases)
    gain = gains[0:1, :]
    kept = [fetch(wt, wt_out, keep.at[2])]

    def project(chip):
        rows = block(chip, 256)
        values = jnp.concatenate([xp[2 * chip], xp[2 * chip + 1]], axis=0).astype(f32)
        scaled = (values * norm_scale(values) * gain).astype(bf16)
        s1[2 * chip] = scaled[0:128]
        s1[2 * chip + 1] = scaled[128:256]
        out = mm_nt(wt[...], scaled)
        cos_part, sin_part = cs[:, rows], sn[:, rows]
        for head in range(2):
            for part in range(2):
                base = part * 128 + head * 64
                former, latter = out[base : base + 32], out[base + 32 : base + 64]
                factor = 0.125 if part == 0 else 1.0
                turned = former * cos_part - latter * sin_part
                other = latter * cos_part + former * sin_part
                at = part * 64
                box[head, at : at + 32, rows] = (turned * factor).astype(bf16)
                box[head, at + 32 : at + 64, rows] = (other * factor).astype(bf16)
            at = 256 + head * 64
            box[head, 128:192, rows] = out[at : at + 64].astype(bf16)

    pieces = []
    for bits in range(1, 16):
        there = (row, flip(col, bits))
        pieces.append(push(cot.at[there[1]], cotr.at[col], sc.at[bits], rc.at[bits], there))
        pieces[-1].start()
    cotr[col] = cot[col]
    turned = []

    def exchange(chip, number):
        lanes = pl.ds(pl.multiple_of(chip * 512 + y * 256, 256), 256)
        copy = push(
            box.at[1 - y, :, block(chip, 256)],
            qkvt.at[:, lanes],
            sz.at[number],
            rz.at[number],
            (row, flip(col, 2)),
        )
        copy.start()
        turned.append(copy)
        qkvt[:, lanes] = box[y, :, block(chip, 256)]

    for k, bits in enumerate((0, 4, 2, 6)):
        if bits == 6:
            rows_in.forward(6)
        rows_in.arrived(bits)
        chip = flip(z, bits // 2)
        project(chip)
        exchange(chip, k)
        if bits == 2:
            target = col // 2 % 2 * 2 + col // 4 % 2
            slot = row * 2 + col % 2
            for plane in range(PLANES):
                there = (col // 8, plane * QUAD + target)
                mine = jnp.logical_and(row * 16 + col == there[0] * 16 + there[1], z == plane)

                @pl.when(jnp.logical_not(mine))
                def _():
                    push(wo, wop.at[slot], sw.at[plane], rw.at[slot], there).start()

                @pl.when(mine)
                def _():
                    wop[slot] = wo[...]

    kept.append(fetch(xp, xp_out, keep.at[0]))
    kept.append(fetch(s1, s1_out, keep.at[1]))
    for copy in blocks:
        copy.wait_recv()
    for j in range(4):
        source = (j // 2, row * 8 + core * 4 + y * 2 + j % 2)
        mine = jnp.logical_and(row == source[0], col == source[1])

        @pl.when(jnp.logical_not(mine))
        def _():
            push(wo, wop.at[j], sw.at[j], rw.at[j], source).wait_recv()

    target = col // 2 % 2 * 2 + col // 4 % 2
    slot = row * 2 + col % 2
    for plane in range(PLANES):
        there = (col // 8, plane * QUAD + target)
        mine = jnp.logical_and(row * 16 + col == there[0] * 16 + there[1], z == plane)

        @pl.when(jnp.logical_not(mine))
        def _():
            push(wo, wop.at[slot], sw.at[plane], rw.at[slot], there).wait_send()

    for copy in pieces:
        copy.wait_recv()
    for j in range(16):
        cots[j * 8 : j * 8 + 8, :] = cotr[jnp.clip(deal[j], 0, 15)]
    for copy in turned:
        copy.wait()
    rows_in.close()
    for copy in first + second + blocks + ways + pieces:
        copy.wait_send()
    for copy in kept:
        copy.wait()


def split_three(value):
    high = value.astype(bf16).astype(f32)
    middle = (value - high).astype(bf16).astype(f32)
    return high, middle, (value - high - middle).astype(bf16).astype(f32)


def window_queries(qa, lanes, first, limit):
    place = first + lax.broadcasted_iota(jnp.int32, (16, WINDOW), 1)
    line = lax.broadcasted_iota(jnp.int32, (16, WINDOW), 0)
    extra = jnp.where(
        jnp.logical_and(line == 12, place >= limit), -1e30, qa[64:80, lanes].astype(f32)
    )
    return jnp.concatenate(
        [qa[0:64, lanes], extra.astype(bf16), jnp.zeros((AUG - 80, WINDOW), bf16)], axis=0
    )


def head_of():
    row, col, z, place = places()
    return (z * 2 + col % 2) * 2 + col // 2 % 2


def read_lengths(labels, info):
    lane = lax.broadcasted_iota(jnp.int32, (1, 128), 1)
    numbers = labels[4:5, 0:128]
    for i in range(NSEQ):
        info[i] = jnp.sum(jnp.where(lane == i, numbers, 0.0)).astype(jnp.int32)


def over_keys(start, length, step, carry):
    carry = lax.fori_loop(
        0, length // 2, lambda k, c: step((start + 2 * k) * 128, 256, c), carry
    )
    return lax.fori_loop(
        0, length % 2, lambda k, c: step((start + length - 1) * 128, 128, c), carry
    )


def attend_body(bias_all, qkvt, labels, att, den, low, qa, ka, kt, info):
    size = qkvt.shape[1]
    head = head_of()
    bias = (bias_all[0, head], bias_all[1, head])
    variate = labels[2:3, :]
    line = lax.broadcasted_iota(jnp.int32, (16, size), 0)
    same = (variate == (line % 4).astype(f32)).astype(f32)
    same_pieces = split_three(jnp.full((16, size), bias[0] - bias[1], f32))
    other_pieces = split_three(jnp.full((16, size), bias[1], f32))

    def choose(pieces, number):
        return jnp.where(number == 0, pieces[0], jnp.where(number == 1, pieces[1], pieces[2]))

    extra_q = jnp.where(line < 12, same, jnp.where(line == 12, 0.0, 1.0))
    extra_k = jnp.where(
        line < 12,
        same * choose(same_pieces, line // 4),
        jnp.where(line == 12, 1.0, choose(other_pieces, line - 13)),
    )
    qa[0:64, 0:size] = qkvt[0:64, :]
    qa[64:80, 0:size] = extra_q.astype(bf16)
    qa[80:AUG, 0:size] = jnp.zeros((AUG - 80, size), bf16)
    qa[:, size:] = jnp.zeros((AUG, WINDOW), bf16)
    kt[0:64, :] = qkvt[64:128, :]
    kt[64:80, :] = extra_k.astype(bf16)
    kt[80:AUG, :] = jnp.zeros((AUG - 80, size), bf16)
    ka[...] = jnp.transpose(kt[...])
    read_lengths(labels, info)

    def sequence(number, start):
        length = info[number]
        limit = (start + length) * 128

        def window(j, unused):
            first = (start + 4 * j) * 128
            lanes = pl.ds(pl.multiple_of(first, 128), WINDOW)
            queries = window_queries(qa, lanes, first, limit)

            def keys(first_key, count, running):
                total, numerator = running
                rows = pl.ds(pl.multiple_of(first_key, 128), count)
                weights = jnp.exp(mm(ka[rows, :], queries))
                total = total + jnp.sum(weights, axis=0, keepdims=True)
                numerator = numerator + mm(qkvt[128:192, rows], weights.astype(bf16))
                return total, numerator

            total, numerator = over_keys(
                start, length, keys, (jnp.zeros((1, WINDOW), f32), jnp.zeros((64, WINDOW), f32))
            )
            attended = numerator / total
            att[:, lanes] = attended
            den[:, lanes] = jnp.broadcast_to(total, (8, WINDOW))
            low[:, lanes] = attended.astype(bf16)
            return unused

        lax.fori_loop(0, (length + 3) // 4, window, 0)
        return start + length

    lax.fori_loop(0, NSEQ, sequence, 0)


def attend_back_body(
    qkvt, qa, ka, labels, freq, grad, att, den,
    dproj, bias_tile,
    dn, cw, vn, dq, dk, dv, info,
):
    size = qkvt.shape[1]
    lanes_all = slice(0, size)
    inverse = 1.0 / den[0:1, lanes_all]
    d_att = grad[...].astype(f32)
    dn[:, lanes_all] = (d_att * inverse).astype(bf16)
    dn[:, size:] = jnp.zeros((64, WINDOW), bf16)
    cw[:, lanes_all] = jnp.broadcast_to(
        jnp.sum(d_att * att[:, lanes_all], axis=0, keepdims=True) * inverse, (8, size)
    )
    cw[:, size:] = jnp.zeros((8, WINDOW), f32)
    vn[...] = jnp.transpose(qkvt[128:192, :])
    dk[...] = jnp.zeros_like(dk)
    dv[...] = jnp.zeros_like(dv)

    read_lengths(labels, info)

    def sequence(number, start):
        length = info[number]
        limit = (start + length) * 128

        def window(j, unused):
            first = (start + 4 * j) * 128
            lanes = pl.ds(pl.multiple_of(first, 128), WINDOW)
            queries = window_queries(qa, lanes, first, limit)
            upstream = dn[:, lanes]
            centre = cw[0:1, lanes]

            def keys(first_key, count, running):
                rows = pl.ds(pl.multiple_of(first_key, 128), count)
                weights = jnp.exp(mm(ka[rows, :], queries))
                d_scores = weights * (mm(vn[rows, :], upstream) - centre)
                rounded = d_scores.astype(bf16)
                dk[:, rows] += mm_nt(queries, rounded)
                dv[:, rows] += mm_nt(upstream, weights.astype(bf16))
                return running + mm(qkvt[64:128, rows], rounded)

            dq[:, lanes] = over_keys(start, length, keys, jnp.zeros((64, WINDOW), f32))
            return unused

        lax.fori_loop(0, (length + 3) // 4, window, 0)
        return start + length

    lax.fori_loop(0, NSEQ, sequence, 0)

    phases = labels[3:4, :] * freq[...]
    cos_part, sin_part = jnp.cos(phases), jnp.sin(phases)
    for part, source, factor in ((0, dq, 0.125), (1, dk, 1.0)):
        former, latter = source[0:32, lanes_all], source[32:64, lanes_all]
        dproj[part * 64 : part * 64 + 32, :] = (
            (former * cos_part + latter * sin_part) * factor
        ).astype(bf16)
        dproj[part * 64 + 32 : part * 64 + 64, :] = (
            (latter * cos_part - former * sin_part) * factor
        ).astype(bf16)
    dproj[128:192, :] = dv[...].astype(bf16)
    variate = labels[2:3, :]
    line = lax.broadcasted_iota(jnp.int32, (16, size), 0)
    match = jnp.logical_and(variate == line.astype(f32), line < 4)
    near = jnp.sum(jnp.where(match, dk[64:80, :], 0.0))
    every = jnp.sum(dk[77:78, :])
    lane = lax.broadcasted_iota(jnp.int32, (8, 128), 1)
    line8 = lax.broadcasted_iota(jnp.int32, (8, 128), 0)
    here = lane == head_of()
    bias_tile[...] = jnp.where(
        jnp.logical_and(here, line8 == 2),
        near,
        jnp.where(jnp.logical_and(here, line8 == 3), every - near, 0.0),
    )


def branch_body(
    low, wop, x, gains, cots,
    atp, hidden, s2, cotp_out,
    cotp, keep, atn, part, sz, rz, sa, ra, inbox, outbox, second, ss, rs,
):
    row, col, z, place = places()
    quarter = col % QUAD
    present = greet(plane_near(row, col) + column_all(row, col))
    rows, lanes = block(z // 2, 64), block(row, 512)
    cotp[place] = cots[...]
    wait_for(present)
    for plane in range(PLANES):
        mine = jnp.logical_and(row == z % 2, z == plane)

        @pl.when(jnp.logical_not(mine))
        def _():
            push(
                low.at[:, plane * 512 : plane * 512 + 512], atp.at[rows, lanes],
                sz.at[plane], rz.at[row * 2 + z // 2], (z % 2, plane * QUAD + quarter),
            ).start()

        @pl.when(mine)
        def _():
            atp[rows, lanes] = low[:, plane * 512 : plane * 512 + 512]

    cot_in = Gather(cotp, sa, ra)
    cot_in.start(cots)
    for j in range(4):
        source = (j // 2, (row + 2 * (j % 2)) * QUAD + quarter)
        mine = jnp.logical_and(row == j // 2, z == row + 2 * (j % 2))

        @pl.when(jnp.logical_not(mine))
        def _():
            push(
                low.at[:, 0:512], atp.at[0:64, 0:512], sz.at[j], rz.at[j], source
            ).wait_recv()

    for plane in range(PLANES):
        mine = jnp.logical_and(row == z % 2, z == plane)

        @pl.when(jnp.logical_not(mine))
        def _():
            push(
                low.at[:, plane * 512 : plane * 512 + 512], atp.at[rows, lanes],
                sz.at[plane], rz.at[row * 2 + z // 2], (z % 2, plane * QUAD + quarter),
            ).wait_send()

    atn[...] = jnp.transpose(atp[...])
    total = Scatter(part, inbox, outbox, second, ss, rs)
    core = col % 2
    for bits in (3, 2, 1, 0):
        chip = flip(place // 2, bits)
        part[2 * chip + 1 - core] = mm(atn[block(2 * chip + 1 - core, 128), :], wop[...]).astype(bf16)
    for bits in range(4):
        total.near(flip(place // 2, bits), bits)
    for bits in (3, 2, 1, 0):
        chip = flip(place // 2, bits)
        part[2 * chip + core] = mm(atn[block(2 * chip + core, 128), :], wop[...]).astype(bf16)
    total.far_all()
    cot_in.finish()
    kept = fetch(cotp, cotp_out, keep.at[0])
    state = x[...].astype(f32) + total.finish()
    hidden[...] = state
    s2[...] = (state * norm_scale(state) * gains[1:2, :]).astype(bf16)
    total.close()
    cot_in.close()
    kept.wait()


def ffn_body(
    s2, cotp_in, wg_in, w_down, hidden, gains,
    out_keep, down_in, gwg_out, d_hidden, low, gain_term,
    cotp, wg, s2p, wgs, wd, actives, factors, inner_s, dgu, d_part, out_part, gwd, gwg, relayed, both_terms,
    keep, sa, ra, sw, rw, sd, rd, inbox, outbox, second, ss, rs,
):
    row, col, z, place = places()
    loads = [fetch(wg_in, wg, keep.at[0]), fetch(cotp_in, cotp, keep.at[1])]
    present = greet(plane_near(row, col) + line_all(row, col))
    s2p[place] = s2[...]
    wd[block(z, 128), :] = w_down[...]
    loads[0].wait()
    for plane in range(PLANES):
        for r in range(2):
            at = (r * PLANES + plane) * 128
            wgs[at : at + 128, :] = wg[plane * 2 + r]
    wait_for(present)
    rows_in = Gather(s2p, sa, ra)
    rows_in.start(s2)
    inner = jnp.logical_or(z == 1, z == 2)
    end = jnp.logical_not(inner)
    downs = {
        bits: push(
            w_down, wd.at[block(z, 128), :], sw.at[bits], rw.at[bits], on_line(row, col, bits)
        )
        for bits in (2, 1, 3)
    }
    passed = wd.at[block(flip(z, 2), 128), :]
    downs[0] = push(passed, passed, sw.at[0], rw.at[3], on_line(row, col, 1))
    downs[2].start()

    @pl.when(inner)
    def _():
        downs[3].start()

    downs[1].start()
    for k in range(4):
        chip = flip(place // 2, k)
        if k:
            rows_in.forward(2 * k)
        rows_in.arrived(2 * k)
        if k == 1:
            downs[2].wait_recv()

            @pl.when(inner)
            def _():
                downs[0].start()

        rows = block(chip, 256)
        scaled = jnp.concatenate([s2p[2 * chip], s2p[2 * chip + 1]], axis=0)
        both = mm(scaled, wgs[...])
        gate, upper = both[:, 0:512], both[:, 512:1024]
        sig = jax.nn.sigmoid(gate)
        active = gate * sig
        inner_s[rows, :] = (active * upper).astype(bf16)
        actives[rows, :] = active
        factors[rows, :] = upper * sig * (1.0 + gate * (1.0 - sig))
    loads[1].wait()
    cot_all = jnp.concatenate([cotp[t] for t in range(MEMBERS)], axis=0)
    for k in range(4):
        cols = slice(k * 128, k * 128 + 128)
        gwd[k] = mm_tn(inner_s[:, cols], cot_all).astype(bf16)
    grads = {
        bits: push(
            gwd.at[flip(z, bits)], down_in.at[bits], sd.at[bits], rd.at[bits], on_line(row, col, bits)
        )
        for bits in (1, 3)
    }
    grads[2] = push(both_terms, down_in.at[2], sd.at[2], rd.at[2], on_line(row, col, 2))
    grads[0] = push(gwd.at[flip(z, 3)], relayed, sd.at[0], rd.at[0], on_line(row, col, 1))

    @pl.when(end)
    def _():
        grads[0].start()
        both_terms[...] = gwd[flip(z, 2)]
        grads[2].start()
        down_in[3] = jnp.zeros(down_in.shape[1:], bf16)

    @pl.when(inner)
    def _():
        grads[3].start()

    grads[1].start()
    down_in[0] = gwd[z]
    total = Scatter(d_part, inbox, outbox, second, ss, rs)
    downs[1].wait_recv()
    downs[3].wait_recv()
    for k in range(4):
        chip = flip(place // 2, k)
        rows = block(chip, 256)
        upstream = jnp.concatenate([cotp[2 * chip], cotp[2 * chip + 1]], axis=0)
        d_inner = mm_nt(upstream, wd[...])
        dgu[rows, 0:512] = (d_inner * factors[rows, :]).astype(bf16)
        dgu[rows, 512:1024] = (d_inner * actives[rows, :]).astype(bf16)
        tile = mm_nt(dgu[rows, :], wgs[...]).astype(bf16)
        d_part[2 * chip] = tile[0:128]
        d_part[2 * chip + 1] = tile[128:256]
        total.near(chip, k)
        if k > 1:
            total.far(k - 1)
        if k == 1:

            @pl.when(inner)
            def _():
                grads[0].wait_recv()
                both_terms[...] = (
                    gwd[flip(z, 2)].astype(f32) + relayed[...].astype(f32)
                ).astype(bf16)
                grads[2].start()

    for k in range(4):
        chip = flip(place // 2, k)
        tile = mm(inner_s[block(chip, 256), :], wd[...]).astype(bf16)
        out_part[2 * chip] = tile[0:128]
        out_part[2 * chip + 1] = tile[128:256]
        if k == 0:
            total.far(3)
    kept = [fetch(out_part, out_keep, keep.at[10])]
    for f in range(8):
        cols = slice(f * 128, f * 128 + 128)
        lhs = jnp.concatenate([s2p[t, :, cols] for t in range(MEMBERS)], axis=0)
        at = (f % PLANES) * 2 + f // PLANES
        gwg[at] = mm_tn(lhs, dgu[...]).astype(bf16)
        kept.append(fetch(gwg.at[at], gwg_out.at[at], keep.at[2 + f]))
    d_scaled = total.finish()
    state = hidden[...]
    scale = norm_scale(state)
    normed = state * scale
    gain_term[...] = jnp.broadcast_to(jnp.sum(d_scaled * normed, axis=0, keepdims=True), (8, 1024))
    d_state = cotp[place].astype(f32) + norm_back(d_scaled * gains[1:2, :], normed, scale)
    d_hidden[...] = d_state
    low[...] = d_state.astype(bf16)
    rows_in.close()
    total.close()
    grads[1].wait_recv()
    grads[2].wait_recv()
    for copy in (downs[1], downs[2], grads[1], grads[2]):
        copy.wait_send()

    @pl.when(inner)
    def _():
        grads[3].wait_recv()
        for copy in (downs[3], downs[0], grads[3]):
            copy.wait_send()

    @pl.when(end)
    def _():
        grads[0].wait_send()

    for copy in kept:
        copy.wait()


def attended_back_body(
    low, wop, atp, out_in, hidden,
    grad, gwo, rows_out,
    out_part, keep, dbp, dat, sg, rg, sz, rz, inbox, outbox, second, ss, rs,
):
    row, col, z, place = places()
    load = fetch(out_in, out_part, keep.at[0])
    present = greet(plane_near(row, col) + column_all(row, col))
    dbp[place] = low[...]
    wait_for(present)
    quarter = col % QUAD
    rows_in = Gather(dbp, sg, rg)
    rows_in.start(low)
    load.wait()
    output = Scatter(out_part, inbox, outbox, second, ss, rs)
    output.near_all()
    for k in range(4):
        chip = flip(place // 2, k)
        if k:
            rows_in.forward(2 * k)
        rows_in.arrived(2 * k)
        for core in range(2):
            dat[:, block(2 * chip + core, 128)] = mm_nt(wop[...], dbp[2 * chip + core]).astype(bf16)
        if k % 2 == 0:
            continue
        group = row if k == 1 else 1 - row
        for head in range(2):
            plane = row + 2 * head
            source = dat.at[head * 64 : head * 64 + 64, block(group, 512)]
            if k == 1:

                @pl.when(z != plane)
                def _():
                    push(
                        source, grad.at[:, block(z, 512)], sz.at[head], rz.at[z],
                        (group, plane * QUAD + quarter),
                    ).start()

                @pl.when(z == plane)
                def _():
                    grad[:, block(z, 512)] = source[...]

            else:
                push(
                    source, grad.at[:, block(z, 512)], sz.at[2 + head], rz.at[z],
                    (group, plane * QUAD + quarter),
                ).start()

    output.far_all()
    total = mm(atp[:, 0:128], dbp[0])
    for q in range(1, MEMBERS):
        total = total + mm(atp[:, q * 128 : q * 128 + 128], dbp[q])
    gwo[...] = total.astype(bf16)
    rows_out[...] = (hidden[...] + output.finish()).astype(bf16)
    output.close()
    for plane in range(PLANES):
        mine = jnp.logical_and(row == z % 2, z == plane)

        @pl.when(jnp.logical_not(mine))
        def _():
            push(
                dat.at[0:64, 0:512], grad.at[:, plane * 512 : plane * 512 + 512], sz.at[0],
                rz.at[plane], (z % 2, plane * QUAD + quarter),
            ).wait_recv()

    for head in range(2):
        plane = row + 2 * head

        @pl.when(z != plane)
        def _():
            push(
                dat.at[0:64, 0:512], grad.at[:, 0:512], sz.at[head], rz.at[z],
                (row, plane * QUAD + quarter),
            ).wait_send()

        push(
            dat.at[0:64, 0:512], grad.at[:, 0:512], sz.at[2 + head], rz.at[z],
            (1 - row, plane * QUAD + quarter),
        ).wait_send()

    rows_in.close()


def last_body(
    dproj, wt_in, s1_in, xp_in, gains, d_hidden, rows_out, gwo, gwg, gain_two, bias_tile, deal,
    grad_tokens, gqin, goin, gwg_in, sums, out,
    wt, s1, xp, pieces, slots, keep, dpt, dpn, part, gq, gqcol, gqsum, pack, packs, packed,
    passed, sz, rz, inbox, outbox, second, ss, rs, sp,
    sq, rq, sv, rv, st, rt, su, ru, sw, rw, sg, rg, sc, rc,
):
    row, col, z, place = places()
    quarter = col % QUAD
    y, core = col // 2 % 2, col % 2
    member = z * 2 + core
    column = row * 2 + y
    loads = [
        fetch(s1_in, s1, keep.at[0]),
        fetch(xp_in, xp, keep.at[1]),
        fetch(wt_in, wt, keep.at[2]),
    ]
    present = greet([anyone(row, col, bits) for bits in range(1, 32)])
    for j in range(16):
        pieces[j] = rows_out[j * 8 : j * 8 + 8, :]
    for d in range(16):
        number = 0
        for j in range(1, 16):
            number = jnp.where(deal[j] == d, j, number)
        slots[d] = pieces[number]
    gwg_in[place] = gwg[place]
    out[col] = slots[col]
    wait_for(present)
    copies = {}
    for bits in (3, 2, 1, 0):
        chip = flip(z, bits)
        ours = pl.ds(pl.multiple_of(chip * 512 + y * 256, 256), 256)
        theirs = pl.ds(pl.multiple_of(chip * 512 + (1 - y) * 256, 256), 256)
        copies[bits] = push(
            dproj.at[:, theirs], dpt.at[y, :, block(chip, 256)], sz.at[bits], rz.at[bits],
            (row, flip(col, 2)),
        )
        copies[bits].start()
        dpt[y, :, block(chip, 256)] = dproj[:, ours]
    owner = core * 4 + y * 2
    for j in range(4):
        there = (j // 2, row * 8 + owner + j % 2)
        mine = jnp.logical_and(row == there[0], col == there[1])

        @pl.when(jnp.logical_not(mine))
        def _():
            push(gwo.at[j], goin.at[z], sw.at[j], rw.at[z], there).start()

        @pl.when(mine)
        def _():
            goin[z] = gwo[j]

    spread = []
    for bits in range(1, 16):
        there = (row, flip(col, bits))
        copy = push(slots.at[there[1]], out.at[col], sc.at[bits], rc.at[bits], there)
        copy.start()
        spread.append(copy)
    for copy in loads:
        copy.wait()
    total = LineScatter(part, inbox, outbox, second, ss, rs, passed, sp)
    term = jnp.zeros((1, 1024), f32)
    for bits in (3, 2, 1, 0):
        chip = flip(z, bits)
        lanes = block(chip, 256)
        copies[bits].wait_recv()
        for kind in range(3):
            both = jnp.concatenate(
                [dpt[head, kind * 64 : kind * 64 + 64, lanes] for head in range(2)], axis=0
            )
            dpn[lanes, kind * 128 : kind * 128 + 128] = jnp.transpose(both)
        d_scaled = mm(dpn[lanes, :], wt[...])
        values = jnp.concatenate([xp[2 * chip], xp[2 * chip + 1]], axis=0).astype(f32)
        term = term + jnp.sum(d_scaled * (values * norm_scale(values)), axis=0, keepdims=True)
        part[2 * chip] = d_scaled[0:128].astype(bf16)
        part[2 * chip + 1] = d_scaled[128:256].astype(bf16)
        total.near(chip, bits)
        if bits < 3:
            total.far(bits + 1)
    for bits in range(1, 8):
        there = in_plane(row, col, bits)
        copy = push(gwg.at[flip(place, bits)], gwg_in.at[place], sg.at[bits], rg.at[bits], there)
        copy.start()
        spread.append(copy)
    for f in range(8):
        if f == 4:
            total.far_second()
        lhs = jnp.concatenate([s1[t, :, f * 128 : f * 128 + 128] for t in range(MEMBERS)], axis=0)
        chunk = mm_tn(lhs, dpn[...]).astype(bf16)
        for j in range(4):
            gq[f // PLANES * 2 + j // 2, f % PLANES * 2 + j % 2] = chunk[j * 32 : j * 32 + 32, :]
    columns = []
    for bits in (3, 2, 1):
        there = (flip(row, bits // 2), flip(col, bits % 2 * 2))
        copy = push(gq.at[flip(column, bits)], gqcol.at[bits - 1], sv.at[bits], rv.at[bits], there)
        copy.start()
        columns.append(copy)
    for k in range(8):
        pack[k] = bias_tile[...]
        pack[k, 0:1, :] = term[:, k * 128 : k * 128 + 128]
        pack[k, 1:2, :] = gain_two[0:1, k * 128 : k * 128 + 128]
    first = []
    for bits in range(1, 8):
        there = in_plane(row, col, bits)
        copy = push(
            pack.at[pl.ds(there[0] * PLANES, PLANES)], packs.at[place], st.at[bits], rt.at[bits], there
        )
        copy.start()
        first.append(copy)
    packs[place] = pack[pl.ds(row * PLANES, PLANES)]
    for copy in first:
        copy.wait_recv()
    summed = packs[0]
    for p in range(1, MEMBERS):
        summed = summed + packs[p]
    packed[...] = summed
    for bits in (1, 2, 3):
        copy = push(
            packed.at[flip(z, bits)], sums.at[z], su.at[bits], ru.at[bits], on_line(row, col, bits)
        )
        copy.start()
        spread.append(copy)
    sums[z] = packed[z]
    for copy in columns:
        copy.wait_recv()
    for m in range(MEMBERS):
        gqsum[m] = (
            (gq[column, m].astype(f32) + gqcol[0, m].astype(f32))
            + (gqcol[1, m].astype(f32) + gqcol[2, m].astype(f32))
        ).astype(bf16)
    for bits in range(7, 0, -1):
        there = in_line(row, col, bits)
        copy = push(gqsum.at[flip(member, bits)], gqin.at[member], sq.at[bits], rq.at[bits], there)
        copy.start()
        spread.append(copy)
    gqin[member] = gqsum[member]
    d_one = total.finish()
    own_rows = xp[member].astype(f32)
    scale = norm_scale(own_rows)
    grad_tokens[...] = (
        d_hidden[...] + norm_back(d_one * gains[0:1, :], own_rows * scale, scale)
    ).astype(bf16)
    for copy in spread:
        copy.wait_recv()
    senders = col // 2 % 2 * 2 + col // 4 % 2
    for plane in range(PLANES):
        mine = jnp.logical_and(row * 16 + col == (col // 8) * 16 + plane * QUAD + senders, z == plane)

        @pl.when(jnp.logical_not(mine))
        def _():
            push(
                gwo.at[0], goin.at[plane], sw.at[0], rw.at[plane],
                (col // 8, plane * QUAD + senders),
            ).wait_recv()

    for j in range(4):
        there = (j // 2, row * 8 + owner + j % 2)
        mine = jnp.logical_and(row == there[0], col == there[1])

        @pl.when(jnp.logical_not(mine))
        def _():
            push(gwo.at[j], goin.at[z], sw.at[j], rw.at[z], there).wait_send()

    for copy in list(copies.values()) + columns + first + spread:
        copy.wait_send()
    total.close()


def finish_body(
    grad_tokens_in, gqin, goin, out_in, gwg, gwd, tiles,
    out, grad_tokens, grad_q, grad_o, grad_gu, grad_d, grad_one, grad_two, grad_bias,
):
    grad_tokens[...] = grad_tokens_in[...]
    out[...] = out_in[...]
    grad_o[...] = (goin[0].astype(f32) + goin[1].astype(f32)) + (
        goin[2].astype(f32) + goin[3].astype(f32)
    )
    grad_d[...] = (gwd[0].astype(f32) + gwd[1].astype(f32)) + (
        gwd[2].astype(f32) + gwd[3].astype(f32)
    )
    for p in range(MEMBERS):
        total = gqin[p].astype(f32)
        for kind in range(3):
            at = kind * 1024 + p * 128
            grad_q[:, at : at + 128] = total[:, kind * 128 : kind * 128 + 128]
        for half in range(2):
            for plane in range(PLANES):
                unit = (p // QUAD) * 16 + plane * QUAD + p % QUAD
                at = half * 512 + plane * 128
                start = half * 4096 + unit * 128
                grad_gu[:, start : start + 128] = gwg[p, :, at : at + 128].astype(f32)
    total = (tiles[0] + tiles[1]) + (tiles[2] + tiles[3])
    quarter = lax.axis_index("col") % QUAD
    chosen = jnp.zeros((2, 32), f32)
    for k in range(4):
        chosen = chosen + jnp.where(quarter == k, total[0:2, k * 32 : k * 32 + 32], 0.0)
    grad_one[...] = chosen[0]
    grad_two[...] = chosen[1]
    grad_bias[...] = total[2:4, 0:16]


def sds(shape, dtype):
    return jax.ShapeDtypeStruct(shape, dtype)


def dma(*shape):
    return pltpu.SemaphoreType.DMA(shape)


def kernel(body, name, specs, outs, scratch, number=None, cost=0, places_out=None):
    params = dict(vmem_limit_bytes=56 << 20)
    if number is not None:
        params.update(collective_id=number, has_side_effects=True)
    return pl.pallas_call(
        body,
        name=name,
        in_specs=specs,
        out_shape=outs,
        out_specs=places_out or [VM] * len(outs),
        scratch_shapes=scratch,
        compiler_params=pltpu.CompilerParams(**params),
        cost_estimate=pl.CostEstimate(flops=cost, bytes_accessed=cost // 300, transcendentals=0),
    )


def plane_shards(
    tokens, variate_ids, time_ids, lengths, deal, w_qkv, w_out, w_gate_up, w_down,
    gain_attn, gain_ffn, var_bias, cotangent,
):
    rows, width = tokens.shape
    lines = [[plane * QUAD + k for plane in range(PLANES)] for k in range(QUAD)]
    freq = jnp.asarray(np.exp(-math.log(10000.0) * np.arange(32) / 32).astype(np.float32)[:, None])
    target = deal[0, 0]

    xp, wt, wop, wgp, s1, qkvt, gains, labels, cot = kernel(
        enter_body,
        "enter",
        [VM] * 9 + [SM, SM, VM],
        [
            sds((8, rows, width), bf16),
            sds((384, 1024), bf16),
            sds((4, 32, 1024), bf16),
            sds((8, 32, 1024), bf16),
            sds((8, rows, width), bf16),
            sds((192, 2048), bf16),
            sds((8, 1024), f32),
            sds((8, 2048), f32),
            sds((rows, width), bf16),
        ],
        [
            pltpu.VMEM((16, 8, width), bf16),
            pltpu.VMEM((8, rows, width), bf16),
            pltpu.VMEM((8, rows, width), bf16),
            dma(4),
            pltpu.VMEM((8, 32, 384), bf16),
            pltpu.VMEM((8, 32, 384), bf16),
            pltpu.VMEM((4, 8, 32, 384), bf16),
            pltpu.VMEM((8, 32, 1024), bf16),
            pltpu.VMEM((8, 128), f32),
            pltpu.VMEM((4, 8, 128), f32),
            pltpu.VMEM((8, 4, 8, 128), f32),
            pltpu.VMEM((384, 1024), bf16),
            pltpu.VMEM((2, 192, 1024), bf16),
            pltpu.VMEM((32, 1024), f32),
            pltpu.VMEM((32, 1024), f32),
            pltpu.VMEM((8, 1024), f32),
        ]
        + [dma(8), dma(8), dma(8), dma(8), dma(4), dma(4), dma(4), dma(4), dma(8), dma(8)]
        + [dma(4), dma(4), dma(8), dma(8), dma(4), dma(4), dma(16), dma(16)],
        number=1,
        places_out=[ANY, ANY, VM, VM, ANY, VM, VM, VM, VM],
    )(
        tokens, w_qkv, w_out, w_gate_up, cotangent.reshape(16, 8, width), gain_attn[None],
        gain_ffn[None], variate_ids[None], time_ids[None], lengths, target, freq,
    )

    gate_up = lax.all_gather(
        wgp.reshape(256, 1024), "col", axis=0, tiled=True, axis_index_groups=lines
    )
    wop = wop.reshape(128, 1024)

    wide = 2048 + WINDOW
    att, den, low, qa, ka = kernel(
        attend_body,
        "attend",
        [SM, VM, VM],
        [
            sds((64, wide), f32),
            sds((8, wide), f32),
            sds((64, wide), bf16),
            sds((AUG, wide), bf16),
            sds((2048, AUG), bf16),
        ],
        [pltpu.VMEM((AUG, 2048), bf16), pltpu.SMEM((8,), jnp.int32)],
        cost=2 * 10**9,
    )(var_bias, qkvt, labels)

    atp, hidden, s2, cotp = kernel(
        branch_body,
        "branch",
        [VM] * 5,
        [
            sds((128, 1024), bf16),
            sds((rows, width), f32),
            sds((rows, width), bf16),
            sds((8, rows, width), bf16),
        ],
        [
            pltpu.VMEM((8, rows, width), bf16),
            dma(1),
            pltpu.VMEM((1024, 128), bf16),
            pltpu.VMEM((8, rows, width), bf16),
            dma(4), dma(4), dma(8), dma(8),
        ]
        + scatter_scratch(rows, width),
        number=2,
        places_out=[VM, VM, VM, ANY],
    )(low, wop, tokens, gains, cot)

    out_part, down_in, gwg, d_hidden, d_branch, gain_two = kernel(
        ffn_body,
        "ffn",
        [VM, ANY, ANY, VM, VM, VM],
        [
            sds((8, rows, width), bf16),
            sds((4, rows, width), bf16),
            sds((8, 128, 1024), bf16),
            sds((rows, width), f32),
            sds((rows, width), bf16),
            sds((8, 1024), f32),
        ],
        [
            pltpu.VMEM((8, rows, width), bf16),
            pltpu.VMEM((8, 128, 1024), bf16),
            pltpu.VMEM((8, rows, width), bf16),
            pltpu.VMEM((1024, 1024), bf16),
            pltpu.VMEM((512, width), bf16),
            pltpu.VMEM((1024, 512), f32),
            pltpu.VMEM((1024, 512), f32),
            pltpu.VMEM((1024, 512), bf16),
            pltpu.VMEM((1024, 1024), bf16),
            pltpu.VMEM((8, rows, width), bf16),
            pltpu.VMEM((8, rows, width), bf16),
            pltpu.VMEM((4, rows, width), bf16),
            pltpu.VMEM((8, 128, 1024), bf16),
            pltpu.VMEM((rows, width), bf16),
            pltpu.VMEM((rows, width), bf16),
            dma(11), dma(8), dma(8), dma(4), dma(4), dma(4), dma(4),
        ]
        + scatter_scratch(rows, width),
        number=3,
        cost=10**10,
        places_out=[ANY, VM, ANY, VM, VM, VM],
    )(s2, cotp, gate_up.reshape(8, 128, 1024), w_down, hidden, gains)

    gate_up_sum = lax.psum_scatter(
        gwg.reshape(1024, 1024), "col", scatter_dimension=0, tiled=True, axis_index_groups=lines
    )

    grad, gwo, rows_out = kernel(
        attended_back_body,
        "attended_back",
        [VM, VM, VM, ANY, VM],
        [sds((64, 2048), bf16), sds((128, 1024), bf16), sds((rows, width), bf16)],
        [
            pltpu.VMEM((8, rows, width), bf16),
            dma(1),
            pltpu.VMEM((8, rows, width), bf16),
            pltpu.VMEM((128, 1024), bf16),
            dma(8), dma(8), dma(4), dma(4),
        ]
        + scatter_scratch(rows, width),
        number=4,
    )(d_branch, wop, atp, out_part, hidden)

    dproj, bias_tile = kernel(
        attend_back_body,
        "attend_back",
        [VM] * 8,
        [sds((192, 2048), bf16), sds((8, 128), f32)],
        [
            pltpu.VMEM((64, wide), bf16),
            pltpu.VMEM((8, wide), f32),
            pltpu.VMEM((2048, 64), bf16),
            pltpu.VMEM((64, wide), f32),
            pltpu.VMEM((AUG, 2048), f32),
            pltpu.VMEM((64, 2048), f32),
            pltpu.SMEM((8,), jnp.int32),
        ],
        cost=5 * 10**9,
    )(qkvt, qa, ka, labels, freq, grad, att, den)

    grad_tokens, gqin, goin, gwg_in, sums, out = kernel(
        last_body,
        "last",
        [VM] + [ANY] * 3 + [VM] * 7 + [SM],
        [
            sds((rows, width), bf16),
            sds((8, 32, 384), bf16),
            sds((4, 32, 1024), bf16),
            sds((8, 32, 1024), bf16),
            sds((4, 8, 128), f32),
            sds((16, 8, width), bf16),
        ],
        [
            pltpu.VMEM((384, 1024), bf16),
            pltpu.VMEM((8, rows, width), bf16),
            pltpu.VMEM((8, rows, width), bf16),
            pltpu.VMEM((16, 8, width), bf16),
            pltpu.VMEM((16, 8, width), bf16),
            dma(3),
            pltpu.VMEM((2, 192, 1024), bf16),
            pltpu.VMEM((1024, 384), bf16),
            pltpu.VMEM((8, rows, width), bf16),
            pltpu.VMEM((4, 8, 32, 384), bf16),
            pltpu.VMEM((3, 8, 32, 384), bf16),
            pltpu.VMEM((8, 32, 384), bf16),
            pltpu.VMEM((8, 8, 128), f32),
            pltpu.VMEM((8, 4, 8, 128), f32),
            pltpu.VMEM((4, 8, 128), f32),
            pltpu.VMEM((rows, width), bf16),
            dma(4), dma(4),
        ]
        + scatter_scratch(rows, width)
        + [dma(2), dma(8), dma(8), dma(4), dma(4), dma(8), dma(8), dma(4), dma(4)]
        + [dma(4), dma(4), dma(8), dma(8), dma(16), dma(16)],
        number=5,
    )(
        dproj, wt, s1, xp, gains, d_hidden, rows_out, gwo.reshape(4, 32, 1024),
        gate_up_sum.reshape(8, 32, 1024), gain_two, bias_tile, target,
    )
    out, grad_tokens, grad_q, grad_o, grad_gate_up, grad_down, gain_one, gain_two_grad, bias_grads = kernel(
        finish_body,
        "finish",
        [VM] * 7,
        [
            sds((rows, width), bf16),
            sds((rows, width), bf16),
            sds((32, 3072), f32),
            sds((32, 1024), f32),
            sds((32, 8192), f32),
            sds((rows, width), f32),
            sds((32,), f32),
            sds((32,), f32),
            sds((2, 16), f32),
        ],
        [],
    )(
        grad_tokens, gqin, goin, out.reshape(rows, width), gwg_in,
        down_in, sums,
    )
    return (
        out,
        grad_tokens,
        grad_q,
        grad_o,
        grad_gate_up,
        grad_down,
        gain_one,
        gain_two_grad,
        bias_grads,
    )


def solution(mesh):
    planes = mesh.shape["row"] == 2 and mesh.shape["col"] == PLANES * QUAD
    return jax.shard_map(
        plane_shards if planes else shards,
        mesh=mesh,
        in_specs=(
            P(("row", "col"), None),
            P(("row", "col")),
            P(("row", "col")),
            P("row", None),
            P("row", "col", None),
            P(("row", "col"), None),
            P(("row", "col"), None),
            P(("row", "col"), None),
            P(("row", "col"), None),
            P(("row", "col")),
            P(("row", "col")),
            P(),
            P(("row", "col"), None),
        ),
        out_specs=(
            P(("row", "col"), None),
            P(("row", "col"), None),
            P(("row", "col"), None),
            P(("row", "col"), None),
            P(("row", "col"), None),
            P(("row", "col"), None),
            P(("row", "col")),
            P(("row", "col")),
            P(),
        ),
        check_vma=False,
    )
```

```python
import math

import jax
import jax.numpy as jnp
import numpy as np
from jax import lax
from jax.experimental import pallas as pl
from jax.experimental.pallas import tpu as pltpu
from jax.sharding import PartitionSpec as P

HEAD_DIM = 64
UNIT = 128
KEY_BLOCK = 1024
NSEQ = 6


epsilon = 1e-05


def contract_rows(operand, factor):
    return lax.dot_general(
        operand, factor, (((0,), (0,)), ((), ())), preferred_element_type=jnp.float32
    )


def contract_cols(operand, factor):
    return lax.dot_general(
        operand, factor, (((1,), (1,)), ((), ())), preferred_element_type=jnp.float32
    )


def angles(time_ids):
    half_dim = HEAD_DIM // 2
    inverse_freq = jnp.exp(-math.log(10000.0) * jnp.arange(half_dim, dtype=jnp.float32) / half_dim)
    phases = time_ids.astype(jnp.float32)[:, None] * inverse_freq[None, :]
    return (jnp.cos(phases)[:, None, :], jnp.sin(phases)[:, None, :])


def rotate(tensor, cos_part, sin_part):
    half_dim = tensor.shape[-1] // 2
    former = tensor[..., :half_dim]
    latter = tensor[..., half_dim:]
    return jnp.concatenate(
        [former * cos_part - latter * sin_part, latter * cos_part + former * sin_part], axis=-1
    )


def unrotate(tensor, cos_part, sin_part):
    half_dim = tensor.shape[-1] // 2
    former = tensor[..., :half_dim]
    latter = tensor[..., half_dim:]
    return jnp.concatenate(
        [former * cos_part + latter * sin_part, latter * cos_part - former * sin_part], axis=-1
    )


def norm_scale(values):
    return lax.rsqrt(jnp.mean(values * values, axis=-1, keepdims=True) + epsilon)


def norm_back(d_normed, normed, scale):
    return scale * (d_normed - normed * jnp.mean(d_normed * normed, axis=-1, keepdims=True))


def score_weights(queries, query_seq, query_var, key_block, seq_block, var_block, var_bias):
    scores = (
        jnp.einsum("qhd,khd->hqk", queries, key_block, preferred_element_type=jnp.float32) * 0.125
    )
    matched = query_var[:, None] == var_block[None, :]
    scores = scores + jnp.where(
        matched[None], var_bias[0][:, None, None], var_bias[1][:, None, None]
    )
    within = query_seq[:, None] == seq_block[None, :]
    return (jnp.where(within[None], jnp.exp(scores), 0.0), matched)


def shards(
    tokens,
    variate_ids,
    time_ids,
    lengths,
    deal,
    w_qkv,
    w_out,
    w_gate_up,
    w_down,
    gain_attn,
    gain_ffn,
    var_bias,
    cotangent,
):
    tok_rows, model_width = tokens.shape
    n_col = lax.axis_size("col")
    col_index = lax.axis_index("col")
    piece_len = tok_rows // n_col
    head_count = model_width // HEAD_DIM
    bounds = jnp.cumsum(lengths[0]) * UNIT
    position = col_index * tok_rows + jnp.arange(tok_rows, dtype=jnp.int32)
    seq_own = jnp.sum((position[:, None] >= bounds[None, :]).astype(jnp.int32), axis=1)
    target = deal[0, 0]
    slots = jnp.arange(n_col, dtype=jnp.int32)
    inverse = jnp.sum(
        slots[:, None] * (target[:, None] == slots[None, :]).astype(jnp.int32), axis=0
    )
    send_rows = jnp.take(tokens.reshape(n_col, piece_len, model_width), inverse, axis=0)
    labels = jnp.stack(
        [
            seq_own.reshape(n_col, piece_len),
            variate_ids.reshape(n_col, piece_len),
            time_ids.reshape(n_col, piece_len),
        ],
        axis=1,
    )
    send_labels = jnp.take(labels, inverse, axis=0)
    got_rows, got_labels = (
        lax.all_to_all(send_rows, "col", split_axis=0, concat_axis=0, tiled=True),
        lax.all_to_all(send_labels, "col", split_axis=0, concat_axis=0, tiled=True),
    )
    inputs = got_rows.reshape(tok_rows, model_width).astype(jnp.float32)
    seq_q = got_labels[:, 0, :].reshape(tok_rows)
    var_q = got_labels[:, 1, :].reshape(tok_rows)
    cos_part, sin_part = angles(got_labels[:, 2, :].reshape(tok_rows))
    qkv_full, out_full, gate_up_full, down_full, gain_one, gain_two = (
        lax.all_gather(w_qkv, ("row", "col"), axis=0, tiled=True),
        lax.all_gather(w_out, ("row", "col"), axis=0, tiled=True),
        lax.all_gather(w_gate_up, ("row", "col"), axis=0, tiled=True),
        lax.all_gather(w_down, ("row", "col"), axis=0, tiled=True),
        lax.all_gather(gain_attn, ("row", "col"), axis=0, tiled=True),
        lax.all_gather(gain_ffn, ("row", "col"), axis=0, tiled=True),
    )
    scale_one = norm_scale(inputs)
    normed_one = inputs * scale_one
    scaled_one = (normed_one * gain_one.astype(jnp.float32)).astype(jnp.bfloat16)
    projected = jnp.dot(scaled_one, qkv_full, preferred_element_type=jnp.float32)
    shaped = projected.reshape(tok_rows, 3, head_count, HEAD_DIM)
    queries = rotate(shaped[:, 0], cos_part, sin_part).astype(jnp.bfloat16)
    key_own = (
        rotate(shaped[:, 1], cos_part, sin_part).astype(jnp.bfloat16).reshape(tok_rows, model_width)
    )
    value_own = projected[:, 2 * model_width :].astype(jnp.bfloat16)
    keys_all, values_all, seq_k, var_k = (
        lax.all_gather(key_own, "col", axis=0, tiled=True),
        lax.all_gather(value_own, "col", axis=0, tiled=True),
        lax.all_gather(seq_q, "col", axis=0, tiled=True),
        lax.all_gather(var_q, "col", axis=0, tiled=True),
    )
    group_size = keys_all.shape[0]
    stride = min(KEY_BLOCK, group_size)
    block_count = group_size // stride

    def split_blocks(key_rows, value_rows, key_seq, key_var):
        return (
            key_rows.reshape(block_count, stride, head_count, HEAD_DIM),
            value_rows.reshape(block_count, stride, head_count, HEAD_DIM),
            key_seq.reshape(block_count, stride),
            key_var.reshape(block_count, stride),
        )

    def forward_step(running, block_data):
        denominator, numerator = running
        key_block, value_block, seq_block, var_block = block_data
        weights = score_weights(queries, seq_q, var_q, key_block, seq_block, var_block, var_bias)[0]
        denominator = denominator + jnp.sum(weights, axis=-1)
        numerator = numerator + jnp.einsum(
            "hqk,khd->qhd",
            weights.astype(jnp.bfloat16),
            value_block,
            preferred_element_type=jnp.float32,
        )
        return ((denominator, numerator), None)

    (denominator, numerator), unused = lax.scan(
        forward_step,
        (
            jnp.zeros((head_count, tok_rows), jnp.float32),
            jnp.zeros((tok_rows, head_count, HEAD_DIM), jnp.float32),
        ),
        split_blocks(keys_all, values_all, seq_k, var_k),
    )
    attended = numerator / denominator.T[:, :, None]
    attn_low = attended.reshape(tok_rows, model_width).astype(jnp.bfloat16)
    hidden_state = inputs + jnp.dot(attn_low, out_full, preferred_element_type=jnp.float32)
    scale_two = norm_scale(hidden_state)
    normed_two = hidden_state * scale_two
    scaled_two = (normed_two * gain_two.astype(jnp.float32)).astype(jnp.bfloat16)
    gate_up = jnp.dot(scaled_two, gate_up_full, preferred_element_type=jnp.float32)
    hidden_units = gate_up_full.shape[1] // 2
    gate_part = gate_up[:, :hidden_units]
    upper_part = gate_up[:, hidden_units:]
    sigmoid_gate = jax.nn.sigmoid(gate_part)
    active = gate_part * sigmoid_gate
    inner_act = (active * upper_part).astype(jnp.bfloat16)
    ffn_branch = jnp.dot(inner_act, down_full, preferred_element_type=jnp.float32)
    output = (hidden_state + ffn_branch).astype(jnp.bfloat16)
    qkv_back, out_back, gate_up_back, down_back, gain_one_back, gain_two_back = (
        lax.all_gather(w_qkv, ("row", "col"), axis=0, tiled=True),
        lax.all_gather(w_out, ("row", "col"), axis=0, tiled=True),
        lax.all_gather(w_gate_up, ("row", "col"), axis=0, tiled=True),
        lax.all_gather(w_down, ("row", "col"), axis=0, tiled=True),
        lax.all_gather(gain_attn, ("row", "col"), axis=0, tiled=True),
        lax.all_gather(gain_ffn, ("row", "col"), axis=0, tiled=True),
    )
    d_inner = contract_cols(cotangent, down_back)
    d_gate = (
        d_inner * upper_part * sigmoid_gate * (1.0 + gate_part * (1.0 - sigmoid_gate))
    ).astype(jnp.bfloat16)
    d_upper = (d_inner * active).astype(jnp.bfloat16)
    d_gate_up = jnp.concatenate([d_gate, d_upper], axis=1)
    d_scaled_two = contract_cols(d_gate_up, gate_up_back)
    term_gain_two = jnp.sum(d_scaled_two * normed_two, axis=0)
    term_gate_up = contract_rows(scaled_two, d_gate_up)
    term_down = contract_rows(inner_act, cotangent)
    d_hidden = cotangent.astype(jnp.float32) + norm_back(
        d_scaled_two * gain_two_back.astype(jnp.float32), normed_two, scale_two
    )
    d_branch = d_hidden.astype(jnp.bfloat16)
    term_out = contract_rows(attn_low, d_branch)
    d_attended = contract_cols(d_branch, out_back).reshape(tok_rows, head_count, HEAD_DIM)
    d_numerator = (d_attended / denominator.T[:, :, None]).astype(jnp.bfloat16)
    centre = (jnp.sum(d_attended * attended, axis=-1) / denominator.T).T
    back_keys = (
        lax.all_gather(key_own, "col", axis=0, tiled=True),
        lax.all_gather(value_own, "col", axis=0, tiled=True),
        lax.all_gather(seq_q, "col", axis=0, tiled=True),
        lax.all_gather(var_q, "col", axis=0, tiled=True),
    )

    def query_step(running, block_data):
        d_queries, same_sum, other_sum = running
        key_block, value_block, seq_block, var_block = block_data
        weights, matched = score_weights(
            queries, seq_q, var_q, key_block, seq_block, var_block, var_bias
        )
        d_probs = jnp.einsum(
            "qhd,khd->hqk", d_numerator, value_block, preferred_element_type=jnp.float32
        )
        d_scores = weights * (d_probs - centre[:, :, None])
        same_sum = same_sum + jnp.sum(jnp.where(matched[None], d_scores, 0.0), axis=(1, 2))
        other_sum = other_sum + jnp.sum(jnp.where(matched[None], 0.0, d_scores), axis=(1, 2))
        d_rounded = d_scores.astype(jnp.bfloat16)
        d_queries = d_queries + jnp.einsum(
            "hqk,khd->qhd", d_rounded, key_block, preferred_element_type=jnp.float32
        )
        return ((d_queries, same_sum, other_sum), (d_rounded, weights.astype(jnp.bfloat16)))

    def query_and_key_step(running, block_data):
        running, rounded = query_step(running, block_data)
        d_rounded, weights_low = rounded
        d_keys = (
            jnp.einsum("hqk,qhd->khd", d_rounded, queries, preferred_element_type=jnp.float32)
            * 0.125
        )
        d_values = jnp.einsum(
            "hqk,qhd->khd", weights_low, d_numerator, preferred_element_type=jnp.float32
        )
        return (running, (d_keys, d_values))

    start_running = (
        jnp.zeros((tok_rows, head_count, HEAD_DIM), jnp.float32),
        jnp.zeros((head_count,), jnp.float32),
        jnp.zeros((head_count,), jnp.float32),
    )
    (d_queries, same_sum, other_sum), (d_keys, d_values) = lax.scan(
        query_and_key_step,
        start_running,
        split_blocks(back_keys[0], back_keys[1], back_keys[2], back_keys[3]),
    )
    key_grad, value_grad = (
        lax.psum_scatter(
            d_keys.reshape(group_size, model_width).astype(jnp.bfloat16),
            "col",
            scatter_dimension=0,
            tiled=True,
        ).astype(jnp.float32),
        lax.psum_scatter(
            d_values.reshape(group_size, model_width).astype(jnp.bfloat16),
            "col",
            scatter_dimension=0,
            tiled=True,
        ).astype(jnp.float32),
    )
    d_query_pre = unrotate(d_queries * 0.125, cos_part, sin_part).reshape(tok_rows, model_width)
    d_key_pre = unrotate(
        key_grad.reshape(tok_rows, head_count, HEAD_DIM), cos_part, sin_part
    ).reshape(tok_rows, model_width)
    d_projected = jnp.concatenate([d_query_pre, d_key_pre, value_grad], axis=1).astype(jnp.bfloat16)
    d_scaled_one = contract_cols(d_projected, qkv_back)
    term_qkv = contract_rows(scaled_one, d_projected)
    term_gain_one = jnp.sum(d_scaled_one * normed_one, axis=0)
    grad_w_qkv, grad_w_out, grad_w_gate_up, grad_w_down, grad_gain_attn, grad_gain_ffn = (
        lax.psum_scatter(term_qkv, ("row", "col"), scatter_dimension=0, tiled=True),
        lax.psum_scatter(term_out, ("row", "col"), scatter_dimension=0, tiled=True),
        lax.psum_scatter(term_gate_up, ("row", "col"), scatter_dimension=0, tiled=True),
        lax.psum_scatter(term_down, ("row", "col"), scatter_dimension=0, tiled=True),
        lax.psum_scatter(term_gain_one, ("row", "col"), scatter_dimension=0, tiled=True),
        lax.psum_scatter(term_gain_two, ("row", "col"), scatter_dimension=0, tiled=True),
    )
    grad_var_bias = lax.psum(jnp.stack([same_sum, other_sum], axis=0), ("row", "col"))
    d_inputs = d_hidden + norm_back(
        d_scaled_one * gain_one_back.astype(jnp.float32), normed_one, scale_one
    )
    returned = lax.all_to_all(
        d_inputs.astype(jnp.bfloat16).reshape(n_col, piece_len, model_width),
        "col",
        split_axis=0,
        concat_axis=0,
        tiled=True,
    )
    grad_tokens = jnp.take(returned, target, axis=0).reshape(tok_rows, model_width)
    return (
        output,
        grad_tokens,
        grad_w_qkv,
        grad_w_out,
        grad_w_gate_up,
        grad_w_down,
        grad_gain_attn,
        grad_gain_ffn,
        grad_var_bias,
    )


PLANES = 4
QUAD = 4
MEMBERS = 8
WINDOW = 512
AUG = 128
f32 = jnp.float32
bf16 = jnp.bfloat16
VM = pl.BlockSpec(memory_space=pltpu.VMEM)
SM = pl.BlockSpec(memory_space=pltpu.SMEM)
ANY = pl.BlockSpec(memory_space=pl.ANY)


def mm(a, b):
    return lax.dot_general(a, b, (((1,), (0,)), ((), ())), preferred_element_type=f32)


def mm_nt(a, b):
    return lax.dot_general(a, b, (((1,), (1,)), ((), ())), preferred_element_type=f32)


def mm_tn(a, b):
    return lax.dot_general(a, b, (((0,), (0,)), ((), ())), preferred_element_type=f32)


def flip(value, bits):
    for bit in (1, 2, 4, 8, 16):
        if bits & bit:
            value = value + bit * (1 - 2 * ((value // bit) % 2))
    return value


def places():
    row = lax.axis_index("row")
    col = lax.axis_index("col")
    return row, col, col // QUAD, row * QUAD + col % QUAD


def in_plane(row, col, bits):
    return flip(row, bits // QUAD), flip(col, bits % QUAD)


def in_line(row, col, bits):
    return row, flip(col, bits // 2 * QUAD + bits % 2)


def on_line(row, col, bits):
    return row, flip(col, bits * QUAD)


def anyone(row, col, bits):
    return flip(row, bits // 16), flip(col, bits % 16)


def push(source, target, send, recv, device):
    return pltpu.make_async_remote_copy(
        src_ref=source,
        dst_ref=target,
        send_sem=send,
        recv_sem=recv,
        device_id={"row": device[0], "col": device[1]},
        device_id_type=pl.DeviceIdType.MESH,
    )


def greet(devices):
    barrier = pltpu.get_barrier_semaphore()
    for device in devices:
        pl.semaphore_signal(
            barrier,
            1,
            device_id={"row": device[0], "col": device[1]},
            device_id_type=pl.DeviceIdType.MESH,
        )
    return len(devices)


def wait_for(number):
    pl.semaphore_wait(pltpu.get_barrier_semaphore(), number)


NEAR = (2, 4, 6, 1)


def plane_near(row, col):
    return [in_plane(row, col, bits) for bits in NEAR]


def line_all(row, col):
    return [on_line(row, col, bits) for bits in (1, 2, 3)]


def column_all(row, col):
    return [
        (flip(row, bits // 4), flip(col, bits % 4 * QUAD)) for bits in (1, 2, 3, 5, 6, 7)
    ]


class Gather:
    def __init__(self, target, send, recv, peer=in_plane, place=None):
        self.target, self.send, self.recv, self.peer = target, send, recv, peer
        self.row, self.col, _, self.place = places()
        if place is not None:
            self.place = place
        self.copies, self.onward = {}, {}

    def start(self, source):
        for bits in NEAR:
            self.copies[bits] = push(
                source,
                self.target.at[self.place],
                self.send.at[bits],
                self.recv.at[bits],
                self.peer(self.row, self.col, bits),
            )
            self.copies[bits].start()

    def forward(self, bits):
        self.copies[bits].wait_recv()
        slot = self.target.at[flip(self.place, bits)]
        self.onward[bits] = push(
            slot,
            slot,
            self.send.at[bits + 1],
            self.recv.at[bits + 1],
            self.peer(self.row, self.col, 1),
        )
        self.onward[bits].start()

    def arrived(self, bits):
        (self.onward[bits] if bits else self.copies[1]).wait_recv()

    def close(self):
        for copy in list(self.copies.values()) + list(self.onward.values()):
            copy.wait_send()

    def finish(self):
        for bits in (2, 4, 6):
            self.forward(bits)
        for bits in (0, 2, 4, 6):
            self.arrived(bits)


class LineGather(Gather):
    def __init__(self, target, send, recv):
        row, col, z, _ = places()
        super().__init__(target, send, recv, in_line, z * 2 + col % 2)
        self.inner = jnp.logical_or(z == 1, z == 2)

    def start(self, source):
        for bits in (4, 2, 6, 1):
            self.copies[bits] = push(
                source,
                self.target.at[self.place],
                self.send.at[bits],
                self.recv.at[bits],
                in_line(self.row, self.col, bits),
            )
            if bits != 6:
                self.copies[bits].start()
        slot = self.target.at[flip(self.place, 4)]
        self.passing = push(
            slot, slot, self.send.at[0], self.recv.at[6], in_line(self.row, self.col, 2)
        )

        @pl.when(self.inner)
        def _():
            self.copies[6].start()

    def forward(self, bits):
        super().forward(bits)
        if bits == 4:

            @pl.when(self.inner)
            def _():
                self.passing.start()

    def close(self):
        for bits in (4, 2, 1):
            self.copies[bits].wait_send()
        for copy in self.onward.values():
            copy.wait_send()

        @pl.when(self.inner)
        def _():
            self.copies[6].wait_send()
            self.passing.wait_send()


class Scatter:
    def __init__(self, part, inbox, outbox, second, send, recv, peer=in_plane, place=None):
        self.part, self.inbox, self.outbox, self.second = part, inbox, outbox, second
        self.send, self.recv, self.peer = send, recv, peer
        self.row, self.col, _, self.place = places()
        if place is not None:
            self.place = place
        self.core = self.col % 2
        self.copies, self.sent = {}, []

    def near(self, chip, number):
        copy = push(
            self.part.at[2 * chip + 1 - self.core],
            self.inbox.at[number],
            self.send.at[number],
            self.recv.at[number],
            self.peer(self.row, self.col, 1),
        )
        copy.start()
        self.copies[number] = copy

    def far(self, bits):
        self.copies[bits].wait_recv()
        chip = flip(self.place // 2, bits)
        total = self.part[2 * chip + self.core].astype(f32) + self.inbox[bits].astype(f32)
        self.outbox[bits - 1] = total.astype(bf16)
        copy = push(
            self.outbox.at[bits - 1],
            self.second.at[bits - 1],
            self.send.at[3 + bits],
            self.recv.at[3 + bits],
            self.peer(self.row, self.col, 2 * bits),
        )
        copy.start()
        self.sent.append(copy)

    def near_all(self):
        for bits in range(4):
            self.near(flip(self.place // 2, bits), bits)

    def far_all(self):
        for bits in (3, 2, 1):
            self.far(bits)

    def finish(self):
        self.copies[0].wait_recv()
        total = self.part[self.place].astype(f32) + self.inbox[0].astype(f32)
        for copy in self.sent:
            copy.wait_recv()
        for i in range(3):
            total = total + self.second[i].astype(f32)
        return total

    def close(self):
        for copy in list(self.copies.values()) + self.sent:
            copy.wait_send()


class LineScatter(Scatter):
    def __init__(self, part, inbox, outbox, second, send, recv, passed, sems):
        row, col, z, _ = places()
        super().__init__(part, inbox, outbox, second, send, recv, in_line, z * 2 + col % 2)
        self.passed, self.sems = passed, sems
        self.inner = jnp.logical_or(z == 1, z == 2)
        self.end = jnp.logical_not(self.inner)

    def sum_for(self, bits):
        self.copies[bits].wait_recv()
        chip = flip(self.place // 2, bits)
        return self.part[2 * chip + self.core].astype(f32) + self.inbox[bits].astype(f32)

    def sum_again(self, bits):
        chip = flip(self.place // 2, bits)
        return self.part[2 * chip + self.core].astype(f32) + self.inbox[bits].astype(f32)

    def to(self, bits):
        return push(
            self.outbox.at[bits - 1],
            self.second.at[bits - 1],
            self.send.at[3 + bits],
            self.recv.at[3 + bits],
            in_line(self.row, self.col, 2 * bits),
        )

    def far(self, bits):
        self.outbox[bits - 1] = self.sum_for(bits).astype(bf16)
        if bits == 1:
            self.sent.append(self.to(1))
            self.sent[-1].start()
        if bits == 2:
            self.added = self.to(2)
            self.sent.append(self.added)

            @pl.when(self.end)
            def _():
                self.added.start()

        if bits == 3:
            self.across = self.to(3)
            self.passing = push(
                self.outbox.at[2],
                self.passed,
                self.sems.at[0],
                self.sems.at[1],
                in_line(self.row, self.col, 2),
            )

            @pl.when(self.end)
            def _():
                self.passing.start()
                self.second[2] = jnp.zeros(self.second.shape[1:], bf16)

            @pl.when(self.inner)
            def _():
                self.across.start()

    def far_second(self):
        @pl.when(self.inner)
        def _():
            self.passing.wait_recv()
            total = self.sum_again(2) + self.passed[...].astype(f32)
            self.outbox[1] = total.astype(bf16)
            self.added.start()

    def finish(self):
        @pl.when(self.inner)
        def _():
            self.across.wait_recv()

        return super().finish()

    def close(self):
        super().close()

        @pl.when(self.inner)
        def _():
            self.across.wait_send()

        @pl.when(self.end)
        def _():
            self.passing.wait_send()


def scatter_scratch(rows, width):
    return [
        pltpu.VMEM((4, rows, width), bf16),
        pltpu.VMEM((3, rows, width), bf16),
        pltpu.VMEM((3, rows, width), bf16),
        pltpu.SemaphoreType.DMA((7,)),
        pltpu.SemaphoreType.DMA((7,)),
    ]


def fetch(source, target, semaphore):
    copy = pltpu.make_async_copy(source, target, semaphore)
    copy.start()
    return copy


def block(number, size):
    return pl.ds(pl.multiple_of(number * size, size), size)


def enter_body(
    x, wq, wo, wg, cot, ga, gf, variate, time, lengths, deal, freq,
    xp_out, wt_out, wop, wgp, s1_out, qkvt, gains, labels, cots,
    cotr, xp, s1, keep, wqs, wline, wqp, wgs, tile, tl, tiles, wt, box, cs, sn, times,
    sx, rx, sq, rq, sv, rv, st, rt, su, ru, sw, rw, sg, rg, sz, rz, sc, rc,
):
    row, col, z, place = places()
    quarter = col % QUAD
    y, core = col // 2 % 2, col % 2
    member = z * 2 + core
    present = greet([anyone(row, col, bits) for bits in range(1, 32)])
    lane = lax.broadcasted_iota(jnp.int32, (1, 128), 1)
    for line, gain in ((0, ga), (1, gf)):
        wide = gain[...].astype(f32)
        wide = jnp.concatenate([wide] * 4, axis=1)
        tile[line : line + 1, :] = jnp.where(lane // 32 == quarter, wide, 0.0)
    tile[2:3, :] = variate[...].astype(f32)
    tile[3:4, :] = time[...].astype(f32)
    numbers = jnp.zeros((1, 128), jnp.int32)
    for i in range(NSEQ):
        numbers = jnp.where(lane == i, lengths[0, i], numbers)
    tile[4:5, :] = numbers.astype(f32)
    tile[5:8, :] = jnp.zeros((3, 128), f32)
    for p in range(MEMBERS):
        for part in range(3):
            at = part * 1024 + p * 128
            wqs[p, :, part * 128 : part * 128 + 128] = wq[:, at : at + 128]
    for p in range(MEMBERS):
        for half in range(2):
            for plane in range(PLANES):
                unit = (p // QUAD) * 16 + plane * QUAD + p % QUAD
                at = half * 512 + plane * 128
                start = half * 4096 + unit * 128
                wgs[p, :, at : at + 128] = wg[:, start : start + 128]
    xp[member] = x[...]
    wline[member] = wqs[member]
    tl[z] = tile[...]
    wait_for(present)
    first = []
    for bits in range(1, 8):
        there = in_line(row, col, bits)
        first.append(push(wqs.at[flip(member, bits)], wline.at[member], sq.at[bits], rq.at[bits], there))
        first[-1].start()
    for bits in (1, 2, 3):
        first.append(push(tile, tl.at[z], st.at[bits], rt.at[bits], on_line(row, col, bits)))
        first[-1].start()
    rows_in = LineGather(xp, sx, rx)
    blocks = []
    for bits in range(1, 8):
        there = in_plane(row, col, bits)
        blocks.append(
            push(wgs.at[flip(place, bits)], wgp.at[place], sg.at[bits], rg.at[bits], there)
        )
        blocks[-1].start()
    wgp[place] = wgs[place]
    for copy in first:
        copy.wait_recv()
    rows_in.start(x)
    column = row * 2 + y
    beside, across = (row, flip(col, 2)), (flip(row, 1), col)
    ways = [
        push(wline, wqp.at[column], sv.at[1], rv.at[1], beside),
        push(wline, wqp.at[column], sv.at[2], rv.at[2], across),
    ]
    for copy in ways:
        copy.start()
    wqp[column] = wline[...]
    second = []
    for bits in range(1, 8):
        there = in_plane(row, col, bits)
        second.append(push(tl, tiles.at[place], su.at[bits], ru.at[bits], there))
        second[-1].start()
    tiles[place] = tl[...]
    ways[0].wait_recv()
    slot = wqp.at[flip(column, 1)]
    ways.append(push(slot, slot, sv.at[3], rv.at[3], across))
    ways[2].start()
    for copy in second:
        copy.wait_recv()
    for k in range(8):
        lanes = slice(k * 128, k * 128 + 128)
        r, plane = k // PLANES, k % PLANES
        gains[:, lanes] = (tiles[r * QUAD, plane] + tiles[r * QUAD + 1, plane]) + (
            tiles[r * QUAD + 2, plane] + tiles[r * QUAD + 3, plane]
        )
        times[:, lanes] = tiles[row * QUAD + y * 2 + k % 2, k // 2]
    for k in range(16):
        labels[:, k * 128 : k * 128 + 128] = tiles[row * QUAD + k % QUAD, k // QUAD]
    phases = times[3:4, :] * freq[...]
    cs[...] = jnp.cos(phases)
    sn[...] = jnp.sin(phases)
    gain = gains[0:1, :]

    def scale(chip):
        values = jnp.concatenate([xp[2 * chip], xp[2 * chip + 1]], axis=0).astype(f32)
        scaled = (values * norm_scale(values) * gain).astype(bf16)
        s1[2 * chip] = scaled[0:128]
        s1[2 * chip + 1] = scaled[128:256]

    rows_in.arrived(0)
    scale(z)
    rows_in.forward(4)
    rows_in.forward(2)
    for copy in ways[1:]:
        copy.wait_recv()
    for k in range(8):
        r, plane = k // PLANES, k % PLANES
        wt[:, k * 128 : k * 128 + 128] = jnp.transpose(
            jnp.concatenate(
                [wqp[r * 2 + j // 2, plane * 2 + j % 2] for j in range(4)], axis=0
            )
        )
    kept = [fetch(wt, wt_out, keep.at[2])]

    def project(chip):
        rows = block(chip, 256)
        scaled = jnp.concatenate([s1[2 * chip], s1[2 * chip + 1]], axis=0)
        out = mm_nt(wt[...], scaled)
        cos_part, sin_part = cs[:, rows], sn[:, rows]
        for head in range(2):
            for part in range(2):
                base = part * 128 + head * 64
                former, latter = out[base : base + 32], out[base + 32 : base + 64]
                factor = 0.125 if part == 0 else 1.0
                turned = former * cos_part - latter * sin_part
                other = latter * cos_part + former * sin_part
                at = part * 64
                box[head, at : at + 32, rows] = (turned * factor).astype(bf16)
                box[head, at + 32 : at + 64, rows] = (other * factor).astype(bf16)
            at = 256 + head * 64
            box[head, 128:192, rows] = out[at : at + 64].astype(bf16)

    pieces = []
    for bits in range(1, 16):
        there = (row, flip(col, bits))
        pieces.append(push(cot.at[there[1]], cotr.at[col], sc.at[bits], rc.at[bits], there))
        pieces[-1].start()
    cotr[col] = cot[col]
    turned = []

    def exchange(chip, number):
        lanes = pl.ds(pl.multiple_of(chip * 512 + y * 256, 256), 256)
        copy = push(
            box.at[1 - y, :, block(chip, 256)],
            qkvt.at[:, lanes],
            sz.at[number],
            rz.at[number],
            (row, flip(col, 2)),
        )
        copy.start()
        turned.append(copy)
        qkvt[:, lanes] = box[y, :, block(chip, 256)]

    for k, bits in enumerate((0, 4, 2, 6)):
        if bits == 6:
            rows_in.forward(6)
        chip = flip(z, bits // 2)
        if bits:
            rows_in.arrived(bits)
            scale(chip)
        project(chip)
        exchange(chip, k)
        if bits == 2:
            target = col // 2 % 2 * 2 + col // 4 % 2
            slot = row * 2 + col % 2
            for plane in range(PLANES):
                there = (col // 8, plane * QUAD + target)
                mine = jnp.logical_and(row * 16 + col == there[0] * 16 + there[1], z == plane)

                @pl.when(jnp.logical_not(mine))
                def _():
                    push(wo, wop.at[slot], sw.at[plane], rw.at[slot], there).start()

                @pl.when(mine)
                def _():
                    wop[slot] = wo[...]

    kept.append(fetch(xp, xp_out, keep.at[0]))
    kept.append(fetch(s1, s1_out, keep.at[1]))
    for copy in blocks:
        copy.wait_recv()
    for j in range(4):
        source = (j // 2, row * 8 + core * 4 + y * 2 + j % 2)
        mine = jnp.logical_and(row == source[0], col == source[1])

        @pl.when(jnp.logical_not(mine))
        def _():
            push(wo, wop.at[j], sw.at[j], rw.at[j], source).wait_recv()

    target = col // 2 % 2 * 2 + col // 4 % 2
    slot = row * 2 + col % 2
    for plane in range(PLANES):
        there = (col // 8, plane * QUAD + target)
        mine = jnp.logical_and(row * 16 + col == there[0] * 16 + there[1], z == plane)

        @pl.when(jnp.logical_not(mine))
        def _():
            push(wo, wop.at[slot], sw.at[plane], rw.at[slot], there).wait_send()

    for copy in pieces:
        copy.wait_recv()
    for j in range(16):
        cots[j * 8 : j * 8 + 8, :] = cotr[jnp.clip(deal[j], 0, 15)]
    for copy in turned:
        copy.wait()
    rows_in.close()
    for copy in first + second + blocks + ways + pieces:
        copy.wait_send()
    for copy in kept:
        copy.wait()


def split_three(value):
    high = value.astype(bf16).astype(f32)
    middle = (value - high).astype(bf16).astype(f32)
    return high, middle, (value - high - middle).astype(bf16).astype(f32)


def window_queries(qa, lanes, first, limit, width):
    place = first + lax.broadcasted_iota(jnp.int32, (16, width), 1)
    line = lax.broadcasted_iota(jnp.int32, (16, width), 0)
    extra = jnp.where(
        jnp.logical_and(line == 12, place >= limit), -1e30, qa[64:80, lanes].astype(f32)
    )
    return jnp.concatenate(
        [qa[0:64, lanes], extra.astype(bf16), jnp.zeros((AUG - 80, width), bf16)], axis=0
    )


def over_windows(start, length, window):
    wide = (length + 1) // 4

    def step(j, unused):
        window((start + 4 * j) * 128, WINDOW)
        return unused

    lax.fori_loop(0, wide, step, 0)

    @pl.when(4 * wide < length)
    def _():
        window((start + 4 * wide) * 128, WINDOW // 2)


def head_of():
    row, col, z, place = places()
    return (z * 2 + col % 2) * 2 + col // 2 % 2


def read_lengths(labels, info):
    lane = lax.broadcasted_iota(jnp.int32, (1, 128), 1)
    numbers = labels[4:5, 0:128]
    for i in range(NSEQ):
        info[i] = jnp.sum(jnp.where(lane == i, numbers, 0.0)).astype(jnp.int32)


def over_keys(start, length, step, carry):
    carry = lax.fori_loop(
        0, length // 2, lambda k, c: step((start + 2 * k) * 128, 256, c), carry
    )
    return lax.fori_loop(
        0, length % 2, lambda k, c: step((start + length - 1) * 128, 128, c), carry
    )


def attend_body(bias_all, qkvt, labels, att, den, low, qa, ka, kt, info):
    size = qkvt.shape[1]
    head = head_of()
    bias = (bias_all[0, head], bias_all[1, head])
    variate = labels[2:3, :]
    line = lax.broadcasted_iota(jnp.int32, (16, size), 0)
    same = (variate == (line % 4).astype(f32)).astype(f32)
    same_pieces = split_three(jnp.full((16, size), bias[0] - bias[1], f32))
    other_pieces = split_three(jnp.full((16, size), bias[1], f32))

    def choose(pieces, number):
        return jnp.where(number == 0, pieces[0], jnp.where(number == 1, pieces[1], pieces[2]))

    extra_q = jnp.where(line < 12, same, jnp.where(line == 12, 0.0, 1.0))
    extra_k = jnp.where(
        line < 12,
        same * choose(same_pieces, line // 4),
        jnp.where(line == 12, 1.0, choose(other_pieces, line - 13)),
    )
    qa[0:64, 0:size] = qkvt[0:64, :]
    qa[64:80, 0:size] = extra_q.astype(bf16)
    qa[80:AUG, 0:size] = jnp.zeros((AUG - 80, size), bf16)
    qa[:, size:] = jnp.zeros((AUG, WINDOW), bf16)
    kt[0:64, :] = qkvt[64:128, :]
    kt[64:80, :] = extra_k.astype(bf16)
    kt[80:AUG, :] = jnp.zeros((AUG - 80, size), bf16)
    ka[...] = jnp.transpose(kt[...])
    read_lengths(labels, info)

    def sequence(number, start):
        length = info[number]
        limit = (start + length) * 128

        def window(first, width):
            lanes = pl.ds(pl.multiple_of(first, 128), width)
            queries = window_queries(qa, lanes, first, limit, width)

            def keys(first_key, count, running):
                total, numerator = running
                rows = pl.ds(pl.multiple_of(first_key, 128), count)
                weights = jnp.exp(mm(ka[rows, :], queries))
                total = total + jnp.sum(weights, axis=0, keepdims=True)
                numerator = numerator + mm(qkvt[128:192, rows], weights.astype(bf16))
                return total, numerator

            total, numerator = over_keys(
                start, length, keys, (jnp.zeros((1, width), f32), jnp.zeros((64, width), f32))
            )
            attended = numerator / total
            att[:, lanes] = attended
            den[:, lanes] = jnp.broadcast_to(total, (8, width))
            low[:, lanes] = attended.astype(bf16)

        over_windows(start, length, window)
        return start + length

    lax.fori_loop(0, NSEQ, sequence, 0)


def attend_back_body(
    qkvt, qa, ka, labels, freq, grad, att, den,
    dproj, bias_tile,
    dn, cw, vn, dq, dk, dv, info,
):
    size = qkvt.shape[1]
    lanes_all = slice(0, size)
    inverse = 1.0 / den[0:1, lanes_all]
    d_att = grad[...].astype(f32)
    dn[:, lanes_all] = (d_att * inverse).astype(bf16)
    dn[:, size:] = jnp.zeros((64, WINDOW), bf16)
    cw[:, lanes_all] = jnp.broadcast_to(
        jnp.sum(d_att * att[:, lanes_all], axis=0, keepdims=True) * inverse, (8, size)
    )
    cw[:, size:] = jnp.zeros((8, WINDOW), f32)
    vn[...] = jnp.transpose(qkvt[128:192, :])
    dk[...] = jnp.zeros_like(dk)
    dv[...] = jnp.zeros_like(dv)

    read_lengths(labels, info)

    def sequence(number, start):
        length = info[number]
        limit = (start + length) * 128

        def window(first, width):
            lanes = pl.ds(pl.multiple_of(first, 128), width)
            queries = window_queries(qa, lanes, first, limit, width)
            upstream = dn[:, lanes]
            centre = cw[0:1, lanes]

            def keys(first_key, count, running):
                rows = pl.ds(pl.multiple_of(first_key, 128), count)
                weights = jnp.exp(mm(ka[rows, :], queries))
                d_scores = weights * (mm(vn[rows, :], upstream) - centre)
                rounded = d_scores.astype(bf16)
                dk[:, rows] += mm_nt(queries, rounded)
                dv[:, rows] += mm_nt(upstream, weights.astype(bf16))
                return running + mm(qkvt[64:128, rows], rounded)

            dq[:, lanes] = over_keys(start, length, keys, jnp.zeros((64, width), f32))

        over_windows(start, length, window)
        return start + length

    lax.fori_loop(0, NSEQ, sequence, 0)

    phases = labels[3:4, :] * freq[...]
    cos_part, sin_part = jnp.cos(phases), jnp.sin(phases)
    for part, source, factor in ((0, dq, 0.125), (1, dk, 1.0)):
        former, latter = source[0:32, lanes_all], source[32:64, lanes_all]
        dproj[part * 64 : part * 64 + 32, :] = (
            (former * cos_part + latter * sin_part) * factor
        ).astype(bf16)
        dproj[part * 64 + 32 : part * 64 + 64, :] = (
            (latter * cos_part - former * sin_part) * factor
        ).astype(bf16)
    dproj[128:192, :] = dv[...].astype(bf16)
    variate = labels[2:3, :]
    line = lax.broadcasted_iota(jnp.int32, (16, size), 0)
    match = jnp.logical_and(variate == line.astype(f32), line < 4)
    near = jnp.sum(jnp.where(match, dk[64:80, :], 0.0))
    every = jnp.sum(dk[77:78, :])
    lane = lax.broadcasted_iota(jnp.int32, (8, 128), 1)
    line8 = lax.broadcasted_iota(jnp.int32, (8, 128), 0)
    here = lane == head_of()
    bias_tile[...] = jnp.where(
        jnp.logical_and(here, line8 == 2),
        near,
        jnp.where(jnp.logical_and(here, line8 == 3), every - near, 0.0),
    )


def branch_body(
    low, wop, x, gains, cots,
    atp, hidden, s2, cotp_out,
    cotp, keep, atn, part, sz, rz, sa, ra, inbox, outbox, second, ss, rs,
):
    row, col, z, place = places()
    quarter = col % QUAD
    present = greet(plane_near(row, col) + column_all(row, col))
    rows, lanes = block(z // 2, 64), block(row, 512)
    cotp[place] = cots[...]
    wait_for(present)
    for plane in range(PLANES):
        mine = jnp.logical_and(row == z % 2, z == plane)

        @pl.when(jnp.logical_not(mine))
        def _():
            push(
                low.at[:, plane * 512 : plane * 512 + 512], atp.at[rows, lanes],
                sz.at[plane], rz.at[row * 2 + z // 2], (z % 2, plane * QUAD + quarter),
            ).start()

        @pl.when(mine)
        def _():
            atp[rows, lanes] = low[:, plane * 512 : plane * 512 + 512]

    cot_in = Gather(cotp, sa, ra)
    cot_in.start(cots)
    for j in range(4):
        source = (j // 2, (row + 2 * (j % 2)) * QUAD + quarter)
        mine = jnp.logical_and(row == j // 2, z == row + 2 * (j % 2))

        @pl.when(jnp.logical_not(mine))
        def _():
            push(
                low.at[:, 0:512], atp.at[0:64, 0:512], sz.at[j], rz.at[j], source
            ).wait_recv()

    for plane in range(PLANES):
        mine = jnp.logical_and(row == z % 2, z == plane)

        @pl.when(jnp.logical_not(mine))
        def _():
            push(
                low.at[:, plane * 512 : plane * 512 + 512], atp.at[rows, lanes],
                sz.at[plane], rz.at[row * 2 + z // 2], (z % 2, plane * QUAD + quarter),
            ).wait_send()

    atn[...] = jnp.transpose(atp[...])
    total = Scatter(part, inbox, outbox, second, ss, rs)
    core = col % 2
    for bits in (3, 2, 1, 0):
        chip = flip(place // 2, bits)
        part[2 * chip + 1 - core] = mm(atn[block(2 * chip + 1 - core, 128), :], wop[...]).astype(bf16)
    for bits in range(4):
        total.near(flip(place // 2, bits), bits)
    for bits in (3, 2, 1, 0):
        chip = flip(place // 2, bits)
        part[2 * chip + core] = mm(atn[block(2 * chip + core, 128), :], wop[...]).astype(bf16)
    total.far_all()
    cot_in.finish()
    kept = fetch(cotp, cotp_out, keep.at[0])
    state = x[...].astype(f32) + total.finish()
    hidden[...] = state
    s2[...] = (state * norm_scale(state) * gains[1:2, :]).astype(bf16)
    total.close()
    cot_in.close()
    kept.wait()


def ffn_body(
    s2, cotp_in, wg_in, w_down, hidden, gains,
    out_keep, down_in, gwg_out, d_hidden, low, gain_term,
    cotp, wg, s2p, wgs, wd, actives, factors, inner_s, dgu, d_part, out_part, gwd, gwg, relayed, both_terms,
    keep, sa, ra, sw, rw, sd, rd, inbox, outbox, second, ss, rs,
):
    row, col, z, place = places()
    loads = [fetch(wg_in, wg, keep.at[0]), fetch(cotp_in, cotp, keep.at[1])]
    present = greet(plane_near(row, col) + line_all(row, col))
    s2p[place] = s2[...]
    wd[block(z, 128), :] = w_down[...]
    loads[0].wait()
    for plane in range(PLANES):
        for r in range(2):
            at = (r * PLANES + plane) * 128
            wgs[at : at + 128, :] = wg[plane * 2 + r]
    wait_for(present)
    rows_in = Gather(s2p, sa, ra)
    rows_in.start(s2)
    inner = jnp.logical_or(z == 1, z == 2)
    end = jnp.logical_not(inner)
    downs = {
        bits: push(
            w_down, wd.at[block(z, 128), :], sw.at[bits], rw.at[bits], on_line(row, col, bits)
        )
        for bits in (2, 1, 3)
    }
    passed = wd.at[block(flip(z, 2), 128), :]
    downs[0] = push(passed, passed, sw.at[0], rw.at[3], on_line(row, col, 1))
    downs[2].start()

    @pl.when(inner)
    def _():
        downs[3].start()

    downs[1].start()
    for k in range(4):
        chip = flip(place // 2, k)
        if k:
            rows_in.forward(2 * k)
        rows_in.arrived(2 * k)
        if k == 2:
            downs[2].wait_recv()

            @pl.when(inner)
            def _():
                downs[0].start()

        rows = block(chip, 256)
        scaled = jnp.concatenate([s2p[2 * chip], s2p[2 * chip + 1]], axis=0)
        both = mm(scaled, wgs[...])
        gate, upper = both[:, 0:512], both[:, 512:1024]
        sig = jax.nn.sigmoid(gate)
        active = gate * sig
        inner_s[rows, :] = (active * upper).astype(bf16)
        actives[rows, :] = active
        factors[rows, :] = upper * sig * (1.0 + gate * (1.0 - sig))
    loads[1].wait()
    cot_all = jnp.concatenate([cotp[t] for t in range(MEMBERS)], axis=0)
    for k in range(4):
        cols = slice(k * 128, k * 128 + 128)
        gwd[k] = mm_tn(inner_s[:, cols], cot_all).astype(bf16)
    grads = {
        bits: push(
            gwd.at[flip(z, bits)], down_in.at[bits], sd.at[bits], rd.at[bits], on_line(row, col, bits)
        )
        for bits in (1, 3)
    }
    grads[2] = push(both_terms, down_in.at[2], sd.at[2], rd.at[2], on_line(row, col, 2))
    grads[0] = push(gwd.at[flip(z, 3)], relayed, sd.at[0], rd.at[0], on_line(row, col, 1))

    @pl.when(end)
    def _():
        grads[0].start()
        both_terms[...] = gwd[flip(z, 2)]
        grads[2].start()
        down_in[3] = jnp.zeros(down_in.shape[1:], bf16)

    @pl.when(inner)
    def _():
        grads[3].start()

    grads[1].start()
    down_in[0] = gwd[z]
    total = Scatter(d_part, inbox, outbox, second, ss, rs)
    downs[1].wait_recv()
    downs[3].wait_recv()
    for k in range(4):
        chip = flip(place // 2, k)
        rows = block(chip, 256)
        upstream = jnp.concatenate([cotp[2 * chip], cotp[2 * chip + 1]], axis=0)
        d_inner = mm_nt(upstream, wd[...])
        dgu[rows, 0:512] = (d_inner * factors[rows, :]).astype(bf16)
        dgu[rows, 512:1024] = (d_inner * actives[rows, :]).astype(bf16)
        tile = mm_nt(dgu[rows, :], wgs[...]).astype(bf16)
        d_part[2 * chip] = tile[0:128]
        d_part[2 * chip + 1] = tile[128:256]
        total.near(chip, k)
        if k > 1:
            total.far(k - 1)
    for k in range(4):
        chip = flip(place // 2, k)
        tile = mm(inner_s[block(chip, 256), :], wd[...]).astype(bf16)
        out_part[2 * chip] = tile[0:128]
        out_part[2 * chip + 1] = tile[128:256]
        if k == 0:
            total.far(3)
        if k == 0:

            @pl.when(inner)
            def _():
                grads[0].wait_recv()
                both_terms[...] = (
                    gwd[flip(z, 2)].astype(f32) + relayed[...].astype(f32)
                ).astype(bf16)
                grads[2].start()
    kept = [fetch(out_part, out_keep, keep.at[10])]
    for f in range(8):
        cols = slice(f * 128, f * 128 + 128)
        lhs = jnp.concatenate([s2p[t, :, cols] for t in range(MEMBERS)], axis=0)
        at = (f % PLANES) * 2 + f // PLANES
        gwg[at] = mm_tn(lhs, dgu[...]).astype(bf16)
        kept.append(fetch(gwg.at[at], gwg_out.at[at], keep.at[2 + f]))
    d_scaled = total.finish()
    state = hidden[...]
    scale = norm_scale(state)
    normed = state * scale
    gain_term[...] = jnp.broadcast_to(jnp.sum(d_scaled * normed, axis=0, keepdims=True), (8, 1024))
    d_state = cotp[place].astype(f32) + norm_back(d_scaled * gains[1:2, :], normed, scale)
    d_hidden[...] = d_state
    low[...] = d_state.astype(bf16)
    rows_in.close()
    total.close()
    grads[1].wait_recv()
    grads[2].wait_recv()
    for copy in (downs[1], downs[2], grads[1], grads[2]):
        copy.wait_send()

    @pl.when(inner)
    def _():
        grads[3].wait_recv()
        for copy in (downs[3], downs[0], grads[3]):
            copy.wait_send()

    @pl.when(end)
    def _():
        grads[0].wait_send()

    for copy in kept:
        copy.wait()


def attended_back_body(
    low, wop, atp, out_in, hidden,
    grad, gwo, rows_out,
    out_part, keep, dbp, dat, sg, rg, sz, rz, inbox, outbox, second, ss, rs,
):
    row, col, z, place = places()
    load = fetch(out_in, out_part, keep.at[0])
    present = greet(plane_near(row, col) + column_all(row, col))
    dbp[place] = low[...]
    wait_for(present)
    quarter = col % QUAD
    rows_in = Gather(dbp, sg, rg)
    rows_in.start(low)
    load.wait()
    output = Scatter(out_part, inbox, outbox, second, ss, rs)
    output.near_all()
    for k in range(4):
        chip = flip(place // 2, k)
        if k:
            rows_in.forward(2 * k)
        rows_in.arrived(2 * k)
        for core in range(2):
            dat[:, block(2 * chip + core, 128)] = mm_nt(wop[...], dbp[2 * chip + core]).astype(bf16)
        if k % 2 == 0:
            continue
        group = row if k == 1 else 1 - row
        for head in range(2):
            plane = row + 2 * head
            source = dat.at[head * 64 : head * 64 + 64, block(group, 512)]
            if k == 1:

                @pl.when(z != plane)
                def _():
                    push(
                        source, grad.at[:, block(z, 512)], sz.at[head], rz.at[z],
                        (group, plane * QUAD + quarter),
                    ).start()

                @pl.when(z == plane)
                def _():
                    grad[:, block(z, 512)] = source[...]

            else:
                push(
                    source, grad.at[:, block(z, 512)], sz.at[2 + head], rz.at[z],
                    (group, plane * QUAD + quarter),
                ).start()

    output.far_all()
    total = mm(atp[:, 0:128], dbp[0])
    for q in range(1, MEMBERS):
        total = total + mm(atp[:, q * 128 : q * 128 + 128], dbp[q])
    gwo[...] = total.astype(bf16)
    rows_out[...] = (hidden[...] + output.finish()).astype(bf16)
    output.close()
    for plane in range(PLANES):
        mine = jnp.logical_and(row == z % 2, z == plane)

        @pl.when(jnp.logical_not(mine))
        def _():
            push(
                dat.at[0:64, 0:512], grad.at[:, plane * 512 : plane * 512 + 512], sz.at[0],
                rz.at[plane], (z % 2, plane * QUAD + quarter),
            ).wait_recv()

    for head in range(2):
        plane = row + 2 * head

        @pl.when(z != plane)
        def _():
            push(
                dat.at[0:64, 0:512], grad.at[:, 0:512], sz.at[head], rz.at[z],
                (row, plane * QUAD + quarter),
            ).wait_send()

        push(
            dat.at[0:64, 0:512], grad.at[:, 0:512], sz.at[2 + head], rz.at[z],
            (1 - row, plane * QUAD + quarter),
        ).wait_send()

    rows_in.close()


def last_body(
    dproj, wt_in, s1_in, xp_in, gains, d_hidden, rows_out, gwo, gwg, gain_two, bias_tile, deal,
    grad_tokens, gqin, goin, gwg_in, sums, out,
    wt, s1, xp, pieces, slots, keep, dpt, dpn, part, gq, gqcol, gqsum, pack, packs, packed,
    passed, sz, rz, inbox, outbox, second, ss, rs, sp,
    sq, rq, sv, rv, st, rt, su, ru, sw, rw, sg, rg, sc, rc,
):
    row, col, z, place = places()
    quarter = col % QUAD
    y, core = col // 2 % 2, col % 2
    member = z * 2 + core
    column = row * 2 + y
    loads = [
        fetch(s1_in, s1, keep.at[0]),
        fetch(xp_in, xp, keep.at[1]),
        fetch(wt_in, wt, keep.at[2]),
    ]
    present = greet([anyone(row, col, bits) for bits in range(1, 32)])
    for j in range(16):
        pieces[j] = rows_out[j * 8 : j * 8 + 8, :]
    for d in range(16):
        number = 0
        for j in range(1, 16):
            number = jnp.where(deal[j] == d, j, number)
        slots[d] = pieces[number]
    gwg_in[place] = gwg[place]
    out[col] = slots[col]
    wait_for(present)
    copies = {}
    for bits in (3, 2, 1, 0):
        chip = flip(z, bits)
        ours = pl.ds(pl.multiple_of(chip * 512 + y * 256, 256), 256)
        theirs = pl.ds(pl.multiple_of(chip * 512 + (1 - y) * 256, 256), 256)
        copies[bits] = push(
            dproj.at[:, theirs], dpt.at[y, :, block(chip, 256)], sz.at[bits], rz.at[bits],
            (row, flip(col, 2)),
        )
        copies[bits].start()
        dpt[y, :, block(chip, 256)] = dproj[:, ours]
    owner = core * 4 + y * 2
    for j in range(4):
        there = (j // 2, row * 8 + owner + j % 2)
        mine = jnp.logical_and(row == there[0], col == there[1])

        @pl.when(jnp.logical_not(mine))
        def _():
            push(gwo.at[j], goin.at[z], sw.at[j], rw.at[z], there).start()

        @pl.when(mine)
        def _():
            goin[z] = gwo[j]

    spread = []
    for bits in range(1, 16):
        there = (row, flip(col, bits))
        copy = push(slots.at[there[1]], out.at[col], sc.at[bits], rc.at[bits], there)
        copy.start()
        spread.append(copy)
    for copy in loads:
        copy.wait()
    total = LineScatter(part, inbox, outbox, second, ss, rs, passed, sp)
    term = jnp.zeros((1, 1024), f32)
    for bits in (3, 2, 1, 0):
        chip = flip(z, bits)
        lanes = block(chip, 256)
        copies[bits].wait_recv()
        for kind in range(3):
            both = jnp.concatenate(
                [dpt[head, kind * 64 : kind * 64 + 64, lanes] for head in range(2)], axis=0
            )
            dpn[lanes, kind * 128 : kind * 128 + 128] = jnp.transpose(both)
        d_scaled = mm(dpn[lanes, :], wt[...])
        values = jnp.concatenate([xp[2 * chip], xp[2 * chip + 1]], axis=0).astype(f32)
        term = term + jnp.sum(d_scaled * (values * norm_scale(values)), axis=0, keepdims=True)
        part[2 * chip] = d_scaled[0:128].astype(bf16)
        part[2 * chip + 1] = d_scaled[128:256].astype(bf16)
        total.near(chip, bits)
        if bits < 3:
            total.far(bits + 1)
    for bits in range(1, 8):
        there = in_plane(row, col, bits)
        copy = push(gwg.at[flip(place, bits)], gwg_in.at[place], sg.at[bits], rg.at[bits], there)
        copy.start()
        spread.append(copy)
    for f in range(8):
        lhs = jnp.concatenate([s1[t, :, f * 128 : f * 128 + 128] for t in range(MEMBERS)], axis=0)
        chunk = mm_tn(lhs, dpn[...]).astype(bf16)
        for j in range(4):
            gq[f // PLANES * 2 + j // 2, f % PLANES * 2 + j % 2] = chunk[j * 32 : j * 32 + 32, :]
    columns = []
    for bits in (3, 2, 1):
        there = (flip(row, bits // 2), flip(col, bits % 2 * 2))
        copy = push(gq.at[flip(column, bits)], gqcol.at[bits - 1], sv.at[bits], rv.at[bits], there)
        copy.start()
        columns.append(copy)
    for k in range(8):
        pack[k] = bias_tile[...]
        pack[k, 0:1, :] = term[:, k * 128 : k * 128 + 128]
        pack[k, 1:2, :] = gain_two[0:1, k * 128 : k * 128 + 128]
    first = []
    for bits in range(1, 8):
        there = in_plane(row, col, bits)
        copy = push(
            pack.at[pl.ds(there[0] * PLANES, PLANES)], packs.at[place], st.at[bits], rt.at[bits], there
        )
        copy.start()
        first.append(copy)
    packs[place] = pack[pl.ds(row * PLANES, PLANES)]
    total.far_second()
    for copy in first:
        copy.wait_recv()
    summed = packs[0]
    for p in range(1, MEMBERS):
        summed = summed + packs[p]
    packed[...] = summed
    for bits in (1, 2, 3):
        copy = push(
            packed.at[flip(z, bits)], sums.at[z], su.at[bits], ru.at[bits], on_line(row, col, bits)
        )
        copy.start()
        spread.append(copy)
    sums[z] = packed[z]
    for copy in columns:
        copy.wait_recv()
    for m in range(MEMBERS):
        gqsum[m] = (
            (gq[column, m].astype(f32) + gqcol[0, m].astype(f32))
            + (gqcol[1, m].astype(f32) + gqcol[2, m].astype(f32))
        ).astype(bf16)
    for bits in range(7, 0, -1):
        there = in_line(row, col, bits)
        copy = push(gqsum.at[flip(member, bits)], gqin.at[member], sq.at[bits], rq.at[bits], there)
        copy.start()
        spread.append(copy)
    gqin[member] = gqsum[member]
    d_one = total.finish()
    own_rows = xp[member].astype(f32)
    scale = norm_scale(own_rows)
    grad_tokens[...] = (
        d_hidden[...] + norm_back(d_one * gains[0:1, :], own_rows * scale, scale)
    ).astype(bf16)
    for copy in spread:
        copy.wait_recv()
    senders = col // 2 % 2 * 2 + col // 4 % 2
    for plane in range(PLANES):
        mine = jnp.logical_and(row * 16 + col == (col // 8) * 16 + plane * QUAD + senders, z == plane)

        @pl.when(jnp.logical_not(mine))
        def _():
            push(
                gwo.at[0], goin.at[plane], sw.at[0], rw.at[plane],
                (col // 8, plane * QUAD + senders),
            ).wait_recv()

    for j in range(4):
        there = (j // 2, row * 8 + owner + j % 2)
        mine = jnp.logical_and(row == there[0], col == there[1])

        @pl.when(jnp.logical_not(mine))
        def _():
            push(gwo.at[j], goin.at[z], sw.at[j], rw.at[z], there).wait_send()

    for copy in list(copies.values()) + columns + first + spread:
        copy.wait_send()
    total.close()


def finish_body(
    grad_tokens_in, gqin, goin, out_in, gwg, gwd, tiles,
    out, grad_tokens, grad_q, grad_o, grad_gu, grad_d, grad_one, grad_two, grad_bias,
):
    grad_tokens[...] = grad_tokens_in[...]
    out[...] = out_in[...]
    grad_o[...] = (goin[0].astype(f32) + goin[1].astype(f32)) + (
        goin[2].astype(f32) + goin[3].astype(f32)
    )
    grad_d[...] = (gwd[0].astype(f32) + gwd[1].astype(f32)) + (
        gwd[2].astype(f32) + gwd[3].astype(f32)
    )
    for p in range(MEMBERS):
        total = gqin[p].astype(f32)
        for kind in range(3):
            at = kind * 1024 + p * 128
            grad_q[:, at : at + 128] = total[:, kind * 128 : kind * 128 + 128]
        for half in range(2):
            for plane in range(PLANES):
                unit = (p // QUAD) * 16 + plane * QUAD + p % QUAD
                at = half * 512 + plane * 128
                start = half * 4096 + unit * 128
                grad_gu[:, start : start + 128] = gwg[p, :, at : at + 128].astype(f32)
    total = (tiles[0] + tiles[1]) + (tiles[2] + tiles[3])
    quarter = lax.axis_index("col") % QUAD
    chosen = jnp.zeros((2, 32), f32)
    for k in range(4):
        chosen = chosen + jnp.where(quarter == k, total[0:2, k * 32 : k * 32 + 32], 0.0)
    grad_one[...] = chosen[0]
    grad_two[...] = chosen[1]
    grad_bias[...] = total[2:4, 0:16]


def sds(shape, dtype):
    return jax.ShapeDtypeStruct(shape, dtype)


def dma(*shape):
    return pltpu.SemaphoreType.DMA(shape)


def kernel(body, name, specs, outs, scratch, number=None, cost=0, places_out=None):
    params = dict(vmem_limit_bytes=56 << 20)
    if number is not None:
        params.update(collective_id=number, has_side_effects=True)
    return pl.pallas_call(
        body,
        name=name,
        in_specs=specs,
        out_shape=outs,
        out_specs=places_out or [VM] * len(outs),
        scratch_shapes=scratch,
        compiler_params=pltpu.CompilerParams(**params),
        cost_estimate=pl.CostEstimate(flops=cost, bytes_accessed=cost // 300, transcendentals=0),
    )


def plane_shards(
    tokens, variate_ids, time_ids, lengths, deal, w_qkv, w_out, w_gate_up, w_down,
    gain_attn, gain_ffn, var_bias, cotangent,
):
    rows, width = tokens.shape
    lines = [[plane * QUAD + k for plane in range(PLANES)] for k in range(QUAD)]
    freq = jnp.asarray(np.exp(-math.log(10000.0) * np.arange(32) / 32).astype(np.float32)[:, None])
    target = deal[0, 0]

    xp, wt, wop, wgp, s1, qkvt, gains, labels, cot = kernel(
        enter_body,
        "enter",
        [VM] * 9 + [SM, SM, VM],
        [
            sds((8, rows, width), bf16),
            sds((384, 1024), bf16),
            sds((4, 32, 1024), bf16),
            sds((8, 32, 1024), bf16),
            sds((8, rows, width), bf16),
            sds((192, 2048), bf16),
            sds((8, 1024), f32),
            sds((8, 2048), f32),
            sds((rows, width), bf16),
        ],
        [
            pltpu.VMEM((16, 8, width), bf16),
            pltpu.VMEM((8, rows, width), bf16),
            pltpu.VMEM((8, rows, width), bf16),
            dma(4),
            pltpu.VMEM((8, 32, 384), bf16),
            pltpu.VMEM((8, 32, 384), bf16),
            pltpu.VMEM((4, 8, 32, 384), bf16),
            pltpu.VMEM((8, 32, 1024), bf16),
            pltpu.VMEM((8, 128), f32),
            pltpu.VMEM((4, 8, 128), f32),
            pltpu.VMEM((8, 4, 8, 128), f32),
            pltpu.VMEM((384, 1024), bf16),
            pltpu.VMEM((2, 192, 1024), bf16),
            pltpu.VMEM((32, 1024), f32),
            pltpu.VMEM((32, 1024), f32),
            pltpu.VMEM((8, 1024), f32),
        ]
        + [dma(8), dma(8), dma(8), dma(8), dma(4), dma(4), dma(4), dma(4), dma(8), dma(8)]
        + [dma(4), dma(4), dma(8), dma(8), dma(4), dma(4), dma(16), dma(16)],
        number=1,
        places_out=[ANY, ANY, VM, VM, ANY, VM, VM, VM, VM],
    )(
        tokens, w_qkv, w_out, w_gate_up, cotangent.reshape(16, 8, width), gain_attn[None],
        gain_ffn[None], variate_ids[None], time_ids[None], lengths, target, freq,
    )

    gate_up = lax.all_gather(
        wgp.reshape(256, 1024), "col", axis=0, tiled=True, axis_index_groups=lines
    )
    wop = wop.reshape(128, 1024)

    wide = 2048 + WINDOW
    att, den, low, qa, ka = kernel(
        attend_body,
        "attend",
        [SM, VM, VM],
        [
            sds((64, wide), f32),
            sds((8, wide), f32),
            sds((64, wide), bf16),
            sds((AUG, wide), bf16),
            sds((2048, AUG), bf16),
        ],
        [pltpu.VMEM((AUG, 2048), bf16), pltpu.SMEM((8,), jnp.int32)],
        cost=2 * 10**9,
    )(var_bias, qkvt, labels)

    atp, hidden, s2, cotp = kernel(
        branch_body,
        "branch",
        [VM] * 5,
        [
            sds((128, 1024), bf16),
            sds((rows, width), f32),
            sds((rows, width), bf16),
            sds((8, rows, width), bf16),
        ],
        [
            pltpu.VMEM((8, rows, width), bf16),
            dma(1),
            pltpu.VMEM((1024, 128), bf16),
            pltpu.VMEM((8, rows, width), bf16),
            dma(4), dma(4), dma(8), dma(8),
        ]
        + scatter_scratch(rows, width),
        number=2,
        places_out=[VM, VM, VM, ANY],
    )(low, wop, tokens, gains, cot)

    out_part, down_in, gwg, d_hidden, d_branch, gain_two = kernel(
        ffn_body,
        "ffn",
        [VM, ANY, ANY, VM, VM, VM],
        [
            sds((8, rows, width), bf16),
            sds((4, rows, width), bf16),
            sds((8, 128, 1024), bf16),
            sds((rows, width), f32),
            sds((rows, width), bf16),
            sds((8, 1024), f32),
        ],
        [
            pltpu.VMEM((8, rows, width), bf16),
            pltpu.VMEM((8, 128, 1024), bf16),
            pltpu.VMEM((8, rows, width), bf16),
            pltpu.VMEM((1024, 1024), bf16),
            pltpu.VMEM((512, width), bf16),
            pltpu.VMEM((1024, 512), f32),
            pltpu.VMEM((1024, 512), f32),
            pltpu.VMEM((1024, 512), bf16),
            pltpu.VMEM((1024, 1024), bf16),
            pltpu.VMEM((8, rows, width), bf16),
            pltpu.VMEM((8, rows, width), bf16),
            pltpu.VMEM((4, rows, width), bf16),
            pltpu.VMEM((8, 128, 1024), bf16),
            pltpu.VMEM((rows, width), bf16),
            pltpu.VMEM((rows, width), bf16),
            dma(11), dma(8), dma(8), dma(4), dma(4), dma(4), dma(4),
        ]
        + scatter_scratch(rows, width),
        number=3,
        cost=10**10,
        places_out=[ANY, VM, ANY, VM, VM, VM],
    )(s2, cotp, gate_up.reshape(8, 128, 1024), w_down, hidden, gains)

    gate_up_sum = lax.psum_scatter(
        gwg.reshape(1024, 1024), "col", scatter_dimension=0, tiled=True, axis_index_groups=lines
    )

    grad, gwo, rows_out = kernel(
        attended_back_body,
        "attended_back",
        [VM, VM, VM, ANY, VM],
        [sds((64, 2048), bf16), sds((128, 1024), bf16), sds((rows, width), bf16)],
        [
            pltpu.VMEM((8, rows, width), bf16),
            dma(1),
            pltpu.VMEM((8, rows, width), bf16),
            pltpu.VMEM((128, 1024), bf16),
            dma(8), dma(8), dma(4), dma(4),
        ]
        + scatter_scratch(rows, width),
        number=4,
    )(d_branch, wop, atp, out_part, hidden)

    dproj, bias_tile = kernel(
        attend_back_body,
        "attend_back",
        [VM] * 8,
        [sds((192, 2048), bf16), sds((8, 128), f32)],
        [
            pltpu.VMEM((64, wide), bf16),
            pltpu.VMEM((8, wide), f32),
            pltpu.VMEM((2048, 64), bf16),
            pltpu.VMEM((64, wide), f32),
            pltpu.VMEM((AUG, 2048), f32),
            pltpu.VMEM((64, 2048), f32),
            pltpu.SMEM((8,), jnp.int32),
        ],
        cost=5 * 10**9,
    )(qkvt, qa, ka, labels, freq, grad, att, den)

    grad_tokens, gqin, goin, gwg_in, sums, out = kernel(
        last_body,
        "last",
        [VM] + [ANY] * 3 + [VM] * 7 + [SM],
        [
            sds((rows, width), bf16),
            sds((8, 32, 384), bf16),
            sds((4, 32, 1024), bf16),
            sds((8, 32, 1024), bf16),
            sds((4, 8, 128), f32),
            sds((16, 8, width), bf16),
        ],
        [
            pltpu.VMEM((384, 1024), bf16),
            pltpu.VMEM((8, rows, width), bf16),
            pltpu.VMEM((8, rows, width), bf16),
            pltpu.VMEM((16, 8, width), bf16),
            pltpu.VMEM((16, 8, width), bf16),
            dma(3),
            pltpu.VMEM((2, 192, 1024), bf16),
            pltpu.VMEM((1024, 384), bf16),
            pltpu.VMEM((8, rows, width), bf16),
            pltpu.VMEM((4, 8, 32, 384), bf16),
            pltpu.VMEM((3, 8, 32, 384), bf16),
            pltpu.VMEM((8, 32, 384), bf16),
            pltpu.VMEM((8, 8, 128), f32),
            pltpu.VMEM((8, 4, 8, 128), f32),
            pltpu.VMEM((4, 8, 128), f32),
            pltpu.VMEM((rows, width), bf16),
            dma(4), dma(4),
        ]
        + scatter_scratch(rows, width)
        + [dma(2), dma(8), dma(8), dma(4), dma(4), dma(8), dma(8), dma(4), dma(4)]
        + [dma(4), dma(4), dma(8), dma(8), dma(16), dma(16)],
        number=5,
    )(
        dproj, wt, s1, xp, gains, d_hidden, rows_out, gwo.reshape(4, 32, 1024),
        gate_up_sum.reshape(8, 32, 1024), gain_two, bias_tile, target,
    )
    out, grad_tokens, grad_q, grad_o, grad_gate_up, grad_down, gain_one, gain_two_grad, bias_grads = kernel(
        finish_body,
        "finish",
        [VM] * 7,
        [
            sds((rows, width), bf16),
            sds((rows, width), bf16),
            sds((32, 3072), f32),
            sds((32, 1024), f32),
            sds((32, 8192), f32),
            sds((rows, width), f32),
            sds((32,), f32),
            sds((32,), f32),
            sds((2, 16), f32),
        ],
        [],
    )(
        grad_tokens, gqin, goin, out.reshape(rows, width), gwg_in,
        down_in, sums,
    )
    return (
        out,
        grad_tokens,
        grad_q,
        grad_o,
        grad_gate_up,
        grad_down,
        gain_one,
        gain_two_grad,
        bias_grads,
    )


def solution(mesh):
    planes = mesh.shape["row"] == 2 and mesh.shape["col"] == PLANES * QUAD
    return jax.shard_map(
        plane_shards if planes else shards,
        mesh=mesh,
        in_specs=(
            P(("row", "col"), None),
            P(("row", "col")),
            P(("row", "col")),
            P("row", None),
            P("row", "col", None),
            P(("row", "col"), None),
            P(("row", "col"), None),
            P(("row", "col"), None),
            P(("row", "col"), None),
            P(("row", "col")),
            P(("row", "col")),
            P(),
            P(("row", "col"), None),
        ),
        out_specs=(
            P(("row", "col"), None),
            P(("row", "col"), None),
            P(("row", "col"), None),
            P(("row", "col"), None),
            P(("row", "col"), None),
            P(("row", "col"), None),
            P(("row", "col")),
            P(("row", "col")),
            P(),
        ),
        check_vma=False,
    )
```
